32 devices in a mesh: dp: 2 (over core), row: 4 (over y, x), col: 4 (over z).
Axes of the slice: x: 2, y: 2, z: 4, core: 2. Of those that a mesh axis runs over, the one named last changes fastest.
Arguments:
- layer_input: bfloat16 [11664, 1152], P(('dp', 'col'), 'row'), may hold values from -6 to 6
- teacher: bfloat16 [11664, 1152], P(('dp', 'col'), 'row'), may hold values from -6 to 6
- valid: int32 [11664], P(('dp', 'col')), may hold values 0 or 1
- proj_in: bfloat16 [1152, 3456], P('row', 'col'), may hold values from -0.1875 to 0.1875
- bias_query: bfloat16 [1152], P('col'), may hold values from -4 to 4
- bias_value: bfloat16 [1152], P('col'), may hold values from -0.4375 to 0.4375
- proj_out: bfloat16 [1152, 1152], P('col', 'row'), may hold values from -3 to 3
- bias_out: bfloat16 [1152], P('row'), may hold values from -4 to 4
- norm1_gain: bfloat16 [1152], P('row'), may hold values from 0.25 to 1.75
- norm1_shift: bfloat16 [1152], P('row'), may hold values from -4 to 4
- norm2_gain: bfloat16 [1152], P('row'), may hold values from 0.25 to 1.75
- norm2_shift: bfloat16 [1152], P('row'), may hold values from -4 to 4
- w_up: bfloat16 [1152, 4304], P('row', 'col'), may hold values from -0.1875 to 0.1875
- bias_up: bfloat16 [4304], P('col'), may hold values from -4 to 4
- w_down: bfloat16 [4304, 1152], P('col', 'row'), may hold values from -0.09375 to 0.09375
- bias_down: bfloat16 [1152], P('row'), may hold values from -4 to 4
Outputs:
- layer_output: bfloat16 [11664, 1152], P(('dp', 'col'), 'row')
- loss_value: float32 [], replicated
- grad_input: float32 [11664, 1152], P(('dp', 'col'), 'row')
- grad_proj_in: float32 [4, 288, 3456], P('row', 'dp', 'col')
- grad_bias_query: float32 [1152], P('col')
- grad_bias_value: float32 [1152], P('col')
- grad_proj_out: float32 [1152, 4, 288], P('col', 'row', 'dp')
- grad_bias_out: float32 [1152], P('row')
- grad_norm1_gain: float32 [1152], P('row')
- grad_norm1_shift: float32 [1152], P('row')
- grad_norm2_gain: float32 [1152], P('row')
- grad_norm2_shift: float32 [1152], P('row')
- grad_w_up: float32 [4, 288, 4304], P('row', 'dp', 'col')
- grad_bias_up: float32 [4304], P('col')
- grad_w_down: float32 [4304, 4, 288], P('col', 'row', 'dp')
- grad_bias_down: float32 [1152], P('row')
The draws below stay inside these ranges and needn't reach their ends.
All inputs are finite; a program needn't handle non-finite values. No bound on the sum of `valid` on one device may be relied on, other than what follows from the above.
Results may differ from the reference program's by a relative error of at most 0.012.
Values may be sent and summed in bfloat16 or wider, within the bound.
A program may use at most 256 MiB of HBM per device.

```python
import jax
import jax.numpy as jnp
from jax import lax

D = 1152
H = 16
HD = 72
FF = 4304
SEQ = 729
IMG_R = 2
TOKENS = 11664
N_ROW = 4


def set_ends(entries, stream_key, least, high):
    longest = entries.shape.index(max(entries.shape))
    spots = []
    for shift in (0, 1):
        where = [jax.random.randint(jax.random.fold_in(stream_key, axis), (), 0, length) for axis, length in enumerate(entries.shape)]
        where[longest] = (where[longest] + shift) % entries.shape[longest]
        spots.append(tuple(where))
    return entries.at[spots[0]].set(least).at[spots[1]].set(high)


def level_of(key, shape, cuts, low, largest):
    def one(position, blocks):
        draws = jax.random.uniform(jax.random.fold_in(jax.random.fold_in(key, 6), position), (blocks,), jnp.float32, low / len(cuts), largest / len(cuts))
        return jnp.repeat(jnp.exp(draws), shape[position] // blocks).reshape((-1,) + (1,) * (len(shape) - position - 1))

    level = one(*cuts[0])
    for cut in cuts[1:]:
        level = level * one(*cut)
    return level


def scatter_about(stream_key, shape, scale, bound, split=(), held_as=jnp.bfloat16):
    entries = scale * jax.random.normal(stream_key, shape, jnp.float32)
    if split:
        entries = entries * level_of(stream_key, shape, split, -0.22, 0.18)
    return jnp.clip(entries, -bound, bound).astype(held_as)


def setup_inputs(seed: int = 0) -> dict:
    streams_of = jax.random.split(jax.random.key(seed), 17)
    return {
        "layer_input": scatter_about(streams_of[0], (TOKENS, D), 1.0, 6.0, ((0, 8), (1, 4))),
        "teacher": scatter_about(streams_of[1], (TOKENS, D), 1.0, 6.0, ((0, 8), (1, 4))),
        "valid": set_ends((jax.random.randint(streams_of[2], (TOKENS,), 0, 10) < 9).astype(jnp.int32), jax.random.fold_in(streams_of[2], 1), 0, 1),
        "proj_in": scatter_about(streams_of[3], (D, 3 * H * HD), D ** -0.5, 0.1875, ((0, 4), (1, 4))),
        "bias_query": scatter_about(streams_of[4], (H * HD,), 0.3, 4.0, ((0, 4),)),
        "bias_value": scatter_about(streams_of[5], (H * HD,), 0.03, 0.4375, ((0, 4),)),
        "proj_out": scatter_about(streams_of[6], (H * HD, D), (H * HD * 3 // SEQ) ** -0.5, 3.0, ((0, 4), (1, 4))),
        "bias_out": scatter_about(streams_of[7], (D,), 0.3, 4.0, ((0, 4),)),
        "norm1_gain": jnp.clip(1.0 + 0.15 * jax.random.normal(streams_of[8], (D,), jnp.float32), 0.25, 1.75).astype(jnp.bfloat16),
        "norm1_shift": scatter_about(streams_of[9], (D,), 0.3, 4.0, ((0, 4),)),
        "norm2_gain": jnp.clip(1.0 + 0.15 * jax.random.normal(streams_of[10], (D,), jnp.float32), 0.25, 1.75).astype(jnp.bfloat16),
        "norm2_shift": scatter_about(streams_of[11], (D,), 0.3, 4.0, ((0, 4),)),
        "w_up": scatter_about(streams_of[12], (D, FF), D ** -0.5, 0.1875, ((0, 4), (1, 4))),
        "bias_up": scatter_about(streams_of[13], (FF,), 0.3, 4.0, ((0, 4),)),
        "w_down": scatter_about(streams_of[14], (FF, D), FF ** -0.5, 0.09375, ((0, 4), (1, 4))),
        "bias_down": scatter_about(streams_of[15], (D,), 0.3, 4.0, ((0, 4),)),
    }


EPS = 1e-06
PRECISE = lax.Precision.HIGHEST

@jax.custom_vjp
def low(v):
    return lax.optimization_barrier(v.astype(jnp.bfloat16)).astype(jnp.float32)

@jax.custom_vjp
def low_back(v):
    return v

def low_keep(v):
    return (low(v), None)

def low_pass(kept, grad):
    return (grad,)

def back_keep(v):
    return (v, None)

def back_low(kept, grad):
    return (low(grad),)
low.defvjp(low_keep, low_pass)
low_back.defvjp(back_keep, back_low)

def norm_rows(values, gain, shift):
    mean_rows = lax.optimization_barrier(jnp.mean(values, axis=-1, keepdims=True))
    centered = values - mean_rows
    var_rows = lax.optimization_barrier(jnp.mean(centered * centered, axis=-1, keepdims=True))
    return centered * lax.rsqrt(var_rows + EPS) * gain + shift

def image_attention(triple_img):
    query_rows = triple_img[:, :, 0]
    key_rows = triple_img[:, :, 1]
    value_rows = triple_img[:, :, 2]
    raw_scores = low_back(jnp.einsum('qhd,khd->hqk', query_rows, key_rows, precision=PRECISE))
    soft_weights = jax.nn.softmax(raw_scores * HD ** (-0.5), axis=-1)
    return jnp.einsum('hqk,khd->qhd', low(soft_weights), value_rows, precision=PRECISE)

def layer_block(weights, values):
    proj_in, bias_query, bias_value, proj_out, bias_out, norm1_gain, norm1_shift, norm2_gain, norm2_shift, w_up, bias_up, w_down, bias_down = weights
    norm1 = low(norm_rows(values, norm1_gain, norm1_shift))
    triple = jnp.dot(norm1, proj_in, precision=PRECISE).reshape(-1, H, 3, HD)
    bias_shift = jnp.stack([bias_query.reshape(H, HD), jnp.zeros((H, HD), triple.dtype), bias_value.reshape(H, HD)], axis=1)
    triple = low(low_back(triple + bias_shift))
    mixed_rows = lax.map(jax.checkpoint(image_attention), triple.reshape(-1, SEQ, H, 3, HD))
    mixed_rows = low(low_back(mixed_rows.reshape(-1, H * HD)))
    attn = low_back(jnp.dot(mixed_rows, proj_out, precision=PRECISE) + bias_out)
    resid1 = values + attn
    norm2 = low(norm_rows(resid1, norm2_gain, norm2_shift))
    pre = low_back(jnp.dot(norm2, w_up, precision=PRECISE) + bias_up)
    activated = low(jax.nn.gelu(pre, approximate=True))
    return resid1 + low_back(jnp.dot(activated, w_down, precision=PRECISE) + bias_down)

def reference(layer_input, teacher, valid, proj_in, bias_query, bias_value, proj_out, bias_out, norm1_gain, norm1_shift, norm2_gain, norm2_shift, w_up, bias_up, w_down, bias_down):
    params = tuple((param.astype(jnp.float32) for param in (proj_in, bias_query, bias_value, proj_out, bias_out, norm1_gain, norm1_shift, norm2_gain, norm2_shift, w_up, bias_up, w_down, bias_down)))
    mask_all = valid.astype(jnp.float32)
    valid_count = jnp.sum(mask_all)
    factor = TOKENS / (2.0 * valid_count)
    span_rows = IMG_R * SEQ
    num_blocks = TOKENS // span_rows
    inputs = layer_input.astype(jnp.float32).reshape(num_blocks, span_rows, D)
    targets = teacher.astype(jnp.float32).reshape(num_blocks, span_rows, D)
    masks = mask_all.reshape(num_blocks, span_rows)

    def objective(weights, values, target, mask_rows):
        result = layer_block(weights, values)
        error_rows = result - target
        err_sum = jnp.sum(mask_rows[:, None] * error_rows * error_rows)
        return (err_sum * factor, (result, err_sum))

    def step(carry, block):
        totals, err_total = carry
        values, target, mask_rows = block
        scaled, pull, aux_out = jax.vjp(lambda weights, rows: objective(weights, rows, target, mask_rows), params, values, has_aux=True)
        grad_weights, grad_values = pull(jnp.ones_like(scaled))
        totals = jax.tree.map(lambda left, right: left + right, totals, grad_weights)
        return ((totals, err_total + aux_out[1]), (aux_out[0], grad_values))
    zeros_tree = jax.tree.map(jnp.zeros_like, params)
    (totals, err_total), (results, grads_in) = lax.scan(step, (zeros_tree, jnp.zeros((), jnp.float32)), (inputs, targets, masks))
    layer_output = results.reshape(TOKENS, D).astype(jnp.bfloat16)
    loss_value = err_total / (valid_count * D)
    grad_input = grads_in.reshape(TOKENS, D)
    block_width = D // N_ROW
    grad_proj_in = totals[0].reshape(N_ROW, block_width, 3 * H * HD)
    grad_proj_out = totals[3].reshape(H * HD, N_ROW, block_width)
    grad_w_up = totals[9].reshape(N_ROW, block_width, FF)
    grad_w_down = totals[11].reshape(FF, N_ROW, block_width)
    return (layer_output, loss_value, grad_input, grad_proj_in, totals[1], totals[2], grad_proj_out, totals[4], totals[5], totals[6], totals[7], totals[8], grad_w_up, totals[10], grad_w_down, totals[12])
```

```python
import jax
import jax.numpy as jnp
from jax import lax
from jax.sharding import PartitionSpec as P

D = 1152
H = 16
HD = 72
FF = 4304
SEQ = 729


EPS = 1e-06


def feature_totals(left, right):
    return lax.psum(
        (jnp.sum(left, axis=-1, keepdims=True), jnp.sum(right, axis=-1, keepdims=True)), "row"
    )


def norm_forward(values, gain, shift):
    first_sum, second_sum = feature_totals(values, values * values)
    mean_rows = first_sum / D
    var_rows = second_sum / D - mean_rows * mean_rows
    inv_scale = lax.rsqrt(var_rows + EPS)
    normed = (values - mean_rows) * inv_scale
    return (normed, inv_scale, normed * gain + shift)


def norm_backward(grad_out, normed, inv_scale, gain):
    grad_normed = grad_out * gain
    first_sum, second_sum = feature_totals(grad_normed, grad_normed * normed)
    return inv_scale * (grad_normed - first_sum / D - normed * second_sum / D)


def first_section(local_rows, weight):
    gathered = lax.all_gather(local_rows, "col", axis=0, tiled=True)
    share_rows = gathered.shape[0] // lax.axis_size("row")

    def partial_term(row_start, row_count):
        return jnp.dot(gathered, weight, preferred_element_type=jnp.float32)

    result = lax.psum_scatter(
        partial_term(jnp.int32(0), lax.axis_size("row") * share_rows),
        "row",
        scatter_dimension=0,
        tiled=True,
    )
    return (gathered, result)


def second_section(quarter_rows, weight):
    gathered = lax.all_gather(quarter_rows, "row", axis=0, tiled=True)
    share_rows = gathered.shape[0] // lax.axis_size("col")

    def partial_term(row_start, row_count):
        return jnp.dot(gathered, weight, preferred_element_type=jnp.float32)

    result = lax.psum_scatter(
        partial_term(jnp.int32(0), lax.axis_size("col") * share_rows),
        "col",
        scatter_dimension=0,
        tiled=True,
    )
    return (gathered, result)


def second_section_back(grad_local, gathered, weight):
    grad_all = lax.all_gather(grad_local, "col", axis=0, tiled=True)
    grad_weight = lax.dot_general(
        gathered, grad_all, (((0,), (0,)), ((), ())), preferred_element_type=jnp.float32
    )
    share_rows = grad_all.shape[0] // lax.axis_size("row")

    def partial_term(row_start, row_count):
        return lax.dot_general(
            grad_all, weight, (((1,), (1,)), ((), ())), preferred_element_type=jnp.float32
        )

    result = lax.psum_scatter(
        partial_term(jnp.int32(0), lax.axis_size("row") * share_rows),
        "row",
        scatter_dimension=0,
        tiled=True,
    )
    return (grad_weight, result)


def first_section_back(grad_quarter, gathered, weight):
    grad_all = lax.all_gather(grad_quarter, "row", axis=0, tiled=True)
    grad_weight = lax.dot_general(
        gathered, grad_all, (((0,), (0,)), ((), ())), preferred_element_type=jnp.float32
    )
    share_rows = grad_all.shape[0] // lax.axis_size("col")

    def partial_term(row_start, row_count):
        return lax.dot_general(
            grad_all, weight, (((1,), (1,)), ((), ())), preferred_element_type=jnp.float32
        )

    result = lax.psum_scatter(
        partial_term(jnp.int32(0), lax.axis_size("col") * share_rows).astype(jnp.bfloat16),
        "col",
        scatter_dimension=0,
        tiled=True,
    ).astype(jnp.float32)
    return (grad_weight, result)


def attend(triple_img):
    score_scale = HD ** (-0.5)
    query_rows = triple_img[:, :, 0]
    key_rows = triple_img[:, :, 1]
    value_rows = triple_img[:, :, 2]
    raw_scores = jnp.einsum(
        "qhd,khd->hqk", query_rows, key_rows, preferred_element_type=jnp.float32
    )
    scaled = raw_scores * score_scale
    peak_score = jnp.max(scaled, axis=-1, keepdims=True)
    exp_scores = jnp.exp(scaled - peak_score)
    exp_total = jnp.sum(exp_scores, axis=-1, keepdims=True)
    soft_weights = (exp_scores / exp_total).astype(jnp.bfloat16)
    mixed_rows = jnp.einsum(
        "hqk,khd->qhd", soft_weights, value_rows, preferred_element_type=jnp.float32
    )
    return (mixed_rows.astype(jnp.bfloat16), peak_score + jnp.log(exp_total))


def attend_back(packed):
    triple_img, log_total, grad_mixed = packed
    score_scale = HD ** (-0.5)
    query_rows = triple_img[:, :, 0]
    key_rows = triple_img[:, :, 1]
    value_rows = triple_img[:, :, 2]
    raw_scores = jnp.einsum(
        "qhd,khd->hqk", query_rows, key_rows, preferred_element_type=jnp.float32
    )
    soft_weights = jnp.exp(raw_scores * score_scale - log_total)
    weights_low = soft_weights.astype(jnp.bfloat16)
    grad_values = jnp.einsum(
        "hqk,qhd->khd", weights_low, grad_mixed, preferred_element_type=jnp.float32
    )
    grad_soft = jnp.einsum(
        "qhd,khd->hqk", grad_mixed, value_rows, preferred_element_type=jnp.float32
    )
    inner_prod = jnp.sum(grad_soft * soft_weights, axis=-1, keepdims=True)
    grad_raw = (score_scale * soft_weights * (grad_soft - inner_prod)).astype(jnp.bfloat16)
    grad_query = jnp.einsum("hqk,khd->qhd", grad_raw, key_rows, preferred_element_type=jnp.float32)
    grad_keys = jnp.einsum("hqk,qhd->khd", grad_raw, query_rows, preferred_element_type=jnp.float32)
    return jnp.stack([grad_query, grad_keys, grad_values], axis=2).astype(jnp.bfloat16)


def on_device(
    layer_input,
    teacher,
    valid,
    proj_in,
    bias_query,
    bias_value,
    proj_out,
    bias_out,
    norm1_gain,
    norm1_shift,
    norm2_gain,
    norm2_shift,
    w_up,
    bias_up,
    w_down,
    bias_down,
):
    heads_here = H // lax.axis_size("col")
    head_width = heads_here * HD
    feat_here = layer_input.shape[1]
    units_here = w_up.shape[1]
    gain_one = norm1_gain.astype(jnp.float32)
    gain_two = norm2_gain.astype(jnp.float32)
    residual_in = layer_input.astype(jnp.float32)
    normed1, scale1, mid_one = norm_forward(residual_in, gain_one, norm1_shift.astype(jnp.float32))
    norm1_all, projected = first_section(mid_one.astype(jnp.bfloat16), proj_in)
    quarter = projected.shape[0]
    images = quarter // SEQ
    bias_shift = jnp.stack(
        [
            bias_query.astype(jnp.float32).reshape(heads_here, HD),
            jnp.zeros((heads_here, HD), jnp.float32),
            bias_value.astype(jnp.float32).reshape(heads_here, HD),
        ],
        axis=1,
    )
    triple = (projected.reshape(quarter, heads_here, 3, HD) + bias_shift).astype(jnp.bfloat16)
    triple_imgs = triple.reshape(images, SEQ, heads_here, 3, HD)
    mixed_imgs, log_totals = lax.map(attend, triple_imgs)
    mixed_all, attn_part = second_section(mixed_imgs.reshape(quarter, head_width), proj_out)
    resid1 = residual_in + attn_part + bias_out.astype(jnp.float32)
    normed2, scale2, mid_two = norm_forward(resid1, gain_two, norm2_shift.astype(jnp.float32))
    norm2_all, pre_part = first_section(mid_two.astype(jnp.bfloat16), w_up)
    pre = pre_part + bias_up.astype(jnp.float32)
    activated, gelu_pull = jax.vjp(lambda entry: jax.nn.gelu(entry, approximate=True), pre)
    act_all, down_part = second_section(activated.astype(jnp.bfloat16), w_down)
    result = resid1 + down_part + bias_down.astype(jnp.float32)
    mask_rows = valid.astype(jnp.float32)
    error_rows = result - teacher.astype(jnp.float32)
    err_part = jnp.sum(mask_rows[:, None] * error_rows * error_rows)
    count_part = jnp.sum(mask_rows) / lax.axis_size("row")
    err_total, valid_count = lax.psum((err_part, count_part), ("dp", "row", "col"))
    loss_value = err_total / (valid_count * D)
    tokens_all = layer_input.shape[0] * lax.axis_size("dp") * lax.axis_size("col")
    factor = tokens_all / (2.0 * valid_count)
    grad_result = 2.0 * error_rows * (mask_rows[:, None] * factor)
    grad_branch2 = grad_result.astype(jnp.bfloat16)
    grad_w_down, grad_act = second_section_back(grad_branch2, act_all, w_down)
    grad_pre = gelu_pull(grad_act)[0].astype(jnp.bfloat16)
    grad_w_up, grad_norm2 = first_section_back(grad_pre, norm2_all, w_up)
    grad_resid1 = grad_result + norm_backward(grad_norm2, normed2, scale2, gain_two)
    grad_branch1 = grad_resid1.astype(jnp.bfloat16)
    grad_proj_out, grad_mixed = second_section_back(grad_branch1, mixed_all, proj_out)
    grad_mixed_imgs = grad_mixed.astype(jnp.bfloat16).reshape(images, SEQ, heads_here, HD)
    grad_triple = lax.map(attend_back, (triple_imgs, log_totals, grad_mixed_imgs))
    grad_triple = grad_triple.reshape(quarter, heads_here, 3, HD)
    grad_proj_in, grad_norm1 = first_section_back(
        grad_triple.reshape(quarter, 3 * head_width), norm1_all, proj_in
    )
    grad_input = grad_resid1 + norm_backward(grad_norm1, normed1, scale1, gain_one)
    row_at = lax.axis_index("row") * feat_here
    col_at = lax.axis_index("col") * head_width
    feature_terms = jnp.stack(
        [
            jnp.sum(grad_norm1 * normed1, axis=0),
            jnp.sum(grad_norm1, axis=0),
            jnp.sum(grad_norm2 * normed2, axis=0),
            jnp.sum(grad_norm2, axis=0),
            jnp.sum(grad_branch1.astype(jnp.float32), axis=0),
            jnp.sum(grad_branch2.astype(jnp.float32), axis=0),
        ]
    )
    feature_full = lax.dynamic_update_slice_in_dim(
        jnp.zeros((6, D), jnp.float32), feature_terms, row_at, 1
    )
    grad_float = grad_triple.astype(jnp.float32)
    head_terms = jnp.stack(
        [
            jnp.sum(grad_float[:, :, 0], axis=0).reshape(head_width),
            jnp.sum(grad_float[:, :, 2], axis=0).reshape(head_width),
        ]
    )
    head_full = lax.dynamic_update_slice_in_dim(
        jnp.zeros((2, H * HD), jnp.float32), head_terms, col_at, 1
    )
    unit_terms = jnp.sum(grad_pre.astype(jnp.float32), axis=0)
    unit_full = lax.dynamic_update_slice_in_dim(
        jnp.zeros((FF,), jnp.float32), unit_terms, lax.axis_index("col") * units_here, 0
    )
    feature_full, head_full, unit_full = lax.psum(
        (feature_full, head_full, unit_full), ("dp", "row", "col")
    )
    feature_mine = lax.dynamic_slice_in_dim(feature_full, row_at, feat_here, 1)
    head_mine = lax.dynamic_slice_in_dim(head_full, col_at, head_width, 1)
    unit_mine = lax.dynamic_slice_in_dim(
        unit_full, lax.axis_index("col") * units_here, units_here, 0
    )
    grad_proj_in, grad_w_up = (
        lax.psum_scatter(
            grad_proj_in.astype(jnp.bfloat16), "dp", scatter_dimension=0, tiled=True
        ).astype(jnp.float32),
        lax.psum_scatter(
            grad_w_up.astype(jnp.bfloat16), "dp", scatter_dimension=0, tiled=True
        ).astype(jnp.float32),
    )
    grad_proj_out, grad_w_down = (
        lax.psum_scatter(
            grad_proj_out.astype(jnp.bfloat16), "dp", scatter_dimension=1, tiled=True
        ).astype(jnp.float32),
        lax.psum_scatter(
            grad_w_down.astype(jnp.bfloat16), "dp", scatter_dimension=1, tiled=True
        ).astype(jnp.float32),
    )
    grad_proj_in = grad_proj_in.reshape(1, grad_proj_in.shape[0], grad_proj_in.shape[1])
    grad_w_up = grad_w_up.reshape(1, grad_w_up.shape[0], grad_w_up.shape[1])
    grad_proj_out = grad_proj_out.reshape(grad_proj_out.shape[0], 1, grad_proj_out.shape[1])
    grad_w_down = grad_w_down.reshape(grad_w_down.shape[0], 1, grad_w_down.shape[1])
    return (
        result.astype(jnp.bfloat16),
        loss_value,
        grad_input,
        grad_proj_in,
        head_mine[0],
        head_mine[1],
        grad_proj_out,
        feature_mine[4],
        feature_mine[0],
        feature_mine[1],
        feature_mine[2],
        feature_mine[3],
        grad_w_up,
        unit_mine,
        grad_w_down,
        feature_mine[5],
    )


def pair_swap(values):
    return lax.ppermute(values, "dp", [(0, 1), (1, 0)])


def row_swap(values, bit):
    return lax.ppermute(values, "row", [(i, i ^ bit) for i in range(lax.axis_size("row"))])


def ring_order(size):
    return list(range(0, size, 2)) + list(range(1, size, 2))[::-1]


def ring_shift(values, step):
    order = ring_order(lax.axis_size("col"))
    size = len(order)
    return lax.ppermute(
        values, "col", [(order[i], order[(i + step) % size]) for i in range(size)]
    )


def gather_ring(shard):
    shards = [shard]
    for _ in range(lax.axis_size("col") - 1):
        shards.append(ring_shift(shards[-1], 1))
    return shards


def gather_plane(block):
    half = block.shape[0] // 2
    one = row_swap(block, 1)
    two = row_swap(block, 2)
    three_low = row_swap(one[:half], 2)
    three_high = row_swap(two[half:], 1)
    return jnp.concatenate([block, one, two, three_low, three_high], axis=0)


def add_low(left, right):
    return (left.astype(jnp.float32) + right.astype(jnp.float32)).astype(jnp.bfloat16)


def scatter_plane(grad):
    rows = grad.shape[0] // 4
    half = rows // 2
    part = [grad[i * half : (i + 1) * half] for i in range(8)]
    one_high = row_swap(part[3], 1)
    two_low = row_swap(part[4], 2)
    one_low = row_swap(add_low(part[2], row_swap(part[6], 2)), 1)
    two_high = row_swap(add_low(part[5], row_swap(part[7], 1)), 2)
    low = part[0].astype(jnp.float32) + one_low.astype(jnp.float32) + two_low.astype(jnp.float32)
    high = part[1].astype(jnp.float32) + one_high.astype(jnp.float32) + two_high.astype(jnp.float32)
    return jnp.concatenate([low, high], axis=0)


def layer_norm(values):
    mean_rows = jnp.mean(values, axis=-1, keepdims=True)
    centered = values - mean_rows
    inv_scale = lax.rsqrt(jnp.mean(centered * centered, axis=-1, keepdims=True) + EPS)
    return centered * inv_scale, inv_scale


def layer_norm_back(grad_out, normed, inv_scale, gain):
    grad_normed = grad_out * gain
    first = jnp.mean(grad_normed, axis=-1, keepdims=True)
    second = jnp.mean(grad_normed * normed, axis=-1, keepdims=True)
    return inv_scale * (grad_normed - first - normed * second)


def dot_nn(left, right):
    return jnp.dot(left, right, preferred_element_type=jnp.float32)


def dot_nt(left, right):
    return lax.dot_general(left, right, (((1,), (1,)), ((), ())), preferred_element_type=jnp.float32)


def dot_tn(left, right):
    return lax.dot_general(left, right, (((0,), (0,)), ((), ())), preferred_element_type=jnp.float32)


def fast_attend(triple, key_bias):
    score_scale = HD ** (-0.5)
    raw = jnp.einsum("qhd,khd->hqk", triple[:, :, 0], triple[:, :, 1], preferred_element_type=jnp.float32)
    scaled = raw * score_scale + key_bias
    peak = jnp.max(scaled, axis=-1, keepdims=True)
    exps = jnp.exp(scaled - peak)
    total = jnp.sum(exps, axis=-1, keepdims=True)
    weights = (exps / total).astype(jnp.bfloat16)
    mixed = jnp.einsum("hqk,khd->qhd", weights, triple[:, :, 2], preferred_element_type=jnp.float32)
    return mixed.astype(jnp.bfloat16), peak + jnp.log(total)


def fast_attend_back(triple, log_total, grad_mixed, key_bias):
    score_scale = HD ** (-0.5)
    query, key, value = triple[:, :, 0], triple[:, :, 1], triple[:, :, 2]
    raw = jnp.einsum("qhd,khd->hqk", query, key, preferred_element_type=jnp.float32)
    weights = jnp.exp(raw * score_scale + key_bias - log_total)
    grad_value = jnp.einsum(
        "hqk,qhd->khd", weights.astype(jnp.bfloat16), grad_mixed, preferred_element_type=jnp.float32
    )
    grad_soft = jnp.einsum("qhd,khd->hqk", grad_mixed, value, preferred_element_type=jnp.float32)
    inner = jnp.sum(grad_soft * weights, axis=-1, keepdims=True)
    grad_raw = (score_scale * weights * (grad_soft - inner)).astype(jnp.bfloat16)
    grad_query = jnp.einsum("hqk,khd->qhd", grad_raw, key, preferred_element_type=jnp.float32)
    grad_key = jnp.einsum("hqk,qhd->khd", grad_raw, query, preferred_element_type=jnp.float32)
    return jnp.stack([grad_query, grad_key, grad_value], axis=2).astype(jnp.bfloat16)


def on_chip(
    layer_input,
    teacher,
    valid,
    proj_in,
    bias_query,
    bias_value,
    proj_out,
    bias_out,
    norm1_gain,
    norm1_shift,
    norm2_gain,
    norm2_shift,
    w_up,
    bias_up,
    w_down,
    bias_down,
):
    core = lax.axis_index("dp")
    row = lax.axis_index("row")
    cols = lax.axis_size("col")
    feat = layer_input.shape[1]
    images = layer_input.shape[0] // SEQ
    half_seq = (SEQ + 31) // 32 * 16
    pad_seq = 2 * half_seq
    units = w_up.shape[1] // 2
    width = proj_out.shape[0] // 2
    heads = width // HD

    def core_half(values, axis):
        size = values.shape[axis] // 2
        return lax.dynamic_slice_in_dim(values, core * size, size, axis)

    def to_chip(values):
        imgs = jnp.pad(values.reshape(images, SEQ, -1), ((0, 0), (0, pad_seq - SEQ), (0, 0)))
        imgs = imgs.reshape(images, 2, half_seq, -1)
        keep = lax.dynamic_index_in_dim(imgs, core, 1, False)
        give = lax.dynamic_index_in_dim(imgs, 1 - core, 1, False)
        got = pair_swap(give)
        first = core == 0
        every = jnp.concatenate([jnp.where(first, keep, got), jnp.where(first, got, keep)], axis=0)
        parts = []
        for k in range(4):
            part = lax.dynamic_index_in_dim(every, row ^ k, 0, False)
            parts.append(row_swap(part, k) if k else part)
        return jnp.concatenate(parts, axis=1)

    def from_chip(values):
        parts = []
        for k in range(4):
            part = values[:, k * feat : (k + 1) * feat]
            parts.append(row_swap(part, k) if k else part)
        stacked = jnp.stack(parts)
        every = jnp.stack([lax.dynamic_index_in_dim(stacked, row ^ i, 0, False) for i in range(4)])
        every = every.reshape(2, images, half_seq, feat)
        mine = lax.dynamic_index_in_dim(every, core, 0, False)
        got = pair_swap(lax.dynamic_index_in_dim(every, 1 - core, 0, False))
        first = core == 0
        both = jnp.stack([jnp.where(first, mine, got), jnp.where(first, got, mine)], axis=1)
        return both.reshape(images, pad_seq, feat)[:, :SEQ].reshape(images * SEQ, feat)

    attn_shard = jnp.concatenate([core_half(proj_in, 1), core_half(proj_out, 0).T], axis=1)
    ff_shard = jnp.concatenate([core_half(w_up, 1), core_half(w_down, 0).T], axis=1)
    features = jnp.stack([norm1_gain, norm1_shift, norm2_gain, norm2_shift, bias_out, bias_down])
    features = jnp.concatenate([features] + [row_swap(features, k) for k in (1, 2, 3)], axis=1)
    features = features.astype(jnp.float32)
    gain1, shift1, gain2, shift2, bias_out_all, bias_down_all = (features[i : i + 1] for i in range(6))
    col_biases = gather_ring(
        jnp.concatenate([core_half(bias_query, 0), core_half(bias_value, 0), core_half(bias_up, 0)])[None]
    )

    x_half = to_chip(layer_input).astype(jnp.float32)
    attn_weights = [gather_plane(block) for block in gather_ring(attn_shard)]
    ff_weights = [gather_plane(block) for block in gather_ring(ff_shard)]
    teacher_half = to_chip(teacher).astype(jnp.float32)
    count = lax.psum(jnp.sum(valid.astype(jnp.float32)), ("dp", "col"))
    valid_imgs = jnp.pad(valid.reshape(images, SEQ), ((0, 0), (0, pad_seq - SEQ)))
    other_valid = pair_swap(valid_imgs)
    from_here = (row // images) == core
    chip_valid = lax.dynamic_index_in_dim(
        jnp.where(from_here, valid_imgs, other_valid), lax.rem(row, images), 0, False
    )
    mask_half = lax.dynamic_slice_in_dim(chip_valid, core * half_seq, half_seq, 0)
    mask_half = mask_half.astype(jnp.float32)[:, None]

    place = jnp.arange(pad_seq)
    token = jnp.where(place < half_seq, place + core * half_seq, place - core * half_seq)
    key_bias = jnp.where(token < SEQ, 0.0, -1e30).astype(jnp.float32)

    def both_cores(values):
        return jnp.concatenate([values, pair_swap(values)], axis=0)

    def sum_cores(values):
        return values[:half_seq] + pair_swap(values[half_seq:])

    normed1, scale1 = layer_norm(x_half)
    norm1_all = both_cores((normed1 * gain1 + shift1).astype(jnp.bfloat16))
    triples, log_totals, mixes = [], [], []
    attn_part = 0.0
    for s in range(cols):
        weight = attn_weights[s]
        triple = dot_nn(norm1_all, weight[:, : 3 * width]).reshape(pad_seq, heads, 3, HD)
        bias = col_biases[s][0].astype(jnp.float32)
        bias_shift = jnp.stack(
            [
                bias[:width].reshape(heads, HD),
                jnp.zeros((heads, HD), jnp.float32),
                bias[width : 2 * width].reshape(heads, HD),
            ],
            axis=1,
        )
        triple = (triple + bias_shift).astype(jnp.bfloat16)
        mixed, log_total = fast_attend(triple, key_bias)
        mixed = mixed.reshape(pad_seq, width)
        attn_part = attn_part + dot_nt(mixed, weight[:, 3 * width :])
        triples.append(triple)
        log_totals.append(log_total)
        mixes.append(mixed)
    resid1 = x_half + sum_cores(attn_part) + bias_out_all
    normed2, scale2 = layer_norm(resid1)
    norm2_all = both_cores((normed2 * gain2 + shift2).astype(jnp.bfloat16))
    pres, acts = [], []
    down_part = 0.0
    for s in range(cols):
        weight = ff_weights[s]
        pre = dot_nn(norm2_all, weight[:, :units]) + col_biases[s][:, 2 * width :].astype(jnp.float32)
        act = jax.nn.gelu(pre, approximate=True).astype(jnp.bfloat16)
        down_part = down_part + dot_nt(act, weight[:, units:])
        pres.append(pre)
        acts.append(act)
    result = resid1 + sum_cores(down_part) + bias_down_all
    layer_output = from_chip(result.astype(jnp.bfloat16))

    error = result - teacher_half
    err_part = jnp.sum(mask_half * error * error)
    tokens_all = layer_input.shape[0] * lax.axis_size("dp") * cols
    factor = tokens_all / (2.0 * count)
    grad_result = 2.0 * error * (mask_half * factor)
    branch2 = grad_result.astype(jnp.bfloat16)
    branch2_all = both_cores(branch2)
    norm2_part = 0.0
    ff_sum, bias_sum = 0.0, 0.0
    bias_up_sum = None
    for s in reversed(range(cols)):
        weight = ff_weights[s]
        grad_act = dot_nn(branch2_all, weight[:, units:])
        _, pull = jax.vjp(lambda entry: jax.nn.gelu(entry, approximate=True), pres[s])
        grad_pre = pull(grad_act)[0].astype(jnp.bfloat16)
        norm2_part = norm2_part + dot_nt(grad_pre, weight[:, :units])
        grad_block = jnp.concatenate(
            [dot_tn(norm2_all, grad_pre), dot_tn(branch2_all, acts[s])], axis=1
        ).astype(jnp.bfloat16)
        mine = scatter_plane(grad_block)
        bias_mine = jnp.sum(grad_pre.astype(jnp.float32), axis=0, keepdims=True)
        if s < cols - 1:
            mine = mine + ring_shift(ff_sum, -1).astype(jnp.float32)
            bias_mine = bias_mine + ring_shift(bias_up_sum, -1)
        ff_sum = mine.astype(jnp.bfloat16)
        bias_up_sum = bias_mine
    grad_norm2 = sum_cores(norm2_part)
    grad_resid1 = grad_result + layer_norm_back(grad_norm2, normed2, scale2, gain2)
    branch1 = grad_resid1.astype(jnp.bfloat16)
    branch1_all = both_cores(branch1)
    norm1_part = 0.0
    attn_sum, head_sum = 0.0, 0.0
    for s in reversed(range(cols)):
        weight = attn_weights[s]
        grad_mixed = dot_nn(branch1_all, weight[:, 3 * width :]).astype(jnp.bfloat16)
        grad_triple = fast_attend_back(
            triples[s], log_totals[s], grad_mixed.reshape(pad_seq, heads, HD), key_bias
        )
        grad_float = grad_triple.astype(jnp.float32)
        head_mine = jnp.stack(
            [
                jnp.sum(grad_float[:, :, 0], axis=0).reshape(width),
                jnp.sum(grad_float[:, :, 2], axis=0).reshape(width),
            ]
        )
        grad_triple = grad_triple.reshape(pad_seq, 3 * width)
        norm1_part = norm1_part + dot_nt(grad_triple, weight[:, : 3 * width])
        grad_block = jnp.concatenate(
            [dot_tn(norm1_all, grad_triple), dot_tn(branch1_all, mixes[s])], axis=1
        ).astype(jnp.bfloat16)
        mine = scatter_plane(grad_block)
        if s < cols - 1:
            mine = mine + ring_shift(attn_sum, -1).astype(jnp.float32)
            head_mine = head_mine + ring_shift(head_sum, -1)
        attn_sum = mine.astype(jnp.bfloat16)
        head_sum = head_mine
    grad_norm1 = sum_cores(norm1_part)
    grad_in = grad_resid1 + layer_norm_back(grad_norm1, normed1, scale1, gain1)
    grad_input = from_chip(grad_in.astype(jnp.bfloat16)).astype(jnp.float32)

    terms = jnp.stack(
        [
            jnp.sum(grad_norm1 * normed1, axis=0),
            jnp.sum(grad_norm1, axis=0),
            jnp.sum(grad_norm2 * normed2, axis=0),
            jnp.sum(grad_norm2, axis=0),
            jnp.sum(branch1.astype(jnp.float32), axis=0),
            jnp.sum(branch2.astype(jnp.float32), axis=0),
        ]
    )
    near = terms[:, : 2 * feat] + row_swap(terms[:, 2 * feat :], 2)
    terms = near[:, :feat] + row_swap(near[:, feat:], 1)

    def plane_sum(values):
        values = values + row_swap(values, 1)
        return values + row_swap(values, 2)

    err_plane = plane_sum(err_part.reshape(1, 1))
    sums = jnp.concatenate([terms, jnp.broadcast_to(err_plane, (1, feat))], axis=0)
    for bit in (1, 2):
        sums = sums + lax.ppermute(sums, "col", [(i, i ^ bit) for i in range(cols)])
    sums = sums + pair_swap(sums)
    loss_value = sums[6, 0] / (count * D)

    def both_halves(values):
        got = pair_swap(values)
        first = core == 0
        return jnp.concatenate(
            [jnp.where(first, values, got), jnp.where(first, got, values)], axis=-1
        )

    unit_mine = both_halves(plane_sum(bias_up_sum))[0]
    head_mine = both_halves(plane_sum(head_sum))

    def weight_rows(total):
        size = feat // 2
        keep = lax.dynamic_slice_in_dim(total, core * size, size, 0)
        give = lax.dynamic_slice_in_dim(total, (1 - core) * size, size, 0)
        return keep, pair_swap(give)

    def joined(keep, got, axis):
        first = core == 0
        return jnp.concatenate(
            [jnp.where(first, keep, got), jnp.where(first, got, keep)], axis=axis
        ).astype(jnp.float32)

    ff_keep, ff_got = weight_rows(ff_sum)
    attn_keep, attn_got = weight_rows(attn_sum)
    grad_w_up = joined(ff_keep[:, :units], ff_got[:, :units], 1)
    grad_w_down = joined(ff_keep[:, units:].T, ff_got[:, units:].T, 0)
    grad_proj_in = joined(attn_keep[:, : 3 * width], attn_got[:, : 3 * width], 1)
    grad_proj_out = joined(attn_keep[:, 3 * width :].T, attn_got[:, 3 * width :].T, 0)
    return (
        layer_output,
        loss_value,
        grad_input,
        grad_proj_in[None],
        head_mine[0],
        head_mine[1],
        grad_proj_out[:, None],
        sums[4],
        sums[0],
        sums[1],
        sums[2],
        sums[3],
        grad_w_up[None],
        unit_mine,
        grad_w_down[:, None],
        sums[5],
    )


def one_image_a_chip(mesh, tokens):
    sizes = mesh.shape
    pairs = sizes["dp"] == 2 and sizes["row"] == 4 and sizes["col"] == 4
    return pairs and tokens == SEQ * sizes["row"] * sizes["col"]


def solution(mesh):
    placed = (
        P(("dp", "col"), "row"),
        P(("dp", "col"), "row"),
        P(("dp", "col")),
        P("row", "col"),
        P("col"),
        P("col"),
        P("col", "row"),
        P("row"),
        P("row"),
        P("row"),
        P("row"),
        P("row"),
        P("row", "col"),
        P("col"),
        P("col", "row"),
        P("row"),
    )
    returned = (
            P(("dp", "col"), "row"),
            P(),
            P(("dp", "col"), "row"),
            P("row", "dp", "col"),
            P("col"),
            P("col"),
            P("col", "row", "dp"),
            P("row"),
            P("row"),
            P("row"),
            P("row"),
            P("row"),
            P("row", "dp", "col"),
            P("col"),
            P("col", "row", "dp"),
            P("row"),
        )

    def whole(layer_input, *others):
        body = on_chip if one_image_a_chip(mesh, layer_input.shape[0]) else on_device
        return jax.shard_map(
            body, mesh=mesh, in_specs=placed, out_specs=returned, check_vma=False
        )(layer_input, *others)

    return whole
```

```python
import jax
import jax.numpy as jnp
from jax import lax
from jax.experimental import pallas as pl
from jax.experimental.pallas import tpu as pltpu
from jax.sharding import PartitionSpec as P

D = 1152
H = 16
HD = 72
FF = 4304
SEQ = 729


EPS = 1e-06


def feature_totals(left, right):
    return lax.psum(
        (jnp.sum(left, axis=-1, keepdims=True), jnp.sum(right, axis=-1, keepdims=True)), "row"
    )


def norm_forward(values, gain, shift):
    first_sum, second_sum = feature_totals(values, values * values)
    mean_rows = first_sum / D
    var_rows = second_sum / D - mean_rows * mean_rows
    inv_scale = lax.rsqrt(var_rows + EPS)
    normed = (values - mean_rows) * inv_scale
    return (normed, inv_scale, normed * gain + shift)


def norm_backward(grad_out, normed, inv_scale, gain):
    grad_normed = grad_out * gain
    first_sum, second_sum = feature_totals(grad_normed, grad_normed * normed)
    return inv_scale * (grad_normed - first_sum / D - normed * second_sum / D)


def first_section(local_rows, weight):
    gathered = lax.all_gather(local_rows, "col", axis=0, tiled=True)
    share_rows = gathered.shape[0] // lax.axis_size("row")

    def partial_term(row_start, row_count):
        return jnp.dot(gathered, weight, preferred_element_type=jnp.float32)

    result = lax.psum_scatter(
        partial_term(jnp.int32(0), lax.axis_size("row") * share_rows),
        "row",
        scatter_dimension=0,
        tiled=True,
    )
    return (gathered, result)


def second_section(quarter_rows, weight):
    gathered = lax.all_gather(quarter_rows, "row", axis=0, tiled=True)
    share_rows = gathered.shape[0] // lax.axis_size("col")

    def partial_term(row_start, row_count):
        return jnp.dot(gathered, weight, preferred_element_type=jnp.float32)

    result = lax.psum_scatter(
        partial_term(jnp.int32(0), lax.axis_size("col") * share_rows),
        "col",
        scatter_dimension=0,
        tiled=True,
    )
    return (gathered, result)


def second_section_back(grad_local, gathered, weight):
    grad_all = lax.all_gather(grad_local, "col", axis=0, tiled=True)
    grad_weight = lax.dot_general(
        gathered, grad_all, (((0,), (0,)), ((), ())), preferred_element_type=jnp.float32
    )
    share_rows = grad_all.shape[0] // lax.axis_size("row")

    def partial_term(row_start, row_count):
        return lax.dot_general(
            grad_all, weight, (((1,), (1,)), ((), ())), preferred_element_type=jnp.float32
        )

    result = lax.psum_scatter(
        partial_term(jnp.int32(0), lax.axis_size("row") * share_rows),
        "row",
        scatter_dimension=0,
        tiled=True,
    )
    return (grad_weight, result)


def first_section_back(grad_quarter, gathered, weight):
    grad_all = lax.all_gather(grad_quarter, "row", axis=0, tiled=True)
    grad_weight = lax.dot_general(
        gathered, grad_all, (((0,), (0,)), ((), ())), preferred_element_type=jnp.float32
    )
    share_rows = grad_all.shape[0] // lax.axis_size("col")

    def partial_term(row_start, row_count):
        return lax.dot_general(
            grad_all, weight, (((1,), (1,)), ((), ())), preferred_element_type=jnp.float32
        )

    result = lax.psum_scatter(
        partial_term(jnp.int32(0), lax.axis_size("col") * share_rows).astype(jnp.bfloat16),
        "col",
        scatter_dimension=0,
        tiled=True,
    ).astype(jnp.float32)
    return (grad_weight, result)


def attend(triple_img):
    score_scale = HD ** (-0.5)
    query_rows = triple_img[:, :, 0]
    key_rows = triple_img[:, :, 1]
    value_rows = triple_img[:, :, 2]
    raw_scores = jnp.einsum(
        "qhd,khd->hqk", query_rows, key_rows, preferred_element_type=jnp.float32
    )
    scaled = raw_scores * score_scale
    peak_score = jnp.max(scaled, axis=-1, keepdims=True)
    exp_scores = jnp.exp(scaled - peak_score)
    exp_total = jnp.sum(exp_scores, axis=-1, keepdims=True)
    soft_weights = (exp_scores / exp_total).astype(jnp.bfloat16)
    mixed_rows = jnp.einsum(
        "hqk,khd->qhd", soft_weights, value_rows, preferred_element_type=jnp.float32
    )
    return (mixed_rows.astype(jnp.bfloat16), peak_score + jnp.log(exp_total))


def attend_back(packed):
    triple_img, log_total, grad_mixed = packed
    score_scale = HD ** (-0.5)
    query_rows = triple_img[:, :, 0]
    key_rows = triple_img[:, :, 1]
    value_rows = triple_img[:, :, 2]
    raw_scores = jnp.einsum(
        "qhd,khd->hqk", query_rows, key_rows, preferred_element_type=jnp.float32
    )
    soft_weights = jnp.exp(raw_scores * score_scale - log_total)
    weights_low = soft_weights.astype(jnp.bfloat16)
    grad_values = jnp.einsum(
        "hqk,qhd->khd", weights_low, grad_mixed, preferred_element_type=jnp.float32
    )
    grad_soft = jnp.einsum(
        "qhd,khd->hqk", grad_mixed, value_rows, preferred_element_type=jnp.float32
    )
    inner_prod = jnp.sum(grad_soft * soft_weights, axis=-1, keepdims=True)
    grad_raw = (score_scale * soft_weights * (grad_soft - inner_prod)).astype(jnp.bfloat16)
    grad_query = jnp.einsum("hqk,khd->qhd", grad_raw, key_rows, preferred_element_type=jnp.float32)
    grad_keys = jnp.einsum("hqk,qhd->khd", grad_raw, query_rows, preferred_element_type=jnp.float32)
    return jnp.stack([grad_query, grad_keys, grad_values], axis=2).astype(jnp.bfloat16)


def on_device(
    layer_input,
    teacher,
    valid,
    proj_in,
    bias_query,
    bias_value,
    proj_out,
    bias_out,
    norm1_gain,
    norm1_shift,
    norm2_gain,
    norm2_shift,
    w_up,
    bias_up,
    w_down,
    bias_down,
):
    heads_here = H // lax.axis_size("col")
    head_width = heads_here * HD
    feat_here = layer_input.shape[1]
    units_here = w_up.shape[1]
    gain_one = norm1_gain.astype(jnp.float32)
    gain_two = norm2_gain.astype(jnp.float32)
    residual_in = layer_input.astype(jnp.float32)
    normed1, scale1, mid_one = norm_forward(residual_in, gain_one, norm1_shift.astype(jnp.float32))
    norm1_all, projected = first_section(mid_one.astype(jnp.bfloat16), proj_in)
    quarter = projected.shape[0]
    images = quarter // SEQ
    bias_shift = jnp.stack(
        [
            bias_query.astype(jnp.float32).reshape(heads_here, HD),
            jnp.zeros((heads_here, HD), jnp.float32),
            bias_value.astype(jnp.float32).reshape(heads_here, HD),
        ],
        axis=1,
    )
    triple = (projected.reshape(quarter, heads_here, 3, HD) + bias_shift).astype(jnp.bfloat16)
    triple_imgs = triple.reshape(images, SEQ, heads_here, 3, HD)
    mixed_imgs, log_totals = lax.map(attend, triple_imgs)
    mixed_all, attn_part = second_section(mixed_imgs.reshape(quarter, head_width), proj_out)
    resid1 = residual_in + attn_part + bias_out.astype(jnp.float32)
    normed2, scale2, mid_two = norm_forward(resid1, gain_two, norm2_shift.astype(jnp.float32))
    norm2_all, pre_part = first_section(mid_two.astype(jnp.bfloat16), w_up)
    pre = pre_part + bias_up.astype(jnp.float32)
    activated, gelu_pull = jax.vjp(lambda entry: jax.nn.gelu(entry, approximate=True), pre)
    act_all, down_part = second_section(activated.astype(jnp.bfloat16), w_down)
    result = resid1 + down_part + bias_down.astype(jnp.float32)
    mask_rows = valid.astype(jnp.float32)
    error_rows = result - teacher.astype(jnp.float32)
    err_part = jnp.sum(mask_rows[:, None] * error_rows * error_rows)
    count_part = jnp.sum(mask_rows) / lax.axis_size("row")
    err_total, valid_count = lax.psum((err_part, count_part), ("dp", "row", "col"))
    loss_value = err_total / (valid_count * D)
    tokens_all = layer_input.shape[0] * lax.axis_size("dp") * lax.axis_size("col")
    factor = tokens_all / (2.0 * valid_count)
    grad_result = 2.0 * error_rows * (mask_rows[:, None] * factor)
    grad_branch2 = grad_result.astype(jnp.bfloat16)
    grad_w_down, grad_act = second_section_back(grad_branch2, act_all, w_down)
    grad_pre = gelu_pull(grad_act)[0].astype(jnp.bfloat16)
    grad_w_up, grad_norm2 = first_section_back(grad_pre, norm2_all, w_up)
    grad_resid1 = grad_result + norm_backward(grad_norm2, normed2, scale2, gain_two)
    grad_branch1 = grad_resid1.astype(jnp.bfloat16)
    grad_proj_out, grad_mixed = second_section_back(grad_branch1, mixed_all, proj_out)
    grad_mixed_imgs = grad_mixed.astype(jnp.bfloat16).reshape(images, SEQ, heads_here, HD)
    grad_triple = lax.map(attend_back, (triple_imgs, log_totals, grad_mixed_imgs))
    grad_triple = grad_triple.reshape(quarter, heads_here, 3, HD)
    grad_proj_in, grad_norm1 = first_section_back(
        grad_triple.reshape(quarter, 3 * head_width), norm1_all, proj_in
    )
    grad_input = grad_resid1 + norm_backward(grad_norm1, normed1, scale1, gain_one)
    row_at = lax.axis_index("row") * feat_here
    col_at = lax.axis_index("col") * head_width
    feature_terms = jnp.stack(
        [
            jnp.sum(grad_norm1 * normed1, axis=0),
            jnp.sum(grad_norm1, axis=0),
            jnp.sum(grad_norm2 * normed2, axis=0),
            jnp.sum(grad_norm2, axis=0),
            jnp.sum(grad_branch1.astype(jnp.float32), axis=0),
            jnp.sum(grad_branch2.astype(jnp.float32), axis=0),
        ]
    )
    feature_full = lax.dynamic_update_slice_in_dim(
        jnp.zeros((6, D), jnp.float32), feature_terms, row_at, 1
    )
    grad_float = grad_triple.astype(jnp.float32)
    head_terms = jnp.stack(
        [
            jnp.sum(grad_float[:, :, 0], axis=0).reshape(head_width),
            jnp.sum(grad_float[:, :, 2], axis=0).reshape(head_width),
        ]
    )
    head_full = lax.dynamic_update_slice_in_dim(
        jnp.zeros((2, H * HD), jnp.float32), head_terms, col_at, 1
    )
    unit_terms = jnp.sum(grad_pre.astype(jnp.float32), axis=0)
    unit_full = lax.dynamic_update_slice_in_dim(
        jnp.zeros((FF,), jnp.float32), unit_terms, lax.axis_index("col") * units_here, 0
    )
    feature_full, head_full, unit_full = lax.psum(
        (feature_full, head_full, unit_full), ("dp", "row", "col")
    )
    feature_mine = lax.dynamic_slice_in_dim(feature_full, row_at, feat_here, 1)
    head_mine = lax.dynamic_slice_in_dim(head_full, col_at, head_width, 1)
    unit_mine = lax.dynamic_slice_in_dim(
        unit_full, lax.axis_index("col") * units_here, units_here, 0
    )
    grad_proj_in, grad_w_up = (
        lax.psum_scatter(
            grad_proj_in.astype(jnp.bfloat16), "dp", scatter_dimension=0, tiled=True
        ).astype(jnp.float32),
        lax.psum_scatter(
            grad_w_up.astype(jnp.bfloat16), "dp", scatter_dimension=0, tiled=True
        ).astype(jnp.float32),
    )
    grad_proj_out, grad_w_down = (
        lax.psum_scatter(
            grad_proj_out.astype(jnp.bfloat16), "dp", scatter_dimension=1, tiled=True
        ).astype(jnp.float32),
        lax.psum_scatter(
            grad_w_down.astype(jnp.bfloat16), "dp", scatter_dimension=1, tiled=True
        ).astype(jnp.float32),
    )
    grad_proj_in = grad_proj_in.reshape(1, grad_proj_in.shape[0], grad_proj_in.shape[1])
    grad_w_up = grad_w_up.reshape(1, grad_w_up.shape[0], grad_w_up.shape[1])
    grad_proj_out = grad_proj_out.reshape(grad_proj_out.shape[0], 1, grad_proj_out.shape[1])
    grad_w_down = grad_w_down.reshape(grad_w_down.shape[0], 1, grad_w_down.shape[1])
    return (
        result.astype(jnp.bfloat16),
        loss_value,
        grad_input,
        grad_proj_in,
        head_mine[0],
        head_mine[1],
        grad_proj_out,
        feature_mine[4],
        feature_mine[0],
        feature_mine[1],
        feature_mine[2],
        feature_mine[3],
        grad_w_up,
        unit_mine,
        grad_w_down,
        feature_mine[5],
    )


def pair_swap(values):
    return lax.ppermute(values, "dp", [(0, 1), (1, 0)])


def row_swap(values, bit):
    return lax.ppermute(values, "row", [(i, i ^ bit) for i in range(lax.axis_size("row"))])


def ring_order(size):
    return [0, 1, 3, 2] if size == 4 else list(range(size))


def ring_shift(values, step):
    order = ring_order(lax.axis_size("col"))
    size = len(order)
    return lax.ppermute(
        values, "col", [(order[i], order[(i + step) % size]) for i in range(size)]
    )


def gather_ring(shard):
    shards = [shard]
    for _ in range(lax.axis_size("col") - 1):
        shards.append(ring_shift(shards[-1], 1))
    return shards


MESH = pl.DeviceIdType.MESH
F32 = jnp.float32
BF16 = jnp.bfloat16
LOG2E = 1.4426950408889634
GELU_ROOT = 0.7978845608028654


def neighbours():
    dp, row, col = lax.axis_index("dp"), lax.axis_index("row"), lax.axis_index("col")
    return dict(
        core=(1 - dp, row, col),
        x=(dp, row + 1 - 2 * lax.rem(row, 2), col),
        y=(dp, lax.rem(row + 2, 4), col),
        next=(dp, row, lax.rem(2 * col + 3 * (col // 2) + 1, 4)),
        prev=(dp, row, lax.rem(2 * col + col // 2 + 2, 4)),
    )


def meet(peers):
    barrier = pltpu.get_barrier_semaphore()
    for peer in peers.values():
        pl.semaphore_signal(barrier, inc=1, device_id=peer, device_id_type=MESH)
    pl.semaphore_wait(barrier, len(peers))


def mm(left, right):
    return jnp.dot(left, right, preferred_element_type=F32)


def mm_nt(left, right):
    return lax.dot_general(left, right, (((1,), (1,)), ((), ())), preferred_element_type=F32)


def each_rows(count, size, body):
    @pl.loop(0, count // size)
    def _(step):
        body(pl.ds(pl.multiple_of(step * size, size), size))


def transpose_into(target, source):
    @pl.loop(0, source.shape[1] // 128)
    def _(step):
        at = pl.ds(pl.multiple_of(step * 128, 128), 128)
        target[at, :] = source[:, at].T


class Sender:
    def __init__(self, send_sems, recv_sems):
        self.sems = (send_sems, recv_sems)
        self.count = 0
        self.copies = []

    def __call__(self, source, target, peer):
        copy = pltpu.make_async_remote_copy(
            source,
            target,
            self.sems[0].at[self.count],
            self.sems[1].at[self.count],
            device_id=peer,
            device_id_type=MESH,
        )
        self.count += 1
        copy.start()
        self.copies.append(copy)
        return copy

    def finish(self):
        for copy in self.copies:
            copy.wait_send()


class Copier:
    def __init__(self, sems):
        self.sems = sems
        self.count = 0

    def __call__(self, source, target):
        copy = pltpu.make_async_copy(source, target, self.sems.at[self.count])
        self.count += 1
        copy.start()
        return copy


def norm_stats(values):
    mean_rows = jnp.mean(values, axis=-1, keepdims=True)
    centered = values - mean_rows
    inv_scale = lax.rsqrt(jnp.mean(centered * centered, axis=-1, keepdims=True) + EPS)
    return centered * inv_scale, inv_scale


def forward_kernel(
    x_ref,
    teacher_ref,
    mask_ref,
    key_ref,
    feature_ref,
    qkv_bias_ref,
    key_lane_ref,
    up_bias_ref,
    rest_bias_ref,
    factor_ref,
    spread_ref,
    rest_spread_ref,
    attn_ref,
    ff_ref,
    wpad_out,
    wff_out,
    triple_out,
    mixed_out,
    act_out,
    slope_out,
    norm1t_out,
    norm2t_out,
    rest_out,
    lse_out,
    act_rest_out,
    slope_rest_out,
    resid_out,
    grad_out,
    branch_out,
    brancht_out,
    result_out,
    err_out,
    wattn,
    wff,
    wpad,
    triple,
    mixed,
    act,
    slope,
    norm1,
    norm2,
    turned,
    part,
    got1,
    got2,
    local_sems,
    send_sems,
    recv_sems,
):
    peers = neighbours()
    meet(peers)
    feat = attn_ref.shape[0]
    half = feat // 2
    depth = 4 * feat
    tokens = norm1.shape[0]
    own = tokens // 2
    main = ff_ref.shape[1] // 2
    qkv = triple.shape[2]
    send = Sender(send_sems, recv_sems)
    keep = Copier(local_sems)

    def rows(block, low=0, size=None):
        return pl.ds(block * feat + low, feat if size is None else size)

    own_attn = keep(attn_ref, wattn.at[0, rows(0)])
    own_ff = keep(ff_ref, wff.at[0, rows(0)])
    az, ax, ay, a_low, a_high = ([None] * 4 for _ in range(5))

    def attn_source(s):
        return attn_ref if s == 0 else wattn.at[s, rows(0)]

    def attn_ring(s):
        az[s + 1] = send(attn_source(s), wattn.at[s + 1, rows(0)], peers["next"])

    def attn_plane(s):
        ax[s] = send(attn_source(s), wattn.at[s, rows(1)], peers["x"])
        ay[s] = send(attn_source(s), wattn.at[s, rows(2)], peers["y"])

    def attn_last(s):
        ax[s].wait_recv()
        a_low[s] = send(
            wattn.at[s, rows(1, 0, half)], wattn.at[s, rows(3, 0, half)], peers["y"]
        )
        ay[s].wait_recv()
        a_high[s] = send(
            wattn.at[s, rows(2, half, half)], wattn.at[s, rows(3, half, half)], peers["x"]
        )

    fz, fy, fx = ([None] * 4 for _ in range(3))

    def ff_first():
        return (
            send(ff_ref.at[pl.ds(0, half)], wff.at[0, rows(1, 0, half)], peers["x"]),
            send(ff_ref.at[pl.ds(half, half)], wff.at[0, rows(2, half, half)], peers["y"]),
        )

    def ff_ring(s):
        fz[s + 1] = [
            send(wff.at[s, piece], wff.at[s + 1, piece], peers["next"])
            for piece in (rows(0), rows(1, 0, half), rows(2, half, half))
        ]

    def ff_last(s):
        fy[s] = [
            send(wff.at[s, rows(k, 0, half)], wff.at[s, rows(k + 2, 0, half)], peers["y"])
            for k in (0, 1)
        ]
        fx[s] = [
            send(wff.at[s, rows(k, half, half)], wff.at[s, rows(k + 1, half, half)], peers["x"])
            for k in (0, 2)
        ]

    def arrive(copies):
        for copy in copies:
            copy.wait_recv()

    def attn_compute(s):
        arrive([a_low[s], a_high[s]])
        slot = s % 2
        if s == 0:
            own_attn.wait()
        if s >= 2:
            for copy in saved[s - 2]:
                copy.wait()

        def unpack(at):
            block = wattn[s, at, :]
            wpad[slot, at, :] = mm(block, spread_ref[...]).astype(BF16)
            extra = mm(block[:, block.shape[1] - 128 :], rest_spread_ref[s]).astype(BF16)
            if s == 0:
                rest_out[at, :] = extra
            else:
                rest_out[at, :] = rest_out[at, :] + extra

        each_rows(depth, feat, unpack)

        def project(at):
            values = mm(norm1[at, :], wpad[slot, :, :qkv]) + qkv_bias_ref[s]
            values = values + key_ref[at, :] * key_lane_ref[...]
            triple[slot, at, :] = values.astype(BF16)

        each_rows(tokens, own, project)
        scale = LOG2E * HD**-0.5
        for h in range(qkv // 384):
            query_at, key_at, value_at = (pl.ds((3 * h + j) * 128, 128) for j in range(3))
            value_turned = triple[slot, :, value_at].T

            def head(at, h=h, query_at=query_at, key_at=key_at, value_turned=value_turned):
                scores = mm_nt(triple[slot, :, key_at], triple[slot, at, query_at])
                peak = jnp.max(scores, axis=0, keepdims=True)
                weights = jnp.exp2((scores - peak) * scale)
                total = jnp.sum(weights, axis=0, keepdims=True)
                lse_out[2 * s + h, :, at] = peak * scale + jnp.log2(total)
                values = mm(value_turned, weights.astype(BF16)) / total
                mixed[s, at, pl.ds(h * 128, 128)] = values.T.astype(BF16)

            each_rows(tokens, 256, head)

        def out(at):
            values = mm_nt(mixed[s, at, :], wpad[slot, :, qkv:])
            part[at, :] = values if s == 0 else part[at, :] + values

        each_rows(tokens, own, out)
        saved.append(
            [
                keep(wpad.at[slot], wpad_out.at[s]),
                keep(triple.at[slot], triple_out.at[s]),
                keep(mixed.at[s], mixed_out.at[s]),
            ]
        )

    def gelu(pre):
        inner = GELU_ROOT * (pre + 0.044715 * pre * pre * pre)
        tanh = jnp.tanh(inner)
        rise = 0.5 * (1.0 + tanh)
        bend = 0.5 * pre * (1.0 - tanh * tanh) * (GELU_ROOT * (1.0 + 0.134145 * pre * pre))
        return (pre * rise).astype(BF16), (rise + bend).astype(BF16)

    def ff_compute(s):
        arrive(fy[s] + fx[s])

        def block(at):
            pre = mm(norm2[at, :], wff[s, :, :main]) + up_bias_ref[s]
            low, bent = gelu(pre)
            act[s, at, :] = low
            slope[s, at, :] = bent
            part[at, :] = part[at, :] + mm_nt(low, wff[s, :, main:])

        each_rows(tokens, own, block)
        ff_saved.extend(
            [
                keep(act.at[s], act_out.at[s]),
                keep(slope.at[s], slope_out.at[s]),
                keep(wff.at[s], wff_out.at[s]),
            ]
        )

    def rest_compute():
        def block(at):
            pre = mm(norm2[at, :], rest_out[:, :128]) + rest_bias_ref[...]
            low, bent = gelu(pre)
            act_rest_out[at, :] = low
            slope_rest_out[at, :] = bent
            part[at, :] = mm_nt(low, rest_out[:, 128:])

        each_rows(tokens, own, block)

    saved, ff_saved = [], []
    attn_ring(0)
    attn_plane(0)

    def first_norm(at):
        normed, _ = norm_stats(x_ref[at, :].astype(F32))
        norm1[at, :] = (normed * feature_ref[0:1] + feature_ref[1:2]).astype(BF16)

    each_rows(own, 16, first_norm)
    swap1 = send(norm1.at[pl.ds(0, own)], norm1.at[pl.ds(own, own)], peers["core"])
    az[1].wait_recv()
    attn_ring(1)
    attn_plane(1)
    attn_last(0)
    swap1.wait_recv()
    az[2].wait_recv()
    attn_ring(2)
    attn_plane(2)
    attn_last(1)
    first = ff_first()
    attn_compute(0)
    az[3].wait_recv()
    attn_plane(3)
    attn_last(2)
    own_ff.wait()
    arrive(first)
    ff_ring(0)
    attn_compute(1)
    attn_last(3)
    ff_last(0)
    attn_compute(2)
    attn_compute(3)
    swap2 = send(part.at[pl.ds(own, own)], got1, peers["core"])
    arrive([swap2])

    def second_norm(at):
        values = x_ref[at, :].astype(F32) + part[at, :] + got1[at, :] + feature_ref[4:5]
        resid_out[at, :] = values
        normed, _ = norm_stats(values)
        norm2[at, :] = (normed * feature_ref[2:3] + feature_ref[3:4]).astype(BF16)

    each_rows(own, 16, second_norm)
    swap2.wait_send()
    swap3 = send(norm2.at[pl.ds(0, own)], norm2.at[pl.ds(own, own)], peers["core"])
    arrive(fz[1])
    ff_ring(1)
    ff_last(1)
    transpose_into(turned, norm1)
    turn1 = keep(turned, norm1t_out)
    arrive([swap3])
    rest_compute()
    turn1.wait()
    transpose_into(turned, norm2)
    turn2 = keep(turned, norm2t_out)
    arrive(fz[2])
    ff_ring(2)
    ff_last(2)
    ff_compute(0)
    ff_compute(1)
    arrive(fz[3])
    ff_last(3)
    ff_compute(2)
    ff_compute(3)
    swap4 = send(part.at[pl.ds(own, own)], got2, peers["core"])
    arrive([swap4])
    err_out[...] = jnp.zeros_like(err_out)

    def finish(at):
        values = resid_out[at, :] + part[at, :] + got2[at, :] + feature_ref[5:6]
        result_out[at, :] = values.astype(BF16)
        error = values - teacher_ref[at, :].astype(F32)
        masked = error * mask_ref[at, :]
        err_out[...] = err_out[...] + error * masked
        grad = masked * factor_ref[...]
        grad_out[at, :] = grad
        branch_out[at, :] = grad.astype(BF16)

    each_rows(own, 16, finish)
    swap5 = send(branch_out.at[pl.ds(0, own)], branch_out.at[pl.ds(own, own)], peers["core"])
    arrive([swap5])
    transpose_into(brancht_out, branch_out)
    turn2.wait()
    for copies in saved[2:]:
        for copy in copies:
            copy.wait()
    for copy in ff_saved:
        copy.wait()
    for copy in send.copies:
        if copy is not swap2:
            copy.wait_send()


def forward_call(arrays, feat, lanes, main, qkv, mix, own, depth):
    tokens = 2 * own
    anywhere = pl.BlockSpec(memory_space=pl.ANY)
    local = pl.BlockSpec(memory_space=pltpu.VMEM)
    shapes = [
        ((4, depth, qkv + mix), BF16, anywhere),
        ((4, depth, 2 * main), BF16, anywhere),
        ((4, tokens, qkv), BF16, anywhere),
        ((4, tokens, mix), BF16, anywhere),
        ((4, tokens, main), BF16, anywhere),
        ((4, tokens, main), BF16, anywhere),
        ((depth, tokens), BF16, anywhere),
        ((depth, tokens), BF16, anywhere),
        ((depth, 256), BF16, local),
        ((8, 1, tokens), F32, local),
        ((tokens, 128), BF16, local),
        ((tokens, 128), BF16, local),
        ((own, depth), F32, local),
        ((own, depth), F32, local),
        ((tokens, depth), BF16, local),
        ((depth, tokens), BF16, local),
        ((own, depth), BF16, local),
        ((16, depth), F32, local),
    ]
    return pl.pallas_call(
        forward_kernel,
        out_shape=[jax.ShapeDtypeStruct(shape, dtype) for shape, dtype, _ in shapes],
        in_specs=[local] * 12 + [anywhere] * 2,
        out_specs=[spec for _, _, spec in shapes],
        scratch_shapes=[
            pltpu.VMEM((4, depth, lanes), BF16),
            pltpu.VMEM((4, depth, 2 * main), BF16),
            pltpu.VMEM((2, depth, qkv + mix), BF16),
            pltpu.VMEM((2, tokens, qkv), BF16),
            pltpu.VMEM((4, tokens, mix), BF16),
            pltpu.VMEM((4, tokens, main), BF16),
            pltpu.VMEM((4, tokens, main), BF16),
            pltpu.VMEM((tokens, depth), BF16),
            pltpu.VMEM((tokens, depth), BF16),
            pltpu.VMEM((depth, tokens), BF16),
            pltpu.VMEM((tokens, depth), F32),
            pltpu.VMEM((own, depth), F32),
            pltpu.VMEM((own, depth), F32),
            pltpu.SemaphoreType.DMA((32,)),
            pltpu.SemaphoreType.DMA((64,)),
            pltpu.SemaphoreType.DMA((64,)),
        ],
        compiler_params=pltpu.CompilerParams(
            collective_id=1, has_side_effects=True, vmem_limit_bytes=62 << 20
        ),
    )(*arrays)


def backward_kernel(
    branch2_ref,
    rest_ref,
    act_rest_ref,
    slope_rest_ref,
    lse_ref,
    feature_ref,
    spread_ref,
    rest_spread_ref,
    x_ref,
    resid_ref,
    grad_hbm,
    norm1t_hbm,
    norm2t_hbm,
    branch2t_hbm,
    wpad_hbm,
    wff_hbm,
    triple_hbm,
    mixed_hbm,
    act_hbm,
    slope_hbm,
    grad_in_out,
    terms_out,
    units_out,
    units_rest_out,
    heads_out,
    attn_out,
    ff_out,
    gattn,
    gff,
    wslot,
    kept,
    grad_pre,
    grad_rest,
    normt,
    brancht,
    branch1,
    part,
    got,
    grad_mid,
    dtriple,
    grad_mixed,
    grad_key,
    grad_value,
    inner_row,
    ra,
    rb,
    r1,
    r2,
    rz,
    ry,
    rx,
    rzl,
    rzh,
    rfx,
    rfy,
    local_sems,
    send_sems,
    recv_sems,
):
    peers = neighbours()
    feat = attn_out.shape[0]
    half = feat // 2
    depth = 4 * feat
    tokens = branch2_ref.shape[0]
    own = tokens // 2
    main = gff.shape[2] // 2
    qkv = triple_hbm.shape[2]
    send = Sender(send_sems, recv_sems)
    keep = Copier(local_sems)

    def rows(block, low=0, size=None):
        return pl.ds(block * feat + low, feat if size is None else size)

    def load_ff(s):
        slot = s % 2
        return [
            keep(wff_hbm.at[s], wslot.at[slot]),
            keep(act_hbm.at[s], kept.at[slot, :, pl.ds(0, main)]),
            keep(slope_hbm.at[s], kept.at[slot, :, pl.ds(main, main)]),
        ]

    def load_attn(s):
        slot = s % 2
        return [
            keep(wpad_hbm.at[s], wslot.at[slot]),
            keep(triple_hbm.at[s], kept.at[slot, :, pl.ds(0, qkv)]),
            keep(mixed_hbm.at[s], kept.at[slot, :, pl.ds(qkv, grad_mixed.shape[1])]),
        ]

    loads = {3: load_ff(3)}
    turns = [keep(norm2t_hbm, normt), keep(branch2t_hbm, brancht)]
    loads[2] = load_ff(2)
    load_grad = keep(grad_hbm, grad_mid)
    meet(peers)
    cy, cx, zl, zh = ([None] * 4 for _ in range(4))
    ca, cb, c1, c2, cz = ([None] * 4 for _ in range(5))

    def add_into(target, at, *sources):
        size = at.size

        @pl.loop(0, size // 16)
        def _(step):
            here = pl.ds(pl.multiple_of(at.start + step * 16, 16), 16)
            there = pl.ds(pl.multiple_of(step * 16, 16), 16)
            total = target[here, :].astype(F32)
            for source in sources:
                total = total + source[there, :].astype(F32)
            target[here, :] = total.astype(BF16)

    def column_sum(values):
        return jnp.sum(values.astype(F32), axis=0, keepdims=True)

    def ff_compute(s):
        slot = s % 2
        for copy in loads[s]:
            copy.wait()
        units_out[s] = jnp.zeros((1, main), F32)

        def block(at):
            grad = mm(branch2_ref[at, :], wslot[slot, :, main : 2 * main])
            low = (grad * kept[slot, at, main:].astype(F32)).astype(BF16)
            grad_pre[at, :] = low
            units_out[s] = units_out[s] + column_sum(low)
            values = mm_nt(low, wslot[slot, :, :main])
            part[at, :] = values if s == 3 else part[at, :] + values

        each_rows(tokens, own, block)
        if s == 3:
            for copy in turns:
                copy.wait()

        def grads(at):
            gff[s, at, :main] = mm(normt[at, :], grad_pre[...]).astype(BF16)
            gff[s, at, main:] = mm(brancht[at, :], kept[slot, :, :main]).astype(BF16)

        each_rows(depth, feat, grads)
        cy[s] = [
            send(gff.at[s, rows(k, 0, half)], ry.at[s, k - 2], peers["y"]) for k in (2, 3)
        ]
        cx[s] = [
            send(gff.at[s, rows(k, half, half)], rx.at[s, k // 2], peers["x"]) for k in (1, 3)
        ]
        if s >= 2:
            loads[s - 2] = load_ff(s - 2)

    def rest_compute():
        units_rest_out[...] = jnp.zeros_like(units_rest_out)

        def block(at):
            grad = mm(branch2_ref[at, :], rest_ref[:, 128:])
            low = (grad * slope_rest_ref[at, :].astype(F32)).astype(BF16)
            grad_pre[at, :128] = low
            units_rest_out[...] = units_rest_out[...] + column_sum(low)
            part[at, :] = part[at, :] + mm_nt(low, rest_ref[:, :128])

        each_rows(tokens, own, block)

        def grads(at):
            grad_rest[at, :128] = mm(normt[at, :], grad_pre[:, :128]).astype(BF16)
            grad_rest[at, 128:] = mm(brancht[at, :], act_rest_ref[...]).astype(BF16)

        each_rows(depth, feat, grads)

    def ff_add(s):
        for copy in cy[s] + cx[s]:
            copy.wait_recv()
        last = s == 3
        if not last:
            for copy in zl[s] + zh[s]:
                copy.wait_recv()
        lows, highs = [], []
        for i, k in enumerate((0, 1)):
            piece = rows(k, 0, half)
            add_into(gff.at[s], piece, ry.at[s, i], *([] if last else [rzl.at[s, i]]))
            lows.append((piece, i))
        for i, k in enumerate((0, 2)):
            piece = rows(k, half, half)
            add_into(gff.at[s], piece, rx.at[s, i], *([] if last else [rzh.at[s, i]]))
            highs.append((piece, i))
        if s:
            zl[s - 1] = [
                send(gff.at[s, piece], rzl.at[s - 1, i], peers["prev"]) for piece, i in lows
            ]
            zh[s - 1] = [
                send(gff.at[s, piece], rzh.at[s - 1, i], peers["prev"]) for piece, i in highs
            ]

    def attn_compute(s):
        slot = s % 2
        for copy in attn_loads[s]:
            copy.wait()

        def back_out(at):
            grad_mixed[at, :] = mm(branch1[at, :], wslot[slot, :, qkv:]).astype(BF16)

        each_rows(tokens, own, back_out)
        scale = HD**-0.5
        for h in range(qkv // 384):
            query_at, key_at, value_at = (pl.ds((3 * h + j) * 128, 128) for j in range(3))
            mix_at = pl.ds(h * 128, 128)
            value_of_mix = pl.ds(qkv + h * 128, 128)
            key_turned = kept[slot, :, key_at].T
            product = grad_mixed[:, mix_at].astype(F32) * kept[slot, :, value_of_mix].astype(F32)
            inner_row[...] = jnp.sum(product.T, axis=0, keepdims=True)
            grad_key[...] = jnp.zeros_like(grad_key)
            grad_value[...] = jnp.zeros_like(grad_value)

            def head(at, h=h, query_at=query_at, key_at=key_at, value_at=value_at,
                     mix_at=mix_at, key_turned=key_turned):
                query = kept[slot, at, query_at]
                grad = grad_mixed[at, mix_at]
                scores = mm_nt(kept[slot, :, key_at], query)
                weights = jnp.exp2(scores * (scale * LOG2E) - lse_ref[2 * s + h, :, at])
                grad_soft = mm_nt(kept[slot, :, value_at], grad)
                grad_raw = (weights * (grad_soft - inner_row[:, at]) * scale).astype(BF16)
                grad_value[...] += mm(weights.astype(BF16), grad)
                grad_key[...] += mm(grad_raw, query)
                dtriple[at, query_at] = mm(key_turned, grad_raw).T.astype(BF16)

            each_rows(tokens, 256, head)
            dtriple[:, key_at] = grad_key[...].astype(BF16)
            dtriple[:, value_at] = grad_value[...].astype(BF16)
        heads_out[s] = jnp.zeros((1, qkv), F32)

        def back_in(at):
            values = mm_nt(dtriple[at, :], wslot[slot, :, :qkv])
            part[at, :] = values if s == 3 else part[at, :] + values
            heads_out[s] = heads_out[s] + column_sum(dtriple[at, :])

        each_rows(tokens, own, back_in)

        def grads(at):
            first = mm(normt[at, :], dtriple[...]).astype(BF16)
            second = mm(brancht[at, :], kept[slot, :, qkv:]).astype(BF16)
            packed = mm_nt(first, spread_ref[:, :qkv]) + mm_nt(second, spread_ref[:, qkv:])
            gattn[s, at, :] = packed.astype(BF16)
            tail = pl.ds(packed.shape[1] - 128, 128)
            extra = mm_nt(grad_rest[at, :], rest_spread_ref[s])
            gattn[s, at, tail] = (gattn[s, at, tail].astype(F32) + extra).astype(BF16)

        each_rows(depth, feat, grads)
        ca[s] = send(gattn.at[s, rows(3, 0, half)], ra.at[s], peers["y"])
        cb[s] = send(gattn.at[s, rows(3, half, half)], rb.at[s], peers["x"])
        if s >= 2:
            attn_loads[s - 2] = load_attn(s - 2)

    def attn_plane(s):
        ca[s].wait_recv()
        add_into(gattn.at[s], rows(1, 0, half), ra.at[s])
        c1[s] = send(gattn.at[s, rows(1)], r1.at[s], peers["x"])
        cb[s].wait_recv()
        add_into(gattn.at[s], rows(2, half, half), rb.at[s])
        c2[s] = send(gattn.at[s, rows(2)], r2.at[s], peers["y"])

    def attn_ring(s):
        c1[s].wait_recv()
        c2[s].wait_recv()
        if s < 3:
            cz[s].wait_recv()
        add_into(gattn.at[s], rows(0), r1.at[s], r2.at[s], *([rz.at[s]] if s < 3 else []))
        if s:
            cz[s - 1] = send(gattn.at[s, rows(0)], rz.at[s - 1], peers["prev"])

    terms_out[...] = jnp.zeros_like(terms_out)

    def add_term(index, values):
        terms_out[index] = terms_out[index] + values

    ff_compute(3)
    ff_compute(2)
    ff_compute(1)
    ff_add(3)
    ff_compute(0)
    attn_loads = {3: load_attn(3), 2: load_attn(2)}
    rest_compute()
    load_norm = keep(norm1t_hbm, normt)
    swap1 = send(part.at[pl.ds(own, own)], got, peers["core"])
    swap1.wait_recv()
    load_grad.wait()

    def mid(at):
        normed, inv_scale = norm_stats(resid_ref[at, :])
        grad_norm = part[at, :] + got[at, :]
        add_term(2, grad_norm * normed)
        add_term(3, grad_norm)
        scaled = grad_norm * feature_ref[2:3]
        first = jnp.mean(scaled, axis=-1, keepdims=True)
        second = jnp.mean(scaled * normed, axis=-1, keepdims=True)
        grad = grad_mid[at, :] + inv_scale * (scaled - first - normed * second)
        grad_mid[at, :] = grad
        low = grad.astype(BF16)
        branch1[at, :] = low
        add_term(4, low.astype(F32))
        add_term(5, branch2_ref[at, :].astype(F32))

    each_rows(own, 16, mid)
    swap1.wait_send()
    swap2 = send(branch1.at[pl.ds(0, own)], branch1.at[pl.ds(own, own)], peers["core"])
    swap2.wait_recv()
    load_norm.wait()
    transpose_into(brancht, branch1)
    attn_compute(3)
    ff_add(2)
    attn_compute(2)
    attn_plane(3)
    attn_compute(1)
    attn_plane(2)
    ff_add(1)
    attn_ring(3)
    attn_compute(0)
    swap3 = send(part.at[pl.ds(own, own)], got, peers["core"])
    attn_plane(1)
    attn_ring(2)
    attn_plane(0)
    swap3.wait_recv()

    def last(at):
        normed, inv_scale = norm_stats(x_ref[at, :].astype(F32))
        grad_norm = part[at, :] + got[at, :]
        add_term(0, grad_norm * normed)
        add_term(1, grad_norm)
        scaled = grad_norm * feature_ref[0:1]
        first = jnp.mean(scaled, axis=-1, keepdims=True)
        second = jnp.mean(scaled * normed, axis=-1, keepdims=True)
        grad = grad_mid[at, :] + inv_scale * (scaled - first - normed * second)
        grad_in_out[at, :] = grad.astype(BF16)

    each_rows(own, 16, last)
    ff_add(0)
    end_low = send(gff.at[0, rows(1, 0, half)], rfx, peers["x"])
    end_high = send(gff.at[0, rows(2, half, half)], rfy, peers["y"])
    attn_ring(1)
    end_low.wait_recv()
    end_high.wait_recv()
    add_into(gff.at[0], rows(0, 0, half), rfx)
    add_into(gff.at[0], rows(0, half, half), rfy)
    ff_done = keep(gff.at[0, rows(0)], ff_out)
    attn_ring(0)
    attn_done = keep(gattn.at[0, rows(0)], attn_out)
    ff_done.wait()
    attn_done.wait()
    for copy in send.copies:
        if copy is not swap1:
            copy.wait_send()


def backward_call(arrays, feat, lanes, main, qkv, mix, own, depth):
    tokens = 2 * own
    half = feat // 2
    anywhere = pl.BlockSpec(memory_space=pl.ANY)
    local = pl.BlockSpec(memory_space=pltpu.VMEM)
    shapes = [
        ((own, depth), BF16, local),
        ((6, 16, depth), F32, local),
        ((4, 1, main), F32, local),
        ((1, 128), F32, local),
        ((4, 1, qkv), F32, local),
        ((feat, lanes), BF16, anywhere),
        ((feat, 2 * main), BF16, anywhere),
    ]
    return pl.pallas_call(
        backward_kernel,
        out_shape=[jax.ShapeDtypeStruct(shape, dtype) for shape, dtype, _ in shapes],
        in_specs=[local] * 10 + [anywhere] * 10,
        out_specs=[spec for _, _, spec in shapes],
        scratch_shapes=[
            pltpu.VMEM((4, depth, lanes), BF16),
            pltpu.VMEM((4, depth, 2 * main), BF16),
            pltpu.VMEM((2, depth, 2 * main), BF16),
            pltpu.VMEM((2, tokens, qkv + mix), BF16),
            pltpu.VMEM((tokens, main), BF16),
            pltpu.VMEM((depth, 256), BF16),
            pltpu.VMEM((depth, tokens), BF16),
            pltpu.VMEM((depth, tokens), BF16),
            pltpu.VMEM((tokens, depth), BF16),
            pltpu.VMEM((tokens, depth), F32),
            pltpu.VMEM((own, depth), F32),
            pltpu.VMEM((own, depth), F32),
            pltpu.VMEM((tokens, qkv), BF16),
            pltpu.VMEM((tokens, mix), BF16),
            pltpu.VMEM((tokens, 128), F32),
            pltpu.VMEM((tokens, 128), F32),
            pltpu.VMEM((1, tokens), F32),
            pltpu.VMEM((4, half, lanes), BF16),
            pltpu.VMEM((4, half, lanes), BF16),
            pltpu.VMEM((4, feat, lanes), BF16),
            pltpu.VMEM((4, feat, lanes), BF16),
            pltpu.VMEM((3, feat, lanes), BF16),
            pltpu.VMEM((4, 2, half, 2 * main), BF16),
            pltpu.VMEM((4, 2, half, 2 * main), BF16),
            pltpu.VMEM((3, 2, half, 2 * main), BF16),
            pltpu.VMEM((3, 2, half, 2 * main), BF16),
            pltpu.VMEM((half, 2 * main), BF16),
            pltpu.VMEM((half, 2 * main), BF16),
            pltpu.SemaphoreType.DMA((32,)),
            pltpu.SemaphoreType.DMA((72,)),
            pltpu.SemaphoreType.DMA((72,)),
        ],
        compiler_params=pltpu.CompilerParams(
            collective_id=2, has_side_effects=True, vmem_limit_bytes=63 << 20
        ),
    )(*arrays)


def on_chip(
    layer_input,
    teacher,
    valid,
    proj_in,
    bias_query,
    bias_value,
    proj_out,
    bias_out,
    norm1_gain,
    norm1_shift,
    norm2_gain,
    norm2_shift,
    w_up,
    bias_up,
    w_down,
    bias_down,
):
    core = lax.axis_index("dp")
    row = lax.axis_index("row")
    cols = lax.axis_size("col")
    feat = layer_input.shape[1]
    images = layer_input.shape[0] // SEQ
    half_seq = (SEQ + 255) // 256 * 128
    pad_seq = 2 * half_seq
    units = w_up.shape[1] // 2
    width = proj_out.shape[0] // 2
    heads = width // HD

    def core_half(values, axis):
        size = values.shape[axis] // 2
        return lax.dynamic_slice_in_dim(values, core * size, size, axis)

    def to_chip(values):
        imgs = jnp.pad(values.reshape(images, SEQ, -1), ((0, 0), (0, pad_seq - SEQ), (0, 0)))
        imgs = imgs.reshape(images, 2, half_seq, -1)
        keep = lax.dynamic_index_in_dim(imgs, core, 1, False)
        give = lax.dynamic_index_in_dim(imgs, 1 - core, 1, False)
        got = pair_swap(give)
        first = core == 0
        every = jnp.concatenate([jnp.where(first, keep, got), jnp.where(first, got, keep)], axis=0)
        parts = []
        for k in range(4):
            part = lax.dynamic_index_in_dim(every, row ^ k, 0, False)
            parts.append(row_swap(part, k) if k else part)
        return jnp.concatenate(parts, axis=1)

    def from_chip(values):
        parts = []
        for k in range(4):
            part = values[:, k * feat : (k + 1) * feat]
            parts.append(row_swap(part, k) if k else part)
        stacked = jnp.stack(parts)
        every = jnp.stack([lax.dynamic_index_in_dim(stacked, row ^ i, 0, False) for i in range(4)])
        every = every.reshape(2, images, half_seq, feat)
        mine = lax.dynamic_index_in_dim(every, core, 0, False)
        got = pair_swap(lax.dynamic_index_in_dim(every, 1 - core, 0, False))
        first = core == 0
        both = jnp.stack([jnp.where(first, mine, got), jnp.where(first, got, mine)], axis=1)
        return both.reshape(images, pad_seq, feat)[:, :SEQ].reshape(images * SEQ, feat)

    main = units // 128 * 128
    rest = units - main
    at = 4 * width
    lanes = (at + 2 * rest + 127) // 128 * 128
    qkv, mix = 3 * heads * 128, heads * 128
    up_half, down_half = core_half(w_up, 1), core_half(w_down, 0).T
    attn_shard = jnp.concatenate(
        [
            core_half(proj_in, 1),
            core_half(proj_out, 0).T,
            up_half[:, main:],
            down_half[:, main:],
            jnp.zeros((feat, lanes - at - 2 * rest), jnp.bfloat16),
        ],
        axis=1,
    )
    ff_shard = jnp.concatenate([up_half[:, :main], down_half[:, :main]], axis=1)
    lane = jnp.arange(lanes)
    spread_at = jnp.where(lane < at, lane // HD * 128 + lane % HD, -1)
    spread = (spread_at[:, None] == jnp.arange(qkv + mix)[None]).astype(jnp.bfloat16)
    tail = lane[-128:]
    rest_spread = []
    for s in range(cols):
        up_at = jnp.where((tail >= at) & (tail < at + rest), tail - at + s * rest, -1)
        down_at = jnp.where(
            (tail >= at + rest) & (tail < at + 2 * rest), tail - at - rest + s * rest + 128, -1
        )
        place = jnp.arange(256)[None]
        rest_spread.append((up_at[:, None] == place) | (down_at[:, None] == place))
    rest_spread = jnp.stack(rest_spread).astype(jnp.bfloat16)
    features = jnp.stack([norm1_gain, norm1_shift, norm2_gain, norm2_shift, bias_out, bias_down])
    features = jnp.concatenate([features] + [row_swap(features, k) for k in (1, 2, 3)], axis=1)
    features = jnp.pad(features.astype(jnp.float32), ((0, 2), (0, 0)))
    col_biases = gather_ring(
        jnp.concatenate([core_half(bias_query, 0), core_half(bias_value, 0), core_half(bias_up, 0)])[None]
    )

    x_half = to_chip(layer_input)
    teacher_half = to_chip(teacher)
    count = jnp.sum(valid.astype(jnp.float32)).reshape(1, 1)
    count = count + pair_swap(count)
    for bit in (1, 2):
        count = count + lax.ppermute(count, "col", [(i, i ^ bit) for i in range(cols)])
    valid_imgs = jnp.pad(valid.reshape(images, SEQ), ((0, 0), (0, pad_seq - SEQ)))
    other_valid = pair_swap(valid_imgs)
    from_here = (row // images) == core
    chip_valid = lax.dynamic_index_in_dim(
        jnp.where(from_here, valid_imgs, other_valid), lax.rem(row, images), 0, False
    )
    mask_half = lax.dynamic_slice_in_dim(chip_valid, core * half_seq, half_seq, 0)
    mask_half = mask_half.astype(jnp.float32)[:, None]

    place = jnp.arange(pad_seq)
    token = jnp.where(place < half_seq, place + core * half_seq, place - core * half_seq)
    key_column = jnp.where(token < SEQ, 0.0, -1e30).astype(jnp.float32)[:, None]
    lane = jnp.arange(qkv)
    key_lane = (lane % 384 == 128 + HD).astype(jnp.float32)[None]
    one_lane = (lane % 384 == HD).astype(jnp.float32)[None]
    qkv_biases, up_biases, rest_biases = [], [], []
    for s in range(cols):
        bias = col_biases[s][0].astype(jnp.float32)
        query, value = bias[:width].reshape(heads, HD), bias[width : 2 * width].reshape(heads, HD)
        spaced = jnp.stack([query, jnp.zeros_like(query), value], axis=1)
        spaced = jnp.pad(spaced, ((0, 0), (0, 0), (0, 128 - HD))).reshape(1, qkv)
        qkv_biases.append(spaced + one_lane)
        up_biases.append(bias[None, 2 * width : 2 * width + main])
        rest_biases.append(bias[2 * width + main :])
    rest_bias = jnp.pad(jnp.concatenate(rest_biases), (0, 128 - cols * rest))[None]
    tokens_all = layer_input.shape[0] * lax.axis_size("dp") * cols
    factor = tokens_all / count

    sizes = (feat, lanes, main, qkv, mix, half_seq, 4 * feat)
    (
        wpad, wff, triple, mixed, act, slope, norm1t, norm2t, rest_weight, lse, act_rest,
        slope_rest, resid1, grad_result, branch2, branch2t, result, err_rows,
    ) = forward_call(
        (
            x_half, teacher_half, mask_half, key_column, features, jnp.stack(qkv_biases),
            key_lane, jnp.stack(up_biases), rest_bias, jnp.broadcast_to(factor, (1, 4 * feat)),
            spread, rest_spread, attn_shard, ff_shard,
        ),
        *sizes,
    )
    layer_output = from_chip(result)
    err_part = jnp.sum(err_rows)
    grad_in, terms, unit_main, unit_rest, head_rows, attn_sum, ff_sum = backward_call(
        (
            branch2, rest_weight, act_rest, slope_rest, lse, features, spread, rest_spread,
            x_half, resid1, grad_result, norm1t, norm2t, branch2t, wpad, wff, triple, mixed,
            act, slope,
        ),
        *sizes,
    )
    grad_input = from_chip(grad_in).astype(jnp.float32)
    terms = jnp.sum(terms, axis=1)
    head_rows = head_rows.reshape(cols, heads, 3, 128)[..., :HD]
    bias_rows = [
        jnp.concatenate(
            [
                head_rows[s, :, 0].reshape(1, width),
                head_rows[s, :, 2].reshape(1, width),
                unit_main[s],
                unit_rest[:, s * rest : (s + 1) * rest],
            ],
            axis=1,
        )
        for s in range(cols)
    ]
    bias_sum = bias_rows[cols - 1]
    for s in reversed(range(cols - 1)):
        bias_sum = bias_rows[s] + ring_shift(bias_sum, -1)
    near = terms[:, : 2 * feat] + row_swap(terms[:, 2 * feat :], 2)
    terms = near[:, :feat] + row_swap(near[:, feat:], 1)

    def plane_sum(values):
        values = values + row_swap(values, 1)
        return values + row_swap(values, 2)

    err_plane = plane_sum(err_part.reshape(1, 1))
    sums = jnp.concatenate([terms, jnp.broadcast_to(err_plane, (1, feat))], axis=0)
    for bit in (1, 2):
        sums = sums + lax.ppermute(sums, "col", [(i, i ^ bit) for i in range(cols)])
    sums = sums + pair_swap(sums)
    loss_value = sums[6, 0] / (count[0, 0] * D)

    def both_halves(values):
        got = pair_swap(values)
        first = core == 0
        return jnp.concatenate(
            [jnp.where(first, values, got), jnp.where(first, got, values)], axis=-1
        )

    bias_sum = plane_sum(bias_sum)[0]
    head_mine = both_halves(bias_sum[: 2 * width].reshape(2, width))
    unit_mine = both_halves(bias_sum[2 * width :])

    def weight_rows(total):
        size = feat // 2
        keep = lax.dynamic_slice_in_dim(total, core * size, size, 0)
        give = lax.dynamic_slice_in_dim(total, (1 - core) * size, size, 0)
        return keep, pair_swap(give)

    def joined(keep, got, axis):
        first = core == 0
        return jnp.concatenate(
            [jnp.where(first, keep, got), jnp.where(first, got, keep)], axis=axis
        ).astype(jnp.float32)

    ff_keep, ff_got = weight_rows(ff_sum)
    attn_keep, attn_got = weight_rows(attn_sum)

    def up_of(attn, ff):
        return jnp.concatenate([ff[:, :main], attn[:, at : at + rest]], axis=1)

    def down_of(attn, ff):
        return jnp.concatenate([ff[:, main:], attn[:, at + rest : at + 2 * rest]], axis=1).T

    grad_w_up = joined(up_of(attn_keep, ff_keep), up_of(attn_got, ff_got), 1)
    grad_w_down = joined(down_of(attn_keep, ff_keep), down_of(attn_got, ff_got), 0)
    grad_proj_in = joined(attn_keep[:, : 3 * width], attn_got[:, : 3 * width], 1)
    grad_proj_out = joined(attn_keep[:, 3 * width : at].T, attn_got[:, 3 * width : at].T, 0)
    return (
        layer_output,
        loss_value,
        grad_input,
        grad_proj_in[None],
        head_mine[0],
        head_mine[1],
        grad_proj_out[:, None],
        sums[4],
        sums[0],
        sums[1],
        sums[2],
        sums[3],
        grad_w_up[None],
        unit_mine,
        grad_w_down[:, None],
        sums[5],
    )


def one_image_a_chip(mesh, tokens):
    sizes = mesh.shape
    pairs = sizes["dp"] == 2 and sizes["row"] == 4 and sizes["col"] == 4
    return pairs and tokens == SEQ * sizes["row"] * sizes["col"]


def solution(mesh):
    placed = (
        P(("dp", "col"), "row"),
        P(("dp", "col"), "row"),
        P(("dp", "col")),
        P("row", "col"),
        P("col"),
        P("col"),
        P("col", "row"),
        P("row"),
        P("row"),
        P("row"),
        P("row"),
        P("row"),
        P("row", "col"),
        P("col"),
        P("col", "row"),
        P("row"),
    )
    returned = (
            P(("dp", "col"), "row"),
            P(),
            P(("dp", "col"), "row"),
            P("row", "dp", "col"),
            P("col"),
            P("col"),
            P("col", "row", "dp"),
            P("row"),
            P("row"),
            P("row"),
            P("row"),
            P("row"),
            P("row", "dp", "col"),
            P("col"),
            P("col", "row", "dp"),
            P("row"),
        )

    def whole(layer_input, *others):
        body = on_chip if one_image_a_chip(mesh, layer_input.shape[0]) else on_device
        return jax.shard_map(
            body, mesh=mesh, in_specs=placed, out_specs=returned, check_vma=False
        )(layer_input, *others)

    return whole
```

```python
import functools

import jax
import jax.numpy as jnp
from jax import lax
from jax.experimental import pallas as pl
from jax.experimental.pallas import tpu as pltpu
from jax.sharding import PartitionSpec as P

D = 1152
H = 16
HD = 72
FF = 4304
SEQ = 729


EPS = 1e-06


def feature_totals(left, right):
    return lax.psum(
        (jnp.sum(left, axis=-1, keepdims=True), jnp.sum(right, axis=-1, keepdims=True)), "row"
    )


def norm_forward(values, gain, shift):
    first_sum, second_sum = feature_totals(values, values * values)
    mean_rows = first_sum / D
    var_rows = second_sum / D - mean_rows * mean_rows
    inv_scale = lax.rsqrt(var_rows + EPS)
    normed = (values - mean_rows) * inv_scale
    return (normed, inv_scale, normed * gain + shift)


def norm_backward(grad_out, normed, inv_scale, gain):
    grad_normed = grad_out * gain
    first_sum, second_sum = feature_totals(grad_normed, grad_normed * normed)
    return inv_scale * (grad_normed - first_sum / D - normed * second_sum / D)


def first_section(local_rows, weight):
    gathered = lax.all_gather(local_rows, "col", axis=0, tiled=True)
    share_rows = gathered.shape[0] // lax.axis_size("row")

    def partial_term(row_start, row_count):
        return jnp.dot(gathered, weight, preferred_element_type=jnp.float32)

    result = lax.psum_scatter(
        partial_term(jnp.int32(0), lax.axis_size("row") * share_rows),
        "row",
        scatter_dimension=0,
        tiled=True,
    )
    return (gathered, result)


def second_section(quarter_rows, weight):
    gathered = lax.all_gather(quarter_rows, "row", axis=0, tiled=True)
    share_rows = gathered.shape[0] // lax.axis_size("col")

    def partial_term(row_start, row_count):
        return jnp.dot(gathered, weight, preferred_element_type=jnp.float32)

    result = lax.psum_scatter(
        partial_term(jnp.int32(0), lax.axis_size("col") * share_rows),
        "col",
        scatter_dimension=0,
        tiled=True,
    )
    return (gathered, result)


def second_section_back(grad_local, gathered, weight):
    grad_all = lax.all_gather(grad_local, "col", axis=0, tiled=True)
    grad_weight = lax.dot_general(
        gathered, grad_all, (((0,), (0,)), ((), ())), preferred_element_type=jnp.float32
    )
    share_rows = grad_all.shape[0] // lax.axis_size("row")

    def partial_term(row_start, row_count):
        return lax.dot_general(
            grad_all, weight, (((1,), (1,)), ((), ())), preferred_element_type=jnp.float32
        )

    result = lax.psum_scatter(
        partial_term(jnp.int32(0), lax.axis_size("row") * share_rows),
        "row",
        scatter_dimension=0,
        tiled=True,
    )
    return (grad_weight, result)


def first_section_back(grad_quarter, gathered, weight):
    grad_all = lax.all_gather(grad_quarter, "row", axis=0, tiled=True)
    grad_weight = lax.dot_general(
        gathered, grad_all, (((0,), (0,)), ((), ())), preferred_element_type=jnp.float32
    )
    share_rows = grad_all.shape[0] // lax.axis_size("col")

    def partial_term(row_start, row_count):
        return lax.dot_general(
            grad_all, weight, (((1,), (1,)), ((), ())), preferred_element_type=jnp.float32
        )

    result = lax.psum_scatter(
        partial_term(jnp.int32(0), lax.axis_size("col") * share_rows).astype(jnp.bfloat16),
        "col",
        scatter_dimension=0,
        tiled=True,
    ).astype(jnp.float32)
    return (grad_weight, result)


def attend(triple_img):
    score_scale = HD ** (-0.5)
    query_rows = triple_img[:, :, 0]
    key_rows = triple_img[:, :, 1]
    value_rows = triple_img[:, :, 2]
    raw_scores = jnp.einsum(
        "qhd,khd->hqk", query_rows, key_rows, preferred_element_type=jnp.float32
    )
    scaled = raw_scores * score_scale
    peak_score = jnp.max(scaled, axis=-1, keepdims=True)
    exp_scores = jnp.exp(scaled - peak_score)
    exp_total = jnp.sum(exp_scores, axis=-1, keepdims=True)
    soft_weights = (exp_scores / exp_total).astype(jnp.bfloat16)
    mixed_rows = jnp.einsum(
        "hqk,khd->qhd", soft_weights, value_rows, preferred_element_type=jnp.float32
    )
    return (mixed_rows.astype(jnp.bfloat16), peak_score + jnp.log(exp_total))


def attend_back(packed):
    triple_img, log_total, grad_mixed = packed
    score_scale = HD ** (-0.5)
    query_rows = triple_img[:, :, 0]
    key_rows = triple_img[:, :, 1]
    value_rows = triple_img[:, :, 2]
    raw_scores = jnp.einsum(
        "qhd,khd->hqk", query_rows, key_rows, preferred_element_type=jnp.float32
    )
    soft_weights = jnp.exp(raw_scores * score_scale - log_total)
    weights_low = soft_weights.astype(jnp.bfloat16)
    grad_values = jnp.einsum(
        "hqk,qhd->khd", weights_low, grad_mixed, preferred_element_type=jnp.float32
    )
    grad_soft = jnp.einsum(
        "qhd,khd->hqk", grad_mixed, value_rows, preferred_element_type=jnp.float32
    )
    inner_prod = jnp.sum(grad_soft * soft_weights, axis=-1, keepdims=True)
    grad_raw = (score_scale * soft_weights * (grad_soft - inner_prod)).astype(jnp.bfloat16)
    grad_query = jnp.einsum("hqk,khd->qhd", grad_raw, key_rows, preferred_element_type=jnp.float32)
    grad_keys = jnp.einsum("hqk,qhd->khd", grad_raw, query_rows, preferred_element_type=jnp.float32)
    return jnp.stack([grad_query, grad_keys, grad_values], axis=2).astype(jnp.bfloat16)


def on_device(
    layer_input,
    teacher,
    valid,
    proj_in,
    bias_query,
    bias_value,
    proj_out,
    bias_out,
    norm1_gain,
    norm1_shift,
    norm2_gain,
    norm2_shift,
    w_up,
    bias_up,
    w_down,
    bias_down,
):
    heads_here = H // lax.axis_size("col")
    head_width = heads_here * HD
    feat_here = layer_input.shape[1]
    units_here = w_up.shape[1]
    gain_one = norm1_gain.astype(jnp.float32)
    gain_two = norm2_gain.astype(jnp.float32)
    residual_in = layer_input.astype(jnp.float32)
    normed1, scale1, mid_one = norm_forward(residual_in, gain_one, norm1_shift.astype(jnp.float32))
    norm1_all, projected = first_section(mid_one.astype(jnp.bfloat16), proj_in)
    quarter = projected.shape[0]
    images = quarter // SEQ
    bias_shift = jnp.stack(
        [
            bias_query.astype(jnp.float32).reshape(heads_here, HD),
            jnp.zeros((heads_here, HD), jnp.float32),
            bias_value.astype(jnp.float32).reshape(heads_here, HD),
        ],
        axis=1,
    )
    triple = (projected.reshape(quarter, heads_here, 3, HD) + bias_shift).astype(jnp.bfloat16)
    triple_imgs = triple.reshape(images, SEQ, heads_here, 3, HD)
    mixed_imgs, log_totals = lax.map(attend, triple_imgs)
    mixed_all, attn_part = second_section(mixed_imgs.reshape(quarter, head_width), proj_out)
    resid1 = residual_in + attn_part + bias_out.astype(jnp.float32)
    normed2, scale2, mid_two = norm_forward(resid1, gain_two, norm2_shift.astype(jnp.float32))
    norm2_all, pre_part = first_section(mid_two.astype(jnp.bfloat16), w_up)
    pre = pre_part + bias_up.astype(jnp.float32)
    activated, gelu_pull = jax.vjp(lambda entry: jax.nn.gelu(entry, approximate=True), pre)
    act_all, down_part = second_section(activated.astype(jnp.bfloat16), w_down)
    result = resid1 + down_part + bias_down.astype(jnp.float32)
    mask_rows = valid.astype(jnp.float32)
    error_rows = result - teacher.astype(jnp.float32)
    err_part = jnp.sum(mask_rows[:, None] * error_rows * error_rows)
    count_part = jnp.sum(mask_rows) / lax.axis_size("row")
    err_total, valid_count = lax.psum((err_part, count_part), ("dp", "row", "col"))
    loss_value = err_total / (valid_count * D)
    tokens_all = layer_input.shape[0] * lax.axis_size("dp") * lax.axis_size("col")
    factor = tokens_all / (2.0 * valid_count)
    grad_result = 2.0 * error_rows * (mask_rows[:, None] * factor)
    grad_branch2 = grad_result.astype(jnp.bfloat16)
    grad_w_down, grad_act = second_section_back(grad_branch2, act_all, w_down)
    grad_pre = gelu_pull(grad_act)[0].astype(jnp.bfloat16)
    grad_w_up, grad_norm2 = first_section_back(grad_pre, norm2_all, w_up)
    grad_resid1 = grad_result + norm_backward(grad_norm2, normed2, scale2, gain_two)
    grad_branch1 = grad_resid1.astype(jnp.bfloat16)
    grad_proj_out, grad_mixed = second_section_back(grad_branch1, mixed_all, proj_out)
    grad_mixed_imgs = grad_mixed.astype(jnp.bfloat16).reshape(images, SEQ, heads_here, HD)
    grad_triple = lax.map(attend_back, (triple_imgs, log_totals, grad_mixed_imgs))
    grad_triple = grad_triple.reshape(quarter, heads_here, 3, HD)
    grad_proj_in, grad_norm1 = first_section_back(
        grad_triple.reshape(quarter, 3 * head_width), norm1_all, proj_in
    )
    grad_input = grad_resid1 + norm_backward(grad_norm1, normed1, scale1, gain_one)
    row_at = lax.axis_index("row") * feat_here
    col_at = lax.axis_index("col") * head_width
    feature_terms = jnp.stack(
        [
            jnp.sum(grad_norm1 * normed1, axis=0),
            jnp.sum(grad_norm1, axis=0),
            jnp.sum(grad_norm2 * normed2, axis=0),
            jnp.sum(grad_norm2, axis=0),
            jnp.sum(grad_branch1.astype(jnp.float32), axis=0),
            jnp.sum(grad_branch2.astype(jnp.float32), axis=0),
        ]
    )
    feature_full = lax.dynamic_update_slice_in_dim(
        jnp.zeros((6, D), jnp.float32), feature_terms, row_at, 1
    )
    grad_float = grad_triple.astype(jnp.float32)
    head_terms = jnp.stack(
        [
            jnp.sum(grad_float[:, :, 0], axis=0).reshape(head_width),
            jnp.sum(grad_float[:, :, 2], axis=0).reshape(head_width),
        ]
    )
    head_full = lax.dynamic_update_slice_in_dim(
        jnp.zeros((2, H * HD), jnp.float32), head_terms, col_at, 1
    )
    unit_terms = jnp.sum(grad_pre.astype(jnp.float32), axis=0)
    unit_full = lax.dynamic_update_slice_in_dim(
        jnp.zeros((FF,), jnp.float32), unit_terms, lax.axis_index("col") * units_here, 0
    )
    feature_full, head_full, unit_full = lax.psum(
        (feature_full, head_full, unit_full), ("dp", "row", "col")
    )
    feature_mine = lax.dynamic_slice_in_dim(feature_full, row_at, feat_here, 1)
    head_mine = lax.dynamic_slice_in_dim(head_full, col_at, head_width, 1)
    unit_mine = lax.dynamic_slice_in_dim(
        unit_full, lax.axis_index("col") * units_here, units_here, 0
    )
    grad_proj_in, grad_w_up = (
        lax.psum_scatter(
            grad_proj_in.astype(jnp.bfloat16), "dp", scatter_dimension=0, tiled=True
        ).astype(jnp.float32),
        lax.psum_scatter(
            grad_w_up.astype(jnp.bfloat16), "dp", scatter_dimension=0, tiled=True
        ).astype(jnp.float32),
    )
    grad_proj_out, grad_w_down = (
        lax.psum_scatter(
            grad_proj_out.astype(jnp.bfloat16), "dp", scatter_dimension=1, tiled=True
        ).astype(jnp.float32),
        lax.psum_scatter(
            grad_w_down.astype(jnp.bfloat16), "dp", scatter_dimension=1, tiled=True
        ).astype(jnp.float32),
    )
    grad_proj_in = grad_proj_in.reshape(1, grad_proj_in.shape[0], grad_proj_in.shape[1])
    grad_w_up = grad_w_up.reshape(1, grad_w_up.shape[0], grad_w_up.shape[1])
    grad_proj_out = grad_proj_out.reshape(grad_proj_out.shape[0], 1, grad_proj_out.shape[1])
    grad_w_down = grad_w_down.reshape(grad_w_down.shape[0], 1, grad_w_down.shape[1])
    return (
        result.astype(jnp.bfloat16),
        loss_value,
        grad_input,
        grad_proj_in,
        head_mine[0],
        head_mine[1],
        grad_proj_out,
        feature_mine[4],
        feature_mine[0],
        feature_mine[1],
        feature_mine[2],
        feature_mine[3],
        grad_w_up,
        unit_mine,
        grad_w_down,
        feature_mine[5],
    )


MESH = pl.DeviceIdType.MESH
F32 = jnp.float32
BF16 = jnp.bfloat16
LOG2E = 1.4426950408889634
GELU_ROOT = 0.7978845608028654


def place():
    return lax.axis_index("dp"), lax.axis_index("row"), lax.axis_index("col")


def flip(row, other):
    return lax.rem(row // 2 + other // 2, 2) * 2 + lax.rem(row + other, 2)


def neighbours():
    dp, row, col = place()
    return dict(
        core=(1 - dp, row, col),
        x=(dp, flip(row, 1), col),
        y=(dp, flip(row, 2), col),
        diagonal=(dp, flip(row, 3), col),
        next=(dp, row, lax.rem(2 * col + 3 * (col // 2) + 1, 4)),
        prev=(dp, row, lax.rem(2 * col + col // 2 + 2, 4)),
    )


def images_group():
    dp, row, col = place()
    steps = [(core, step) for core in (0, 1) for step in range(4)][1:]
    return [(lax.rem(dp + core, 2), row, lax.rem(col + step, 4)) for core, step in steps]


def meet():
    dp, row, col = place()
    plane = [(core, k) for core in (0, 1) for k in range(4)][1:]
    peers = [(lax.rem(dp + core, 2), flip(row, k), col) for core, k in plane]
    peers += [peer for i, peer in enumerate(images_group()) if i != 3]
    barrier = pltpu.get_barrier_semaphore()
    for peer in peers:
        pl.semaphore_signal(barrier, inc=1, device_id=peer, device_id_type=MESH)
    pl.semaphore_wait(barrier, len(peers))


class Shuffle:
    def __init__(self, send_sems, recv_sems, local_sem):
        self.sems = send_sems, recv_sems, local_sem
        self.pending = []

    def remote(self, source, target, i, slot, peer):
        return pltpu.make_async_remote_copy(
            source, target, self.sems[0].at[i], self.sems[1].at[slot],
            device_id=peer, device_id_type=MESH,
        )

    def spread(self, pieces, blocks):
        dp, row, col = place()
        for image in (0, 1):
            for half in (0, 1):
                chip = 2 * dp + image
                slot = flip(chip, row)
                mine = (dp == half) & (chip == row)
                index = 2 * image + half
                copy = self.remote(
                    pieces.at[image, half], blocks.at[slot], index, slot, (half, chip, col)
                )
                here = pltpu.make_async_copy(
                    pieces.at[image, half], blocks.at[0], self.sems[2]
                )
                self.start(copy, here, mine)
        own = dp == row // 2
        self.into = [(blocks.at[k], k, own if k == 0 else None) for k in range(4)]

    def collect(self, blocks, pieces):
        dp, row, col = place()
        image = lax.rem(row, 2)
        for k in range(4):
            owner = flip(row, k)
            index = 2 * image + dp
            mine = (dp == row // 2) & (owner == row)
            copy = self.remote(
                blocks.at[k], pieces.at[image, dp], k, index, (row // 2, owner, col)
            )
            here = pltpu.make_async_copy(blocks.at[k], pieces.at[image, dp], self.sems[2])
            self.start(copy, here, mine)
        self.into = []
        for image in (0, 1):
            for half in (0, 1):
                own = (dp == half) & (2 * dp + image == row)
                self.into.append((pieces.at[image, half], 2 * image + half, own))

    def start(self, copy, here, mine):
        pl.when(jnp.logical_not(mine))(copy.start)
        pl.when(mine)(here.start)
        self.pending.append((copy, here, mine))

    def arrive(self):
        dp, row, col = place()
        here = self.pending[0][1]
        for target, slot, own in self.into:
            copy = self.remote(target, target, 0, slot, (1 - dp, row, col))
            if own is None:
                copy.wait_recv()
            else:
                pl.when(jnp.logical_not(own))(copy.wait_recv)
                pl.when(own)(here.wait)

    def finish(self):
        for copy, _, mine in self.pending:
            pl.when(jnp.logical_not(mine))(copy.wait_send)


def mm(left, right):
    return jnp.dot(left, right, preferred_element_type=F32)


def mm_nt(left, right):
    return lax.dot_general(left, right, (((1,), (1,)), ((), ())), preferred_element_type=F32)


def each_rows(count, size, body):
    @pl.loop(0, count // size)
    def _(step):
        body(pl.ds(pl.multiple_of(step * size, size), size))


def transpose_into(target, source):
    @pl.loop(0, source.shape[1] // 128)
    def _(step):
        at = pl.ds(pl.multiple_of(step * 128, 128), 128)
        target[at, :] = source[:, at].T


class Sender:
    def __init__(self, send_sems, recv_sems):
        self.sems = (send_sems, recv_sems)
        self.count = 0
        self.copies = []

    def __call__(self, source, target, peer):
        copy = pltpu.make_async_remote_copy(
            source,
            target,
            self.sems[0].at[self.count],
            self.sems[1].at[self.count],
            device_id=peer,
            device_id_type=MESH,
        )
        self.count += 1
        copy.start()
        self.copies.append(copy)
        return copy

    def finish(self):
        for copy in self.copies:
            copy.wait_send()


class Copier:
    def __init__(self, sems):
        self.sems = sems
        self.count = 0

    def __call__(self, source, target):
        copy = pltpu.make_async_copy(source, target, self.sems.at[self.count])
        self.count += 1
        copy.start()
        return copy


def norm_stats(values):
    mean_rows = jnp.mean(values, axis=-1, keepdims=True)
    centered = values - mean_rows
    inv_scale = lax.rsqrt(jnp.mean(centered * centered, axis=-1, keepdims=True) + EPS)
    return centered * inv_scale, inv_scale


def forward_kernel(
    own_tokens,
    x_pieces,
    teacher_pieces,
    count_ref,
    params_ref,
    key_ref,
    key_lane_ref,
    spread_ref,
    rest_spread_ref,
    attn_ref,
    ff_ref,
    wpad_out,
    wff_out,
    triple_out,
    mixed_out,
    act_out,
    slope_out,
    norm1t_out,
    norm2t_out,
    rest_out,
    lse_out,
    act_rest_out,
    slope_rest_out,
    resid_out,
    grad_out,
    branch_out,
    brancht_out,
    result_out,
    err_out,
    x_ref,
    feature_ref,
    count_out,
    teacher_ref,
    features_in,
    biases_in,
    counts_in,
    wattn,
    wff,
    wpad,
    triple,
    mixed,
    act,
    slope,
    norm1,
    norm2,
    turned,
    part,
    got1,
    got2,
    local_sems,
    send_sems,
    recv_sems,
    shuffle_sems,
):
    peers = neighbours()
    meet()
    feat = attn_ref.shape[0]
    half = feat // 2
    depth = 4 * feat
    tokens = norm1.shape[0]
    own = tokens // 2
    main = ff_ref.shape[1] // 2
    qkv = triple.shape[2]
    wide = features_in.shape[2]
    pitch = wide // 6
    send = Sender(send_sems, recv_sems)
    keep = Copier(local_sems)

    def rows(block, low=0, size=None):
        return pl.ds(block * feat + low, feat if size is None else size)

    own_attn = keep(attn_ref, wattn.at[0, rows(0)])
    own_ff = keep(ff_ref, wff.at[0, rows(0)])
    az, ax, ay, a_low, a_high = ([None] * 4 for _ in range(5))

    def attn_source(s):
        return attn_ref if s == 0 else wattn.at[s, rows(0)]

    def attn_ring(s):
        az[s + 1] = send(attn_source(s), wattn.at[s + 1, rows(0)], peers["next"])

    def attn_plane(s):
        ax[s] = send(attn_source(s), wattn.at[s, rows(1)], peers["x"])
        ay[s] = send(attn_source(s), wattn.at[s, rows(2)], peers["y"])

    def attn_last(s):
        ax[s].wait_recv()
        a_low[s] = send(
            wattn.at[s, rows(1, 0, half)], wattn.at[s, rows(3, 0, half)], peers["y"]
        )
        ay[s].wait_recv()
        a_high[s] = send(
            wattn.at[s, rows(2, half, half)], wattn.at[s, rows(3, half, half)], peers["x"]
        )

    fz, fy, fx = ([None] * 4 for _ in range(3))

    def ff_first():
        return (
            send(ff_ref.at[pl.ds(0, half)], wff.at[0, rows(1, 0, half)], peers["x"]),
            send(ff_ref.at[pl.ds(half, half)], wff.at[0, rows(2, half, half)], peers["y"]),
        )

    def ff_ring(s):
        fz[s + 1] = [
            send(wff.at[s, piece], wff.at[s + 1, piece], peers["next"])
            for piece in (rows(0), rows(1, 0, half), rows(2, half, half))
        ]

    def ff_last(s):
        fy[s] = [
            send(wff.at[s, rows(k, 0, half)], wff.at[s, rows(k + 2, 0, half)], peers["y"])
            for k in (0, 1)
        ]
        fx[s] = [
            send(wff.at[s, rows(k, half, half)], wff.at[s, rows(k + 1, half, half)], peers["x"])
            for k in (0, 2)
        ]

    def arrive(copies):
        for copy in copies:
            copy.wait_recv()

    def attn_compute(s):
        arrive([a_low[s], a_high[s]])
        slot = s % 2
        if s == 0:
            own_attn.wait()
        if s >= 2:
            for copy in saved[s - 2]:
                copy.wait()

        def unpack(at):
            block = wattn[s, at, :]
            wpad[slot, at, :] = mm(block, spread_ref[...]).astype(BF16)
            extra = mm(block[:, block.shape[1] - 128 :], rest_spread_ref[s]).astype(BF16)
            if s == 0:
                rest_out[at, :] = extra
            else:
                rest_out[at, :] = rest_out[at, :] + extra

        each_rows(depth, feat, unpack)

        def project(at):
            values = mm(norm1[at, :], wpad[slot, :, :qkv]) + biases_in[s, 0:1, :qkv]
            values = values + key_ref[at, :] * key_lane_ref[...]
            triple[slot, at, :] = values.astype(BF16)

        each_rows(tokens, own, project)
        scale = LOG2E * HD**-0.5
        for h in range(qkv // 384):
            query_at, key_at, value_at = (pl.ds((3 * h + j) * 128, 128) for j in range(3))
            value_turned = triple[slot, :, value_at].T

            def head(at, h=h, query_at=query_at, key_at=key_at, value_turned=value_turned):
                scores = mm_nt(triple[slot, :, key_at], triple[slot, at, query_at])
                peak = jnp.max(scores, axis=0, keepdims=True)
                weights = jnp.exp2((scores - peak) * scale)
                total = jnp.sum(weights, axis=0, keepdims=True)
                lse_out[2 * s + h, :, at] = peak * scale + jnp.log2(total)
                values = mm(value_turned, weights.astype(BF16)) / total
                mixed[s, at, pl.ds(h * 128, 128)] = values.T.astype(BF16)

            each_rows(tokens, 256, head)

        def out(at):
            values = mm_nt(mixed[s, at, :], wpad[slot, :, qkv:])
            part[at, :] = values if s == 0 else part[at, :] + values

        each_rows(tokens, own, out)
        saved.append(
            [
                keep(wpad.at[slot], wpad_out.at[s]),
                keep(triple.at[slot], triple_out.at[s]),
                keep(mixed.at[s], mixed_out.at[s]),
            ]
        )

    def gelu(pre):
        inner = GELU_ROOT * (pre + 0.044715 * pre * pre * pre)
        tanh = jnp.tanh(inner)
        rise = 0.5 * (1.0 + tanh)
        bend = 0.5 * pre * (1.0 - tanh * tanh) * (GELU_ROOT * (1.0 + 0.134145 * pre * pre))
        return (pre * rise).astype(BF16), (rise + bend).astype(BF16)

    def ff_compute(s):
        arrive(fy[s] + fx[s])

        def block(at):
            pre = mm(norm2[at, :], wff[s, :, :main]) + biases_in[s, 0:1, qkv : qkv + main]
            low, bent = gelu(pre)
            act[s, at, :] = low
            slope[s, at, :] = bent
            part[at, :] = part[at, :] + mm_nt(low, wff[s, :, main:])

        each_rows(tokens, own, block)
        ff_saved.extend(
            [
                keep(act.at[s], act_out.at[s]),
                keep(slope.at[s], slope_out.at[s]),
                keep(wff.at[s], wff_out.at[s]),
            ]
        )

    def rest_compute():
        bias = mm(biases_in[0, :, qkv + main :].astype(BF16), rest_spread_ref[0, :, :128])
        for s in (1, 2, 3):
            values = biases_in[s, :, qkv + main :].astype(BF16)
            bias = bias + mm(values, rest_spread_ref[s, :, :128])

        def block(at):
            pre = mm(norm2[at, :], rest_out[:, :128]) + bias[0:1]
            low, bent = gelu(pre)
            act_rest_out[at, :] = low
            slope_rest_out[at, :] = bent
            part[at, :] = mm_nt(low, rest_out[:, 128:])

        each_rows(tokens, own, block)

    saved, ff_saved = [], []
    x_move = Shuffle(shuffle_sems.at[0], shuffle_sems.at[1], shuffle_sems.at[2, 0])
    x_move.spread(x_pieces, x_ref)
    attn_ring(0)
    attn_plane(0)
    own_params = [
        keep(params_ref.at[:, pl.ds(0, wide)], features_in.at[0]),
        keep(params_ref.at[:, pl.ds(wide, biases_in.shape[2])], biases_in.at[0]),
        keep(count_ref, counts_in.at[0]),
    ]
    smalls = [
        send(params_ref.at[:, pl.ds(0, wide)], features_in.at[k], peers[name])
        for k, name in ((1, "x"), (2, "y"), (3, "diagonal"))
    ]
    dp, row, col = place()
    ring_two = (dp, row, 3 - col)
    smalls += [
        send(params_ref.at[:, pl.ds(wide, biases_in.shape[2])], biases_in.at[s], peer)
        for s, peer in ((1, peers["next"]), (2, ring_two), (3, peers["prev"]))
    ]
    counts = [
        send(count_ref, counts_in.at[1 + i], peer) for i, peer in enumerate(images_group())
    ]
    teacher_move = Shuffle(shuffle_sems.at[3], shuffle_sems.at[4], shuffle_sems.at[2, 1])

    def token_rows(at):
        return jnp.concatenate([x_ref[k, at, :].astype(F32) for k in range(4)], axis=1)

    for copy in own_params:
        copy.wait()
    arrive(smalls)
    feature_ref[...] = jnp.zeros_like(feature_ref)
    for i in range(6):
        feature_ref[i : i + 1, :] = jnp.concatenate(
            [features_in[k, 0:1, pitch * i : pitch * i + feat] for k in range(4)], axis=1
        )
    x_move.arrive()

    def first_norm(at):
        normed, _ = norm_stats(token_rows(at))
        norm1[at, :] = (normed * feature_ref[0:1] + feature_ref[1:2]).astype(BF16)

    each_rows(own, 16, first_norm)
    swap1 = send(norm1.at[pl.ds(0, own)], norm1.at[pl.ds(own, own)], peers["core"])
    az[1].wait_recv()
    attn_ring(1)
    attn_plane(1)
    attn_last(0)
    swap1.wait_recv()
    az[2].wait_recv()
    attn_ring(2)
    attn_plane(2)
    attn_last(1)
    first = ff_first()
    attn_compute(0)
    az[3].wait_recv()
    attn_plane(3)
    attn_last(2)
    own_ff.wait()
    arrive(first)
    ff_ring(0)
    teacher_move.spread(teacher_pieces, teacher_ref)
    attn_compute(1)
    attn_last(3)
    ff_last(0)
    attn_compute(2)
    attn_compute(3)
    swap2 = send(part.at[pl.ds(own, own)], got1, peers["core"])
    arrive([swap2])

    def second_norm(at):
        values = token_rows(at) + part[at, :] + got1[at, :] + feature_ref[4:5]
        resid_out[at, :] = values
        normed, _ = norm_stats(values)
        norm2[at, :] = (normed * feature_ref[2:3] + feature_ref[3:4]).astype(BF16)

    each_rows(own, 16, second_norm)
    swap2.wait_send()
    swap3 = send(norm2.at[pl.ds(0, own)], norm2.at[pl.ds(own, own)], peers["core"])
    arrive(fz[1])
    ff_ring(1)
    ff_last(1)
    transpose_into(turned, norm1)
    turn1 = keep(turned, norm1t_out)
    arrive([swap3])
    rest_compute()
    turn1.wait()
    transpose_into(turned, norm2)
    turn2 = keep(turned, norm2t_out)
    arrive(fz[2])
    ff_ring(2)
    ff_last(2)
    ff_compute(0)
    ff_compute(1)
    arrive(fz[3])
    ff_last(3)
    ff_compute(2)
    ff_compute(3)
    swap4 = send(part.at[pl.ds(own, own)], got2, peers["core"])
    arrive([swap4])
    err_out[...] = jnp.zeros_like(err_out)
    teacher_move.arrive()
    arrive(counts)
    count = counts_in[0]
    for i in range(1, 8):
        count = count + counts_in[i]
    count_out[...] = count
    factor = (own_tokens * 8.0) / count[0:1, 0:1]

    def finish(at):
        values = resid_out[at, :] + part[at, :] + got2[at, :] + feature_ref[5:6]
        for k in range(4):
            result_out[k, at, :] = values[:, k * feat : (k + 1) * feat].astype(BF16)
        target = [teacher_ref[k, at, :feat].astype(F32) for k in range(4)]
        error = values - jnp.concatenate(target, axis=1)
        masked = error * teacher_ref[0, at, feat : feat + 1].astype(F32)
        err_out[...] = err_out[...] + error * masked
        grad = masked * factor
        grad_out[at, :] = grad
        branch_out[at, :] = grad.astype(BF16)

    each_rows(own, 16, finish)
    swap5 = send(branch_out.at[pl.ds(0, own)], branch_out.at[pl.ds(own, own)], peers["core"])
    arrive([swap5])
    transpose_into(brancht_out, branch_out)
    turn2.wait()
    for copies in saved[2:]:
        for copy in copies:
            copy.wait()
    for copy in ff_saved:
        copy.wait()
    for copy in send.copies:
        if copy is not swap2:
            copy.wait_send()
    x_move.finish()
    teacher_move.finish()


def forward_call(arrays, own_tokens, feat, lanes, main, qkv, mix, own, depth):
    tokens = 2 * own
    wide, narrow = 6 * ((feat + 127) // 128 * 128), qkv + main + 128
    anywhere = pl.BlockSpec(memory_space=pl.ANY)
    local = pl.BlockSpec(memory_space=pltpu.VMEM)
    shapes = [
        ((4, depth, qkv + mix), BF16, anywhere),
        ((4, depth, 2 * main), BF16, anywhere),
        ((4, tokens, qkv), BF16, anywhere),
        ((4, tokens, mix), BF16, anywhere),
        ((4, tokens, main), BF16, anywhere),
        ((4, tokens, main), BF16, anywhere),
        ((depth, tokens), BF16, anywhere),
        ((depth, tokens), BF16, anywhere),
        ((depth, 256), BF16, local),
        ((8, 1, tokens), F32, local),
        ((tokens, 128), BF16, local),
        ((tokens, 128), BF16, local),
        ((own, depth), F32, local),
        ((own, depth), F32, local),
        ((tokens, depth), BF16, local),
        ((depth, tokens), BF16, local),
        ((4, own, feat), BF16, local),
        ((16, depth), F32, local),
        ((4, own, feat), BF16, local),
        ((8, depth), F32, local),
        ((8, 128), F32, local),
    ]
    return pl.pallas_call(
        functools.partial(forward_kernel, own_tokens),
        out_shape=[jax.ShapeDtypeStruct(shape, dtype) for shape, dtype, _ in shapes],
        in_specs=[anywhere] * 2 + [local] * 6 + [anywhere] * 2,
        out_specs=[spec for _, _, spec in shapes],
        scratch_shapes=[
            pltpu.VMEM((4, own, arrays[1].shape[-1]), BF16),
            pltpu.VMEM((4, 8, wide), F32),
            pltpu.VMEM((4, 8, narrow), F32),
            pltpu.VMEM((8, 8, 128), F32),
            pltpu.VMEM((4, depth, lanes), BF16),
            pltpu.VMEM((4, depth, 2 * main), BF16),
            pltpu.VMEM((2, depth, qkv + mix), BF16),
            pltpu.VMEM((2, tokens, qkv), BF16),
            pltpu.VMEM((4, tokens, mix), BF16),
            pltpu.VMEM((4, tokens, main), BF16),
            pltpu.VMEM((4, tokens, main), BF16),
            pltpu.VMEM((tokens, depth), BF16),
            pltpu.VMEM((tokens, depth), BF16),
            pltpu.VMEM((depth, tokens), BF16),
            pltpu.VMEM((tokens, depth), F32),
            pltpu.VMEM((own, depth), F32),
            pltpu.VMEM((own, depth), F32),
            pltpu.SemaphoreType.DMA((32,)),
            pltpu.SemaphoreType.DMA((72,)),
            pltpu.SemaphoreType.DMA((72,)),
            pltpu.SemaphoreType.DMA((5, 4)),
        ],
        compiler_params=pltpu.CompilerParams(
            collective_id=1, has_side_effects=True, vmem_limit_bytes=62 << 20
        ),
    )(*arrays)


def backward_kernel(
    branch2_ref,
    rest_ref,
    act_rest_ref,
    slope_rest_ref,
    lse_ref,
    feature_ref,
    spread_ref,
    rest_spread_ref,
    x_ref,
    resid_ref,
    err_ref,
    result_blocks,
    grad_hbm,
    norm1t_hbm,
    norm2t_hbm,
    branch2t_hbm,
    wpad_hbm,
    wff_hbm,
    triple_hbm,
    mixed_hbm,
    act_hbm,
    slope_hbm,
    grad_pieces,
    result_pieces,
    sums_out,
    bias_out,
    attn_out,
    ff_out,
    grad_blocks,
    terms,
    terms_mine,
    terms_in,
    sums_in,
    bias_mine,
    bias_turn,
    bias_in,
    bias_plane,
    units_out,
    units_rest_out,
    heads_out,
    gattn,
    gff,
    wslot,
    kept,
    grad_pre,
    grad_rest,
    normt,
    brancht,
    branch1,
    part,
    got,
    grad_mid,
    dtriple,
    grad_mixed,
    grad_key,
    grad_value,
    inner_row,
    ra,
    rb,
    r1,
    r2,
    rz,
    ry,
    rx,
    rzl,
    rzh,
    rfx,
    rfy,
    local_sems,
    send_sems,
    recv_sems,
    shuffle_sems,
):
    peers = neighbours()
    feat = 2 * attn_out.shape[1]
    half = feat // 2
    depth = 4 * feat
    tokens = branch2_ref.shape[0]
    own = tokens // 2
    main = gff.shape[2] // 2
    qkv = triple_hbm.shape[2]
    send = Sender(send_sems, recv_sems)
    keep = Copier(local_sems)

    def rows(block, low=0, size=None):
        return pl.ds(block * feat + low, feat if size is None else size)

    def load_ff(s):
        slot = s % 2
        return [
            keep(wff_hbm.at[s], wslot.at[slot]),
            keep(act_hbm.at[s], kept.at[slot, :, pl.ds(0, main)]),
            keep(slope_hbm.at[s], kept.at[slot, :, pl.ds(main, main)]),
        ]

    def load_attn(s):
        slot = s % 2
        return [
            keep(wpad_hbm.at[s], wslot.at[slot]),
            keep(triple_hbm.at[s], kept.at[slot, :, pl.ds(0, qkv)]),
            keep(mixed_hbm.at[s], kept.at[slot, :, pl.ds(qkv, grad_mixed.shape[1])]),
        ]

    loads = {3: load_ff(3)}
    turns = [keep(norm2t_hbm, normt), keep(branch2t_hbm, brancht)]
    loads[2] = load_ff(2)
    load_grad = keep(grad_hbm, grad_mid)
    meet()
    result_move = Shuffle(shuffle_sems.at[0], shuffle_sems.at[1], shuffle_sems.at[2, 0])
    grad_move = Shuffle(shuffle_sems.at[3], shuffle_sems.at[4], shuffle_sems.at[2, 1])
    cy, cx, zl, zh = ([None] * 4 for _ in range(4))
    ca, cb, c1, c2, cz = ([None] * 4 for _ in range(5))

    def add_into(target, at, *sources):
        size = at.size

        @pl.loop(0, size // 16)
        def _(step):
            here = pl.ds(pl.multiple_of(at.start + step * 16, 16), 16)
            there = pl.ds(pl.multiple_of(step * 16, 16), 16)
            total = target[here, :].astype(F32)
            for source in sources:
                total = total + source[there, :].astype(F32)
            target[here, :] = total.astype(BF16)

    def column_sum(values):
        return jnp.sum(values.astype(F32), axis=0, keepdims=True)

    def ff_compute(s):
        slot = s % 2
        for copy in loads[s]:
            copy.wait()
        units_out[s] = jnp.zeros((1, main), F32)

        def block(at):
            grad = mm(branch2_ref[at, :], wslot[slot, :, main : 2 * main])
            low = (grad * kept[slot, at, main:].astype(F32)).astype(BF16)
            grad_pre[at, :] = low
            units_out[s] = units_out[s] + column_sum(low)
            values = mm_nt(low, wslot[slot, :, :main])
            part[at, :] = values if s == 3 else part[at, :] + values

        each_rows(tokens, own, block)
        if s == 3:
            for copy in turns:
                copy.wait()

        def grads(at):
            gff[s, at, :main] = mm(normt[at, :], grad_pre[...]).astype(BF16)
            gff[s, at, main:] = mm(brancht[at, :], kept[slot, :, :main]).astype(BF16)

        each_rows(depth, feat, grads)
        cy[s] = [
            send(gff.at[s, rows(k, 0, half)], ry.at[s, k - 2], peers["y"]) for k in (2, 3)
        ]
        cx[s] = [
            send(gff.at[s, rows(k, half, half)], rx.at[s, k // 2], peers["x"]) for k in (1, 3)
        ]
        if s >= 2:
            loads[s - 2] = load_ff(s - 2)

    def rest_compute():
        units_rest_out[...] = jnp.zeros_like(units_rest_out)

        def block(at):
            grad = mm(branch2_ref[at, :], rest_ref[:, 128:])
            low = (grad * slope_rest_ref[at, :].astype(F32)).astype(BF16)
            grad_pre[at, :128] = low
            units_rest_out[...] = units_rest_out[...] + column_sum(low)
            part[at, :] = part[at, :] + mm_nt(low, rest_ref[:, :128])

        each_rows(tokens, own, block)

        def grads(at):
            grad_rest[at, :128] = mm(normt[at, :], grad_pre[:, :128]).astype(BF16)
            grad_rest[at, 128:] = mm(brancht[at, :], act_rest_ref[...]).astype(BF16)

        each_rows(depth, feat, grads)

    def ff_add(s):
        for copy in cy[s] + cx[s]:
            copy.wait_recv()
        last = s == 3
        if not last:
            for copy in zl[s] + zh[s]:
                copy.wait_recv()
        lows, highs = [], []
        for i, k in enumerate((0, 1)):
            piece = rows(k, 0, half)
            add_into(gff.at[s], piece, ry.at[s, i], *([] if last else [rzl.at[s, i]]))
            lows.append((piece, i))
        for i, k in enumerate((0, 2)):
            piece = rows(k, half, half)
            add_into(gff.at[s], piece, rx.at[s, i], *([] if last else [rzh.at[s, i]]))
            highs.append((piece, i))
        if s:
            zl[s - 1] = [
                send(gff.at[s, piece], rzl.at[s - 1, i], peers["prev"]) for piece, i in lows
            ]
            zh[s - 1] = [
                send(gff.at[s, piece], rzh.at[s - 1, i], peers["prev"]) for piece, i in highs
            ]

    def attn_compute(s):
        slot = s % 2
        for copy in attn_loads[s]:
            copy.wait()

        def back_out(at):
            grad_mixed[at, :] = mm(branch1[at, :], wslot[slot, :, qkv:]).astype(BF16)

        each_rows(tokens, own, back_out)
        scale = HD**-0.5
        for h in range(qkv // 384):
            query_at, key_at, value_at = (pl.ds((3 * h + j) * 128, 128) for j in range(3))
            mix_at = pl.ds(h * 128, 128)
            value_of_mix = pl.ds(qkv + h * 128, 128)
            key_turned = kept[slot, :, key_at].T
            product = grad_mixed[:, mix_at].astype(F32) * kept[slot, :, value_of_mix].astype(F32)
            inner_row[...] = jnp.sum(product.T, axis=0, keepdims=True)
            grad_key[...] = jnp.zeros_like(grad_key)
            grad_value[...] = jnp.zeros_like(grad_value)

            def head(at, h=h, query_at=query_at, key_at=key_at, value_at=value_at,
                     mix_at=mix_at, key_turned=key_turned):
                query = kept[slot, at, query_at]
                grad = grad_mixed[at, mix_at]
                scores = mm_nt(kept[slot, :, key_at], query)
                weights = jnp.exp2(scores * (scale * LOG2E) - lse_ref[2 * s + h, :, at])
                grad_soft = mm_nt(kept[slot, :, value_at], grad)
                grad_raw = (weights * (grad_soft - inner_row[:, at]) * scale).astype(BF16)
                grad_value[...] += mm(weights.astype(BF16), grad)
                grad_key[...] += mm(grad_raw, query)
                dtriple[at, query_at] = mm(key_turned, grad_raw).T.astype(BF16)

            each_rows(tokens, 256, head)
            dtriple[:, key_at] = grad_key[...].astype(BF16)
            dtriple[:, value_at] = grad_value[...].astype(BF16)
        heads_out[s] = jnp.zeros((1, qkv), F32)

        def back_in(at):
            values = mm_nt(dtriple[at, :], wslot[slot, :, :qkv])
            part[at, :] = values if s == 3 else part[at, :] + values
            heads_out[s] = heads_out[s] + column_sum(dtriple[at, :])

        each_rows(tokens, own, back_in)

        def grads(at):
            first = mm(normt[at, :], dtriple[...]).astype(BF16)
            second = mm(brancht[at, :], kept[slot, :, qkv:]).astype(BF16)
            packed = mm_nt(first, spread_ref[:, :qkv]) + mm_nt(second, spread_ref[:, qkv:])
            gattn[s, at, :] = packed.astype(BF16)
            tail = pl.ds(packed.shape[1] - 128, 128)
            extra = mm_nt(grad_rest[at, :], rest_spread_ref[s])
            gattn[s, at, tail] = (gattn[s, at, tail].astype(F32) + extra).astype(BF16)

        each_rows(depth, feat, grads)
        ca[s] = send(gattn.at[s, rows(3, 0, half)], ra.at[s], peers["y"])
        cb[s] = send(gattn.at[s, rows(3, half, half)], rb.at[s], peers["x"])
        if s >= 2:
            attn_loads[s - 2] = load_attn(s - 2)

    def attn_plane(s):
        ca[s].wait_recv()
        add_into(gattn.at[s], rows(1, 0, half), ra.at[s])
        c1[s] = send(gattn.at[s, rows(1)], r1.at[s], peers["x"])
        cb[s].wait_recv()
        add_into(gattn.at[s], rows(2, half, half), rb.at[s])
        c2[s] = send(gattn.at[s, rows(2)], r2.at[s], peers["y"])

    def attn_ring(s):
        c1[s].wait_recv()
        c2[s].wait_recv()
        if s < 3:
            cz[s].wait_recv()
        add_into(gattn.at[s], rows(0), r1.at[s], r2.at[s], *([rz.at[s]] if s < 3 else []))
        if s:
            cz[s - 1] = send(gattn.at[s, rows(0)], rz.at[s - 1], peers["prev"])

    terms[...] = jnp.zeros_like(terms)

    def add_term(index, values):
        terms[index] = terms[index] + values

    ff_compute(3)
    ff_compute(2)
    result_move.collect(result_blocks, result_pieces)
    ff_compute(1)
    ff_add(3)
    ff_compute(0)
    attn_loads = {3: load_attn(3), 2: load_attn(2)}
    rest_compute()
    load_norm = keep(norm1t_hbm, normt)
    swap1 = send(part.at[pl.ds(own, own)], got, peers["core"])
    swap1.wait_recv()
    load_grad.wait()

    def mid(at):
        normed, inv_scale = norm_stats(resid_ref[at, :])
        grad_norm = part[at, :] + got[at, :]
        add_term(2, grad_norm * normed)
        add_term(3, grad_norm)
        scaled = grad_norm * feature_ref[2:3]
        first = jnp.mean(scaled, axis=-1, keepdims=True)
        second = jnp.mean(scaled * normed, axis=-1, keepdims=True)
        grad = grad_mid[at, :] + inv_scale * (scaled - first - normed * second)
        grad_mid[at, :] = grad
        low = grad.astype(BF16)
        branch1[at, :] = low
        add_term(4, low.astype(F32))
        add_term(5, branch2_ref[at, :].astype(F32))

    each_rows(own, 16, mid)
    swap1.wait_send()
    swap2 = send(branch1.at[pl.ds(0, own)], branch1.at[pl.ds(own, own)], peers["core"])
    swap2.wait_recv()
    load_norm.wait()
    transpose_into(brancht, branch1)
    attn_compute(3)
    ff_add(2)
    attn_compute(2)
    attn_plane(3)
    attn_compute(1)
    attn_plane(2)
    ff_add(1)
    attn_ring(3)
    attn_compute(0)
    swap3 = send(part.at[pl.ds(own, own)], got, peers["core"])
    attn_plane(1)
    attn_ring(2)
    attn_plane(0)
    swap3.wait_recv()

    def token_rows(at):
        return jnp.concatenate([x_ref[k, at, :].astype(F32) for k in range(4)], axis=1)

    def last(at):
        normed, inv_scale = norm_stats(token_rows(at))
        grad_norm = part[at, :] + got[at, :]
        add_term(0, grad_norm * normed)
        add_term(1, grad_norm)
        scaled = grad_norm * feature_ref[0:1]
        first = jnp.mean(scaled, axis=-1, keepdims=True)
        second = jnp.mean(scaled * normed, axis=-1, keepdims=True)
        grad = grad_mid[at, :] + inv_scale * (scaled - first - normed * second)
        for k in range(4):
            grad_blocks[k, at, :] = grad[:, k * feat : (k + 1) * feat].astype(BF16)

    each_rows(own, 16, last)
    grad_move.collect(grad_blocks, grad_pieces)
    terms_mine[...] = jnp.zeros_like(terms_mine)
    bias_mine[...] = jnp.zeros_like(bias_mine)
    for i in range(7):
        if i < 6:
            row_sum = jnp.sum(terms[i], axis=0, keepdims=True)
        else:
            err = jnp.sum(jnp.sum(err_ref[...], axis=0, keepdims=True), axis=1, keepdims=True)
            row_sum = jnp.broadcast_to(err, (1, depth))
        for k in range(4):
            terms_mine[k, i : i + 1, :] = row_sum[:, k * feat : (k + 1) * feat]
    wide = bias_mine.shape[2]
    for s in range(4):
        bias_mine[s, 0:1, :qkv] = heads_out[s]
        bias_mine[s, 0:1, qkv : qkv + main] = units_out[s]
        bias_mine[s, 0:1, qkv + main :] = units_rest_out[...]
    dp, row, col = place()
    ring_two = (dp, row, 3 - col)
    sides = ((1, "x"), (2, "y"), (3, "diagonal"))
    term_sends = [send(terms_mine.at[k], terms_in.at[k - 1], peers[name]) for k, name in sides]
    bias_sends = [
        send(bias_mine.at[s], bias_turn.at[s - 1], peer)
        for s, peer in ((1, peers["prev"]), (2, ring_two), (3, peers["next"]))
    ]
    ff_add(0)
    end_low = send(gff.at[0, rows(1, 0, half)], rfx, peers["x"])
    end_high = send(gff.at[0, rows(2, half, half)], rfy, peers["y"])
    attn_ring(1)
    for copy in term_sends + bias_sends:
        copy.wait_recv()
    terms_mine[0] = terms_mine[0] + terms_in[0] + terms_in[1] + terms_in[2]
    sum_sends = [
        send(terms_mine.at[0], sums_in.at[i], peer) for i, peer in enumerate(images_group())
    ]
    bias_plane[...] = bias_mine[0]
    for s in (1, 2, 3):
        bias_plane[s : s + 1, :] = bias_turn[s - 1, 0:1, :]
    plane_sends = [send(bias_plane, bias_in.at[k - 1], peers[name]) for k, name in sides]
    end_low.wait_recv()
    end_high.wait_recv()
    add_into(gff.at[0], rows(0, 0, half), rfx)
    add_into(gff.at[0], rows(0, half, half), rfy)
    quarter = feat // 2
    keep_at = pl.ds(pl.multiple_of(dp * quarter, 16), quarter)
    give_at = pl.ds(pl.multiple_of((1 - dp) * quarter, 16), quarter)
    done = [keep(gff.at[0, keep_at], ff_out.at[0])]
    pair_sends = [send(gff.at[0, give_at], ff_out.at[1], peers["core"])]
    for copy in plane_sends + sum_sends:
        copy.wait_recv()
    bias_out[0] = bias_plane[...] + bias_in[0] + bias_in[1] + bias_in[2]
    pair_sends.append(send(bias_out.at[0], bias_out.at[1], peers["core"]))
    total = terms_mine[0]
    for i in range(7):
        total = total + sums_in[i]
    sums_out[...] = total
    attn_ring(0)
    done.append(keep(gattn.at[0, keep_at], attn_out.at[0]))
    pair_sends.append(send(gattn.at[0, give_at], attn_out.at[1], peers["core"]))
    for copy in pair_sends:
        copy.wait_recv()
    for copy in done:
        copy.wait()
    result_move.arrive()
    grad_move.arrive()
    for copy in send.copies:
        if copy is not swap1:
            copy.wait_send()
    result_move.finish()
    grad_move.finish()


def backward_call(arrays, feat, lanes, main, qkv, mix, own, depth):
    tokens = 2 * own
    half = feat // 2
    narrow = qkv + main + 128
    anywhere = pl.BlockSpec(memory_space=pl.ANY)
    local = pl.BlockSpec(memory_space=pltpu.VMEM)
    shapes = [
        ((2, 2, own, feat), BF16, anywhere),
        ((2, 2, own, feat), BF16, anywhere),
        ((8, feat), F32, local),
        ((2, 8, narrow), F32, local),
        ((2, half, lanes), BF16, anywhere),
        ((2, half, 2 * main), BF16, anywhere),
    ]
    return pl.pallas_call(
        backward_kernel,
        out_shape=[jax.ShapeDtypeStruct(shape, dtype) for shape, dtype, _ in shapes],
        in_specs=[local] * 11 + [anywhere] * 11,
        out_specs=[spec for _, _, spec in shapes],
        scratch_shapes=[
            pltpu.VMEM((4, own, feat), BF16),
            pltpu.VMEM((6, 16, depth), F32),
            pltpu.VMEM((4, 8, feat), F32),
            pltpu.VMEM((3, 8, feat), F32),
            pltpu.VMEM((7, 8, feat), F32),
            pltpu.VMEM((4, 8, narrow), F32),
            pltpu.VMEM((3, 8, narrow), F32),
            pltpu.VMEM((3, 8, narrow), F32),
            pltpu.VMEM((8, narrow), F32),
            pltpu.VMEM((4, 1, main), F32),
            pltpu.VMEM((1, 128), F32),
            pltpu.VMEM((4, 1, qkv), F32),
            pltpu.VMEM((4, depth, lanes), BF16),
            pltpu.VMEM((4, depth, 2 * main), BF16),
            pltpu.VMEM((2, depth, 2 * main), BF16),
            pltpu.VMEM((2, tokens, qkv + mix), BF16),
            pltpu.VMEM((tokens, main), BF16),
            pltpu.VMEM((depth, 256), BF16),
            pltpu.VMEM((depth, tokens), BF16),
            pltpu.VMEM((depth, tokens), BF16),
            pltpu.VMEM((tokens, depth), BF16),
            pltpu.VMEM((tokens, depth), F32),
            pltpu.VMEM((own, depth), F32),
            pltpu.VMEM((own, depth), F32),
            pltpu.VMEM((tokens, qkv), BF16),
            pltpu.VMEM((tokens, mix), BF16),
            pltpu.VMEM((tokens, 128), F32),
            pltpu.VMEM((tokens, 128), F32),
            pltpu.VMEM((1, tokens), F32),
            pltpu.VMEM((4, half, lanes), BF16),
            pltpu.VMEM((4, half, lanes), BF16),
            pltpu.VMEM((4, feat, lanes), BF16),
            pltpu.VMEM((4, feat, lanes), BF16),
            pltpu.VMEM((3, feat, lanes), BF16),
            pltpu.VMEM((4, 2, half, 2 * main), BF16),
            pltpu.VMEM((4, 2, half, 2 * main), BF16),
            pltpu.VMEM((3, 2, half, 2 * main), BF16),
            pltpu.VMEM((3, 2, half, 2 * main), BF16),
            pltpu.VMEM((half, 2 * main), BF16),
            pltpu.VMEM((half, 2 * main), BF16),
            pltpu.SemaphoreType.DMA((32,)),
            pltpu.SemaphoreType.DMA((104,)),
            pltpu.SemaphoreType.DMA((104,)),
            pltpu.SemaphoreType.DMA((5, 4)),
        ],
        compiler_params=pltpu.CompilerParams(
            collective_id=2, has_side_effects=True, vmem_limit_bytes=63 << 20
        ),
    )(*arrays)
def on_chip(
    layer_input,
    teacher,
    valid,
    proj_in,
    bias_query,
    bias_value,
    proj_out,
    bias_out,
    norm1_gain,
    norm1_shift,
    norm2_gain,
    norm2_shift,
    w_up,
    bias_up,
    w_down,
    bias_down,
):
    core = lax.axis_index("dp")
    first = core == 0
    cols = lax.axis_size("col")
    feat = layer_input.shape[1]
    images = layer_input.shape[0] // SEQ
    half_seq = (SEQ + 255) // 256 * 128
    pad_seq = 2 * half_seq
    units = w_up.shape[1] // 2
    width = proj_out.shape[0] // 2
    heads = width // HD
    main = units // 128 * 128
    rest = units - main
    at = 4 * width
    lanes = (at + 2 * rest + 127) // 128 * 128
    qkv, mix = 3 * heads * 128, heads * 128

    def core_half(values, axis):
        low, high = jnp.split(values, 2, axis=axis)
        return jnp.where(first, low, high)

    def pieces(values):
        values = jnp.pad(values.reshape(images, SEQ, -1), ((0, 0), (0, pad_seq - SEQ), (0, 0)))
        return values.reshape(images, 2, half_seq, -1)

    up_half, down_half = core_half(w_up, 1), core_half(w_down, 0).T
    attn_shard = jnp.concatenate(
        [
            core_half(proj_in, 1),
            core_half(proj_out, 0).T,
            up_half[:, main:],
            down_half[:, main:],
            jnp.zeros((feat, lanes - at - 2 * rest), jnp.bfloat16),
        ],
        axis=1,
    )
    ff_shard = jnp.concatenate([up_half[:, :main], down_half[:, :main]], axis=1)
    lane = jnp.arange(lanes)
    spread_at = jnp.where(lane < at, lane // HD * 128 + lane % HD, -1)
    spread = (spread_at[:, None] == jnp.arange(qkv + mix)[None]).astype(jnp.bfloat16)
    tail = lane[-128:]
    part = jnp.arange(cols)[:, None]
    up_at = jnp.where((tail >= at) & (tail < at + rest), tail - at + part * rest, -1)
    down_at = jnp.where(
        (tail >= at + rest) & (tail < at + 2 * rest), tail - at - rest + part * rest + 128, -1
    )
    spot = jnp.arange(256)
    rest_spread = (up_at[..., None] == spot) | (down_at[..., None] == spot)
    rest_spread = rest_spread.astype(jnp.bfloat16)

    place_of = jnp.arange(pad_seq)
    token = jnp.where(
        place_of < half_seq, place_of + core * half_seq, place_of - core * half_seq
    )
    key_column = jnp.where(token < SEQ, 0.0, -1e30).astype(jnp.float32)[:, None]
    key_lane = (jnp.arange(qkv) % 384 == 128 + HD).astype(jnp.float32)[None]

    query_bias, value_bias = core_half(bias_query, 0), core_half(bias_value, 0)
    unit_bias = core_half(bias_up, 0)
    pitch = (feat + 127) // 128 * 128
    one = jnp.ones((1,), jnp.bfloat16)

    def gap(size):
        return jnp.zeros((size,), jnp.bfloat16)

    params = []
    for vector in (norm1_gain, norm1_shift, norm2_gain, norm2_shift, bias_out, bias_down):
        params += [vector, gap(pitch - feat)]
    for h in range(heads):
        head_at = slice(h * HD, (h + 1) * HD)
        params += [query_bias[head_at], one, gap(127 - HD + 128)]
        params += [value_bias[head_at], gap(128 - HD)]
    params += [unit_bias[:main], gap(at - lanes + 128), unit_bias[main:]]
    params.append(gap(lanes - at - rest))
    params = jnp.concatenate(params).astype(jnp.float32)
    params = jnp.broadcast_to(params[None], (8, params.shape[0]))
    count = jnp.broadcast_to(jnp.sum(valid).astype(jnp.float32), (8, 128))

    marked = jnp.concatenate(
        [
            teacher,
            valid.astype(jnp.bfloat16)[:, None],
            jnp.zeros((teacher.shape[0], pitch - feat - 1), jnp.bfloat16),
        ],
        axis=1,
    )
    sizes = (feat, lanes, main, qkv, mix, half_seq, 4 * feat)
    (
        wpad, wff, triple, mixed, act, slope, norm1t, norm2t, rest_weight, lse, act_rest,
        slope_rest, resid1, grad_result, branch2, branch2t, result, err_rows, x_blocks,
        features, counted,
    ) = forward_call(
        (
            pieces(layer_input), pieces(marked), count, params, key_column, key_lane, spread,
            rest_spread, attn_shard, ff_shard,
        ),
        layer_input.shape[0],
        *sizes,
    )
    grad_pieces, result_pieces, sums, bias_rows, attn_sum, ff_sum = backward_call(
        (
            branch2, rest_weight, act_rest, slope_rest, lse, features, spread, rest_spread,
            x_blocks, resid1, err_rows, result, grad_result, norm1t, norm2t, branch2t, wpad,
            wff, triple, mixed, act, slope,
        ),
        *sizes,
    )

    def rows_of(values):
        return values.reshape(images, pad_seq, feat)[:, :SEQ].reshape(images * SEQ, feat)

    def both(keep, got, axis=-1):
        return jnp.concatenate(
            [jnp.where(first, keep, got), jnp.where(first, got, keep)], axis=axis
        ).astype(jnp.float32)

    def up_of(i):
        return jnp.concatenate([ff_sum[i][:, :main], attn_sum[i][:, at : at + rest]], axis=1)

    def down_of(i):
        block = [ff_sum[i][:, main:], attn_sum[i][:, at + rest : at + 2 * rest]]
        return jnp.concatenate(block, axis=1).T

    loss_value = sums[6, 0] / (counted[0, 0] * D)
    main_rows = jnp.sum(bias_rows[:, :cols, : qkv + main], axis=1)
    head_rows = main_rows[:, :qkv].reshape(2, heads, 3, 128)[..., :HD]
    tail_rows = bias_rows[:, :cols, qkv + main :]
    tail_rows = sum(tail_rows[:, s, s * rest : (s + 1) * rest] for s in range(cols))
    unit_rows = jnp.concatenate([main_rows[:, qkv:], tail_rows], axis=1)
    return (
        rows_of(result_pieces),
        loss_value,
        rows_of(grad_pieces).astype(jnp.float32),
        both(attn_sum[0][:, : 3 * width], attn_sum[1][:, : 3 * width])[None],
        both(head_rows[0, :, 0].reshape(width), head_rows[1, :, 0].reshape(width)),
        both(head_rows[0, :, 2].reshape(width), head_rows[1, :, 2].reshape(width)),
        both(attn_sum[0][:, 3 * width : at].T, attn_sum[1][:, 3 * width : at].T, 0)[:, None],
        sums[4],
        sums[0],
        sums[1],
        sums[2],
        sums[3],
        both(up_of(0), up_of(1))[None],
        both(unit_rows[0], unit_rows[1]),
        both(down_of(0), down_of(1), 0)[:, None],
        sums[5],
    )


def one_image_a_chip(mesh, tokens):
    sizes = mesh.shape
    pairs = sizes["dp"] == 2 and sizes["row"] == 4 and sizes["col"] == 4
    return pairs and tokens == SEQ * sizes["row"] * sizes["col"]


def solution(mesh):
    placed = (
        P(("dp", "col"), "row"),
        P(("dp", "col"), "row"),
        P(("dp", "col")),
        P("row", "col"),
        P("col"),
        P("col"),
        P("col", "row"),
        P("row"),
        P("row"),
        P("row"),
        P("row"),
        P("row"),
        P("row", "col"),
        P("col"),
        P("col", "row"),
        P("row"),
    )
    returned = (
            P(("dp", "col"), "row"),
            P(),
            P(("dp", "col"), "row"),
            P("row", "dp", "col"),
            P("col"),
            P("col"),
            P("col", "row", "dp"),
            P("row"),
            P("row"),
            P("row"),
            P("row"),
            P("row"),
            P("row", "dp", "col"),
            P("col"),
            P("col", "row", "dp"),
            P("row"),
        )

    def whole(layer_input, *others):
        body = on_chip if one_image_a_chip(mesh, layer_input.shape[0]) else on_device
        return jax.shard_map(
            body, mesh=mesh, in_specs=placed, out_specs=returned, check_vma=False
        )(layer_input, *others)

    return whole
```

```python
import functools

import jax
import jax.numpy as jnp
from jax import lax
from jax.experimental import pallas as pl
from jax.experimental.pallas import tpu as pltpu
from jax.sharding import PartitionSpec as P

D = 1152
H = 16
HD = 72
FF = 4304
SEQ = 729


EPS = 1e-06


def feature_totals(left, right):
    return lax.psum(
        (jnp.sum(left, axis=-1, keepdims=True), jnp.sum(right, axis=-1, keepdims=True)), "row"
    )


def norm_forward(values, gain, shift):
    first_sum, second_sum = feature_totals(values, values * values)
    mean_rows = first_sum / D
    var_rows = second_sum / D - mean_rows * mean_rows
    inv_scale = lax.rsqrt(var_rows + EPS)
    normed = (values - mean_rows) * inv_scale
    return (normed, inv_scale, normed * gain + shift)


def norm_backward(grad_out, normed, inv_scale, gain):
    grad_normed = grad_out * gain
    first_sum, second_sum = feature_totals(grad_normed, grad_normed * normed)
    return inv_scale * (grad_normed - first_sum / D - normed * second_sum / D)


def first_section(local_rows, weight):
    gathered = lax.all_gather(local_rows, "col", axis=0, tiled=True)
    share_rows = gathered.shape[0] // lax.axis_size("row")

    def partial_term(row_start, row_count):
        return jnp.dot(gathered, weight, preferred_element_type=jnp.float32)

    result = lax.psum_scatter(
        partial_term(jnp.int32(0), lax.axis_size("row") * share_rows),
        "row",
        scatter_dimension=0,
        tiled=True,
    )
    return (gathered, result)


def second_section(quarter_rows, weight):
    gathered = lax.all_gather(quarter_rows, "row", axis=0, tiled=True)
    share_rows = gathered.shape[0] // lax.axis_size("col")

    def partial_term(row_start, row_count):
        return jnp.dot(gathered, weight, preferred_element_type=jnp.float32)

    result = lax.psum_scatter(
        partial_term(jnp.int32(0), lax.axis_size("col") * share_rows),
        "col",
        scatter_dimension=0,
        tiled=True,
    )
    return (gathered, result)


def second_section_back(grad_local, gathered, weight):
    grad_all = lax.all_gather(grad_local, "col", axis=0, tiled=True)
    grad_weight = lax.dot_general(
        gathered, grad_all, (((0,), (0,)), ((), ())), preferred_element_type=jnp.float32
    )
    share_rows = grad_all.shape[0] // lax.axis_size("row")

    def partial_term(row_start, row_count):
        return lax.dot_general(
            grad_all, weight, (((1,), (1,)), ((), ())), preferred_element_type=jnp.float32
        )

    result = lax.psum_scatter(
        partial_term(jnp.int32(0), lax.axis_size("row") * share_rows),
        "row",
        scatter_dimension=0,
        tiled=True,
    )
    return (grad_weight, result)


def first_section_back(grad_quarter, gathered, weight):
    grad_all = lax.all_gather(grad_quarter, "row", axis=0, tiled=True)
    grad_weight = lax.dot_general(
        gathered, grad_all, (((0,), (0,)), ((), ())), preferred_element_type=jnp.float32
    )
    share_rows = grad_all.shape[0] // lax.axis_size("col")

    def partial_term(row_start, row_count):
        return lax.dot_general(
            grad_all, weight, (((1,), (1,)), ((), ())), preferred_element_type=jnp.float32
        )

    result = lax.psum_scatter(
        partial_term(jnp.int32(0), lax.axis_size("col") * share_rows).astype(jnp.bfloat16),
        "col",
        scatter_dimension=0,
        tiled=True,
    ).astype(jnp.float32)
    return (grad_weight, result)


def attend(triple_img):
    score_scale = HD ** (-0.5)
    query_rows = triple_img[:, :, 0]
    key_rows = triple_img[:, :, 1]
    value_rows = triple_img[:, :, 2]
    raw_scores = jnp.einsum(
        "qhd,khd->hqk", query_rows, key_rows, preferred_element_type=jnp.float32
    )
    scaled = raw_scores * score_scale
    peak_score = jnp.max(scaled, axis=-1, keepdims=True)
    exp_scores = jnp.exp(scaled - peak_score)
    exp_total = jnp.sum(exp_scores, axis=-1, keepdims=True)
    soft_weights = (exp_scores / exp_total).astype(jnp.bfloat16)
    mixed_rows = jnp.einsum(
        "hqk,khd->qhd", soft_weights, value_rows, preferred_element_type=jnp.float32
    )
    return (mixed_rows.astype(jnp.bfloat16), peak_score + jnp.log(exp_total))


def attend_back(packed):
    triple_img, log_total, grad_mixed = packed
    score_scale = HD ** (-0.5)
    query_rows = triple_img[:, :, 0]
    key_rows = triple_img[:, :, 1]
    value_rows = triple_img[:, :, 2]
    raw_scores = jnp.einsum(
        "qhd,khd->hqk", query_rows, key_rows, preferred_element_type=jnp.float32
    )
    soft_weights = jnp.exp(raw_scores * score_scale - log_total)
    weights_low = soft_weights.astype(jnp.bfloat16)
    grad_values = jnp.einsum(
        "hqk,qhd->khd", weights_low, grad_mixed, preferred_element_type=jnp.float32
    )
    grad_soft = jnp.einsum(
        "qhd,khd->hqk", grad_mixed, value_rows, preferred_element_type=jnp.float32
    )
    inner_prod = jnp.sum(grad_soft * soft_weights, axis=-1, keepdims=True)
    grad_raw = (score_scale * soft_weights * (grad_soft - inner_prod)).astype(jnp.bfloat16)
    grad_query = jnp.einsum("hqk,khd->qhd", grad_raw, key_rows, preferred_element_type=jnp.float32)
    grad_keys = jnp.einsum("hqk,qhd->khd", grad_raw, query_rows, preferred_element_type=jnp.float32)
    return jnp.stack([grad_query, grad_keys, grad_values], axis=2).astype(jnp.bfloat16)


def on_device(
    layer_input,
    teacher,
    valid,
    proj_in,
    bias_query,
    bias_value,
    proj_out,
    bias_out,
    norm1_gain,
    norm1_shift,
    norm2_gain,
    norm2_shift,
    w_up,
    bias_up,
    w_down,
    bias_down,
):
    heads_here = H // lax.axis_size("col")
    head_width = heads_here * HD
    feat_here = layer_input.shape[1]
    units_here = w_up.shape[1]
    gain_one = norm1_gain.astype(jnp.float32)
    gain_two = norm2_gain.astype(jnp.float32)
    residual_in = layer_input.astype(jnp.float32)
    normed1, scale1, mid_one = norm_forward(residual_in, gain_one, norm1_shift.astype(jnp.float32))
    norm1_all, projected = first_section(mid_one.astype(jnp.bfloat16), proj_in)
    quarter = projected.shape[0]
    images = quarter // SEQ
    bias_shift = jnp.stack(
        [
            bias_query.astype(jnp.float32).reshape(heads_here, HD),
            jnp.zeros((heads_here, HD), jnp.float32),
            bias_value.astype(jnp.float32).reshape(heads_here, HD),
        ],
        axis=1,
    )
    triple = (projected.reshape(quarter, heads_here, 3, HD) + bias_shift).astype(jnp.bfloat16)
    triple_imgs = triple.reshape(images, SEQ, heads_here, 3, HD)
    mixed_imgs, log_totals = lax.map(attend, triple_imgs)
    mixed_all, attn_part = second_section(mixed_imgs.reshape(quarter, head_width), proj_out)
    resid1 = residual_in + attn_part + bias_out.astype(jnp.float32)
    normed2, scale2, mid_two = norm_forward(resid1, gain_two, norm2_shift.astype(jnp.float32))
    norm2_all, pre_part = first_section(mid_two.astype(jnp.bfloat16), w_up)
    pre = pre_part + bias_up.astype(jnp.float32)
    activated, gelu_pull = jax.vjp(lambda entry: jax.nn.gelu(entry, approximate=True), pre)
    act_all, down_part = second_section(activated.astype(jnp.bfloat16), w_down)
    result = resid1 + down_part + bias_down.astype(jnp.float32)
    mask_rows = valid.astype(jnp.float32)
    error_rows = result - teacher.astype(jnp.float32)
    err_part = jnp.sum(mask_rows[:, None] * error_rows * error_rows)
    count_part = jnp.sum(mask_rows) / lax.axis_size("row")
    err_total, valid_count = lax.psum((err_part, count_part), ("dp", "row", "col"))
    loss_value = err_total / (valid_count * D)
    tokens_all = layer_input.shape[0] * lax.axis_size("dp") * lax.axis_size("col")
    factor = tokens_all / (2.0 * valid_count)
    grad_result = 2.0 * error_rows * (mask_rows[:, None] * factor)
    grad_branch2 = grad_result.astype(jnp.bfloat16)
    grad_w_down, grad_act = second_section_back(grad_branch2, act_all, w_down)
    grad_pre = gelu_pull(grad_act)[0].astype(jnp.bfloat16)
    grad_w_up, grad_norm2 = first_section_back(grad_pre, norm2_all, w_up)
    grad_resid1 = grad_result + norm_backward(grad_norm2, normed2, scale2, gain_two)
    grad_branch1 = grad_resid1.astype(jnp.bfloat16)
    grad_proj_out, grad_mixed = second_section_back(grad_branch1, mixed_all, proj_out)
    grad_mixed_imgs = grad_mixed.astype(jnp.bfloat16).reshape(images, SEQ, heads_here, HD)
    grad_triple = lax.map(attend_back, (triple_imgs, log_totals, grad_mixed_imgs))
    grad_triple = grad_triple.reshape(quarter, heads_here, 3, HD)
    grad_proj_in, grad_norm1 = first_section_back(
        grad_triple.reshape(quarter, 3 * head_width), norm1_all, proj_in
    )
    grad_input = grad_resid1 + norm_backward(grad_norm1, normed1, scale1, gain_one)
    row_at = lax.axis_index("row") * feat_here
    col_at = lax.axis_index("col") * head_width
    feature_terms = jnp.stack(
        [
            jnp.sum(grad_norm1 * normed1, axis=0),
            jnp.sum(grad_norm1, axis=0),
            jnp.sum(grad_norm2 * normed2, axis=0),
            jnp.sum(grad_norm2, axis=0),
            jnp.sum(grad_branch1.astype(jnp.float32), axis=0),
            jnp.sum(grad_branch2.astype(jnp.float32), axis=0),
        ]
    )
    feature_full = lax.dynamic_update_slice_in_dim(
        jnp.zeros((6, D), jnp.float32), feature_terms, row_at, 1
    )
    grad_float = grad_triple.astype(jnp.float32)
    head_terms = jnp.stack(
        [
            jnp.sum(grad_float[:, :, 0], axis=0).reshape(head_width),
            jnp.sum(grad_float[:, :, 2], axis=0).reshape(head_width),
        ]
    )
    head_full = lax.dynamic_update_slice_in_dim(
        jnp.zeros((2, H * HD), jnp.float32), head_terms, col_at, 1
    )
    unit_terms = jnp.sum(grad_pre.astype(jnp.float32), axis=0)
    unit_full = lax.dynamic_update_slice_in_dim(
        jnp.zeros((FF,), jnp.float32), unit_terms, lax.axis_index("col") * units_here, 0
    )
    feature_full, head_full, unit_full = lax.psum(
        (feature_full, head_full, unit_full), ("dp", "row", "col")
    )
    feature_mine = lax.dynamic_slice_in_dim(feature_full, row_at, feat_here, 1)
    head_mine = lax.dynamic_slice_in_dim(head_full, col_at, head_width, 1)
    unit_mine = lax.dynamic_slice_in_dim(
        unit_full, lax.axis_index("col") * units_here, units_here, 0
    )
    grad_proj_in, grad_w_up = (
        lax.psum_scatter(
            grad_proj_in.astype(jnp.bfloat16), "dp", scatter_dimension=0, tiled=True
        ).astype(jnp.float32),
        lax.psum_scatter(
            grad_w_up.astype(jnp.bfloat16), "dp", scatter_dimension=0, tiled=True
        ).astype(jnp.float32),
    )
    grad_proj_out, grad_w_down = (
        lax.psum_scatter(
            grad_proj_out.astype(jnp.bfloat16), "dp", scatter_dimension=1, tiled=True
        ).astype(jnp.float32),
        lax.psum_scatter(
            grad_w_down.astype(jnp.bfloat16), "dp", scatter_dimension=1, tiled=True
        ).astype(jnp.float32),
    )
    grad_proj_in = grad_proj_in.reshape(1, grad_proj_in.shape[0], grad_proj_in.shape[1])
    grad_w_up = grad_w_up.reshape(1, grad_w_up.shape[0], grad_w_up.shape[1])
    grad_proj_out = grad_proj_out.reshape(grad_proj_out.shape[0], 1, grad_proj_out.shape[1])
    grad_w_down = grad_w_down.reshape(grad_w_down.shape[0], 1, grad_w_down.shape[1])
    return (
        result.astype(jnp.bfloat16),
        loss_value,
        grad_input,
        grad_proj_in,
        head_mine[0],
        head_mine[1],
        grad_proj_out,
        feature_mine[4],
        feature_mine[0],
        feature_mine[1],
        feature_mine[2],
        feature_mine[3],
        grad_w_up,
        unit_mine,
        grad_w_down,
        feature_mine[5],
    )


MESH = pl.DeviceIdType.MESH
F32 = jnp.float32
BF16 = jnp.bfloat16
LOG2E = 1.4426950408889634
GELU_ROOT = 0.7978845608028654


def place():
    return lax.axis_index("dp"), lax.axis_index("row"), lax.axis_index("col")


def flip(row, other):
    return lax.rem(row // 2 + other // 2, 2) * 2 + lax.rem(row + other, 2)


def neighbours():
    dp, row, col = place()
    return dict(
        core=(1 - dp, row, col),
        x=(dp, flip(row, 1), col),
        y=(dp, flip(row, 2), col),
        diagonal=(dp, flip(row, 3), col),
        next=(dp, row, lax.rem(2 * col + 3 * (col // 2) + 1, 4)),
        prev=(dp, row, lax.rem(2 * col + col // 2 + 2, 4)),
    )


def images_group():
    dp, row, col = place()
    steps = [(core, step) for core in (0, 1) for step in range(4)][1:]
    return [(lax.rem(dp + core, 2), row, lax.rem(col + step, 4)) for core, step in steps]


def meet():
    dp, row, col = place()
    plane = [(core, k) for core in (0, 1) for k in range(4)][1:]
    peers = [(lax.rem(dp + core, 2), flip(row, k), col) for core, k in plane]
    peers += [peer for i, peer in enumerate(images_group()) if i != 3]
    barrier = pltpu.get_barrier_semaphore()
    for peer in peers:
        pl.semaphore_signal(barrier, inc=1, device_id=peer, device_id_type=MESH)
    pl.semaphore_wait(barrier, len(peers))


class Shuffle:
    def __init__(self, send_sems, recv_sems, local_sem):
        self.sems = send_sems, recv_sems, local_sem
        self.pending = []

    def remote(self, source, target, i, slot, peer):
        return pltpu.make_async_remote_copy(
            source, target, self.sems[0].at[i], self.sems[1].at[slot],
            device_id=peer, device_id_type=MESH,
        )

    def spread(self, pieces, blocks):
        dp, row, col = place()
        for image in (0, 1):
            for half in (0, 1):
                chip = 2 * dp + image
                slot = flip(chip, row)
                mine = (dp == half) & (chip == row)
                index = 2 * image + half
                copy = self.remote(
                    pieces.at[image, half], blocks.at[slot], index, slot, (half, chip, col)
                )
                here = pltpu.make_async_copy(
                    pieces.at[image, half], blocks.at[0], self.sems[2]
                )
                self.start(copy, here, mine)
        own = dp == row // 2
        self.into = [(blocks.at[k], k, own if k == 0 else None) for k in range(4)]

    def collect(self, blocks, pieces):
        dp, row, col = place()
        image = lax.rem(row, 2)
        for k in range(4):
            owner = flip(row, k)
            index = 2 * image + dp
            mine = (dp == row // 2) & (owner == row)
            copy = self.remote(
                blocks.at[k], pieces.at[image, dp], k, index, (row // 2, owner, col)
            )
            here = pltpu.make_async_copy(blocks.at[k], pieces.at[image, dp], self.sems[2])
            self.start(copy, here, mine)
        self.into = []
        for image in (0, 1):
            for half in (0, 1):
                own = (dp == half) & (2 * dp + image == row)
                self.into.append((pieces.at[image, half], 2 * image + half, own))

    def start(self, copy, here, mine):
        pl.when(jnp.logical_not(mine))(copy.start)
        pl.when(mine)(here.start)
        self.pending.append((copy, here, mine))

    def arrive(self):
        dp, row, col = place()
        here = self.pending[0][1]
        for target, slot, own in self.into:
            copy = self.remote(target, target, 0, slot, (1 - dp, row, col))
            if own is None:
                copy.wait_recv()
            else:
                pl.when(jnp.logical_not(own))(copy.wait_recv)
                pl.when(own)(here.wait)

    def finish(self):
        for copy, _, mine in self.pending:
            pl.when(jnp.logical_not(mine))(copy.wait_send)


def mm(left, right):
    return jnp.dot(left, right, preferred_element_type=F32)


def mm_nt(left, right):
    return lax.dot_general(left, right, (((1,), (1,)), ((), ())), preferred_element_type=F32)


def each_rows(count, size, body):
    @pl.loop(0, count // size)
    def _(step):
        body(pl.ds(pl.multiple_of(step * size, size), size))


def fold(values):
    return sum(values[i : i + 16] for i in range(0, values.shape[0], 16))


def spread_lanes(source, spread, width):
    blocks = []
    for j in range(width // 256):
        low = 2 * HD * j // 128 * 128
        blocks.append(mm(source[:, low : low + 256], spread[low : low + 256, 256 * j : 256 * j + 256]))
    return jnp.concatenate(blocks, axis=1)


def transpose_into(target, source):
    @pl.loop(0, source.shape[1] // 128)
    def _(step):
        at = pl.ds(pl.multiple_of(step * 128, 128), 128)
        target[at, :] = source[:, at].T


class Sender:
    def __init__(self, send_sems, recv_sems):
        self.sems = (send_sems, recv_sems)
        self.count = 0
        self.copies = []

    def __call__(self, source, target, peer):
        copy = pltpu.make_async_remote_copy(
            source,
            target,
            self.sems[0].at[self.count],
            self.sems[1].at[self.count],
            device_id=peer,
            device_id_type=MESH,
        )
        self.count += 1
        copy.start()
        self.copies.append(copy)
        return copy

    def finish(self):
        for copy in self.copies:
            copy.wait_send()


class Copier:
    def __init__(self, sems):
        self.sems = sems
        self.count = 0

    def __call__(self, source, target):
        copy = pltpu.make_async_copy(source, target, self.sems.at[self.count])
        self.count += 1
        copy.start()
        return copy


def norm_stats(values):
    mean_rows = jnp.mean(values, axis=-1, keepdims=True)
    centered = values - mean_rows
    inv_scale = lax.rsqrt(jnp.mean(centered * centered, axis=-1, keepdims=True) + EPS)
    return centered * inv_scale, inv_scale


def forward_kernel(
    own_tokens,
    x_pieces,
    teacher_pieces,
    count_ref,
    params_ref,
    key_ref,
    key_lane_ref,
    spread_ref,
    rest_spread_ref,
    attn_ref,
    ff_ref,
    wpad_out,
    wff_out,
    triple_out,
    mixed_out,
    act_out,
    slope_out,
    norm1t_out,
    norm2t_out,
    rest_out,
    lse_out,
    act_rest_out,
    slope_rest_out,
    resid_out,
    grad_out,
    branch_out,
    brancht_out,
    result_out,
    err_out,
    x_ref,
    feature_ref,
    count_out,
    teacher_ref,
    features_in,
    biases_in,
    counts_in,
    wattn,
    wff,
    wpad,
    triple,
    mixed,
    act,
    slope,
    norm1,
    norm2,
    turned,
    part,
    give1,
    got1,
    give2,
    got2,
    local_sems,
    send_sems,
    recv_sems,
    shuffle_sems,
):
    peers = neighbours()
    meet()
    feat = attn_ref.shape[0]
    half = feat // 2
    depth = 4 * feat
    tokens = norm1.shape[0]
    own = tokens // 2
    main = ff_ref.shape[1] // 2
    qkv = triple.shape[2]
    wide = features_in.shape[2]
    pitch = wide // 6
    send = Sender(send_sems, recv_sems)
    keep = Copier(local_sems)

    def rows(block, low=0, size=None):
        return pl.ds(block * feat + low, feat if size is None else size)

    own_attn = keep(attn_ref, wattn.at[0, rows(0)])
    own_ff = keep(ff_ref, wff.at[0, rows(0)])
    az, ax, ay, a_low, a_high = ([None] * 4 for _ in range(5))

    def attn_source(s):
        return attn_ref if s == 0 else wattn.at[s, rows(0)]

    def attn_ring(s):
        az[s + 1] = send(attn_source(s), wattn.at[s + 1, rows(0)], peers["next"])

    def attn_plane(s):
        ax[s] = send(attn_source(s), wattn.at[s, rows(1)], peers["x"])
        ay[s] = send(attn_source(s), wattn.at[s, rows(2)], peers["y"])

    def attn_last(s):
        ax[s].wait_recv()
        a_low[s] = send(
            wattn.at[s, rows(1, 0, half)], wattn.at[s, rows(3, 0, half)], peers["y"]
        )
        ay[s].wait_recv()
        a_high[s] = send(
            wattn.at[s, rows(2, half, half)], wattn.at[s, rows(3, half, half)], peers["x"]
        )

    fz, fy, fx = ([None] * 4 for _ in range(3))

    def ff_first():
        return (
            send(ff_ref.at[pl.ds(0, half)], wff.at[0, rows(1, 0, half)], peers["x"]),
            send(ff_ref.at[pl.ds(half, half)], wff.at[0, rows(2, half, half)], peers["y"]),
        )

    def ff_ring(s):
        fz[s + 1] = [
            send(wff.at[s, piece], wff.at[s + 1, piece], peers["next"])
            for piece in (rows(0), rows(1, 0, half), rows(2, half, half))
        ]

    def ff_last(s):
        fy[s] = [
            send(wff.at[s, rows(k, 0, half)], wff.at[s, rows(k + 2, 0, half)], peers["y"])
            for k in (0, 1)
        ]
        fx[s] = [
            send(wff.at[s, rows(k, half, half)], wff.at[s, rows(k + 1, half, half)], peers["x"])
            for k in (0, 2)
        ]

    def arrive(copies):
        for copy in copies:
            copy.wait_recv()

    def attn_compute(s):
        arrive([a_low[s], a_high[s]])
        slot = s % 2
        if s == 0:
            own_attn.wait()
        if s >= 2:
            for copy in saved[s - 2]:
                copy.wait()

        def unpack(at):
            block = wattn[s, at, :]
            wpad[slot, at, :] = spread_lanes(block, spread_ref, wpad.shape[2]).astype(BF16)
            extra = mm(block[:, block.shape[1] - 128 :], rest_spread_ref[s]).astype(BF16)
            if s == 0:
                rest_out[at, :] = extra
            else:
                rest_out[at, :] = rest_out[at, :] + extra

        each_rows(depth, feat, unpack)

        def project(at):
            values = mm(norm1[at, :], wpad[slot, :, :qkv]) + biases_in[s, 0:1, :qkv]
            values = values + key_ref[at, :] * key_lane_ref[...]
            triple[slot, at, :] = values.astype(BF16)

        each_rows(tokens, tokens, project)
        scale = LOG2E * HD**-0.5
        for h in range(qkv // 384):
            query_at, key_at, value_at = (pl.ds((3 * h + j) * 128, 128) for j in range(3))
            value_turned = triple[slot, :, value_at].T

            def head(at, h=h, query_at=query_at, key_at=key_at, value_turned=value_turned):
                scores = mm_nt(triple[slot, :, key_at], triple[slot, at, query_at])
                peak = jnp.max(scores, axis=0, keepdims=True)
                weights = jnp.exp2((scores - peak) * scale)
                total = jnp.sum(weights, axis=0, keepdims=True)
                lse_out[2 * s + h, :, at] = peak * scale + jnp.log2(total)
                values = mm(value_turned, weights.astype(BF16)) / total
                mixed[s, at, pl.ds(h * 128, 128)] = values.T.astype(BF16)

            each_rows(tokens, own, head)

        def out(at):
            values = mm_nt(mixed[s, at, :], wpad[slot, :, qkv:])
            return values if s == 0 else part[at, :] + values

        swap = None
        if s < 3:
            part[...] = out(pl.ds(0, tokens))
        else:
            give1[...] = out(pl.ds(own, own)).astype(BF16)
            swap = send(give1, got1, peers["core"])
            part[pl.ds(0, own), :] = out(pl.ds(0, own))
        saved.append(
            [
                keep(wpad.at[slot], wpad_out.at[s]),
                keep(triple.at[slot], triple_out.at[s]),
                keep(mixed.at[s], mixed_out.at[s]),
            ]
        )
        return swap

    def gelu(pre):
        inner = GELU_ROOT * (pre + 0.044715 * pre * pre * pre)
        tanh = jnp.tanh(inner)
        rise = 0.5 * (1.0 + tanh)
        bend = 0.5 * pre * (1.0 - tanh * tanh) * (GELU_ROOT * (1.0 + 0.134145 * pre * pre))
        return (pre * rise).astype(BF16), (rise + bend).astype(BF16)

    def ff_compute(s):
        arrive(fy[s] + fx[s])

        def block(at):
            pre = mm(norm2[at, :], wff[s, :, :main]) + biases_in[s, 0:1, qkv : qkv + main]
            low, bent = gelu(pre)
            act[s, at, :] = low
            slope[s, at, :] = bent
            return part[at, :] + mm_nt(low, wff[s, :, main:])

        swap = None
        if s < 3:
            part[...] = block(pl.ds(0, tokens))
        else:
            give2[...] = block(pl.ds(own, own)).astype(BF16)
            swap = send(give2, got2, peers["core"])
            part[pl.ds(0, own), :] = block(pl.ds(0, own))
        ff_saved.extend(
            [
                keep(act.at[s], act_out.at[s]),
                keep(slope.at[s], slope_out.at[s]),
                keep(wff.at[s], wff_out.at[s]),
            ]
        )
        return swap

    def rest_compute():
        bias = mm(biases_in[0, :, qkv + main :].astype(BF16), rest_spread_ref[0, :, :128])
        for s in (1, 2, 3):
            values = biases_in[s, :, qkv + main :].astype(BF16)
            bias = bias + mm(values, rest_spread_ref[s, :, :128])

        def block(at):
            pre = mm(norm2[at, :], rest_out[:, :128]) + bias[0:1]
            low, bent = gelu(pre)
            act_rest_out[at, :] = low
            slope_rest_out[at, :] = bent
            part[at, :] = mm_nt(low, rest_out[:, 128:])

        each_rows(tokens, tokens, block)

    saved, ff_saved = [], []
    x_move = Shuffle(shuffle_sems.at[0], shuffle_sems.at[1], shuffle_sems.at[2, 0])
    x_move.spread(x_pieces, x_ref)
    attn_ring(0)
    attn_plane(0)
    own_params = [
        keep(params_ref.at[:, pl.ds(0, wide)], features_in.at[0]),
        keep(params_ref.at[:, pl.ds(wide, biases_in.shape[2])], biases_in.at[0]),
        keep(count_ref, counts_in.at[0]),
    ]
    smalls = [
        send(params_ref.at[:, pl.ds(0, wide)], features_in.at[k], peers[name])
        for k, name in ((1, "x"), (2, "y"), (3, "diagonal"))
    ]
    dp, row, col = place()
    ring_two = (dp, row, 3 - col)
    smalls += [
        send(params_ref.at[:, pl.ds(wide, biases_in.shape[2])], biases_in.at[s], peer)
        for s, peer in ((1, peers["next"]), (2, ring_two), (3, peers["prev"]))
    ]
    counts = [
        send(count_ref, counts_in.at[1 + i], peer) for i, peer in enumerate(images_group())
    ]
    teacher_move = Shuffle(shuffle_sems.at[3], shuffle_sems.at[4], shuffle_sems.at[2, 1])

    def token_rows(at):
        return jnp.concatenate([x_ref[k, at, :].astype(F32) for k in range(4)], axis=1)

    az[1].wait_recv()
    attn_ring(1)
    attn_plane(1)
    attn_last(0)
    az[2].wait_recv()
    attn_ring(2)
    attn_plane(2)
    first = ff_first()
    for copy in own_params:
        copy.wait()
    arrive(smalls)
    feature_ref[...] = jnp.zeros_like(feature_ref)
    for i in range(6):
        feature_ref[i : i + 1, :] = jnp.concatenate(
            [features_in[k, 0:1, pitch * i : pitch * i + feat] for k in range(4)], axis=1
        )
    x_move.arrive()

    def first_norm(at):
        normed, _ = norm_stats(token_rows(at))
        norm1[at, :] = (normed * feature_ref[0:1] + feature_ref[1:2]).astype(BF16)

    each_rows(own, 128, first_norm)
    swap1 = send(norm1.at[pl.ds(0, own)], norm1.at[pl.ds(own, own)], peers["core"])
    az[3].wait_recv()
    attn_plane(3)
    own_ff.wait()
    arrive(first)
    ff_ring(0)
    attn_last(1)
    swap1.wait_recv()
    attn_compute(0)
    attn_last(2)
    attn_compute(1)
    attn_last(3)
    ff_last(0)
    arrive(fz[1])
    ff_ring(1)
    ff_last(1)
    attn_compute(2)
    swap2 = attn_compute(3)
    swap2.wait_recv()

    def second_norm(at):
        values = token_rows(at) + part[at, :] + got1[at, :].astype(F32) + feature_ref[4:5]
        resid_out[at, :] = values
        normed, _ = norm_stats(values)
        norm2[at, :] = (normed * feature_ref[2:3] + feature_ref[3:4]).astype(BF16)

    each_rows(own, 128, second_norm)
    swap3 = send(norm2.at[pl.ds(0, own)], norm2.at[pl.ds(own, own)], peers["core"])
    arrive(fz[2])
    ff_ring(2)
    ff_last(2)
    transpose_into(turned, norm1)
    turn1 = keep(turned, norm1t_out)
    swap3.wait_recv()
    rest_compute()
    turn1.wait()
    transpose_into(turned, norm2)
    turn2 = keep(turned, norm2t_out)
    ff_compute(0)
    arrive(fz[3])
    ff_last(3)
    teacher_move.spread(teacher_pieces, teacher_ref)
    ff_compute(1)
    ff_compute(2)
    swap4 = ff_compute(3)
    err_out[...] = jnp.zeros_like(err_out)
    arrive(counts)
    count = counts_in[0]
    for i in range(1, 8):
        count = count + counts_in[i]
    count_out[...] = count
    factor = (own_tokens * 8.0) / count[0:1, 0:1]
    teacher_move.arrive()
    swap4.wait_recv()

    def finish(at):
        values = resid_out[at, :] + part[at, :] + got2[at, :].astype(F32) + feature_ref[5:6]
        for k in range(4):
            result_out[k, at, :] = values[:, k * feat : (k + 1) * feat].astype(BF16)
        target = [teacher_ref[k, at, :feat].astype(F32) for k in range(4)]
        error = values - jnp.concatenate(target, axis=1)
        masked = error * teacher_ref[0, at, feat : feat + 1].astype(F32)
        err_out[...] = err_out[...] + fold(error * masked)
        grad = masked * factor
        grad_out[at, :] = grad
        branch_out[at, :] = grad.astype(BF16)

    def turn(start):
        brancht_out[:, pl.ds(start, 128)] = branch_out[pl.ds(start, 128), :].T

    swaps = []
    for start in range(0, own, 128):
        finish(pl.ds(start, 128))
        swaps.append(
            send(
                branch_out.at[pl.ds(start, 128)],
                branch_out.at[pl.ds(own + start, 128)],
                peers["core"],
            )
        )
        turn(start)
    for start, swap in zip(range(own, tokens, 128), swaps):
        swap.wait_recv()
        turn(start)
    turn2.wait()
    for copies in saved[2:]:
        for copy in copies:
            copy.wait()
    for copy in ff_saved:
        copy.wait()
    send.finish()
    x_move.finish()
    teacher_move.finish()


def forward_call(arrays, own_tokens, feat, lanes, main, qkv, mix, own, depth):
    tokens = 2 * own
    wide, narrow = 6 * ((feat + 127) // 128 * 128), qkv + main + 128
    anywhere = pl.BlockSpec(memory_space=pl.ANY)
    local = pl.BlockSpec(memory_space=pltpu.VMEM)
    shapes = [
        ((4, depth, qkv + mix), BF16, anywhere),
        ((4, depth, 2 * main), BF16, anywhere),
        ((4, tokens, qkv), BF16, anywhere),
        ((4, tokens, mix), BF16, anywhere),
        ((4, tokens, main), BF16, anywhere),
        ((4, tokens, main), BF16, anywhere),
        ((depth, tokens), BF16, anywhere),
        ((depth, tokens), BF16, anywhere),
        ((depth, 256), BF16, local),
        ((8, 1, tokens), F32, local),
        ((tokens, 128), BF16, local),
        ((tokens, 128), BF16, local),
        ((own, depth), F32, local),
        ((own, depth), F32, local),
        ((tokens, depth), BF16, local),
        ((depth, tokens), BF16, local),
        ((4, own, feat), BF16, local),
        ((16, depth), F32, local),
        ((4, own, feat), BF16, local),
        ((8, depth), F32, local),
        ((8, 128), F32, local),
    ]
    return pl.pallas_call(
        functools.partial(forward_kernel, own_tokens),
        out_shape=[jax.ShapeDtypeStruct(shape, dtype) for shape, dtype, _ in shapes],
        in_specs=[anywhere] * 2 + [local] * 6 + [anywhere] * 2,
        out_specs=[spec for _, _, spec in shapes],
        scratch_shapes=[
            pltpu.VMEM((4, own, arrays[1].shape[-1]), BF16),
            pltpu.VMEM((4, 8, wide), F32),
            pltpu.VMEM((4, 8, narrow), F32),
            pltpu.VMEM((8, 8, 128), F32),
            pltpu.VMEM((4, depth, lanes), BF16),
            pltpu.VMEM((4, depth, 2 * main), BF16),
            pltpu.VMEM((2, depth, qkv + mix), BF16),
            pltpu.VMEM((2, tokens, qkv), BF16),
            pltpu.VMEM((4, tokens, mix), BF16),
            pltpu.VMEM((4, tokens, main), BF16),
            pltpu.VMEM((4, tokens, main), BF16),
            pltpu.VMEM((tokens, depth), BF16),
            pltpu.VMEM((tokens, depth), BF16),
            pltpu.VMEM((depth, tokens), BF16),
            pltpu.VMEM((tokens, depth), F32),
            pltpu.VMEM((own, depth), BF16),
            pltpu.VMEM((own, depth), BF16),
            pltpu.VMEM((own, depth), BF16),
            pltpu.VMEM((own, depth), BF16),
            pltpu.SemaphoreType.DMA((32,)),
            pltpu.SemaphoreType.DMA((72,)),
            pltpu.SemaphoreType.DMA((72,)),
            pltpu.SemaphoreType.DMA((5, 4)),
        ],
        compiler_params=pltpu.CompilerParams(
            collective_id=1, has_side_effects=True, vmem_limit_bytes=62 << 20
        ),
    )(*arrays)


def backward_kernel(
    branch2_ref,
    rest_ref,
    act_rest_ref,
    slope_rest_ref,
    lse_ref,
    feature_ref,
    spread_ref,
    rest_spread_ref,
    x_ref,
    resid_ref,
    err_ref,
    result_blocks,
    grad_hbm,
    norm1t_hbm,
    norm2t_hbm,
    branch2t_hbm,
    wpad_hbm,
    wff_hbm,
    triple_hbm,
    mixed_hbm,
    act_hbm,
    slope_hbm,
    grad_pieces,
    result_pieces,
    sums_out,
    bias_out,
    attn_out,
    ff_out,
    grad_blocks,
    terms,
    terms_mine,
    terms_in,
    sums_in,
    bias_mine,
    bias_turn,
    bias_in,
    bias_plane,
    units_out,
    units_rest_out,
    heads_out,
    gattn,
    gff,
    wslot,
    kept,
    grad_pre,
    grad_rest,
    normt,
    brancht,
    branch1,
    part,
    give,
    got,
    grad_mid,
    dtriple,
    grad_mixed,
    grad_key,
    grad_value,
    inner_row,
    ra,
    rb,
    r1,
    r2,
    rz,
    ry,
    rx,
    rzl,
    rzh,
    rfx,
    rfy,
    local_sems,
    send_sems,
    recv_sems,
    shuffle_sems,
):
    peers = neighbours()
    feat = 2 * attn_out.shape[1]
    half = feat // 2
    depth = 4 * feat
    tokens = branch2_ref.shape[0]
    own = tokens // 2
    main = gff.shape[2] // 2
    qkv = triple_hbm.shape[2]
    send = Sender(send_sems, recv_sems)
    keep = Copier(local_sems)

    def rows(block, low=0, size=None):
        return pl.ds(block * feat + low, feat if size is None else size)

    def load_ff(s):
        slot = s % 2
        return [
            keep(wff_hbm.at[s], wslot.at[slot]),
            keep(act_hbm.at[s], kept.at[slot, :, pl.ds(0, main)]),
            keep(slope_hbm.at[s], kept.at[slot, :, pl.ds(main, main)]),
        ]

    def load_attn(s):
        slot = s % 2
        return [
            keep(wpad_hbm.at[s], wslot.at[slot]),
            keep(triple_hbm.at[s], kept.at[slot, :, pl.ds(0, qkv)]),
            keep(mixed_hbm.at[s], kept.at[slot, :, pl.ds(qkv, grad_mixed.shape[1])]),
        ]

    loads = {3: load_ff(3)}
    turns = [keep(norm2t_hbm, normt), keep(branch2t_hbm, brancht)]
    loads[2] = load_ff(2)
    load_grad = keep(grad_hbm, grad_mid)
    meet()
    result_move = Shuffle(shuffle_sems.at[0], shuffle_sems.at[1], shuffle_sems.at[2, 0])
    grad_move = Shuffle(shuffle_sems.at[3], shuffle_sems.at[4], shuffle_sems.at[2, 1])
    cy, cx, zl, zh = ([None] * 4 for _ in range(4))
    ca, cb, c1, c2, cz = ([None] * 4 for _ in range(5))

    def add_into(target, at, *sources):
        size = at.size

        @pl.loop(0, size // 16)
        def _(step):
            here = pl.ds(pl.multiple_of(at.start + step * 16, 16), 16)
            there = pl.ds(pl.multiple_of(step * 16, 16), 16)
            total = target[here, :].astype(F32)
            for source in sources:
                total = total + source[there, :].astype(F32)
            target[here, :] = total.astype(BF16)

    def column_sum(values):
        return jnp.sum(values.astype(F32), axis=0, keepdims=True)

    def ff_compute(s):
        slot = s % 2
        for copy in loads[s]:
            copy.wait()
        units_out[s] = jnp.zeros((1, main), F32)

        def block(at):
            grad = mm(branch2_ref[at, :], wslot[slot, :, main : 2 * main])
            low = (grad * kept[slot, at, main:].astype(F32)).astype(BF16)
            grad_pre[at, :] = low
            units_out[s] = units_out[s] + column_sum(low)
            values = mm_nt(low, wslot[slot, :, :main])
            part[at, :] = values if s == 3 else part[at, :] + values

        each_rows(tokens, own, block)
        if s == 3:
            for copy in turns:
                copy.wait()

        def grads(at):
            gff[s, at, :main] = mm(normt[at, :], grad_pre[...]).astype(BF16)
            gff[s, at, main:] = mm(brancht[at, :], kept[slot, :, :main]).astype(BF16)

        each_rows(depth, 2 * feat, grads)
        cy[s] = [
            send(gff.at[s, rows(k, 0, half)], ry.at[s, k - 2], peers["y"]) for k in (2, 3)
        ]
        cx[s] = [
            send(gff.at[s, rows(k, half, half)], rx.at[s, k // 2], peers["x"]) for k in (1, 3)
        ]
        if s >= 2:
            loads[s - 2] = load_ff(s - 2)

    def rest_compute():
        units_rest_out[...] = jnp.zeros_like(units_rest_out)

        def block(at):
            grad = mm(branch2_ref[at, :], rest_ref[:, 128:])
            low = (grad * slope_rest_ref[at, :].astype(F32)).astype(BF16)
            grad_pre[at, :128] = low
            units_rest_out[...] = units_rest_out[...] + column_sum(low)
            return part[at, :] + mm_nt(low, rest_ref[:, :128])

        give[...] = block(pl.ds(own, own)).astype(BF16)
        swap = send(give, got, peers["core"])
        part[pl.ds(0, own), :] = block(pl.ds(0, own))

        def grads(at):
            grad_rest[at, :128] = mm(normt[at, :], grad_pre[:, :128]).astype(BF16)
            grad_rest[at, 128:] = mm(brancht[at, :], act_rest_ref[...]).astype(BF16)

        each_rows(depth, 2 * feat, grads)
        return swap

    def ff_add(s):
        for copy in cy[s] + cx[s]:
            copy.wait_recv()
        last = s == 3
        if not last:
            for copy in zl[s] + zh[s]:
                copy.wait_recv()
        lows, highs = [], []
        for i, k in enumerate((0, 1)):
            piece = rows(k, 0, half)
            add_into(gff.at[s], piece, ry.at[s, i], *([] if last else [rzl.at[s, i]]))
            lows.append((piece, i))
        for i, k in enumerate((0, 2)):
            piece = rows(k, half, half)
            add_into(gff.at[s], piece, rx.at[s, i], *([] if last else [rzh.at[s, i]]))
            highs.append((piece, i))
        if s:
            zl[s - 1] = [
                send(gff.at[s, piece], rzl.at[s - 1, i], peers["prev"]) for piece, i in lows
            ]
            zh[s - 1] = [
                send(gff.at[s, piece], rzh.at[s - 1, i], peers["prev"]) for piece, i in highs
            ]

    def attn_compute(s):
        slot = s % 2
        for copy in attn_loads[s]:
            copy.wait()

        def back_out(at):
            grad_mixed[at, :] = mm(branch1[at, :], wslot[slot, :, qkv:]).astype(BF16)

        each_rows(tokens, tokens, back_out)
        scale = HD**-0.5
        for h in range(qkv // 384):
            query_at, key_at, value_at = (pl.ds((3 * h + j) * 128, 128) for j in range(3))
            mix_at = pl.ds(h * 128, 128)
            value_of_mix = pl.ds(qkv + h * 128, 128)
            key_turned = kept[slot, :, key_at].T
            product = grad_mixed[:, mix_at].astype(F32) * kept[slot, :, value_of_mix].astype(F32)
            inner_row[...] = jnp.sum(product.T, axis=0, keepdims=True)
            grad_key[...] = jnp.zeros_like(grad_key)
            grad_value[...] = jnp.zeros_like(grad_value)

            def head(at, h=h, query_at=query_at, key_at=key_at, value_at=value_at,
                     mix_at=mix_at, key_turned=key_turned):
                query = kept[slot, at, query_at]
                grad = grad_mixed[at, mix_at]
                scores = mm_nt(kept[slot, :, key_at], query)
                weights = jnp.exp2(scores * (scale * LOG2E) - lse_ref[2 * s + h, :, at])
                grad_soft = mm_nt(kept[slot, :, value_at], grad)
                grad_raw = (weights * (grad_soft - inner_row[:, at]) * scale).astype(BF16)
                grad_value[...] += mm(weights.astype(BF16), grad)
                grad_key[...] += mm(grad_raw, query)
                dtriple[at, query_at] = mm(key_turned, grad_raw).T.astype(BF16)

            each_rows(tokens, own, head)
            dtriple[:, key_at] = grad_key[...].astype(BF16)
            dtriple[:, value_at] = grad_value[...].astype(BF16)
        heads_out[s] = jnp.zeros((1, qkv), F32)

        def back_in(at):
            values = mm_nt(dtriple[at, :], wslot[slot, :, :qkv])
            heads_out[s] = heads_out[s] + column_sum(dtriple[at, :])
            return values if s == 3 else part[at, :] + values

        swap = None
        if s:
            for at in (pl.ds(0, own), pl.ds(own, own)):
                part[at, :] = back_in(at)
        else:
            give[...] = back_in(pl.ds(own, own)).astype(BF16)
            swap = send(give, got, peers["core"])
            part[pl.ds(0, own), :] = back_in(pl.ds(0, own))

        def grads(at):
            first = mm(normt[at, :], dtriple[...]).astype(BF16)
            second = mm(brancht[at, :], kept[slot, :, qkv:]).astype(BF16)
            tiles = [0.0] * (gattn.shape[2] // 128)
            for j in range((qkv + second.shape[1]) // 256):
                low, to = 2 * HD * j // 128 * 128, 256 * j
                block = first[:, to : to + 256] if to < qkv else second[:, to - qkv : to - qkv + 256]
                moved = mm_nt(block, spread_ref[low : low + 256, to : to + 256])
                for i in (0, 1):
                    tiles[low // 128 + i] += moved[:, 128 * i : 128 * i + 128]
            tiles[-1] += mm_nt(grad_rest[at, :], rest_spread_ref[s])
            gattn[s, at, :] = jnp.concatenate(tiles, axis=1).astype(BF16)

        each_rows(depth, 2 * feat, grads)
        ca[s] = send(gattn.at[s, rows(3, 0, half)], ra.at[s], peers["y"])
        cb[s] = send(gattn.at[s, rows(3, half, half)], rb.at[s], peers["x"])
        if s >= 2:
            attn_loads[s - 2] = load_attn(s - 2)
        return swap

    def attn_plane(s):
        ca[s].wait_recv()
        add_into(gattn.at[s], rows(1, 0, half), ra.at[s])
        c1[s] = send(gattn.at[s, rows(1)], r1.at[s], peers["x"])
        cb[s].wait_recv()
        add_into(gattn.at[s], rows(2, half, half), rb.at[s])
        c2[s] = send(gattn.at[s, rows(2)], r2.at[s], peers["y"])

    def attn_ring(s):
        c1[s].wait_recv()
        c2[s].wait_recv()
        if s < 3:
            cz[s].wait_recv()
        add_into(gattn.at[s], rows(0), r1.at[s], r2.at[s], *([rz.at[s]] if s < 3 else []))
        if s:
            cz[s - 1] = send(gattn.at[s, rows(0)], rz.at[s - 1], peers["prev"])

    terms[...] = jnp.zeros_like(terms)

    def add_term(index, values):
        terms[index] = terms[index] + fold(values)

    result_move.collect(result_blocks, result_pieces)
    ff_compute(3)
    ff_compute(2)
    ff_compute(1)
    ff_add(3)
    ff_compute(0)
    attn_loads = {3: load_attn(3), 2: load_attn(2)}
    swap1 = rest_compute()
    load_norm = keep(norm1t_hbm, normt)
    swap1.wait_recv()
    load_grad.wait()

    def mid(at):
        normed, inv_scale = norm_stats(resid_ref[at, :])
        grad_norm = part[at, :] + got[at, :].astype(F32)
        add_term(2, grad_norm * normed)
        add_term(3, grad_norm)
        scaled = grad_norm * feature_ref[2:3]
        first = jnp.mean(scaled, axis=-1, keepdims=True)
        second = jnp.mean(scaled * normed, axis=-1, keepdims=True)
        grad = grad_mid[at, :] + inv_scale * (scaled - first - normed * second)
        grad_mid[at, :] = grad
        low = grad.astype(BF16)
        branch1[at, :] = low
        add_term(4, low.astype(F32))
        add_term(5, branch2_ref[at, :].astype(F32))

    each_rows(own, 64, mid)
    swap2 = send(branch1.at[pl.ds(0, own)], branch1.at[pl.ds(own, own)], peers["core"])
    swap2.wait_recv()
    load_norm.wait()
    transpose_into(brancht, branch1)
    attn_compute(3)
    ff_add(2)
    attn_compute(2)
    attn_plane(3)
    attn_compute(1)
    attn_plane(2)
    ff_add(1)
    attn_ring(3)
    swap1.wait_send()
    swap3 = attn_compute(0)
    attn_plane(1)
    attn_ring(2)
    attn_plane(0)
    swap3.wait_recv()

    def token_rows(at):
        return jnp.concatenate([x_ref[k, at, :].astype(F32) for k in range(4)], axis=1)

    def last(at):
        normed, inv_scale = norm_stats(token_rows(at))
        grad_norm = part[at, :] + got[at, :].astype(F32)
        add_term(0, grad_norm * normed)
        add_term(1, grad_norm)
        scaled = grad_norm * feature_ref[0:1]
        first = jnp.mean(scaled, axis=-1, keepdims=True)
        second = jnp.mean(scaled * normed, axis=-1, keepdims=True)
        grad = grad_mid[at, :] + inv_scale * (scaled - first - normed * second)
        for k in range(4):
            grad_blocks[k, at, :] = grad[:, k * feat : (k + 1) * feat].astype(BF16)

    each_rows(own, 64, last)
    grad_move.collect(grad_blocks, grad_pieces)
    terms_mine[...] = jnp.zeros_like(terms_mine)
    bias_mine[...] = jnp.zeros_like(bias_mine)
    for i in range(7):
        if i < 6:
            row_sum = jnp.sum(terms[i], axis=0, keepdims=True)
        else:
            err = jnp.sum(jnp.sum(err_ref[...], axis=0, keepdims=True), axis=1, keepdims=True)
            row_sum = jnp.broadcast_to(err, (1, depth))
        for k in range(4):
            terms_mine[k, i : i + 1, :] = row_sum[:, k * feat : (k + 1) * feat]
    wide = bias_mine.shape[2]
    for s in range(4):
        bias_mine[s, 0:1, :qkv] = heads_out[s]
        bias_mine[s, 0:1, qkv : qkv + main] = units_out[s]
        bias_mine[s, 0:1, qkv + main :] = units_rest_out[...]
    dp, row, col = place()
    ring_two = (dp, row, 3 - col)
    sides = ((1, "x"), (2, "y"), (3, "diagonal"))
    term_sends = [send(terms_mine.at[k], terms_in.at[k - 1], peers[name]) for k, name in sides]
    bias_sends = [
        send(bias_mine.at[s], bias_turn.at[s - 1], peer)
        for s, peer in ((1, peers["prev"]), (2, ring_two), (3, peers["next"]))
    ]
    ff_add(0)
    end_low = send(gff.at[0, rows(1, 0, half)], rfx, peers["x"])
    end_high = send(gff.at[0, rows(2, half, half)], rfy, peers["y"])
    attn_ring(1)
    for copy in term_sends + bias_sends:
        copy.wait_recv()
    terms_mine[0] = terms_mine[0] + terms_in[0] + terms_in[1] + terms_in[2]
    sum_sends = [
        send(terms_mine.at[0], sums_in.at[i], peer) for i, peer in enumerate(images_group())
    ]
    bias_plane[...] = bias_mine[0]
    for s in (1, 2, 3):
        bias_plane[s : s + 1, :] = bias_turn[s - 1, 0:1, :]
    plane_sends = [send(bias_plane, bias_in.at[k - 1], peers[name]) for k, name in sides]
    end_low.wait_recv()
    end_high.wait_recv()
    add_into(gff.at[0], rows(0, 0, half), rfx)
    add_into(gff.at[0], rows(0, half, half), rfy)
    quarter = feat // 2
    keep_at = pl.ds(pl.multiple_of(dp * quarter, 16), quarter)
    give_at = pl.ds(pl.multiple_of((1 - dp) * quarter, 16), quarter)
    done = [keep(gff.at[0, keep_at], ff_out.at[0])]
    pair_sends = [send(gff.at[0, give_at], ff_out.at[1], peers["core"])]
    for copy in plane_sends + sum_sends:
        copy.wait_recv()
    bias_out[0] = bias_plane[...] + bias_in[0] + bias_in[1] + bias_in[2]
    pair_sends.append(send(bias_out.at[0], bias_out.at[1], peers["core"]))
    total = terms_mine[0]
    for i in range(7):
        total = total + sums_in[i]
    sums_out[...] = total
    attn_ring(0)
    done.append(keep(gattn.at[0, keep_at], attn_out.at[0]))
    pair_sends.append(send(gattn.at[0, give_at], attn_out.at[1], peers["core"]))
    for copy in pair_sends:
        copy.wait_recv()
    for copy in done:
        copy.wait()
    result_move.arrive()
    grad_move.arrive()
    for copy in send.copies:
        if copy is not swap1:
            copy.wait_send()
    result_move.finish()
    grad_move.finish()


def backward_call(arrays, feat, lanes, main, qkv, mix, own, depth):
    tokens = 2 * own
    half = feat // 2
    narrow = qkv + main + 128
    anywhere = pl.BlockSpec(memory_space=pl.ANY)
    local = pl.BlockSpec(memory_space=pltpu.VMEM)
    shapes = [
        ((2, 2, own, feat), BF16, anywhere),
        ((2, 2, own, feat), BF16, anywhere),
        ((8, feat), F32, local),
        ((2, 8, narrow), F32, local),
        ((2, half, lanes), BF16, anywhere),
        ((2, half, 2 * main), BF16, anywhere),
    ]
    return pl.pallas_call(
        backward_kernel,
        out_shape=[jax.ShapeDtypeStruct(shape, dtype) for shape, dtype, _ in shapes],
        in_specs=[local] * 11 + [anywhere] * 11,
        out_specs=[spec for _, _, spec in shapes],
        scratch_shapes=[
            pltpu.VMEM((4, own, feat), BF16),
            pltpu.VMEM((6, 16, depth), F32),
            pltpu.VMEM((4, 8, feat), F32),
            pltpu.VMEM((3, 8, feat), F32),
            pltpu.VMEM((7, 8, feat), F32),
            pltpu.VMEM((4, 8, narrow), F32),
            pltpu.VMEM((3, 8, narrow), F32),
            pltpu.VMEM((3, 8, narrow), F32),
            pltpu.VMEM((8, narrow), F32),
            pltpu.VMEM((4, 1, main), F32),
            pltpu.VMEM((1, 128), F32),
            pltpu.VMEM((4, 1, qkv), F32),
            pltpu.VMEM((4, depth, lanes), BF16),
            pltpu.VMEM((4, depth, 2 * main), BF16),
            pltpu.VMEM((2, depth, 2 * main), BF16),
            pltpu.VMEM((2, tokens, qkv + mix), BF16),
            pltpu.VMEM((tokens, main), BF16),
            pltpu.VMEM((depth, 256), BF16),
            pltpu.VMEM((depth, tokens), BF16),
            pltpu.VMEM((depth, tokens), BF16),
            pltpu.VMEM((tokens, depth), BF16),
            pltpu.VMEM((tokens, depth), F32),
            pltpu.VMEM((own, depth), BF16),
            pltpu.VMEM((own, depth), BF16),
            pltpu.VMEM((own, depth), F32),
            pltpu.VMEM((tokens, qkv), BF16),
            pltpu.VMEM((tokens, mix), BF16),
            pltpu.VMEM((tokens, 128), F32),
            pltpu.VMEM((tokens, 128), F32),
            pltpu.VMEM((1, tokens), F32),
            pltpu.VMEM((4, half, lanes), BF16),
            pltpu.VMEM((4, half, lanes), BF16),
            pltpu.VMEM((4, feat, lanes), BF16),
            pltpu.VMEM((4, feat, lanes), BF16),
            pltpu.VMEM((3, feat, lanes), BF16),
            pltpu.VMEM((4, 2, half, 2 * main), BF16),
            pltpu.VMEM((4, 2, half, 2 * main), BF16),
            pltpu.VMEM((3, 2, half, 2 * main), BF16),
            pltpu.VMEM((3, 2, half, 2 * main), BF16),
            pltpu.VMEM((half, 2 * main), BF16),
            pltpu.VMEM((half, 2 * main), BF16),
            pltpu.SemaphoreType.DMA((32,)),
            pltpu.SemaphoreType.DMA((104,)),
            pltpu.SemaphoreType.DMA((104,)),
            pltpu.SemaphoreType.DMA((5, 4)),
        ],
        compiler_params=pltpu.CompilerParams(
            collective_id=2, has_side_effects=True, vmem_limit_bytes=63 << 20
        ),
    )(*arrays)
def on_chip(
    layer_input,
    teacher,
    valid,
    proj_in,
    bias_query,
    bias_value,
    proj_out,
    bias_out,
    norm1_gain,
    norm1_shift,
    norm2_gain,
    norm2_shift,
    w_up,
    bias_up,
    w_down,
    bias_down,
):
    core = lax.axis_index("dp")
    first = core == 0
    cols = lax.axis_size("col")
    feat = layer_input.shape[1]
    images = layer_input.shape[0] // SEQ
    half_seq = (SEQ + 255) // 256 * 128
    pad_seq = 2 * half_seq
    units = w_up.shape[1] // 2
    width = proj_out.shape[0] // 2
    heads = width // HD
    main = units // 128 * 128
    rest = units - main
    at = 4 * width
    lanes = (at + 2 * rest + 127) // 128 * 128
    qkv, mix = 3 * heads * 128, heads * 128

    def core_half(values, axis):
        low, high = jnp.split(values, 2, axis=axis)
        return jnp.where(first, low, high)

    def pieces(values):
        values = jnp.pad(values.reshape(images, SEQ, -1), ((0, 0), (0, pad_seq - SEQ), (0, 0)))
        return values.reshape(images, 2, half_seq, -1)

    up_half, down_half = core_half(w_up, 1), core_half(w_down, 0).T
    attn_shard = jnp.concatenate(
        [
            core_half(proj_in, 1),
            core_half(proj_out, 0).T,
            up_half[:, main:],
            down_half[:, main:],
            jnp.zeros((feat, lanes - at - 2 * rest), jnp.bfloat16),
        ],
        axis=1,
    )
    ff_shard = jnp.concatenate([up_half[:, :main], down_half[:, :main]], axis=1)
    lane = jnp.arange(lanes)
    spread_at = jnp.where(lane < at, lane // HD * 128 + lane % HD, -1)
    spread = (spread_at[:, None] == jnp.arange(qkv + mix)[None]).astype(jnp.bfloat16)
    tail = lane[-128:]
    part = jnp.arange(cols)[:, None]
    up_at = jnp.where((tail >= at) & (tail < at + rest), tail - at + part * rest, -1)
    down_at = jnp.where(
        (tail >= at + rest) & (tail < at + 2 * rest), tail - at - rest + part * rest + 128, -1
    )
    spot = jnp.arange(256)
    rest_spread = (up_at[..., None] == spot) | (down_at[..., None] == spot)
    rest_spread = rest_spread.astype(jnp.bfloat16)

    place_of = jnp.arange(pad_seq)
    token = jnp.where(
        place_of < half_seq, place_of + core * half_seq, place_of - core * half_seq
    )
    key_column = jnp.where(token < SEQ, 0.0, -1e30).astype(jnp.float32)[:, None]
    key_lane = (jnp.arange(qkv) % 384 == 128 + HD).astype(jnp.float32)[None]

    query_bias, value_bias = core_half(bias_query, 0), core_half(bias_value, 0)
    unit_bias = core_half(bias_up, 0)
    pitch = (feat + 127) // 128 * 128
    one = jnp.ones((1,), jnp.bfloat16)

    def gap(size):
        return jnp.zeros((size,), jnp.bfloat16)

    params = []
    for vector in (norm1_gain, norm1_shift, norm2_gain, norm2_shift, bias_out, bias_down):
        params += [vector, gap(pitch - feat)]
    for h in range(heads):
        head_at = slice(h * HD, (h + 1) * HD)
        params += [query_bias[head_at], one, gap(127 - HD + 128)]
        params += [value_bias[head_at], gap(128 - HD)]
    params += [unit_bias[:main], gap(at - lanes + 128), unit_bias[main:]]
    params.append(gap(lanes - at - rest))
    params = jnp.concatenate(params).astype(jnp.float32)
    params = jnp.broadcast_to(params[None], (8, params.shape[0]))
    count = jnp.broadcast_to(jnp.sum(valid).astype(jnp.float32), (8, 128))

    marked = jnp.concatenate(
        [
            teacher,
            valid.astype(jnp.bfloat16)[:, None],
            jnp.zeros((teacher.shape[0], pitch - feat - 1), jnp.bfloat16),
        ],
        axis=1,
    )
    sizes = (feat, lanes, main, qkv, mix, half_seq, 4 * feat)
    (
        wpad, wff, triple, mixed, act, slope, norm1t, norm2t, rest_weight, lse, act_rest,
        slope_rest, resid1, grad_result, branch2, branch2t, result, err_rows, x_blocks,
        features, counted,
    ) = forward_call(
        (
            pieces(layer_input), pieces(marked), count, params, key_column, key_lane, spread,
            rest_spread, attn_shard, ff_shard,
        ),
        layer_input.shape[0],
        *sizes,
    )
    grad_pieces, result_pieces, sums, bias_rows, attn_sum, ff_sum = backward_call(
        (
            branch2, rest_weight, act_rest, slope_rest, lse, features, spread, rest_spread,
            x_blocks, resid1, err_rows, result, grad_result, norm1t, norm2t, branch2t, wpad,
            wff, triple, mixed, act, slope,
        ),
        *sizes,
    )

    def rows_of(values):
        return values.reshape(images, pad_seq, feat)[:, :SEQ].reshape(images * SEQ, feat)

    def both(keep, got, axis=-1):
        return jnp.concatenate(
            [jnp.where(first, keep, got), jnp.where(first, got, keep)], axis=axis
        ).astype(jnp.float32)

    def up_of(i):
        return jnp.concatenate([ff_sum[i][:, :main], attn_sum[i][:, at : at + rest]], axis=1)

    def down_of(i):
        block = [ff_sum[i][:, main:], attn_sum[i][:, at + rest : at + 2 * rest]]
        return jnp.concatenate(block, axis=1).T

    loss_value = sums[6, 0] / (counted[0, 0] * D)
    main_rows = jnp.sum(bias_rows[:, :cols, : qkv + main], axis=1)
    head_rows = main_rows[:, :qkv].reshape(2, heads, 3, 128)[..., :HD]
    tail_rows = bias_rows[:, :cols, qkv + main :]
    tail_rows = sum(tail_rows[:, s, s * rest : (s + 1) * rest] for s in range(cols))
    unit_rows = jnp.concatenate([main_rows[:, qkv:], tail_rows], axis=1)
    return (
        rows_of(result_pieces),
        loss_value,
        rows_of(grad_pieces).astype(jnp.float32),
        both(attn_sum[0][:, : 3 * width], attn_sum[1][:, : 3 * width])[None],
        both(head_rows[0, :, 0].reshape(width), head_rows[1, :, 0].reshape(width)),
        both(head_rows[0, :, 2].reshape(width), head_rows[1, :, 2].reshape(width)),
        both(attn_sum[0][:, 3 * width : at].T, attn_sum[1][:, 3 * width : at].T, 0)[:, None],
        sums[4],
        sums[0],
        sums[1],
        sums[2],
        sums[3],
        both(up_of(0), up_of(1))[None],
        both(unit_rows[0], unit_rows[1]),
        both(down_of(0), down_of(1), 0)[:, None],
        sums[5],
    )


def one_image_a_chip(mesh, tokens):
    sizes = mesh.shape
    pairs = sizes["dp"] == 2 and sizes["row"] == 4 and sizes["col"] == 4
    return pairs and tokens == SEQ * sizes["row"] * sizes["col"]


def solution(mesh):
    placed = (
        P(("dp", "col"), "row"),
        P(("dp", "col"), "row"),
        P(("dp", "col")),
        P("row", "col"),
        P("col"),
        P("col"),
        P("col", "row"),
        P("row"),
        P("row"),
        P("row"),
        P("row"),
        P("row"),
        P("row", "col"),
        P("col"),
        P("col", "row"),
        P("row"),
    )
    returned = (
            P(("dp", "col"), "row"),
            P(),
            P(("dp", "col"), "row"),
            P("row", "dp", "col"),
            P("col"),
            P("col"),
            P("col", "row", "dp"),
            P("row"),
            P("row"),
            P("row"),
            P("row"),
            P("row"),
            P("row", "dp", "col"),
            P("col"),
            P("col", "row", "dp"),
            P("row"),
        )

    def whole(layer_input, *others):
        body = on_chip if one_image_a_chip(mesh, layer_input.shape[0]) else on_device
        return jax.shard_map(
            body, mesh=mesh, in_specs=placed, out_specs=returned, check_vma=False
        )(layer_input, *others)

    return whole
```

```python
import functools

import jax
import jax.numpy as jnp
import numpy as np
from jax import lax
from jax.experimental import pallas as pl
from jax.experimental.pallas import tpu as pltpu
from jax.sharding import PartitionSpec as P

D = 1152
H = 16
HD = 72
FF = 4304
SEQ = 729


EPS = 1e-06


def feature_totals(left, right):
    return lax.psum(
        (jnp.sum(left, axis=-1, keepdims=True), jnp.sum(right, axis=-1, keepdims=True)), "row"
    )


def norm_forward(values, gain, shift):
    first_sum, second_sum = feature_totals(values, values * values)
    mean_rows = first_sum / D
    var_rows = second_sum / D - mean_rows * mean_rows
    inv_scale = lax.rsqrt(var_rows + EPS)
    normed = (values - mean_rows) * inv_scale
    return (normed, inv_scale, normed * gain + shift)


def norm_backward(grad_out, normed, inv_scale, gain):
    grad_normed = grad_out * gain
    first_sum, second_sum = feature_totals(grad_normed, grad_normed * normed)
    return inv_scale * (grad_normed - first_sum / D - normed * second_sum / D)


def first_section(local_rows, weight):
    gathered = lax.all_gather(local_rows, "col", axis=0, tiled=True)
    share_rows = gathered.shape[0] // lax.axis_size("row")

    def partial_term(row_start, row_count):
        return jnp.dot(gathered, weight, preferred_element_type=jnp.float32)

    result = lax.psum_scatter(
        partial_term(jnp.int32(0), lax.axis_size("row") * share_rows),
        "row",
        scatter_dimension=0,
        tiled=True,
    )
    return (gathered, result)


def second_section(quarter_rows, weight):
    gathered = lax.all_gather(quarter_rows, "row", axis=0, tiled=True)
    share_rows = gathered.shape[0] // lax.axis_size("col")

    def partial_term(row_start, row_count):
        return jnp.dot(gathered, weight, preferred_element_type=jnp.float32)

    result = lax.psum_scatter(
        partial_term(jnp.int32(0), lax.axis_size("col") * share_rows),
        "col",
        scatter_dimension=0,
        tiled=True,
    )
    return (gathered, result)


def second_section_back(grad_local, gathered, weight):
    grad_all = lax.all_gather(grad_local, "col", axis=0, tiled=True)
    grad_weight = lax.dot_general(
        gathered, grad_all, (((0,), (0,)), ((), ())), preferred_element_type=jnp.float32
    )
    share_rows = grad_all.shape[0] // lax.axis_size("row")

    def partial_term(row_start, row_count):
        return lax.dot_general(
            grad_all, weight, (((1,), (1,)), ((), ())), preferred_element_type=jnp.float32
        )

    result = lax.psum_scatter(
        partial_term(jnp.int32(0), lax.axis_size("row") * share_rows),
        "row",
        scatter_dimension=0,
        tiled=True,
    )
    return (grad_weight, result)


def first_section_back(grad_quarter, gathered, weight):
    grad_all = lax.all_gather(grad_quarter, "row", axis=0, tiled=True)
    grad_weight = lax.dot_general(
        gathered, grad_all, (((0,), (0,)), ((), ())), preferred_element_type=jnp.float32
    )
    share_rows = grad_all.shape[0] // lax.axis_size("col")

    def partial_term(row_start, row_count):
        return lax.dot_general(
            grad_all, weight, (((1,), (1,)), ((), ())), preferred_element_type=jnp.float32
        )

    result = lax.psum_scatter(
        partial_term(jnp.int32(0), lax.axis_size("col") * share_rows).astype(jnp.bfloat16),
        "col",
        scatter_dimension=0,
        tiled=True,
    ).astype(jnp.float32)
    return (grad_weight, result)


def attend(triple_img):
    score_scale = HD ** (-0.5)
    query_rows = triple_img[:, :, 0]
    key_rows = triple_img[:, :, 1]
    value_rows = triple_img[:, :, 2]
    raw_scores = jnp.einsum(
        "qhd,khd->hqk", query_rows, key_rows, preferred_element_type=jnp.float32
    )
    scaled = raw_scores * score_scale
    peak_score = jnp.max(scaled, axis=-1, keepdims=True)
    exp_scores = jnp.exp(scaled - peak_score)
    exp_total = jnp.sum(exp_scores, axis=-1, keepdims=True)
    soft_weights = (exp_scores / exp_total).astype(jnp.bfloat16)
    mixed_rows = jnp.einsum(
        "hqk,khd->qhd", soft_weights, value_rows, preferred_element_type=jnp.float32
    )
    return (mixed_rows.astype(jnp.bfloat16), peak_score + jnp.log(exp_total))


def attend_back(packed):
    triple_img, log_total, grad_mixed = packed
    score_scale = HD ** (-0.5)
    query_rows = triple_img[:, :, 0]
    key_rows = triple_img[:, :, 1]
    value_rows = triple_img[:, :, 2]
    raw_scores = jnp.einsum(
        "qhd,khd->hqk", query_rows, key_rows, preferred_element_type=jnp.float32
    )
    soft_weights = jnp.exp(raw_scores * score_scale - log_total)
    weights_low = soft_weights.astype(jnp.bfloat16)
    grad_values = jnp.einsum(
        "hqk,qhd->khd", weights_low, grad_mixed, preferred_element_type=jnp.float32
    )
    grad_soft = jnp.einsum(
        "qhd,khd->hqk", grad_mixed, value_rows, preferred_element_type=jnp.float32
    )
    inner_prod = jnp.sum(grad_soft * soft_weights, axis=-1, keepdims=True)
    grad_raw = (score_scale * soft_weights * (grad_soft - inner_prod)).astype(jnp.bfloat16)
    grad_query = jnp.einsum("hqk,khd->qhd", grad_raw, key_rows, preferred_element_type=jnp.float32)
    grad_keys = jnp.einsum("hqk,qhd->khd", grad_raw, query_rows, preferred_element_type=jnp.float32)
    return jnp.stack([grad_query, grad_keys, grad_values], axis=2).astype(jnp.bfloat16)


def on_device(
    layer_input,
    teacher,
    valid,
    proj_in,
    bias_query,
    bias_value,
    proj_out,
    bias_out,
    norm1_gain,
    norm1_shift,
    norm2_gain,
    norm2_shift,
    w_up,
    bias_up,
    w_down,
    bias_down,
):
    heads_here = H // lax.axis_size("col")
    head_width = heads_here * HD
    feat_here = layer_input.shape[1]
    units_here = w_up.shape[1]
    gain_one = norm1_gain.astype(jnp.float32)
    gain_two = norm2_gain.astype(jnp.float32)
    residual_in = layer_input.astype(jnp.float32)
    normed1, scale1, mid_one = norm_forward(residual_in, gain_one, norm1_shift.astype(jnp.float32))
    norm1_all, projected = first_section(mid_one.astype(jnp.bfloat16), proj_in)
    quarter = projected.shape[0]
    images = quarter // SEQ
    bias_shift = jnp.stack(
        [
            bias_query.astype(jnp.float32).reshape(heads_here, HD),
            jnp.zeros((heads_here, HD), jnp.float32),
            bias_value.astype(jnp.float32).reshape(heads_here, HD),
        ],
        axis=1,
    )
    triple = (projected.reshape(quarter, heads_here, 3, HD) + bias_shift).astype(jnp.bfloat16)
    triple_imgs = triple.reshape(images, SEQ, heads_here, 3, HD)
    mixed_imgs, log_totals = lax.map(attend, triple_imgs)
    mixed_all, attn_part = second_section(mixed_imgs.reshape(quarter, head_width), proj_out)
    resid1 = residual_in + attn_part + bias_out.astype(jnp.float32)
    normed2, scale2, mid_two = norm_forward(resid1, gain_two, norm2_shift.astype(jnp.float32))
    norm2_all, pre_part = first_section(mid_two.astype(jnp.bfloat16), w_up)
    pre = pre_part + bias_up.astype(jnp.float32)
    activated, gelu_pull = jax.vjp(lambda entry: jax.nn.gelu(entry, approximate=True), pre)
    act_all, down_part = second_section(activated.astype(jnp.bfloat16), w_down)
    result = resid1 + down_part + bias_down.astype(jnp.float32)
    mask_rows = valid.astype(jnp.float32)
    error_rows = result - teacher.astype(jnp.float32)
    err_part = jnp.sum(mask_rows[:, None] * error_rows * error_rows)
    count_part = jnp.sum(mask_rows) / lax.axis_size("row")
    err_total, valid_count = lax.psum((err_part, count_part), ("dp", "row", "col"))
    loss_value = err_total / (valid_count * D)
    tokens_all = layer_input.shape[0] * lax.axis_size("dp") * lax.axis_size("col")
    factor = tokens_all / (2.0 * valid_count)
    grad_result = 2.0 * error_rows * (mask_rows[:, None] * factor)
    grad_branch2 = grad_result.astype(jnp.bfloat16)
    grad_w_down, grad_act = second_section_back(grad_branch2, act_all, w_down)
    grad_pre = gelu_pull(grad_act)[0].astype(jnp.bfloat16)
    grad_w_up, grad_norm2 = first_section_back(grad_pre, norm2_all, w_up)
    grad_resid1 = grad_result + norm_backward(grad_norm2, normed2, scale2, gain_two)
    grad_branch1 = grad_resid1.astype(jnp.bfloat16)
    grad_proj_out, grad_mixed = second_section_back(grad_branch1, mixed_all, proj_out)
    grad_mixed_imgs = grad_mixed.astype(jnp.bfloat16).reshape(images, SEQ, heads_here, HD)
    grad_triple = lax.map(attend_back, (triple_imgs, log_totals, grad_mixed_imgs))
    grad_triple = grad_triple.reshape(quarter, heads_here, 3, HD)
    grad_proj_in, grad_norm1 = first_section_back(
        grad_triple.reshape(quarter, 3 * head_width), norm1_all, proj_in
    )
    grad_input = grad_resid1 + norm_backward(grad_norm1, normed1, scale1, gain_one)
    row_at = lax.axis_index("row") * feat_here
    col_at = lax.axis_index("col") * head_width
    feature_terms = jnp.stack(
        [
            jnp.sum(grad_norm1 * normed1, axis=0),
            jnp.sum(grad_norm1, axis=0),
            jnp.sum(grad_norm2 * normed2, axis=0),
            jnp.sum(grad_norm2, axis=0),
            jnp.sum(grad_branch1.astype(jnp.float32), axis=0),
            jnp.sum(grad_branch2.astype(jnp.float32), axis=0),
        ]
    )
    feature_full = lax.dynamic_update_slice_in_dim(
        jnp.zeros((6, D), jnp.float32), feature_terms, row_at, 1
    )
    grad_float = grad_triple.astype(jnp.float32)
    head_terms = jnp.stack(
        [
            jnp.sum(grad_float[:, :, 0], axis=0).reshape(head_width),
            jnp.sum(grad_float[:, :, 2], axis=0).reshape(head_width),
        ]
    )
    head_full = lax.dynamic_update_slice_in_dim(
        jnp.zeros((2, H * HD), jnp.float32), head_terms, col_at, 1
    )
    unit_terms = jnp.sum(grad_pre.astype(jnp.float32), axis=0)
    unit_full = lax.dynamic_update_slice_in_dim(
        jnp.zeros((FF,), jnp.float32), unit_terms, lax.axis_index("col") * units_here, 0
    )
    feature_full, head_full, unit_full = lax.psum(
        (feature_full, head_full, unit_full), ("dp", "row", "col")
    )
    feature_mine = lax.dynamic_slice_in_dim(feature_full, row_at, feat_here, 1)
    head_mine = lax.dynamic_slice_in_dim(head_full, col_at, head_width, 1)
    unit_mine = lax.dynamic_slice_in_dim(
        unit_full, lax.axis_index("col") * units_here, units_here, 0
    )
    grad_proj_in, grad_w_up = (
        lax.psum_scatter(
            grad_proj_in.astype(jnp.bfloat16), "dp", scatter_dimension=0, tiled=True
        ).astype(jnp.float32),
        lax.psum_scatter(
            grad_w_up.astype(jnp.bfloat16), "dp", scatter_dimension=0, tiled=True
        ).astype(jnp.float32),
    )
    grad_proj_out, grad_w_down = (
        lax.psum_scatter(
            grad_proj_out.astype(jnp.bfloat16), "dp", scatter_dimension=1, tiled=True
        ).astype(jnp.float32),
        lax.psum_scatter(
            grad_w_down.astype(jnp.bfloat16), "dp", scatter_dimension=1, tiled=True
        ).astype(jnp.float32),
    )
    grad_proj_in = grad_proj_in.reshape(1, grad_proj_in.shape[0], grad_proj_in.shape[1])
    grad_w_up = grad_w_up.reshape(1, grad_w_up.shape[0], grad_w_up.shape[1])
    grad_proj_out = grad_proj_out.reshape(grad_proj_out.shape[0], 1, grad_proj_out.shape[1])
    grad_w_down = grad_w_down.reshape(grad_w_down.shape[0], 1, grad_w_down.shape[1])
    return (
        result.astype(jnp.bfloat16),
        loss_value,
        grad_input,
        grad_proj_in,
        head_mine[0],
        head_mine[1],
        grad_proj_out,
        feature_mine[4],
        feature_mine[0],
        feature_mine[1],
        feature_mine[2],
        feature_mine[3],
        grad_w_up,
        unit_mine,
        grad_w_down,
        feature_mine[5],
    )


MESH = pl.DeviceIdType.MESH
F32 = jnp.float32
BF16 = jnp.bfloat16
LOG2E = 1.4426950408889634
GELU_ROOT = 0.7978845608028654


def place():
    return lax.axis_index("dp"), lax.axis_index("row"), lax.axis_index("col")


def flip(row, other):
    return lax.rem(row // 2 + other // 2, 2) * 2 + lax.rem(row + other, 2)


def neighbours():
    dp, row, col = place()
    return dict(
        core=(1 - dp, row, col),
        x=(dp, flip(row, 1), col),
        y=(dp, flip(row, 2), col),
        diagonal=(dp, flip(row, 3), col),
        next=(dp, row, lax.rem(2 * col + 3 * (col // 2) + 1, 4)),
        prev=(dp, row, lax.rem(2 * col + col // 2 + 2, 4)),
    )


def images_group():
    dp, row, col = place()
    steps = [(core, step) for core in (0, 1) for step in range(4)][1:]
    return [(lax.rem(dp + core, 2), row, lax.rem(col + step, 4)) for core, step in steps]


def meet():
    dp, row, col = place()
    plane = [(core, k) for core in (0, 1) for k in range(4)][1:]
    peers = [(lax.rem(dp + core, 2), flip(row, k), col) for core, k in plane]
    peers += [peer for i, peer in enumerate(images_group()) if i != 3]
    barrier = pltpu.get_barrier_semaphore()
    for peer in peers:
        pl.semaphore_signal(barrier, inc=1, device_id=peer, device_id_type=MESH)
    pl.semaphore_wait(barrier, len(peers))


class Shuffle:
    def __init__(self, send_sems, recv_sems, local_sem):
        self.sems = send_sems, recv_sems, local_sem
        self.pending = []

    def remote(self, source, target, i, slot, peer):
        return pltpu.make_async_remote_copy(
            source, target, self.sems[0].at[i], self.sems[1].at[slot],
            device_id=peer, device_id_type=MESH,
        )

    def spread(self, pieces, blocks):
        dp, row, col = place()
        feat, own = pieces.shape[1], blocks.shape[1]
        for image in (0, 1):
            for half in (0, 1):
                chip = 2 * dp + image
                slot = flip(chip, row)
                mine = (dp == half) & (chip == row)
                source = pieces.at[image, :, pl.ds(half * own, own)]
                target = blocks.at[pl.ds(pl.multiple_of(slot * feat, 16), feat)]
                copy = self.remote(source, target, 2 * image + half, slot, (half, chip, col))
                here = pltpu.make_async_copy(source, blocks.at[pl.ds(0, feat)], self.sems[2])
                self.start(copy, here, mine)
        mine = dp == row // 2
        self.into = [
            (blocks.at[pl.ds(k * feat, feat)], k, None if k else mine) for k in range(4)
        ]

    def collect(self, blocks, pieces):
        dp, row, col = place()
        feat, own = pieces.shape[1], blocks.shape[1]
        image = lax.rem(row, 2)
        for k in range(4):
            owner = flip(row, k)
            mine = (dp == row // 2) & (owner == row)
            source = blocks.at[pl.ds(k * feat, feat)]
            target = pieces.at[image, :, pl.ds(pl.multiple_of(dp * own, 128), own)]
            copy = self.remote(source, target, k, 2 * image + dp, (row // 2, owner, col))
            here = pltpu.make_async_copy(source, target, self.sems[2])
            self.start(copy, here, mine)
        self.into = []
        for image in (0, 1):
            for half in (0, 1):
                mine = (dp == half) & (2 * dp + image == row)
                target = pieces.at[image, :, pl.ds(half * own, own)]
                self.into.append((target, 2 * image + half, mine))

    def start(self, copy, here, mine):
        pl.when(jnp.logical_not(mine))(copy.start)
        pl.when(mine)(here.start)
        self.pending.append((copy, here, mine))

    def arrive(self):
        dp, row, col = place()
        here = self.pending[0][1]
        for target, slot, own in self.into:
            copy = self.remote(target, target, 0, slot, (1 - dp, row, col))
            if own is None:
                copy.wait_recv()
            else:
                pl.when(jnp.logical_not(own))(copy.wait_recv)
                pl.when(own)(here.wait)

    def finish(self):
        for copy, _, mine in self.pending:
            pl.when(jnp.logical_not(mine))(copy.wait_send)


def mm(left, right):
    return jnp.dot(left, right, preferred_element_type=F32)


def mm_nt(left, right):
    return lax.dot_general(left, right, (((1,), (1,)), ((), ())), preferred_element_type=F32)


def each_rows(count, size, body):
    @pl.loop(0, count // size)
    def _(step):
        body(pl.ds(pl.multiple_of(step * size, size), size))


def fold(values):
    return sum(values[i : i + 16] for i in range(0, values.shape[0], 16))


def spread_lanes(source, spread, width):
    blocks = []
    for j in range(width // 256):
        low = 2 * HD * j // 128 * 128
        blocks.append(mm(source[:, low : low + 256], spread[low : low + 256, 256 * j : 256 * j + 256]))
    return jnp.concatenate(blocks, axis=1)


def transpose_into(target, source):
    @pl.loop(0, source.shape[1] // 128)
    def _(step):
        at = pl.ds(pl.multiple_of(step * 128, 128), 128)
        target[at, :] = source[:, at].T


class Sender:
    def __init__(self, send_sems, recv_sems):
        self.sems = (send_sems, recv_sems)
        self.count = 0
        self.copies = []

    def __call__(self, source, target, peer):
        copy = pltpu.make_async_remote_copy(
            source,
            target,
            self.sems[0].at[self.count],
            self.sems[1].at[self.count],
            device_id=peer,
            device_id_type=MESH,
        )
        self.count += 1
        copy.start()
        self.copies.append(copy)
        return copy

    def finish(self):
        for copy in self.copies:
            copy.wait_send()


class Copier:
    def __init__(self, sems):
        self.sems = sems
        self.count = 0

    def __call__(self, source, target):
        copy = pltpu.make_async_copy(source, target, self.sems.at[self.count])
        self.count += 1
        copy.start()
        return copy


def norm_stats(values):
    mean_rows = jnp.mean(values, axis=-1, keepdims=True)
    centered = values - mean_rows
    inv_scale = lax.rsqrt(jnp.mean(centered * centered, axis=-1, keepdims=True) + EPS)
    return centered * inv_scale, inv_scale


def forward_kernel(
    own_tokens,
    x_pieces,
    teacher_pieces,
    count_ref,
    valid_ref,
    params_ref,
    key_ref,
    key_lane_ref,
    spread_ref,
    rest_spread_ref,
    attn_ref,
    ff_ref,
    wpad_out,
    wff_out,
    triple_out,
    mixed_out,
    act_out,
    slope_out,
    norm1t_out,
    norm2t_out,
    rest_hbm,
    lse_hbm,
    act_rest_hbm,
    slope_rest_hbm,
    resid_hbm,
    x_hbm,
    branch_out,
    brancht_out,
    result_out,
    err_out,
    feature_ref,
    count_out,
    rest_out,
    lse_out,
    act_rest_out,
    slope_rest_out,
    resid_out,
    x_rows,
    x_blocks,
    teacher_blocks,
    valid_in,
    features_in,
    biases_in,
    counts_in,
    wattn,
    wff,
    wpad,
    triple,
    mixed,
    act,
    slope,
    norm1,
    norm2,
    turned,
    part,
    give1,
    got1,
    give2,
    got2,
    local_sems,
    send_sems,
    recv_sems,
    shuffle_sems,
):
    peers = neighbours()
    meet()
    feat = attn_ref.shape[0]
    half = feat // 2
    depth = 4 * feat
    tokens = norm1.shape[0]
    own = tokens // 2
    main = ff_ref.shape[1] // 2
    qkv = triple.shape[2]
    wide = features_in.shape[2]
    pitch = wide // 6
    send = Sender(send_sems, recv_sems)
    keep = Copier(local_sems)

    def rows(block, low=0, size=None):
        return pl.ds(block * feat + low, feat if size is None else size)

    own_attn = keep(attn_ref, wattn.at[0, rows(0)])
    own_ff = keep(ff_ref, wff.at[0, rows(0)])
    az, ax, ay, a_low, a_high = ([None] * 4 for _ in range(5))

    def attn_source(s):
        return attn_ref if s == 0 else wattn.at[s, rows(0)]

    def attn_ring(s):
        az[s + 1] = send(attn_source(s), wattn.at[s + 1, rows(0)], peers["next"])

    def attn_plane(s):
        ax[s] = send(attn_source(s), wattn.at[s, rows(1)], peers["x"])
        ay[s] = send(attn_source(s), wattn.at[s, rows(2)], peers["y"])

    def attn_last(s):
        ax[s].wait_recv()
        a_low[s] = send(
            wattn.at[s, rows(1, 0, half)], wattn.at[s, rows(3, 0, half)], peers["y"]
        )
        ay[s].wait_recv()
        a_high[s] = send(
            wattn.at[s, rows(2, half, half)], wattn.at[s, rows(3, half, half)], peers["x"]
        )

    fz, fy, fx = ([None] * 4 for _ in range(3))

    def ff_first():
        return (
            send(ff_ref.at[pl.ds(0, half)], wff.at[0, rows(1, 0, half)], peers["x"]),
            send(ff_ref.at[pl.ds(half, half)], wff.at[0, rows(2, half, half)], peers["y"]),
        )

    def ff_ring(s):
        fz[s + 1] = [
            send(wff.at[s, piece], wff.at[s + 1, piece], peers["next"])
            for piece in (rows(0), rows(1, 0, half), rows(2, half, half))
        ]

    def ff_last(s):
        fy[s] = [
            send(wff.at[s, rows(k, 0, half)], wff.at[s, rows(k + 2, 0, half)], peers["y"])
            for k in (0, 1)
        ]
        fx[s] = [
            send(wff.at[s, rows(k, half, half)], wff.at[s, rows(k + 1, half, half)], peers["x"])
            for k in (0, 2)
        ]

    def arrive(copies):
        for copy in copies:
            copy.wait_recv()

    def attn_compute(s):
        arrive([a_low[s], a_high[s]])
        slot = s % 2
        if s == 0:
            own_attn.wait()
        if s >= 2:
            for copy in saved[s - 2]:
                copy.wait()

        def unpack(at):
            block = wattn[s, at, :]
            wpad[slot, at, :] = spread_lanes(block, spread_ref, wpad.shape[2]).astype(BF16)
            extra = mm(block[:, block.shape[1] - 128 :], rest_spread_ref[s]).astype(BF16)
            if s == 0:
                rest_out[at, :] = extra
            else:
                rest_out[at, :] = rest_out[at, :] + extra

        each_rows(depth, feat, unpack)

        def project(at):
            values = mm(norm1[at, :], wpad[slot, :, :qkv]) + biases_in[s, 0:1, :qkv]
            values = values + key_ref[at, :] * key_lane_ref[...]
            triple[slot, at, :] = values.astype(BF16)

        each_rows(tokens, tokens, project)
        scale = LOG2E * HD**-0.5
        for h in range(qkv // 384):
            query_at, key_at, value_at = (pl.ds((3 * h + j) * 128, 128) for j in range(3))
            value_turned = triple[slot, :, value_at].T

            def head(at, h=h, query_at=query_at, key_at=key_at, value_turned=value_turned):
                scores = mm_nt(triple[slot, :, key_at], triple[slot, at, query_at])
                peak = jnp.max(scores, axis=0, keepdims=True)
                weights = jnp.exp2((scores - peak) * scale)
                total = jnp.sum(weights, axis=0, keepdims=True)
                lse_out[2 * s + h, :, at] = peak * scale + jnp.log2(total)
                values = mm(value_turned, weights.astype(BF16)) / total
                mixed[s, at, pl.ds(h * 128, 128)] = values.T.astype(BF16)

            each_rows(tokens, own, head)

        def out(at):
            values = mm_nt(mixed[s, at, :], wpad[slot, :, qkv:])
            return values if s == 0 else part[at, :] + values

        swap = None
        if s < 3:
            part[...] = out(pl.ds(0, tokens))
        else:
            give1[...] = out(pl.ds(own, own)).astype(BF16)
            swap = send(give1, got1, peers["core"])
            part[pl.ds(0, own), :] = out(pl.ds(0, own))
        saved.append(
            [
                keep(wpad.at[slot], wpad_out.at[s]),
                keep(triple.at[slot], triple_out.at[s]),
                keep(mixed.at[s], mixed_out.at[s]),
            ]
        )
        return swap

    def gelu(pre):
        inner = GELU_ROOT * (pre + 0.044715 * pre * pre * pre)
        tanh = jnp.tanh(inner)
        rise = 0.5 * (1.0 + tanh)
        bend = 0.5 * pre * (1.0 - tanh * tanh) * (GELU_ROOT * (1.0 + 0.134145 * pre * pre))
        return (pre * rise).astype(BF16), (rise + bend).astype(BF16)

    def ff_compute(s):
        arrive(fy[s] + fx[s])

        def block(at):
            pre = mm(norm2[at, :], wff[s, :, :main]) + biases_in[s, 0:1, qkv : qkv + main]
            low, bent = gelu(pre)
            act[s, at, :] = low
            slope[s, at, :] = bent
            return part[at, :] + mm_nt(low, wff[s, :, main:])

        swap = None
        if s < 3:
            part[...] = block(pl.ds(0, tokens))
        else:
            give2[...] = block(pl.ds(own, own)).astype(BF16)
            swap = send(give2, got2, peers["core"])
            part[pl.ds(0, own), :] = block(pl.ds(0, own))
        ff_saved.extend(
            [
                keep(act.at[s], act_out.at[s]),
                keep(slope.at[s], slope_out.at[s]),
                keep(wff.at[s], wff_out.at[s]),
            ]
        )
        return swap

    def rest_compute():
        bias = mm(biases_in[0, :, qkv + main :].astype(BF16), rest_spread_ref[0, :, :128])
        for s in (1, 2, 3):
            values = biases_in[s, :, qkv + main :].astype(BF16)
            bias = bias + mm(values, rest_spread_ref[s, :, :128])

        def block(at):
            pre = mm(norm2[at, :], rest_out[:, :128]) + bias[0:1]
            low, bent = gelu(pre)
            act_rest_out[at, :] = low
            slope_rest_out[at, :] = bent
            part[at, :] = mm_nt(low, rest_out[:, 128:])

        each_rows(tokens, tokens, block)

    saved, ff_saved = [], []
    x_move = Shuffle(shuffle_sems.at[0], shuffle_sems.at[1], shuffle_sems.at[2, 0])
    x_move.spread(x_pieces, x_blocks)
    attn_ring(0)
    first = ff_first()
    attn_plane(0)
    own_params = [
        keep(params_ref.at[:, pl.ds(0, wide)], features_in.at[0]),
        keep(params_ref.at[:, pl.ds(wide, biases_in.shape[2])], biases_in.at[0]),
        keep(count_ref, counts_in.at[0]),
    ]
    smalls = [
        send(params_ref.at[:, pl.ds(0, wide)], features_in.at[k], peers[name])
        for k, name in ((1, "x"), (2, "y"), (3, "diagonal"))
    ]
    dp, row, col = place()
    ring_two = (dp, row, 3 - col)
    smalls += [
        send(params_ref.at[:, pl.ds(wide, biases_in.shape[2])], biases_in.at[s], peer)
        for s, peer in ((1, peers["next"]), (2, ring_two), (3, peers["prev"]))
    ]
    counts = [
        send(count_ref, counts_in.at[1 + i], peer) for i, peer in enumerate(images_group())
    ]
    teacher_move = Shuffle(shuffle_sems.at[3], shuffle_sems.at[4], shuffle_sems.at[2, 1])

    valid_move = send(valid_ref, valid_in, peers["core"])

    az[1].wait_recv()
    attn_ring(1)
    attn_plane(1)
    attn_last(0)
    az[2].wait_recv()
    attn_ring(2)
    attn_plane(2)
    for copy in own_params:
        copy.wait()
    arrive(smalls)
    feature_ref[...] = jnp.zeros_like(feature_ref)
    for i in range(6):
        feature_ref[i : i + 1, :] = jnp.concatenate(
            [features_in[k, 0:1, pitch * i : pitch * i + feat] for k in range(4)], axis=1
        )
    x_move.arrive()
    for start in range(0, own, 128):
        x_rows[pl.ds(start, 128), :] = x_blocks[:, pl.ds(start, 128)].T
    late = [keep(x_rows, x_hbm)]

    def first_norm(at):
        normed, _ = norm_stats(x_rows[at, :].astype(F32))
        norm1[at, :] = (normed * feature_ref[0:1] + feature_ref[1:2]).astype(BF16)

    each_rows(own, 128, first_norm)
    swap1 = send(norm1.at[pl.ds(0, own)], norm1.at[pl.ds(own, own)], peers["core"])
    az[3].wait_recv()
    attn_plane(3)
    own_ff.wait()
    arrive(first)
    ff_ring(0)
    attn_last(1)
    swap1.wait_recv()
    attn_compute(0)
    attn_last(2)
    attn_compute(1)
    attn_last(3)
    ff_last(0)
    arrive(fz[1])
    ff_ring(1)
    ff_last(1)
    teacher_move.spread(teacher_pieces, teacher_blocks)
    attn_compute(2)
    swap2 = attn_compute(3)
    swap2.wait_recv()

    def second_norm(at):
        values = x_rows[at, :].astype(F32) + part[at, :] + got1[at, :].astype(F32) + feature_ref[4:5]
        resid_out[at, :] = values
        normed, _ = norm_stats(values)
        norm2[at, :] = (normed * feature_ref[2:3] + feature_ref[3:4]).astype(BF16)

    each_rows(own, 128, second_norm)
    late += [keep(resid_out, resid_hbm), keep(rest_out, rest_hbm), keep(lse_out, lse_hbm)]
    swap3 = send(norm2.at[pl.ds(0, own)], norm2.at[pl.ds(own, own)], peers["core"])
    arrive(fz[2])
    ff_ring(2)
    ff_last(2)
    transpose_into(turned, norm1)
    turn1 = keep(turned, norm1t_out)
    swap3.wait_recv()
    rest_compute()
    late += [keep(act_rest_out, act_rest_hbm), keep(slope_rest_out, slope_rest_hbm)]
    turn1.wait()
    transpose_into(turned, norm2)
    turn2 = keep(turned, norm2t_out)
    ff_compute(0)
    arrive(fz[3])
    ff_last(3)
    ff_compute(1)
    ff_compute(2)
    swap4 = ff_compute(3)
    err_out[...] = jnp.zeros_like(err_out)
    arrive(counts)
    count = counts_in[0]
    for i in range(1, 8):
        count = count + counts_in[i]
    count_out[...] = count
    factor = (own_tokens * 8.0) / count[0:1, 0:1]
    teacher_move.arrive()
    swap4.wait_recv()

    valid_move.wait_recv()
    image, from_here = lax.rem(row, 2), dp == row // 2

    def finish(start):
        at = pl.ds(start, 128)
        values = resid_out[at, :] + part[at, :] + got2[at, :].astype(F32) + feature_ref[5:6]
        result_out[:, at] = values.astype(BF16).T
        error = values - teacher_blocks[:, at].T.astype(F32)
        lanes_at = pl.ds(pl.multiple_of(dp * own + start, 128), 128)
        counts_row = jnp.where(
            from_here, valid_ref[image, :, lanes_at], valid_in[image, :, lanes_at]
        )
        masked = error * counts_row.T[:, 0:1]
        err_out[...] = err_out[...] + fold(error * masked)
        branch_out[at, :] = (masked * factor).astype(BF16)

    def turn(start):
        brancht_out[:, pl.ds(start, 128)] = branch_out[pl.ds(start, 128), :].T

    swaps = []
    for start in range(0, own, 128):
        finish(start)
        swaps.append(
            send(
                branch_out.at[pl.ds(start, 128)],
                branch_out.at[pl.ds(own + start, 128)],
                peers["core"],
            )
        )
        turn(start)
    for start, swap in zip(range(own, tokens, 128), swaps):
        swap.wait_recv()
        turn(start)
    turn2.wait()
    for copies in saved[2:]:
        for copy in copies:
            copy.wait()
    for copy in ff_saved:
        copy.wait()
    for copy in late:
        copy.wait()
    send.finish()
    x_move.finish()
    teacher_move.finish()


def forward_call(arrays, own_tokens, feat, lanes, main, qkv, mix, own, depth):
    tokens = 2 * own
    wide, narrow = 6 * ((feat + 127) // 128 * 128), qkv + main + 128
    anywhere = pl.BlockSpec(memory_space=pl.ANY)
    local = pl.BlockSpec(memory_space=pltpu.VMEM)
    shapes = [
        ((4, depth, qkv + mix), BF16, anywhere),
        ((4, depth, 2 * main), BF16, anywhere),
        ((4, tokens, qkv), BF16, anywhere),
        ((4, tokens, mix), BF16, anywhere),
        ((4, tokens, main), BF16, anywhere),
        ((4, tokens, main), BF16, anywhere),
        ((depth, tokens), BF16, anywhere),
        ((depth, tokens), BF16, anywhere),
        ((depth, 256), BF16, anywhere),
        ((8, 1, tokens), F32, anywhere),
        ((tokens, 128), BF16, anywhere),
        ((tokens, 128), BF16, anywhere),
        ((own, depth), F32, anywhere),
        ((own, depth), BF16, anywhere),
        ((tokens, depth), BF16, local),
        ((depth, tokens), BF16, local),
        ((depth, own), BF16, local),
        ((16, depth), F32, local),
        ((8, depth), F32, local),
        ((8, 128), F32, local),
    ]
    return pl.pallas_call(
        functools.partial(forward_kernel, own_tokens),
        out_shape=[jax.ShapeDtypeStruct(shape, dtype) for shape, dtype, _ in shapes],
        in_specs=[anywhere] * 2 + [local] * 7 + [anywhere] * 2,
        out_specs=[spec for _, _, spec in shapes],
        scratch_shapes=[
            pltpu.VMEM((depth, 256), BF16),
            pltpu.VMEM((8, 1, tokens), F32),
            pltpu.VMEM((tokens, 128), BF16),
            pltpu.VMEM((tokens, 128), BF16),
            pltpu.VMEM((own, depth), F32),
            pltpu.VMEM((own, depth), BF16),
            pltpu.VMEM((depth, own), BF16),
            pltpu.VMEM((depth, own), BF16),
            pltpu.VMEM((2, 8, tokens), F32),
            pltpu.VMEM((4, 8, wide), F32),
            pltpu.VMEM((4, 8, narrow), F32),
            pltpu.VMEM((8, 8, 128), F32),
            pltpu.VMEM((4, depth, lanes), BF16),
            pltpu.VMEM((4, depth, 2 * main), BF16),
            pltpu.VMEM((2, depth, qkv + mix), BF16),
            pltpu.VMEM((2, tokens, qkv), BF16),
            pltpu.VMEM((4, tokens, mix), BF16),
            pltpu.VMEM((4, tokens, main), BF16),
            pltpu.VMEM((4, tokens, main), BF16),
            pltpu.VMEM((tokens, depth), BF16),
            pltpu.VMEM((tokens, depth), BF16),
            pltpu.VMEM((depth, tokens), BF16),
            pltpu.VMEM((tokens, depth), F32),
            pltpu.VMEM((own, depth), BF16),
            pltpu.VMEM((own, depth), BF16),
            pltpu.VMEM((own, depth), BF16),
            pltpu.VMEM((own, depth), BF16),
            pltpu.SemaphoreType.DMA((40,)),
            pltpu.SemaphoreType.DMA((72,)),
            pltpu.SemaphoreType.DMA((72,)),
            pltpu.SemaphoreType.DMA((5, 4)),
        ],
        compiler_params=pltpu.CompilerParams(
            collective_id=1, has_side_effects=True, vmem_limit_bytes=62 << 20
        ),
    )(*arrays)


def backward_kernel(
    branch2_ref,
    rest_ref,
    act_rest_ref,
    slope_rest_ref,
    lse_ref,
    feature_ref,
    spread_ref,
    rest_spread_ref,
    err_ref,
    result_blocks,
    x_hbm,
    resid_hbm,
    norm1t_hbm,
    norm2t_hbm,
    branch2t_hbm,
    wpad_hbm,
    wff_hbm,
    triple_hbm,
    mixed_hbm,
    act_hbm,
    slope_hbm,
    grad_pieces,
    result_pieces,
    sums_out,
    bias_out,
    attn_out,
    ff_out,
    x_rows,
    grad_blocks,
    terms,
    terms_mine,
    terms_in,
    sums_in,
    bias_mine,
    bias_turn,
    bias_in,
    bias_plane,
    units_out,
    units_rest_out,
    heads_out,
    gattn,
    gff,
    wslot,
    kept,
    grad_pre,
    grad_rest,
    normt,
    brancht,
    branch1,
    part,
    give,
    got,
    grad_mid,
    dtriple,
    grad_mixed,
    grad_key,
    grad_value,
    inner_row,
    ra,
    rb,
    r1,
    r2,
    rz,
    ry,
    rx,
    rzl,
    rzh,
    rfx,
    rfy,
    local_sems,
    send_sems,
    recv_sems,
    shuffle_sems,
):
    peers = neighbours()
    feat = 2 * attn_out.shape[1]
    half = feat // 2
    depth = 4 * feat
    tokens = branch2_ref.shape[0]
    own = tokens // 2
    main = gff.shape[2] // 2
    qkv = triple_hbm.shape[2]
    send = Sender(send_sems, recv_sems)
    keep = Copier(local_sems)

    def rows(block, low=0, size=None):
        return pl.ds(block * feat + low, feat if size is None else size)

    def load_ff(s):
        slot = s % 2
        return [
            keep(wff_hbm.at[s], wslot.at[slot]),
            keep(act_hbm.at[s], kept.at[slot, :, pl.ds(0, main)]),
            keep(slope_hbm.at[s], kept.at[slot, :, pl.ds(main, main)]),
        ]

    def load_attn(s):
        slot = s % 2
        return [
            keep(wpad_hbm.at[s], wslot.at[slot]),
            keep(triple_hbm.at[s], kept.at[slot, :, pl.ds(0, qkv)]),
            keep(mixed_hbm.at[s], kept.at[slot, :, pl.ds(qkv, grad_mixed.shape[1])]),
        ]

    loads = {3: load_ff(3)}
    turns = [keep(norm2t_hbm, normt), keep(branch2t_hbm, brancht)]
    loads[2] = load_ff(2)
    load_late = [keep(resid_hbm, grad_mid), keep(x_hbm, x_rows)]
    meet()
    result_move = Shuffle(shuffle_sems.at[0], shuffle_sems.at[1], shuffle_sems.at[2, 0])
    grad_move = Shuffle(shuffle_sems.at[3], shuffle_sems.at[4], shuffle_sems.at[2, 1])
    cy, cx, zl, zh = ([None] * 4 for _ in range(4))
    ca, cb, c1, c2, cz = ([None] * 4 for _ in range(5))

    def add_into(target, at, *sources):
        size = at.size

        @pl.loop(0, size // 16)
        def _(step):
            here = pl.ds(pl.multiple_of(at.start + step * 16, 16), 16)
            there = pl.ds(pl.multiple_of(step * 16, 16), 16)
            total = target[here, :].astype(F32)
            for source in sources:
                total = total + source[there, :].astype(F32)
            target[here, :] = total.astype(BF16)

    def column_sum(values):
        return jnp.sum(values.astype(F32), axis=0, keepdims=True)

    def ff_compute(s):
        slot = s % 2
        for copy in loads[s]:
            copy.wait()
        units_out[s] = jnp.zeros((1, main), F32)

        def block(at):
            grad = mm(branch2_ref[at, :], wslot[slot, :, main : 2 * main])
            low = (grad * kept[slot, at, main:].astype(F32)).astype(BF16)
            grad_pre[at, :] = low
            units_out[s] = units_out[s] + column_sum(low)
            values = mm_nt(low, wslot[slot, :, :main])
            part[at, :] = values if s == 3 else part[at, :] + values

        each_rows(tokens, own, block)
        if s == 3:
            for copy in turns:
                copy.wait()

        def grads(at):
            gff[s, at, :main] = mm(normt[at, :], grad_pre[...]).astype(BF16)
            gff[s, at, main:] = mm(brancht[at, :], kept[slot, :, :main]).astype(BF16)

        each_rows(depth, 2 * feat, grads)
        cy[s] = [
            send(gff.at[s, rows(k, 0, half)], ry.at[s, k - 2], peers["y"]) for k in (2, 3)
        ]
        cx[s] = [
            send(gff.at[s, rows(k, half, half)], rx.at[s, k // 2], peers["x"]) for k in (1, 3)
        ]
        if s >= 2:
            loads[s - 2] = load_ff(s - 2)

    def rest_compute():
        units_rest_out[...] = jnp.zeros_like(units_rest_out)

        def block(at):
            grad = mm(branch2_ref[at, :], rest_ref[:, 128:])
            low = (grad * slope_rest_ref[at, :].astype(F32)).astype(BF16)
            grad_pre[at, :128] = low
            units_rest_out[...] = units_rest_out[...] + column_sum(low)
            return part[at, :] + mm_nt(low, rest_ref[:, :128])

        give[...] = block(pl.ds(own, own)).astype(BF16)
        swap = send(give, got, peers["core"])
        part[pl.ds(0, own), :] = block(pl.ds(0, own))

        def grads(at):
            grad_rest[at, :128] = mm(normt[at, :], grad_pre[:, :128]).astype(BF16)
            grad_rest[at, 128:] = mm(brancht[at, :], act_rest_ref[...]).astype(BF16)

        each_rows(depth, 2 * feat, grads)
        return swap

    def ff_add(s):
        for copy in cy[s] + cx[s]:
            copy.wait_recv()
        last = s == 3
        if not last:
            for copy in zl[s] + zh[s]:
                copy.wait_recv()
        lows, highs = [], []
        for i, k in enumerate((0, 1)):
            piece = rows(k, 0, half)
            add_into(gff.at[s], piece, ry.at[s, i], *([] if last else [rzl.at[s, i]]))
            lows.append((piece, i))
        for i, k in enumerate((0, 2)):
            piece = rows(k, half, half)
            add_into(gff.at[s], piece, rx.at[s, i], *([] if last else [rzh.at[s, i]]))
            highs.append((piece, i))
        if s:
            zl[s - 1] = [
                send(gff.at[s, piece], rzl.at[s - 1, i], peers["prev"]) for piece, i in lows
            ]
            zh[s - 1] = [
                send(gff.at[s, piece], rzh.at[s - 1, i], peers["prev"]) for piece, i in highs
            ]

    def attn_compute(s):
        slot = s % 2
        for copy in attn_loads[s]:
            copy.wait()

        def back_out(at):
            grad_mixed[at, :] = mm(branch1[at, :], wslot[slot, :, qkv:]).astype(BF16)

        each_rows(tokens, tokens, back_out)
        scale = HD**-0.5
        for h in range(qkv // 384):
            query_at, key_at, value_at = (pl.ds((3 * h + j) * 128, 128) for j in range(3))
            mix_at = pl.ds(h * 128, 128)
            value_of_mix = pl.ds(qkv + h * 128, 128)
            key_turned = kept[slot, :, key_at].T
            product = grad_mixed[:, mix_at].astype(F32) * kept[slot, :, value_of_mix].astype(F32)
            inner_row[...] = jnp.sum(product.T, axis=0, keepdims=True)
            grad_key[...] = jnp.zeros_like(grad_key)
            grad_value[...] = jnp.zeros_like(grad_value)

            def head(at, h=h, query_at=query_at, key_at=key_at, value_at=value_at,
                     mix_at=mix_at, key_turned=key_turned):
                query = kept[slot, at, query_at]
                grad = grad_mixed[at, mix_at]
                scores = mm_nt(kept[slot, :, key_at], query)
                weights = jnp.exp2(scores * (scale * LOG2E) - lse_ref[2 * s + h, :, at])
                grad_soft = mm_nt(kept[slot, :, value_at], grad)
                grad_raw = (weights * (grad_soft - inner_row[:, at]) * scale).astype(BF16)
                grad_value[...] += mm(weights.astype(BF16), grad)
                grad_key[...] += mm(grad_raw, query)
                dtriple[at, query_at] = mm(key_turned, grad_raw).T.astype(BF16)

            each_rows(tokens, own, head)
            dtriple[:, key_at] = grad_key[...].astype(BF16)
            dtriple[:, value_at] = grad_value[...].astype(BF16)
        heads_out[s] = jnp.zeros((1, qkv), F32)

        def back_in(at):
            values = mm_nt(dtriple[at, :], wslot[slot, :, :qkv])
            heads_out[s] = heads_out[s] + column_sum(dtriple[at, :])
            return values if s == 3 else part[at, :] + values

        swap = None
        if s:
            for at in (pl.ds(0, own), pl.ds(own, own)):
                part[at, :] = back_in(at)
        else:
            give[...] = back_in(pl.ds(own, own)).astype(BF16)
            swap = send(give, got, peers["core"])
            part[pl.ds(0, own), :] = back_in(pl.ds(0, own))

        def grads(at):
            first = mm(normt[at, :], dtriple[...]).astype(BF16)
            second = mm(brancht[at, :], kept[slot, :, qkv:]).astype(BF16)
            tiles = [0.0] * (gattn.shape[2] // 128)
            for j in range((qkv + second.shape[1]) // 256):
                low, to = 2 * HD * j // 128 * 128, 256 * j
                block = first[:, to : to + 256] if to < qkv else second[:, to - qkv : to - qkv + 256]
                moved = mm_nt(block, spread_ref[low : low + 256, to : to + 256])
                for i in (0, 1):
                    tiles[low // 128 + i] += moved[:, 128 * i : 128 * i + 128]
            tiles[-1] += mm_nt(grad_rest[at, :], rest_spread_ref[s])
            gattn[s, at, :] = jnp.concatenate(tiles, axis=1).astype(BF16)

        each_rows(depth, 2 * feat, grads)
        ca[s] = send(gattn.at[s, rows(3, 0, half)], ra.at[s], peers["y"])
        cb[s] = send(gattn.at[s, rows(3, half, half)], rb.at[s], peers["x"])
        if s >= 2:
            attn_loads[s - 2] = load_attn(s - 2)
        return swap

    def attn_plane(s):
        ca[s].wait_recv()
        add_into(gattn.at[s], rows(1, 0, half), ra.at[s])
        c1[s] = send(gattn.at[s, rows(1)], r1.at[s], peers["x"])
        cb[s].wait_recv()
        add_into(gattn.at[s], rows(2, half, half), rb.at[s])
        c2[s] = send(gattn.at[s, rows(2)], r2.at[s], peers["y"])

    def attn_ring(s):
        c1[s].wait_recv()
        c2[s].wait_recv()
        if s < 3:
            cz[s].wait_recv()
        add_into(gattn.at[s], rows(0), r1.at[s], r2.at[s], *([rz.at[s]] if s < 3 else []))
        if s:
            cz[s - 1] = send(gattn.at[s, rows(0)], rz.at[s - 1], peers["prev"])

    terms[...] = jnp.zeros_like(terms)

    def add_term(index, values):
        terms[index] = terms[index] + fold(values)

    result_move.collect(result_blocks, result_pieces)
    ff_compute(3)
    ff_compute(2)
    ff_compute(1)
    ff_add(3)
    ff_compute(0)
    attn_loads = {3: load_attn(3), 2: load_attn(2)}
    swap1 = rest_compute()
    load_norm = keep(norm1t_hbm, normt)
    swap1.wait_recv()
    for copy in load_late:
        copy.wait()

    def mid(at):
        normed, inv_scale = norm_stats(grad_mid[at, :])
        grad_norm = part[at, :] + got[at, :].astype(F32)
        add_term(2, grad_norm * normed)
        add_term(3, grad_norm)
        scaled = grad_norm * feature_ref[2:3]
        first = jnp.mean(scaled, axis=-1, keepdims=True)
        second = jnp.mean(scaled * normed, axis=-1, keepdims=True)
        grad = branch2_ref[at, :].astype(F32)
        grad = grad + inv_scale * (scaled - first - normed * second)
        grad_mid[at, :] = grad
        low = grad.astype(BF16)
        branch1[at, :] = low
        add_term(4, low.astype(F32))
        add_term(5, branch2_ref[at, :].astype(F32))

    each_rows(own, 64, mid)
    swap2 = send(branch1.at[pl.ds(0, own)], branch1.at[pl.ds(own, own)], peers["core"])
    swap2.wait_recv()
    load_norm.wait()
    transpose_into(brancht, branch1)
    attn_compute(3)
    ff_add(2)
    attn_compute(2)
    attn_plane(3)
    attn_compute(1)
    attn_plane(2)
    attn_ring(3)
    ff_add(1)
    swap1.wait_send()
    swap3 = attn_compute(0)
    attn_plane(1)
    attn_ring(2)
    attn_plane(0)
    swap3.wait_recv()

    def last(at):
        normed, inv_scale = norm_stats(x_rows[at, :].astype(F32))
        grad_norm = part[at, :] + got[at, :].astype(F32)
        add_term(0, grad_norm * normed)
        add_term(1, grad_norm)
        scaled = grad_norm * feature_ref[0:1]
        first = jnp.mean(scaled, axis=-1, keepdims=True)
        second = jnp.mean(scaled * normed, axis=-1, keepdims=True)
        grad = grad_mid[at, :] + inv_scale * (scaled - first - normed * second)
        grad_blocks[:, at] = grad.astype(BF16).T

    each_rows(own, 128, last)
    grad_move.collect(grad_blocks, grad_pieces)
    terms_mine[...] = jnp.zeros_like(terms_mine)
    bias_mine[...] = jnp.zeros_like(bias_mine)
    for i in range(7):
        if i < 6:
            row_sum = jnp.sum(terms[i], axis=0, keepdims=True)
        else:
            err = jnp.sum(jnp.sum(err_ref[...], axis=0, keepdims=True), axis=1, keepdims=True)
            row_sum = jnp.broadcast_to(err, (1, depth))
        for k in range(4):
            terms_mine[k, i : i + 1, :] = row_sum[:, k * feat : (k + 1) * feat]
    wide = bias_mine.shape[2]
    for s in range(4):
        bias_mine[s, 0:1, :qkv] = heads_out[s]
        bias_mine[s, 0:1, qkv : qkv + main] = units_out[s]
        bias_mine[s, 0:1, qkv + main :] = units_rest_out[...]
    dp, row, col = place()
    ring_two = (dp, row, 3 - col)
    sides = ((1, "x"), (2, "y"), (3, "diagonal"))
    term_sends = [send(terms_mine.at[k], terms_in.at[k - 1], peers[name]) for k, name in sides]
    bias_sends = [
        send(bias_mine.at[s], bias_turn.at[s - 1], peer)
        for s, peer in ((1, peers["prev"]), (2, ring_two), (3, peers["next"]))
    ]
    ff_add(0)
    end_low = send(gff.at[0, rows(1, 0, half)], rfx, peers["x"])
    end_high = send(gff.at[0, rows(2, half, half)], rfy, peers["y"])
    attn_ring(1)
    for copy in term_sends + bias_sends:
        copy.wait_recv()
    terms_mine[0] = terms_mine[0] + terms_in[0] + terms_in[1] + terms_in[2]
    sum_sends = [
        send(terms_mine.at[0], sums_in.at[i], peer) for i, peer in enumerate(images_group())
    ]
    bias_plane[...] = bias_mine[0]
    for s in (1, 2, 3):
        bias_plane[s : s + 1, :] = bias_turn[s - 1, 0:1, :]
    plane_sends = [send(bias_plane, bias_in.at[k - 1], peers[name]) for k, name in sides]
    end_low.wait_recv()
    end_high.wait_recv()
    add_into(gff.at[0], rows(0, 0, half), rfx)
    add_into(gff.at[0], rows(0, half, half), rfy)
    quarter = feat // 2
    keep_at = pl.ds(pl.multiple_of(dp * quarter, 16), quarter)
    give_at = pl.ds(pl.multiple_of((1 - dp) * quarter, 16), quarter)
    done = [keep(gff.at[0, keep_at], ff_out.at[0])]
    pair_sends = [send(gff.at[0, give_at], ff_out.at[1], peers["core"])]
    for copy in plane_sends + sum_sends:
        copy.wait_recv()
    bias_out[0] = bias_plane[...] + bias_in[0] + bias_in[1] + bias_in[2]
    pair_sends.append(send(bias_out.at[0], bias_out.at[1], peers["core"]))
    total = terms_mine[0]
    for i in range(7):
        total = total + sums_in[i]
    sums_out[...] = total
    attn_ring(0)
    done.append(keep(gattn.at[0, keep_at], attn_out.at[0]))
    pair_sends.append(send(gattn.at[0, give_at], attn_out.at[1], peers["core"]))
    for copy in pair_sends:
        copy.wait_recv()
    for copy in done:
        copy.wait()
    result_move.arrive()
    grad_move.arrive()
    for copy in send.copies:
        if copy is not swap1:
            copy.wait_send()
    result_move.finish()
    grad_move.finish()


def backward_call(arrays, feat, lanes, main, qkv, mix, own, depth):
    tokens = 2 * own
    half = feat // 2
    narrow = qkv + main + 128
    anywhere = pl.BlockSpec(memory_space=pl.ANY)
    local = pl.BlockSpec(memory_space=pltpu.VMEM)
    shapes = [
        ((2, feat, tokens), BF16, anywhere),
        ((2, feat, tokens), BF16, anywhere),
        ((8, feat), F32, local),
        ((2, 8, narrow), F32, local),
        ((2, half, lanes), BF16, anywhere),
        ((2, half, 2 * main), BF16, anywhere),
    ]
    return pl.pallas_call(
        backward_kernel,
        out_shape=[jax.ShapeDtypeStruct(shape, dtype) for shape, dtype, _ in shapes],
        in_specs=[local] * 9 + [anywhere] * 12,
        out_specs=[spec for _, _, spec in shapes],
        scratch_shapes=[
            pltpu.VMEM((own, depth), BF16),
            pltpu.VMEM((depth, own), BF16),
            pltpu.VMEM((6, 16, depth), F32),
            pltpu.VMEM((4, 8, feat), F32),
            pltpu.VMEM((3, 8, feat), F32),
            pltpu.VMEM((7, 8, feat), F32),
            pltpu.VMEM((4, 8, narrow), F32),
            pltpu.VMEM((3, 8, narrow), F32),
            pltpu.VMEM((3, 8, narrow), F32),
            pltpu.VMEM((8, narrow), F32),
            pltpu.VMEM((4, 1, main), F32),
            pltpu.VMEM((1, 128), F32),
            pltpu.VMEM((4, 1, qkv), F32),
            pltpu.VMEM((4, depth, lanes), BF16),
            pltpu.VMEM((4, depth, 2 * main), BF16),
            pltpu.VMEM((2, depth, 2 * main), BF16),
            pltpu.VMEM((2, tokens, qkv + mix), BF16),
            pltpu.VMEM((tokens, main), BF16),
            pltpu.VMEM((depth, 256), BF16),
            pltpu.VMEM((depth, tokens), BF16),
            pltpu.VMEM((depth, tokens), BF16),
            pltpu.VMEM((tokens, depth), BF16),
            pltpu.VMEM((tokens, depth), F32),
            pltpu.VMEM((own, depth), BF16),
            pltpu.VMEM((own, depth), BF16),
            pltpu.VMEM((own, depth), F32),
            pltpu.VMEM((tokens, qkv), BF16),
            pltpu.VMEM((tokens, mix), BF16),
            pltpu.VMEM((tokens, 128), F32),
            pltpu.VMEM((tokens, 128), F32),
            pltpu.VMEM((1, tokens), F32),
            pltpu.VMEM((4, half, lanes), BF16),
            pltpu.VMEM((4, half, lanes), BF16),
            pltpu.VMEM((4, feat, lanes), BF16),
            pltpu.VMEM((4, feat, lanes), BF16),
            pltpu.VMEM((3, feat, lanes), BF16),
            pltpu.VMEM((4, 2, half, 2 * main), BF16),
            pltpu.VMEM((4, 2, half, 2 * main), BF16),
            pltpu.VMEM((3, 2, half, 2 * main), BF16),
            pltpu.VMEM((3, 2, half, 2 * main), BF16),
            pltpu.VMEM((half, 2 * main), BF16),
            pltpu.VMEM((half, 2 * main), BF16),
            pltpu.SemaphoreType.DMA((32,)),
            pltpu.SemaphoreType.DMA((104,)),
            pltpu.SemaphoreType.DMA((104,)),
            pltpu.SemaphoreType.DMA((5, 4)),
        ],
        compiler_params=pltpu.CompilerParams(
            collective_id=2, has_side_effects=True, vmem_limit_bytes=63 << 20
        ),
    )(*arrays)
def on_chip(
    layer_input,
    teacher,
    valid,
    proj_in,
    bias_query,
    bias_value,
    proj_out,
    bias_out,
    norm1_gain,
    norm1_shift,
    norm2_gain,
    norm2_shift,
    w_up,
    bias_up,
    w_down,
    bias_down,
):
    core = lax.axis_index("dp")
    first = core == 0
    cols = lax.axis_size("col")
    feat = layer_input.shape[1]
    images = layer_input.shape[0] // SEQ
    half_seq = (SEQ + 255) // 256 * 128
    pad_seq = 2 * half_seq
    units = w_up.shape[1] // 2
    width = proj_out.shape[0] // 2
    heads = width // HD
    main = units // 128 * 128
    rest = units - main
    at = 4 * width
    lanes = (at + 2 * rest + 127) // 128 * 128
    qkv, mix = 3 * heads * 128, heads * 128

    def core_half(values, axis):
        low, high = jnp.split(values, 2, axis=axis)
        return jnp.where(first, low, high)

    def pieces(values):
        values = values.reshape(images, SEQ, -1).transpose(0, 2, 1)
        return jnp.pad(values, ((0, 0), (0, 0), (0, pad_seq - SEQ)))

    up_half, down_half = core_half(w_up, 1), core_half(w_down, 0).T
    attn_shard = jnp.concatenate(
        [
            core_half(proj_in, 1),
            core_half(proj_out, 0).T,
            up_half[:, main:],
            down_half[:, main:],
            jnp.zeros((feat, lanes - at - 2 * rest), jnp.bfloat16),
        ],
        axis=1,
    )
    ff_shard = jnp.concatenate([up_half[:, :main], down_half[:, :main]], axis=1)
    lane = np.arange(lanes)
    spread_at = np.where(lane < at, lane // HD * 128 + lane % HD, -1)
    spread = jnp.asarray(spread_at[:, None] == np.arange(qkv + mix), jnp.bfloat16)
    tail = lane[-128:]
    part = np.arange(cols)[:, None]
    up_at = np.where((tail >= at) & (tail < at + rest), tail - at + part * rest, -1)
    down_at = np.where(
        (tail >= at + rest) & (tail < at + 2 * rest), tail - at - rest + part * rest + 128, -1
    )
    spot = np.arange(256)
    rest_spread = (up_at[..., None] == spot) | (down_at[..., None] == spot)
    rest_spread = jnp.asarray(rest_spread, jnp.bfloat16)

    place_of = jnp.arange(pad_seq)
    token = jnp.where(
        place_of < half_seq, place_of + core * half_seq, place_of - core * half_seq
    )
    key_column = jnp.where(token < SEQ, 0.0, -1e30).astype(jnp.float32)[:, None]
    key_lane = jnp.asarray(np.arange(qkv) % 384 == 128 + HD, jnp.float32)[None]

    query_bias, value_bias = core_half(bias_query, 0), core_half(bias_value, 0)
    unit_bias = core_half(bias_up, 0)
    pitch = (feat + 127) // 128 * 128
    one = jnp.ones((1,), jnp.bfloat16)

    def gap(size):
        return jnp.zeros((size,), jnp.bfloat16)

    params = []
    for vector in (norm1_gain, norm1_shift, norm2_gain, norm2_shift, bias_out, bias_down):
        params += [vector, gap(pitch - feat)]
    for h in range(heads):
        head_at = slice(h * HD, (h + 1) * HD)
        params += [query_bias[head_at], one, gap(127 - HD + 128)]
        params += [value_bias[head_at], gap(128 - HD)]
    params += [unit_bias[:main], gap(at - lanes + 128), unit_bias[main:]]
    params.append(gap(lanes - at - rest))
    params = jnp.concatenate(params).astype(jnp.float32)
    params = jnp.broadcast_to(params[None], (8, params.shape[0]))
    count = jnp.broadcast_to(jnp.sum(valid).astype(jnp.float32), (8, 128))

    valid_rows = jnp.pad(valid.reshape(images, SEQ), ((0, 0), (0, pad_seq - SEQ)))
    valid_rows = jnp.broadcast_to(valid_rows.astype(jnp.float32)[:, None], (images, 8, pad_seq))
    sizes = (feat, lanes, main, qkv, mix, half_seq, 4 * feat)
    (
        wpad, wff, triple, mixed, act, slope, norm1t, norm2t, rest_weight, lse, act_rest,
        slope_rest, resid1, x_rows, branch2, branch2t, result, err_rows, features, counted,
    ) = forward_call(
        (
            pieces(layer_input), pieces(teacher), count, valid_rows, params, key_column, key_lane,
            spread, rest_spread, attn_shard, ff_shard,
        ),
        layer_input.shape[0],
        *sizes,
    )
    grad_pieces, result_pieces, sums, bias_rows, attn_sum, ff_sum = backward_call(
        (
            branch2, rest_weight, act_rest, slope_rest, lse, features, spread, rest_spread,
            err_rows, result, x_rows, resid1, norm1t, norm2t, branch2t, wpad,
            wff, triple, mixed, act, slope,
        ),
        *sizes,
    )

    def rows_of(values):
        return values[:, :, :SEQ].transpose(0, 2, 1).reshape(images * SEQ, feat)

    def both(keep, got, axis=-1):
        return jnp.concatenate(
            [jnp.where(first, keep, got), jnp.where(first, got, keep)], axis=axis
        ).astype(jnp.float32)

    def up_of(i):
        return jnp.concatenate([ff_sum[i][:, :main], attn_sum[i][:, at : at + rest]], axis=1)

    def down_of(i):
        block = [ff_sum[i][:, main:], attn_sum[i][:, at + rest : at + 2 * rest]]
        return jnp.concatenate(block, axis=1).T

    loss_value = sums[6, 0] / (counted[0, 0] * D)
    main_rows = jnp.sum(bias_rows[:, :cols, : qkv + main], axis=1)
    head_rows = main_rows[:, :qkv].reshape(2, heads, 3, 128)[..., :HD]
    tail_rows = bias_rows[:, :cols, qkv + main :]
    tail_rows = sum(tail_rows[:, s, s * rest : (s + 1) * rest] for s in range(cols))
    unit_rows = jnp.concatenate([main_rows[:, qkv:], tail_rows], axis=1)
    return (
        rows_of(result_pieces),
        loss_value,
        rows_of(grad_pieces).astype(jnp.float32),
        both(attn_sum[0][:, : 3 * width], attn_sum[1][:, : 3 * width])[None],
        both(head_rows[0, :, 0].reshape(width), head_rows[1, :, 0].reshape(width)),
        both(head_rows[0, :, 2].reshape(width), head_rows[1, :, 2].reshape(width)),
        both(attn_sum[0][:, 3 * width : at].T, attn_sum[1][:, 3 * width : at].T, 0)[:, None],
        sums[4],
        sums[0],
        sums[1],
        sums[2],
        sums[3],
        both(up_of(0), up_of(1))[None],
        both(unit_rows[0], unit_rows[1]),
        both(down_of(0), down_of(1), 0)[:, None],
        sums[5],
    )


def one_image_a_chip(mesh, tokens):
    sizes = mesh.shape
    pairs = sizes["dp"] == 2 and sizes["row"] == 4 and sizes["col"] == 4
    return pairs and tokens == SEQ * sizes["row"] * sizes["col"]


def solution(mesh):
    placed = (
        P(("dp", "col"), "row"),
        P(("dp", "col"), "row"),
        P(("dp", "col")),
        P("row", "col"),
        P("col"),
        P("col"),
        P("col", "row"),
        P("row"),
        P("row"),
        P("row"),
        P("row"),
        P("row"),
        P("row", "col"),
        P("col"),
        P("col", "row"),
        P("row"),
    )
    returned = (
            P(("dp", "col"), "row"),
            P(),
            P(("dp", "col"), "row"),
            P("row", "dp", "col"),
            P("col"),
            P("col"),
            P("col", "row", "dp"),
            P("row"),
            P("row"),
            P("row"),
            P("row"),
            P("row"),
            P("row", "dp", "col"),
            P("col"),
            P("col", "row", "dp"),
            P("row"),
        )

    def whole(layer_input, *others):
        body = on_chip if one_image_a_chip(mesh, layer_input.shape[0]) else on_device
        return jax.shard_map(
            body, mesh=mesh, in_specs=placed, out_specs=returned, check_vma=False
        )(layer_input, *others)

    return whole
```

```python
import functools

import jax
import jax.numpy as jnp
import numpy as np
from jax import lax
from jax.experimental import pallas as pl
from jax.experimental.pallas import tpu as pltpu
from jax.sharding import PartitionSpec as P

D = 1152
H = 16
HD = 72
FF = 4304
SEQ = 729


EPS = 1e-06


def feature_totals(left, right):
    return lax.psum(
        (jnp.sum(left, axis=-1, keepdims=True), jnp.sum(right, axis=-1, keepdims=True)), "row"
    )


def norm_forward(values, gain, shift):
    first_sum, second_sum = feature_totals(values, values * values)
    mean_rows = first_sum / D
    var_rows = second_sum / D - mean_rows * mean_rows
    inv_scale = lax.rsqrt(var_rows + EPS)
    normed = (values - mean_rows) * inv_scale
    return (normed, inv_scale, normed * gain + shift)


def norm_backward(grad_out, normed, inv_scale, gain):
    grad_normed = grad_out * gain
    first_sum, second_sum = feature_totals(grad_normed, grad_normed * normed)
    return inv_scale * (grad_normed - first_sum / D - normed * second_sum / D)


def first_section(local_rows, weight):
    gathered = lax.all_gather(local_rows, "col", axis=0, tiled=True)
    share_rows = gathered.shape[0] // lax.axis_size("row")

    def partial_term(row_start, row_count):
        return jnp.dot(gathered, weight, preferred_element_type=jnp.float32)

    result = lax.psum_scatter(
        partial_term(jnp.int32(0), lax.axis_size("row") * share_rows),
        "row",
        scatter_dimension=0,
        tiled=True,
    )
    return (gathered, result)


def second_section(quarter_rows, weight):
    gathered = lax.all_gather(quarter_rows, "row", axis=0, tiled=True)
    share_rows = gathered.shape[0] // lax.axis_size("col")

    def partial_term(row_start, row_count):
        return jnp.dot(gathered, weight, preferred_element_type=jnp.float32)

    result = lax.psum_scatter(
        partial_term(jnp.int32(0), lax.axis_size("col") * share_rows),
        "col",
        scatter_dimension=0,
        tiled=True,
    )
    return (gathered, result)


def second_section_back(grad_local, gathered, weight):
    grad_all = lax.all_gather(grad_local, "col", axis=0, tiled=True)
    grad_weight = lax.dot_general(
        gathered, grad_all, (((0,), (0,)), ((), ())), preferred_element_type=jnp.float32
    )
    share_rows = grad_all.shape[0] // lax.axis_size("row")

    def partial_term(row_start, row_count):
        return lax.dot_general(
            grad_all, weight, (((1,), (1,)), ((), ())), preferred_element_type=jnp.float32
        )

    result = lax.psum_scatter(
        partial_term(jnp.int32(0), lax.axis_size("row") * share_rows),
        "row",
        scatter_dimension=0,
        tiled=True,
    )
    return (grad_weight, result)


def first_section_back(grad_quarter, gathered, weight):
    grad_all = lax.all_gather(grad_quarter, "row", axis=0, tiled=True)
    grad_weight = lax.dot_general(
        gathered, grad_all, (((0,), (0,)), ((), ())), preferred_element_type=jnp.float32
    )
    share_rows = grad_all.shape[0] // lax.axis_size("col")

    def partial_term(row_start, row_count):
        return lax.dot_general(
            grad_all, weight, (((1,), (1,)), ((), ())), preferred_element_type=jnp.float32
        )

    result = lax.psum_scatter(
        partial_term(jnp.int32(0), lax.axis_size("col") * share_rows).astype(jnp.bfloat16),
        "col",
        scatter_dimension=0,
        tiled=True,
    ).astype(jnp.float32)
    return (grad_weight, result)


def attend(triple_img):
    score_scale = HD ** (-0.5)
    query_rows = triple_img[:, :, 0]
    key_rows = triple_img[:, :, 1]
    value_rows = triple_img[:, :, 2]
    raw_scores = jnp.einsum(
        "qhd,khd->hqk", query_rows, key_rows, preferred_element_type=jnp.float32
    )
    scaled = raw_scores * score_scale
    peak_score = jnp.max(scaled, axis=-1, keepdims=True)
    exp_scores = jnp.exp(scaled - peak_score)
    exp_total = jnp.sum(exp_scores, axis=-1, keepdims=True)
    soft_weights = (exp_scores / exp_total).astype(jnp.bfloat16)
    mixed_rows = jnp.einsum(
        "hqk,khd->qhd", soft_weights, value_rows, preferred_element_type=jnp.float32
    )
    return (mixed_rows.astype(jnp.bfloat16), peak_score + jnp.log(exp_total))


def attend_back(packed):
    triple_img, log_total, grad_mixed = packed
    score_scale = HD ** (-0.5)
    query_rows = triple_img[:, :, 0]
    key_rows = triple_img[:, :, 1]
    value_rows = triple_img[:, :, 2]
    raw_scores = jnp.einsum(
        "qhd,khd->hqk", query_rows, key_rows, preferred_element_type=jnp.float32
    )
    soft_weights = jnp.exp(raw_scores * score_scale - log_total)
    weights_low = soft_weights.astype(jnp.bfloat16)
    grad_values = jnp.einsum(
        "hqk,qhd->khd", weights_low, grad_mixed, preferred_element_type=jnp.float32
    )
    grad_soft = jnp.einsum(
        "qhd,khd->hqk", grad_mixed, value_rows, preferred_element_type=jnp.float32
    )
    inner_prod = jnp.sum(grad_soft * soft_weights, axis=-1, keepdims=True)
    grad_raw = (score_scale * soft_weights * (grad_soft - inner_prod)).astype(jnp.bfloat16)
    grad_query = jnp.einsum("hqk,khd->qhd", grad_raw, key_rows, preferred_element_type=jnp.float32)
    grad_keys = jnp.einsum("hqk,qhd->khd", grad_raw, query_rows, preferred_element_type=jnp.float32)
    return jnp.stack([grad_query, grad_keys, grad_values], axis=2).astype(jnp.bfloat16)


def on_device(
    layer_input,
    teacher,
    valid,
    proj_in,
    bias_query,
    bias_value,
    proj_out,
    bias_out,
    norm1_gain,
    norm1_shift,
    norm2_gain,
    norm2_shift,
    w_up,
    bias_up,
    w_down,
    bias_down,
):
    heads_here = H // lax.axis_size("col")
    head_width = heads_here * HD
    feat_here = layer_input.shape[1]
    units_here = w_up.shape[1]
    gain_one = norm1_gain.astype(jnp.float32)
    gain_two = norm2_gain.astype(jnp.float32)
    residual_in = layer_input.astype(jnp.float32)
    normed1, scale1, mid_one = norm_forward(residual_in, gain_one, norm1_shift.astype(jnp.float32))
    norm1_all, projected = first_section(mid_one.astype(jnp.bfloat16), proj_in)
    quarter = projected.shape[0]
    images = quarter // SEQ
    bias_shift = jnp.stack(
        [
            bias_query.astype(jnp.float32).reshape(heads_here, HD),
            jnp.zeros((heads_here, HD), jnp.float32),
            bias_value.astype(jnp.float32).reshape(heads_here, HD),
        ],
        axis=1,
    )
    triple = (projected.reshape(quarter, heads_here, 3, HD) + bias_shift).astype(jnp.bfloat16)
    triple_imgs = triple.reshape(images, SEQ, heads_here, 3, HD)
    mixed_imgs, log_totals = lax.map(attend, triple_imgs)
    mixed_all, attn_part = second_section(mixed_imgs.reshape(quarter, head_width), proj_out)
    resid1 = residual_in + attn_part + bias_out.astype(jnp.float32)
    normed2, scale2, mid_two = norm_forward(resid1, gain_two, norm2_shift.astype(jnp.float32))
    norm2_all, pre_part = first_section(mid_two.astype(jnp.bfloat16), w_up)
    pre = pre_part + bias_up.astype(jnp.float32)
    activated, gelu_pull = jax.vjp(lambda entry: jax.nn.gelu(entry, approximate=True), pre)
    act_all, down_part = second_section(activated.astype(jnp.bfloat16), w_down)
    result = resid1 + down_part + bias_down.astype(jnp.float32)
    mask_rows = valid.astype(jnp.float32)
    error_rows = result - teacher.astype(jnp.float32)
    err_part = jnp.sum(mask_rows[:, None] * error_rows * error_rows)
    count_part = jnp.sum(mask_rows) / lax.axis_size("row")
    err_total, valid_count = lax.psum((err_part, count_part), ("dp", "row", "col"))
    loss_value = err_total / (valid_count * D)
    tokens_all = layer_input.shape[0] * lax.axis_size("dp") * lax.axis_size("col")
    factor = tokens_all / (2.0 * valid_count)
    grad_result = 2.0 * error_rows * (mask_rows[:, None] * factor)
    grad_branch2 = grad_result.astype(jnp.bfloat16)
    grad_w_down, grad_act = second_section_back(grad_branch2, act_all, w_down)
    grad_pre = gelu_pull(grad_act)[0].astype(jnp.bfloat16)
    grad_w_up, grad_norm2 = first_section_back(grad_pre, norm2_all, w_up)
    grad_resid1 = grad_result + norm_backward(grad_norm2, normed2, scale2, gain_two)
    grad_branch1 = grad_resid1.astype(jnp.bfloat16)
    grad_proj_out, grad_mixed = second_section_back(grad_branch1, mixed_all, proj_out)
    grad_mixed_imgs = grad_mixed.astype(jnp.bfloat16).reshape(images, SEQ, heads_here, HD)
    grad_triple = lax.map(attend_back, (triple_imgs, log_totals, grad_mixed_imgs))
    grad_triple = grad_triple.reshape(quarter, heads_here, 3, HD)
    grad_proj_in, grad_norm1 = first_section_back(
        grad_triple.reshape(quarter, 3 * head_width), norm1_all, proj_in
    )
    grad_input = grad_resid1 + norm_backward(grad_norm1, normed1, scale1, gain_one)
    row_at = lax.axis_index("row") * feat_here
    col_at = lax.axis_index("col") * head_width
    feature_terms = jnp.stack(
        [
            jnp.sum(grad_norm1 * normed1, axis=0),
            jnp.sum(grad_norm1, axis=0),
            jnp.sum(grad_norm2 * normed2, axis=0),
            jnp.sum(grad_norm2, axis=0),
            jnp.sum(grad_branch1.astype(jnp.float32), axis=0),
            jnp.sum(grad_branch2.astype(jnp.float32), axis=0),
        ]
    )
    feature_full = lax.dynamic_update_slice_in_dim(
        jnp.zeros((6, D), jnp.float32), feature_terms, row_at, 1
    )
    grad_float = grad_triple.astype(jnp.float32)
    head_terms = jnp.stack(
        [
            jnp.sum(grad_float[:, :, 0], axis=0).reshape(head_width),
            jnp.sum(grad_float[:, :, 2], axis=0).reshape(head_width),
        ]
    )
    head_full = lax.dynamic_update_slice_in_dim(
        jnp.zeros((2, H * HD), jnp.float32), head_terms, col_at, 1
    )
    unit_terms = jnp.sum(grad_pre.astype(jnp.float32), axis=0)
    unit_full = lax.dynamic_update_slice_in_dim(
        jnp.zeros((FF,), jnp.float32), unit_terms, lax.axis_index("col") * units_here, 0
    )
    feature_full, head_full, unit_full = lax.psum(
        (feature_full, head_full, unit_full), ("dp", "row", "col")
    )
    feature_mine = lax.dynamic_slice_in_dim(feature_full, row_at, feat_here, 1)
    head_mine = lax.dynamic_slice_in_dim(head_full, col_at, head_width, 1)
    unit_mine = lax.dynamic_slice_in_dim(
        unit_full, lax.axis_index("col") * units_here, units_here, 0
    )
    grad_proj_in, grad_w_up = (
        lax.psum_scatter(
            grad_proj_in.astype(jnp.bfloat16), "dp", scatter_dimension=0, tiled=True
        ).astype(jnp.float32),
        lax.psum_scatter(
            grad_w_up.astype(jnp.bfloat16), "dp", scatter_dimension=0, tiled=True
        ).astype(jnp.float32),
    )
    grad_proj_out, grad_w_down = (
        lax.psum_scatter(
            grad_proj_out.astype(jnp.bfloat16), "dp", scatter_dimension=1, tiled=True
        ).astype(jnp.float32),
        lax.psum_scatter(
            grad_w_down.astype(jnp.bfloat16), "dp", scatter_dimension=1, tiled=True
        ).astype(jnp.float32),
    )
    grad_proj_in = grad_proj_in.reshape(1, grad_proj_in.shape[0], grad_proj_in.shape[1])
    grad_w_up = grad_w_up.reshape(1, grad_w_up.shape[0], grad_w_up.shape[1])
    grad_proj_out = grad_proj_out.reshape(grad_proj_out.shape[0], 1, grad_proj_out.shape[1])
    grad_w_down = grad_w_down.reshape(grad_w_down.shape[0], 1, grad_w_down.shape[1])
    return (
        result.astype(jnp.bfloat16),
        loss_value,
        grad_input,
        grad_proj_in,
        head_mine[0],
        head_mine[1],
        grad_proj_out,
        feature_mine[4],
        feature_mine[0],
        feature_mine[1],
        feature_mine[2],
        feature_mine[3],
        grad_w_up,
        unit_mine,
        grad_w_down,
        feature_mine[5],
    )


MESH = pl.DeviceIdType.MESH
F32 = jnp.float32
BF16 = jnp.bfloat16
LOG2E = 1.4426950408889634
GELU_ROOT = 0.7978845608028654


def place():
    return lax.axis_index("dp"), lax.axis_index("row"), lax.axis_index("col")


def flip(row, other):
    return lax.rem(row // 2 + other // 2, 2) * 2 + lax.rem(row + other, 2)


def neighbours():
    dp, row, col = place()
    return dict(
        core=(1 - dp, row, col),
        x=(dp, flip(row, 1), col),
        y=(dp, flip(row, 2), col),
        diagonal=(dp, flip(row, 3), col),
        next=(dp, row, lax.rem(2 * col + 3 * (col // 2) + 1, 4)),
        prev=(dp, row, lax.rem(2 * col + col // 2 + 2, 4)),
    )


def images_group():
    dp, row, col = place()
    steps = [(core, step) for core in (0, 1) for step in range(4)][1:]
    return [(lax.rem(dp + core, 2), row, lax.rem(col + step, 4)) for core, step in steps]


def meet():
    dp, row, col = place()
    plane = [(core, k) for core in (0, 1) for k in range(4)][1:]
    peers = [(lax.rem(dp + core, 2), flip(row, k), col) for core, k in plane]
    peers += [peer for i, peer in enumerate(images_group()) if i != 3]
    barrier = pltpu.get_barrier_semaphore()
    for peer in peers:
        pl.semaphore_signal(barrier, inc=1, device_id=peer, device_id_type=MESH)
    pl.semaphore_wait(barrier, len(peers))


class Shuffle:
    def __init__(self, send_sems, recv_sems, local_sem):
        self.sems = send_sems, recv_sems, local_sem
        self.pending = []

    def remote(self, source, target, i, slot, peer):
        return pltpu.make_async_remote_copy(
            source, target, self.sems[0].at[i], self.sems[1].at[slot],
            device_id=peer, device_id_type=MESH,
        )

    def spread(self, pieces, blocks):
        dp, row, col = place()
        feat, own = pieces[0].shape[0], blocks.shape[1]
        for image in (0, 1):
            for half in (0, 1):
                chip = 2 * dp + image
                slot = flip(chip, row)
                mine = (dp == half) & (chip == row)
                source = pieces[image].at[:, pl.ds(half * own, own)]
                target = blocks.at[pl.ds(pl.multiple_of(slot * feat, 16), feat)]
                copy = self.remote(source, target, 2 * image + half, slot, (half, chip, col))
                here = pltpu.make_async_copy(source, blocks.at[pl.ds(0, feat)], self.sems[2])
                self.start(copy, here, mine)
        mine = dp == row // 2
        self.into = [
            (blocks.at[pl.ds(k * feat, feat)], k, None if k else mine) for k in range(4)
        ]

    def collect(self, blocks, pieces):
        dp, row, col = place()
        feat, own = pieces.shape[1], blocks.shape[1]
        image = lax.rem(row, 2)
        for k in range(4):
            owner = flip(row, k)
            mine = (dp == row // 2) & (owner == row)
            source = blocks.at[pl.ds(k * feat, feat)]
            target = pieces.at[image, :, pl.ds(pl.multiple_of(dp * own, 128), own)]
            copy = self.remote(source, target, k, 2 * image + dp, (row // 2, owner, col))
            here = pltpu.make_async_copy(source, target, self.sems[2])
            self.start(copy, here, mine)
        self.into = []
        for image in (0, 1):
            for half in (0, 1):
                mine = (dp == half) & (2 * dp + image == row)
                target = pieces.at[image, :, pl.ds(half * own, own)]
                self.into.append((target, 2 * image + half, mine))

    def start(self, copy, here, mine):
        pl.when(jnp.logical_not(mine))(copy.start)
        pl.when(mine)(here.start)
        self.pending.append((copy, here, mine))

    def arrive(self):
        dp, row, col = place()
        here = self.pending[0][1]
        for target, slot, own in self.into:
            copy = self.remote(target, target, 0, slot, (1 - dp, row, col))
            if own is None:
                copy.wait_recv()
            else:
                pl.when(jnp.logical_not(own))(copy.wait_recv)
                pl.when(own)(here.wait)

    def finish(self):
        for copy, _, mine in self.pending:
            pl.when(jnp.logical_not(mine))(copy.wait_send)


def mm(left, right):
    return jnp.dot(left, right, preferred_element_type=F32)


def mm_nt(left, right):
    return lax.dot_general(left, right, (((1,), (1,)), ((), ())), preferred_element_type=F32)


def each_rows(count, size, body):
    @pl.loop(0, count // size)
    def _(step):
        body(pl.ds(pl.multiple_of(step * size, size), size))


def fold(values):
    return sum(values[i : i + 16] for i in range(0, values.shape[0], 16))


def spread_lanes(source, spread, width):
    blocks = []
    for j in range(width // 256):
        low = 2 * HD * j // 128 * 128
        blocks.append(mm(source[:, low : low + 256], spread[low : low + 256, 256 * j : 256 * j + 256]))
    return jnp.concatenate(blocks, axis=1)


def transpose_into(target, source):
    @pl.loop(0, source.shape[1] // 128)
    def _(step):
        at = pl.ds(pl.multiple_of(step * 128, 128), 128)
        target[at, :] = source[:, at].T


class Sender:
    def __init__(self, send_sems, recv_sems):
        self.sems = (send_sems, recv_sems)
        self.count = 0
        self.copies = []

    def __call__(self, source, target, peer):
        copy = pltpu.make_async_remote_copy(
            source,
            target,
            self.sems[0].at[self.count],
            self.sems[1].at[self.count],
            device_id=peer,
            device_id_type=MESH,
        )
        self.count += 1
        copy.start()
        self.copies.append(copy)
        return copy

    def finish(self):
        for copy in self.copies:
            copy.wait_send()


class Copier:
    def __init__(self, sems):
        self.sems = sems
        self.count = 0

    def __call__(self, source, target):
        copy = pltpu.make_async_copy(source, target, self.sems.at[self.count])
        self.count += 1
        copy.start()
        return copy


def norm_stats(values):
    mean_rows = jnp.mean(values, axis=-1, keepdims=True)
    centered = values - mean_rows
    inv_scale = lax.rsqrt(jnp.mean(centered * centered, axis=-1, keepdims=True) + EPS)
    return centered * inv_scale, inv_scale


def forward_kernel(
    own_tokens,
    x_first,
    x_second,
    teacher_first,
    teacher_second,
    valid_ref,
    params_ref,
    key_lane_ref,
    one_lane_ref,
    bias_spread_ref,
    spread_ref,
    rest_spread_ref,
    attn_ref,
    ff_ref,
    wpad_out,
    wff_out,
    triple_out,
    mixed_out,
    act_out,
    slope_out,
    norm1t_out,
    norm2t_out,
    rest_hbm,
    lse_hbm,
    act_rest_hbm,
    slope_rest_hbm,
    resid_hbm,
    x_hbm,
    branch_out,
    brancht_out,
    result_out,
    err_out,
    feature_ref,
    count_out,
    rest_out,
    lse_out,
    act_rest_out,
    slope_rest_out,
    resid_out,
    x_rows,
    x_blocks,
    teacher_blocks,
    valid_in,
    features_in,
    biases_in,
    counts_in,
    wattn,
    wff,
    wpad,
    triple,
    mixed,
    act,
    slope,
    norm1,
    norm2,
    turned,
    part,
    give1,
    got1,
    give2,
    got2,
    local_sems,
    send_sems,
    recv_sems,
    shuffle_sems,
):
    peers = neighbours()
    meet()
    feat = attn_ref.shape[0]
    half = feat // 2
    depth = 4 * feat
    tokens = norm1.shape[0]
    own = tokens // 2
    main = ff_ref.shape[1] // 2
    qkv = triple.shape[2]
    wide = features_in.shape[2]
    heads_wide = bias_spread_ref.shape[0]
    send = Sender(send_sems, recv_sems)
    keep = Copier(local_sems)

    def rows(block, low=0, size=None):
        return pl.ds(block * feat + low, feat if size is None else size)

    own_attn = keep(attn_ref, wattn.at[0, rows(0)])
    own_ff = keep(ff_ref, wff.at[0, rows(0)])
    az, ax, ay, a_low, a_high = ([None] * 4 for _ in range(5))

    def attn_source(s):
        return attn_ref if s == 0 else wattn.at[s, rows(0)]

    def attn_ring(s):
        az[s + 1] = send(attn_source(s), wattn.at[s + 1, rows(0)], peers["next"])

    def attn_plane(s):
        ax[s] = send(attn_source(s), wattn.at[s, rows(1)], peers["x"])
        ay[s] = send(attn_source(s), wattn.at[s, rows(2)], peers["y"])

    def attn_last(s):
        ax[s].wait_recv()
        a_low[s] = send(
            wattn.at[s, rows(1, 0, half)], wattn.at[s, rows(3, 0, half)], peers["y"]
        )
        ay[s].wait_recv()
        a_high[s] = send(
            wattn.at[s, rows(2, half, half)], wattn.at[s, rows(3, half, half)], peers["x"]
        )

    fz, fy, fx = ([None] * 4 for _ in range(3))

    def ff_first():
        return (
            send(ff_ref.at[pl.ds(0, half)], wff.at[0, rows(1, 0, half)], peers["x"]),
            send(ff_ref.at[pl.ds(half, half)], wff.at[0, rows(2, half, half)], peers["y"]),
        )

    def ff_ring(s):
        fz[s + 1] = [
            send(wff.at[s, piece], wff.at[s + 1, piece], peers["next"])
            for piece in (rows(0), rows(1, 0, half), rows(2, half, half))
        ]

    def ff_last(s):
        fy[s] = [
            send(wff.at[s, rows(k, 0, half)], wff.at[s, rows(k + 2, 0, half)], peers["y"])
            for k in (0, 1)
        ]
        fx[s] = [
            send(wff.at[s, rows(k, half, half)], wff.at[s, rows(k + 1, half, half)], peers["x"])
            for k in (0, 2)
        ]

    def arrive(copies):
        for copy in copies:
            copy.wait_recv()

    def attn_compute(s):
        arrive([a_low[s], a_high[s]])
        slot = s % 2
        if s == 0:
            own_attn.wait()
        if s >= 2:
            for copy in saved[s - 2]:
                copy.wait()

        def unpack(at):
            block = wattn[s, at, :]
            wpad[slot, at, :] = spread_lanes(block, spread_ref, wpad.shape[2]).astype(BF16)
            extra = mm(block[:, block.shape[1] - 128 :], rest_spread_ref[s]).astype(BF16)
            if s == 0:
                rest_out[at, :] = extra
            else:
                rest_out[at, :] = rest_out[at, :] + extra

        each_rows(depth, feat, unpack)

        def project(at):
            bias = mm(biases_in[s, :, :heads_wide].astype(BF16), bias_spread_ref[...])
            values = mm(norm1[at, :], wpad[slot, :, :qkv]) + (bias[0:1] + one_lane_ref[...])
            spot = lax.broadcasted_iota(jnp.int32, (tokens, 1), 0)
            shift = lax.axis_index("dp") * own
            token = jnp.where(spot < own, spot + shift, spot - shift)
            values = values + jnp.where(token < SEQ, 0.0, -1e30) * key_lane_ref[...]
            triple[slot, at, :] = values.astype(BF16)

        each_rows(tokens, tokens, project)
        scale = LOG2E * HD**-0.5
        for h in range(qkv // 384):
            query_at, key_at, value_at = (pl.ds((3 * h + j) * 128, 128) for j in range(3))
            value_turned = triple[slot, :, value_at].T

            def head(at, h=h, query_at=query_at, key_at=key_at, value_turned=value_turned):
                scores = mm_nt(triple[slot, :, key_at], triple[slot, at, query_at])
                peak = jnp.max(scores, axis=0, keepdims=True)
                weights = jnp.exp2((scores - peak) * scale)
                total = jnp.sum(weights, axis=0, keepdims=True)
                lse_out[2 * s + h, :, at] = peak * scale + jnp.log2(total)
                values = mm(value_turned, weights.astype(BF16)) / total
                mixed[s, at, pl.ds(h * 128, 128)] = values.T.astype(BF16)

            each_rows(tokens, own, head)

        def out(at):
            values = mm_nt(mixed[s, at, :], wpad[slot, :, qkv:])
            return values if s == 0 else part[at, :] + values

        swap = None
        if s < 3:
            part[...] = out(pl.ds(0, tokens))
        else:
            give1[...] = out(pl.ds(own, own)).astype(BF16)
            swap = send(give1, got1, peers["core"])
            part[pl.ds(0, own), :] = out(pl.ds(0, own))
        saved.append(
            [
                keep(wpad.at[slot], wpad_out.at[s]),
                keep(triple.at[slot], triple_out.at[s]),
                keep(mixed.at[s], mixed_out.at[s]),
            ]
        )
        return swap

    def gelu(pre):
        inner = GELU_ROOT * (pre + 0.044715 * pre * pre * pre)
        tanh = jnp.tanh(inner)
        rise = 0.5 * (1.0 + tanh)
        bend = 0.5 * pre * (1.0 - tanh * tanh) * (GELU_ROOT * (1.0 + 0.134145 * pre * pre))
        return (pre * rise).astype(BF16), (rise + bend).astype(BF16)

    def ff_compute(s):
        arrive(fy[s] + fx[s])

        def block(at):
            pre = mm(norm2[at, :], wff[s, :, :main]) + biases_in[s, 0:1, heads_wide : heads_wide + main]
            low, bent = gelu(pre)
            act[s, at, :] = low
            slope[s, at, :] = bent
            return part[at, :] + mm_nt(low, wff[s, :, main:])

        swap = None
        if s < 3:
            part[...] = block(pl.ds(0, tokens))
        else:
            give2[...] = block(pl.ds(own, own)).astype(BF16)
            swap = send(give2, got2, peers["core"])
            part[pl.ds(0, own), :] = block(pl.ds(0, own))
        ff_saved.extend(
            [
                keep(act.at[s], act_out.at[s]),
                keep(slope.at[s], slope_out.at[s]),
                keep(wff.at[s], wff_out.at[s]),
            ]
        )
        return swap

    def rest_compute():
        tail_at = heads_wide + main - (2 * heads_wide - wattn.shape[2] + 128)
        bias = mm(biases_in[0, :, tail_at : tail_at + 128].astype(BF16), rest_spread_ref[0, :, :128])
        for s in (1, 2, 3):
            values = biases_in[s, :, tail_at : tail_at + 128].astype(BF16)
            bias = bias + mm(values, rest_spread_ref[s, :, :128])

        def block(at):
            pre = mm(norm2[at, :], rest_out[:, :128]) + bias[0:1]
            low, bent = gelu(pre)
            act_rest_out[at, :] = low
            slope_rest_out[at, :] = bent
            part[at, :] = mm_nt(low, rest_out[:, 128:])

        each_rows(tokens, tokens, block)

    saved, ff_saved = [], []
    x_move = Shuffle(shuffle_sems.at[0], shuffle_sems.at[1], shuffle_sems.at[2, 0])
    x_move.spread((x_first, x_second), x_blocks)
    attn_ring(0)
    first = ff_first()
    attn_plane(0)
    valid_row = valid_ref[0, 0:1, :] + valid_ref[1, 0:1, :]
    counts_in[0] = jnp.broadcast_to(jnp.sum(valid_row, axis=1, keepdims=True), (8, 128))
    own_params = [
        keep(params_ref.at[:, pl.ds(0, wide)], features_in.at[0]),
        keep(params_ref.at[:, pl.ds(wide, biases_in.shape[2])], biases_in.at[0]),
    ]
    smalls = [
        send(params_ref.at[:, pl.ds(0, wide)], features_in.at[k], peers[name])
        for k, name in ((1, "x"), (2, "y"), (3, "diagonal"))
    ]
    dp, row, col = place()
    ring_two = (dp, row, 3 - col)
    smalls += [
        send(params_ref.at[:, pl.ds(wide, biases_in.shape[2])], biases_in.at[s], peer)
        for s, peer in ((1, peers["next"]), (2, ring_two), (3, peers["prev"]))
    ]
    counts = [
        send(counts_in.at[0], counts_in.at[1 + i], peer) for i, peer in enumerate(images_group())
    ]
    teacher_move = Shuffle(shuffle_sems.at[3], shuffle_sems.at[4], shuffle_sems.at[2, 1])

    valid_move = send(valid_ref, valid_in, peers["core"])

    az[1].wait_recv()
    attn_ring(1)
    attn_plane(1)
    attn_last(0)
    az[2].wait_recv()
    attn_ring(2)
    attn_plane(2)
    for copy in own_params:
        copy.wait()
    arrive(smalls)
    feature_ref[...] = jnp.zeros_like(feature_ref)
    for i in range(6):
        feature_ref[i : i + 1, :] = jnp.concatenate(
            [features_in[k, 0:1, feat * i : feat * (i + 1)] for k in range(4)], axis=1
        )
    x_move.arrive()
    for start in range(0, own, 128):
        x_rows[pl.ds(start, 128), :] = x_blocks[:, pl.ds(start, 128)].T
    late = [keep(x_rows, x_hbm)]

    def first_norm(at):
        normed, _ = norm_stats(x_rows[at, :].astype(F32))
        norm1[at, :] = (normed * feature_ref[0:1] + feature_ref[1:2]).astype(BF16)

    each_rows(own, 128, first_norm)
    swap1 = send(norm1.at[pl.ds(0, own)], norm1.at[pl.ds(own, own)], peers["core"])
    az[3].wait_recv()
    attn_plane(3)
    own_ff.wait()
    arrive(first)
    ff_ring(0)
    attn_last(1)
    swap1.wait_recv()
    attn_compute(0)
    attn_last(2)
    attn_compute(1)
    attn_last(3)
    ff_last(0)
    arrive(fz[1])
    ff_ring(1)
    ff_last(1)
    teacher_move.spread((teacher_first, teacher_second), teacher_blocks)
    attn_compute(2)
    swap2 = attn_compute(3)
    swap2.wait_recv()

    def second_norm(at):
        values = x_rows[at, :].astype(F32) + part[at, :] + got1[at, :].astype(F32) + feature_ref[4:5]
        resid_out[at, :] = values
        normed, _ = norm_stats(values)
        norm2[at, :] = (normed * feature_ref[2:3] + feature_ref[3:4]).astype(BF16)

    each_rows(own, 128, second_norm)
    late += [keep(resid_out, resid_hbm), keep(rest_out, rest_hbm), keep(lse_out, lse_hbm)]
    swap3 = send(norm2.at[pl.ds(0, own)], norm2.at[pl.ds(own, own)], peers["core"])
    arrive(fz[2])
    ff_ring(2)
    ff_last(2)
    transpose_into(turned, norm1)
    turn1 = keep(turned, norm1t_out)
    swap3.wait_recv()
    rest_compute()
    late += [keep(act_rest_out, act_rest_hbm), keep(slope_rest_out, slope_rest_hbm)]
    turn1.wait()
    transpose_into(turned, norm2)
    turn2 = keep(turned, norm2t_out)
    ff_compute(0)
    arrive(fz[3])
    ff_last(3)
    ff_compute(1)
    ff_compute(2)
    swap4 = ff_compute(3)
    err_out[...] = jnp.zeros_like(err_out)
    arrive(counts)
    count = counts_in[0]
    for i in range(1, 8):
        count = count + counts_in[i]
    count_out[...] = count
    factor = (own_tokens * 8.0) / count[0:1, 0:1]
    teacher_move.arrive()
    swap4.wait_recv()

    valid_move.wait_recv()
    image, from_here = lax.rem(row, 2), dp == row // 2

    def finish(start):
        at = pl.ds(start, 128)
        values = resid_out[at, :] + part[at, :] + got2[at, :].astype(F32) + feature_ref[5:6]
        result_out[:, at] = values.astype(BF16).T
        error = values - teacher_blocks[:, at].T.astype(F32)
        lanes_at = pl.ds(pl.multiple_of(dp * own + start, 128), 128)
        counts_row = jnp.where(
            from_here, valid_ref[image, :, lanes_at], valid_in[image, :, lanes_at]
        )
        masked = error * counts_row.T[:, 0:1]
        err_out[...] = err_out[...] + fold(error * masked)
        branch_out[at, :] = (masked * factor).astype(BF16)

    def turn(start):
        brancht_out[:, pl.ds(start, 128)] = branch_out[pl.ds(start, 128), :].T

    swaps = []
    for start in range(0, own, 128):
        finish(start)
        swaps.append(
            send(
                branch_out.at[pl.ds(start, 128)],
                branch_out.at[pl.ds(own + start, 128)],
                peers["core"],
            )
        )
        turn(start)
    for start, swap in zip(range(own, tokens, 128), swaps):
        swap.wait_recv()
        turn(start)
    turn2.wait()
    for copies in saved[2:]:
        for copy in copies:
            copy.wait()
    for copy in ff_saved:
        copy.wait()
    for copy in late:
        copy.wait()
    send.finish()
    x_move.finish()
    teacher_move.finish()


def forward_call(arrays, own_tokens, feat, lanes, main, qkv, mix, own, depth):
    tokens = 2 * own
    wide = (6 * feat + 127) // 128 * 128
    narrow = arrays[5].shape[1] - wide
    anywhere = pl.BlockSpec(memory_space=pl.ANY)
    local = pl.BlockSpec(memory_space=pltpu.VMEM)
    shapes = [
        ((4, depth, qkv + mix), BF16, anywhere),
        ((4, depth, 2 * main), BF16, anywhere),
        ((4, tokens, qkv), BF16, anywhere),
        ((4, tokens, mix), BF16, anywhere),
        ((4, tokens, main), BF16, anywhere),
        ((4, tokens, main), BF16, anywhere),
        ((depth, tokens), BF16, anywhere),
        ((depth, tokens), BF16, anywhere),
        ((depth, 256), BF16, anywhere),
        ((8, 1, tokens), F32, anywhere),
        ((tokens, 128), BF16, anywhere),
        ((tokens, 128), BF16, anywhere),
        ((own, depth), F32, anywhere),
        ((own, depth), BF16, anywhere),
        ((tokens, depth), BF16, local),
        ((depth, tokens), BF16, local),
        ((depth, own), BF16, local),
        ((16, depth), F32, local),
        ((8, depth), F32, local),
        ((8, 128), F32, local),
    ]
    return pl.pallas_call(
        functools.partial(forward_kernel, own_tokens),
        out_shape=[jax.ShapeDtypeStruct(shape, dtype) for shape, dtype, _ in shapes],
        in_specs=[anywhere] * 4 + [local] * 7 + [anywhere] * 2,
        out_specs=[spec for _, _, spec in shapes],
        scratch_shapes=[
            pltpu.VMEM((depth, 256), BF16),
            pltpu.VMEM((8, 1, tokens), F32),
            pltpu.VMEM((tokens, 128), BF16),
            pltpu.VMEM((tokens, 128), BF16),
            pltpu.VMEM((own, depth), F32),
            pltpu.VMEM((own, depth), BF16),
            pltpu.VMEM((depth, own), BF16),
            pltpu.VMEM((depth, own), BF16),
            pltpu.VMEM((2, 8, tokens), F32),
            pltpu.VMEM((4, 8, wide), F32),
            pltpu.VMEM((4, 8, narrow), F32),
            pltpu.VMEM((8, 8, 128), F32),
            pltpu.VMEM((4, depth, lanes), BF16),
            pltpu.VMEM((4, depth, 2 * main), BF16),
            pltpu.VMEM((2, depth, qkv + mix), BF16),
            pltpu.VMEM((2, tokens, qkv), BF16),
            pltpu.VMEM((4, tokens, mix), BF16),
            pltpu.VMEM((4, tokens, main), BF16),
            pltpu.VMEM((4, tokens, main), BF16),
            pltpu.VMEM((tokens, depth), BF16),
            pltpu.VMEM((tokens, depth), BF16),
            pltpu.VMEM((depth, tokens), BF16),
            pltpu.VMEM((tokens, depth), F32),
            pltpu.VMEM((own, depth), BF16),
            pltpu.VMEM((own, depth), BF16),
            pltpu.VMEM((own, depth), BF16),
            pltpu.VMEM((own, depth), BF16),
            pltpu.SemaphoreType.DMA((40,)),
            pltpu.SemaphoreType.DMA((72,)),
            pltpu.SemaphoreType.DMA((72,)),
            pltpu.SemaphoreType.DMA((5, 4)),
        ],
        compiler_params=pltpu.CompilerParams(
            collective_id=1, has_side_effects=True, vmem_limit_bytes=62 << 20
        ),
    )(*arrays)


def backward_kernel(
    branch2_ref,
    rest_ref,
    act_rest_ref,
    slope_rest_ref,
    lse_ref,
    feature_ref,
    spread_ref,
    rest_spread_ref,
    err_ref,
    count_ref,
    result_blocks,
    x_hbm,
    resid_hbm,
    norm1t_hbm,
    norm2t_hbm,
    branch2t_hbm,
    wpad_hbm,
    wff_hbm,
    triple_hbm,
    mixed_hbm,
    act_hbm,
    slope_hbm,
    grad_pieces,
    result_pieces,
    sums_out,
    bias_out,
    attn_out,
    ff_out,
    x_rows,
    grad_blocks,
    terms,
    terms_mine,
    terms_in,
    sums_in,
    bias_mine,
    bias_turn,
    bias_in,
    bias_plane,
    units_out,
    units_rest_out,
    heads_out,
    gattn,
    gff,
    wslot,
    kept,
    grad_pre,
    grad_rest,
    normt,
    brancht,
    branch1,
    part,
    give,
    got,
    grad_mid,
    dtriple,
    grad_mixed,
    grad_key,
    grad_value,
    inner_row,
    ra,
    rb,
    r1,
    r2,
    rz,
    ry,
    rx,
    rzl,
    rzh,
    rfx,
    rfy,
    local_sems,
    send_sems,
    recv_sems,
    shuffle_sems,
):
    peers = neighbours()
    feat = 2 * attn_out.shape[1]
    half = feat // 2
    depth = 4 * feat
    tokens = branch2_ref.shape[0]
    own = tokens // 2
    main = gff.shape[2] // 2
    qkv = triple_hbm.shape[2]
    send = Sender(send_sems, recv_sems)
    keep = Copier(local_sems)

    def rows(block, low=0, size=None):
        return pl.ds(block * feat + low, feat if size is None else size)

    def load_ff(s):
        slot = s % 2
        return [
            keep(wff_hbm.at[s], wslot.at[slot]),
            keep(act_hbm.at[s], kept.at[slot, :, pl.ds(0, main)]),
            keep(slope_hbm.at[s], kept.at[slot, :, pl.ds(main, main)]),
        ]

    def load_attn(s):
        slot = s % 2
        return [
            keep(wpad_hbm.at[s], wslot.at[slot]),
            keep(triple_hbm.at[s], kept.at[slot, :, pl.ds(0, qkv)]),
            keep(mixed_hbm.at[s], kept.at[slot, :, pl.ds(qkv, grad_mixed.shape[1])]),
        ]

    loads = {3: load_ff(3)}
    turns = [keep(norm2t_hbm, normt), keep(branch2t_hbm, brancht)]
    loads[2] = load_ff(2)
    load_late = [keep(resid_hbm, grad_mid), keep(x_hbm, x_rows)]
    meet()
    result_move = Shuffle(shuffle_sems.at[0], shuffle_sems.at[1], shuffle_sems.at[2, 0])
    grad_move = Shuffle(shuffle_sems.at[3], shuffle_sems.at[4], shuffle_sems.at[2, 1])
    cy, cx, zl, zh = ([None] * 4 for _ in range(4))
    ca, cb, c1, c2, cz = ([None] * 4 for _ in range(5))

    def add_into(target, at, *sources):
        size = at.size

        @pl.loop(0, size // 16)
        def _(step):
            here = pl.ds(pl.multiple_of(at.start + step * 16, 16), 16)
            there = pl.ds(pl.multiple_of(step * 16, 16), 16)
            total = target[here, :].astype(F32)
            for source in sources:
                total = total + source[there, :].astype(F32)
            target[here, :] = total.astype(BF16)

    def column_sum(values):
        return jnp.sum(values.astype(F32), axis=0, keepdims=True)

    def ff_compute(s):
        slot = s % 2
        for copy in loads[s]:
            copy.wait()
        units_out[s] = jnp.zeros((1, main), F32)

        def block(at):
            grad = mm(branch2_ref[at, :], wslot[slot, :, main : 2 * main])
            low = (grad * kept[slot, at, main:].astype(F32)).astype(BF16)
            grad_pre[at, :] = low
            units_out[s] = units_out[s] + column_sum(low)
            values = mm_nt(low, wslot[slot, :, :main])
            part[at, :] = values if s == 3 else part[at, :] + values

        each_rows(tokens, own, block)
        if s == 3:
            for copy in turns:
                copy.wait()

        def grads(at):
            gff[s, at, :main] = mm(normt[at, :], grad_pre[...]).astype(BF16)
            gff[s, at, main:] = mm(brancht[at, :], kept[slot, :, :main]).astype(BF16)

        each_rows(depth, 2 * feat, grads)
        cy[s] = [
            send(gff.at[s, rows(k, 0, half)], ry.at[s, k - 2], peers["y"]) for k in (2, 3)
        ]
        cx[s] = [
            send(gff.at[s, rows(k, half, half)], rx.at[s, k // 2], peers["x"]) for k in (1, 3)
        ]
        if s >= 2:
            loads[s - 2] = load_ff(s - 2)

    def rest_compute():
        units_rest_out[...] = jnp.zeros_like(units_rest_out)

        def block(at):
            grad = mm(branch2_ref[at, :], rest_ref[:, 128:])
            low = (grad * slope_rest_ref[at, :].astype(F32)).astype(BF16)
            grad_pre[at, :128] = low
            units_rest_out[...] = units_rest_out[...] + column_sum(low)
            return part[at, :] + mm_nt(low, rest_ref[:, :128])

        give[...] = block(pl.ds(own, own)).astype(BF16)
        swap = send(give, got, peers["core"])
        part[pl.ds(0, own), :] = block(pl.ds(0, own))

        def grads(at):
            grad_rest[at, :128] = mm(normt[at, :], grad_pre[:, :128]).astype(BF16)
            grad_rest[at, 128:] = mm(brancht[at, :], act_rest_ref[...]).astype(BF16)

        each_rows(depth, 2 * feat, grads)
        return swap

    def ff_add(s):
        for copy in cy[s] + cx[s]:
            copy.wait_recv()
        last = s == 3
        if not last:
            for copy in zl[s] + zh[s]:
                copy.wait_recv()
        lows, highs = [], []
        for i, k in enumerate((0, 1)):
            piece = rows(k, 0, half)
            add_into(gff.at[s], piece, ry.at[s, i], *([] if last else [rzl.at[s, i]]))
            lows.append((piece, i))
        for i, k in enumerate((0, 2)):
            piece = rows(k, half, half)
            add_into(gff.at[s], piece, rx.at[s, i], *([] if last else [rzh.at[s, i]]))
            highs.append((piece, i))
        if s:
            zl[s - 1] = [
                send(gff.at[s, piece], rzl.at[s - 1, i], peers["prev"]) for piece, i in lows
            ]
            zh[s - 1] = [
                send(gff.at[s, piece], rzh.at[s - 1, i], peers["prev"]) for piece, i in highs
            ]

    def attn_compute(s):
        slot = s % 2
        for copy in attn_loads[s]:
            copy.wait()

        def back_out(at):
            grad_mixed[at, :] = mm(branch1[at, :], wslot[slot, :, qkv:]).astype(BF16)

        each_rows(tokens, tokens, back_out)
        scale = HD**-0.5
        for h in range(qkv // 384):
            query_at, key_at, value_at = (pl.ds((3 * h + j) * 128, 128) for j in range(3))
            mix_at = pl.ds(h * 128, 128)
            value_of_mix = pl.ds(qkv + h * 128, 128)
            key_turned = kept[slot, :, key_at].T
            product = grad_mixed[:, mix_at].astype(F32) * kept[slot, :, value_of_mix].astype(F32)
            inner_row[...] = jnp.sum(product.T, axis=0, keepdims=True)
            grad_key[...] = jnp.zeros_like(grad_key)
            grad_value[...] = jnp.zeros_like(grad_value)

            def head(at, h=h, query_at=query_at, key_at=key_at, value_at=value_at,
                     mix_at=mix_at, key_turned=key_turned):
                query = kept[slot, at, query_at]
                grad = grad_mixed[at, mix_at]
                scores = mm_nt(kept[slot, :, key_at], query)
                weights = jnp.exp2(scores * (scale * LOG2E) - lse_ref[2 * s + h, :, at])
                grad_soft = mm_nt(kept[slot, :, value_at], grad)
                grad_raw = (weights * (grad_soft - inner_row[:, at]) * scale).astype(BF16)
                grad_value[...] += mm(weights.astype(BF16), grad)
                grad_key[...] += mm(grad_raw, query)
                dtriple[at, query_at] = mm(key_turned, grad_raw).T.astype(BF16)

            each_rows(tokens, own, head)
            dtriple[:, key_at] = grad_key[...].astype(BF16)
            dtriple[:, value_at] = grad_value[...].astype(BF16)
        heads_out[s] = jnp.zeros((1, qkv), F32)

        def back_in(at):
            values = mm_nt(dtriple[at, :], wslot[slot, :, :qkv])
            heads_out[s] = heads_out[s] + column_sum(dtriple[at, :])
            return values if s == 3 else part[at, :] + values

        swap = None
        if s:
            for at in (pl.ds(0, own), pl.ds(own, own)):
                part[at, :] = back_in(at)
        else:
            give[...] = back_in(pl.ds(own, own)).astype(BF16)
            swap = send(give, got, peers["core"])
            part[pl.ds(0, own), :] = back_in(pl.ds(0, own))

        def grads(at):
            first = mm(normt[at, :], dtriple[...]).astype(BF16)
            second = mm(brancht[at, :], kept[slot, :, qkv:]).astype(BF16)
            tiles = [0.0] * (gattn.shape[2] // 128)
            for j in range((qkv + second.shape[1]) // 256):
                low, to = 2 * HD * j // 128 * 128, 256 * j
                block = first[:, to : to + 256] if to < qkv else second[:, to - qkv : to - qkv + 256]
                moved = mm_nt(block, spread_ref[low : low + 256, to : to + 256])
                for i in (0, 1):
                    tiles[low // 128 + i] += moved[:, 128 * i : 128 * i + 128]
            tiles[-1] += mm_nt(grad_rest[at, :], rest_spread_ref[s])
            gattn[s, at, :] = jnp.concatenate(tiles, axis=1).astype(BF16)

        each_rows(depth, 2 * feat, grads)
        ca[s] = send(gattn.at[s, rows(3, 0, half)], ra.at[s], peers["y"])
        cb[s] = send(gattn.at[s, rows(3, half, half)], rb.at[s], peers["x"])
        if s >= 2:
            attn_loads[s - 2] = load_attn(s - 2)
        return swap

    def attn_plane(s):
        ca[s].wait_recv()
        add_into(gattn.at[s], rows(1, 0, half), ra.at[s])
        c1[s] = send(gattn.at[s, rows(1)], r1.at[s], peers["x"])
        cb[s].wait_recv()
        add_into(gattn.at[s], rows(2, half, half), rb.at[s])
        c2[s] = send(gattn.at[s, rows(2)], r2.at[s], peers["y"])

    def attn_ring(s):
        c1[s].wait_recv()
        c2[s].wait_recv()
        if s < 3:
            cz[s].wait_recv()
        add_into(gattn.at[s], rows(0), r1.at[s], r2.at[s], *([rz.at[s]] if s < 3 else []))
        if s:
            cz[s - 1] = send(gattn.at[s, rows(0)], rz.at[s - 1], peers["prev"])

    terms[...] = jnp.zeros_like(terms)

    def add_term(index, values):
        terms[index] = terms[index] + fold(values)

    result_move.collect(result_blocks, result_pieces)
    ff_compute(3)
    ff_compute(2)
    ff_compute(1)
    ff_add(3)
    ff_compute(0)
    attn_loads = {3: load_attn(3), 2: load_attn(2)}
    swap1 = rest_compute()
    load_norm = keep(norm1t_hbm, normt)
    swap1.wait_recv()
    for copy in load_late:
        copy.wait()

    def mid(at):
        normed, inv_scale = norm_stats(grad_mid[at, :])
        grad_norm = part[at, :] + got[at, :].astype(F32)
        add_term(2, grad_norm * normed)
        add_term(3, grad_norm)
        scaled = grad_norm * feature_ref[2:3]
        first = jnp.mean(scaled, axis=-1, keepdims=True)
        second = jnp.mean(scaled * normed, axis=-1, keepdims=True)
        grad = branch2_ref[at, :].astype(F32)
        grad = grad + inv_scale * (scaled - first - normed * second)
        grad_mid[at, :] = grad
        low = grad.astype(BF16)
        branch1[at, :] = low
        add_term(4, low.astype(F32))
        add_term(5, branch2_ref[at, :].astype(F32))

    each_rows(own, 64, mid)
    swap2 = send(branch1.at[pl.ds(0, own)], branch1.at[pl.ds(own, own)], peers["core"])
    swap2.wait_recv()
    load_norm.wait()
    transpose_into(brancht, branch1)
    attn_compute(3)
    ff_add(2)
    attn_compute(2)
    attn_plane(3)
    attn_compute(1)
    attn_plane(2)
    attn_ring(3)
    ff_add(1)
    swap1.wait_send()
    swap3 = attn_compute(0)
    attn_plane(1)
    attn_ring(2)
    attn_plane(0)
    swap3.wait_recv()

    def last(at):
        normed, inv_scale = norm_stats(x_rows[at, :].astype(F32))
        grad_norm = part[at, :] + got[at, :].astype(F32)
        add_term(0, grad_norm * normed)
        add_term(1, grad_norm)
        scaled = grad_norm * feature_ref[0:1]
        first = jnp.mean(scaled, axis=-1, keepdims=True)
        second = jnp.mean(scaled * normed, axis=-1, keepdims=True)
        grad = grad_mid[at, :] + inv_scale * (scaled - first - normed * second)
        grad_blocks[:, at] = grad.astype(BF16).T

    each_rows(own, 128, last)
    grad_move.collect(grad_blocks, grad_pieces)
    terms_mine[...] = jnp.zeros_like(terms_mine)
    bias_mine[...] = jnp.zeros_like(bias_mine)
    for i in range(7):
        if i < 6:
            row_sum = jnp.sum(terms[i], axis=0, keepdims=True)
        else:
            err = jnp.sum(jnp.sum(err_ref[...], axis=0, keepdims=True), axis=1, keepdims=True)
            row_sum = jnp.broadcast_to(err, (1, depth))
        for k in range(4):
            terms_mine[k, i : i + 1, :] = row_sum[:, k * feat : (k + 1) * feat]
    wide = bias_mine.shape[2]
    for s in range(4):
        bias_mine[s, 0:1, :qkv] = heads_out[s]
        bias_mine[s, 0:1, qkv : qkv + main] = units_out[s]
        bias_mine[s, 0:1, qkv + main :] = units_rest_out[...]
    dp, row, col = place()
    ring_two = (dp, row, 3 - col)
    sides = ((1, "x"), (2, "y"), (3, "diagonal"))
    term_sends = [send(terms_mine.at[k], terms_in.at[k - 1], peers[name]) for k, name in sides]
    bias_sends = [
        send(bias_mine.at[s], bias_turn.at[s - 1], peer)
        for s, peer in ((1, peers["prev"]), (2, ring_two), (3, peers["next"]))
    ]
    ff_add(0)
    end_low = send(gff.at[0, rows(1, 0, half)], rfx, peers["x"])
    end_high = send(gff.at[0, rows(2, half, half)], rfy, peers["y"])
    attn_ring(1)
    for copy in term_sends + bias_sends:
        copy.wait_recv()
    terms_mine[0] = terms_mine[0] + terms_in[0] + terms_in[1] + terms_in[2]
    sum_sends = [
        send(terms_mine.at[0], sums_in.at[i], peer) for i, peer in enumerate(images_group())
    ]
    bias_plane[...] = bias_mine[0]
    for s in (1, 2, 3):
        bias_plane[s : s + 1, :] = bias_turn[s - 1, 0:1, :]
    plane_sends = [send(bias_plane, bias_in.at[k - 1], peers[name]) for k, name in sides]
    end_low.wait_recv()
    end_high.wait_recv()
    add_into(gff.at[0], rows(0, 0, half), rfx)
    add_into(gff.at[0], rows(0, half, half), rfy)
    quarter = feat // 2
    keep_at = pl.ds(pl.multiple_of(dp * quarter, 16), quarter)
    give_at = pl.ds(pl.multiple_of((1 - dp) * quarter, 16), quarter)
    done = [keep(gff.at[0, keep_at], ff_out.at[0])]
    pair_sends = [send(gff.at[0, give_at], ff_out.at[1], peers["core"])]
    for copy in plane_sends + sum_sends:
        copy.wait_recv()
    bias_out[0] = bias_plane[...] + bias_in[0] + bias_in[1] + bias_in[2]
    pair_sends.append(send(bias_out.at[0], bias_out.at[1], peers["core"]))
    total = terms_mine[0]
    for i in range(7):
        total = total + sums_in[i]
    sums_out[...] = total
    sums_out[7:8, :] = total[6:7] / (count_ref[0:1, 0:1] * depth)
    attn_ring(0)
    done.append(keep(gattn.at[0, keep_at], attn_out.at[0]))
    pair_sends.append(send(gattn.at[0, give_at], attn_out.at[1], peers["core"]))
    for copy in pair_sends:
        copy.wait_recv()
    for copy in done:
        copy.wait()
    result_move.arrive()
    grad_move.arrive()
    for copy in send.copies:
        if copy is not swap1:
            copy.wait_send()
    result_move.finish()
    grad_move.finish()


def backward_call(arrays, feat, lanes, main, qkv, mix, own, depth):
    tokens = 2 * own
    half = feat // 2
    narrow = qkv + main + 128
    anywhere = pl.BlockSpec(memory_space=pl.ANY)
    local = pl.BlockSpec(memory_space=pltpu.VMEM)
    shapes = [
        ((2, feat, tokens), BF16, anywhere),
        ((2, feat, tokens), BF16, anywhere),
        ((8, feat), F32, local),
        ((2, 8, narrow), F32, local),
        ((2, half, lanes), BF16, anywhere),
        ((2, half, 2 * main), BF16, anywhere),
    ]
    return pl.pallas_call(
        backward_kernel,
        out_shape=[jax.ShapeDtypeStruct(shape, dtype) for shape, dtype, _ in shapes],
        in_specs=[local] * 10 + [anywhere] * 12,
        out_specs=[spec for _, _, spec in shapes],
        scratch_shapes=[
            pltpu.VMEM((own, depth), BF16),
            pltpu.VMEM((depth, own), BF16),
            pltpu.VMEM((6, 16, depth), F32),
            pltpu.VMEM((4, 8, feat), F32),
            pltpu.VMEM((3, 8, feat), F32),
            pltpu.VMEM((7, 8, feat), F32),
            pltpu.VMEM((4, 8, narrow), F32),
            pltpu.VMEM((3, 8, narrow), F32),
            pltpu.VMEM((3, 8, narrow), F32),
            pltpu.VMEM((8, narrow), F32),
            pltpu.VMEM((4, 1, main), F32),
            pltpu.VMEM((1, 128), F32),
            pltpu.VMEM((4, 1, qkv), F32),
            pltpu.VMEM((4, depth, lanes), BF16),
            pltpu.VMEM((4, depth, 2 * main), BF16),
            pltpu.VMEM((2, depth, 2 * main), BF16),
            pltpu.VMEM((2, tokens, qkv + mix), BF16),
            pltpu.VMEM((tokens, main), BF16),
            pltpu.VMEM((depth, 256), BF16),
            pltpu.VMEM((depth, tokens), BF16),
            pltpu.VMEM((depth, tokens), BF16),
            pltpu.VMEM((tokens, depth), BF16),
            pltpu.VMEM((tokens, depth), F32),
            pltpu.VMEM((own, depth), BF16),
            pltpu.VMEM((own, depth), BF16),
            pltpu.VMEM((own, depth), F32),
            pltpu.VMEM((tokens, qkv), BF16),
            pltpu.VMEM((tokens, mix), BF16),
            pltpu.VMEM((tokens, 128), F32),
            pltpu.VMEM((tokens, 128), F32),
            pltpu.VMEM((1, tokens), F32),
            pltpu.VMEM((4, half, lanes), BF16),
            pltpu.VMEM((4, half, lanes), BF16),
            pltpu.VMEM((4, feat, lanes), BF16),
            pltpu.VMEM((4, feat, lanes), BF16),
            pltpu.VMEM((3, feat, lanes), BF16),
            pltpu.VMEM((4, 2, half, 2 * main), BF16),
            pltpu.VMEM((4, 2, half, 2 * main), BF16),
            pltpu.VMEM((3, 2, half, 2 * main), BF16),
            pltpu.VMEM((3, 2, half, 2 * main), BF16),
            pltpu.VMEM((half, 2 * main), BF16),
            pltpu.VMEM((half, 2 * main), BF16),
            pltpu.SemaphoreType.DMA((32,)),
            pltpu.SemaphoreType.DMA((104,)),
            pltpu.SemaphoreType.DMA((104,)),
            pltpu.SemaphoreType.DMA((5, 4)),
        ],
        compiler_params=pltpu.CompilerParams(
            collective_id=2, has_side_effects=True, vmem_limit_bytes=63 << 20
        ),
    )(*arrays)
def on_chip(
    layer_input,
    teacher,
    valid,
    proj_in,
    bias_query,
    bias_value,
    proj_out,
    bias_out,
    norm1_gain,
    norm1_shift,
    norm2_gain,
    norm2_shift,
    w_up,
    bias_up,
    w_down,
    bias_down,
):
    core = lax.axis_index("dp")
    first = core == 0
    cols = lax.axis_size("col")
    feat = layer_input.shape[1]
    images = layer_input.shape[0] // SEQ
    half_seq = (SEQ + 255) // 256 * 128
    pad_seq = 2 * half_seq
    units = w_up.shape[1] // 2
    width = proj_out.shape[0] // 2
    heads = width // HD
    main = units // 128 * 128
    rest = units - main
    at = 4 * width
    lanes = (at + 2 * rest + 127) // 128 * 128
    qkv, mix = 3 * heads * 128, heads * 128

    def core_half(values, axis):
        low, high = jnp.split(values, 2, axis=axis)
        return jnp.where(first, low, high)

    def pieces(values):
        turned = values.T
        second = turned[:, SEQ:]
        return turned, jnp.pad(second, ((0, 0), (0, pad_seq - SEQ)))

    up_half, down_half = core_half(w_up, 1), core_half(w_down, 0).T
    attn_shard = jnp.concatenate(
        [
            core_half(proj_in, 1),
            core_half(proj_out, 0).T,
            up_half[:, main:],
            down_half[:, main:],
            jnp.zeros((feat, lanes - at - 2 * rest), jnp.bfloat16),
        ],
        axis=1,
    )
    ff_shard = jnp.concatenate([up_half[:, :main], down_half[:, :main]], axis=1)
    lane = np.arange(lanes)
    spread_at = np.where(lane < at, lane // HD * 128 + lane % HD, -1)
    spread = jnp.asarray(spread_at[:, None] == np.arange(qkv + mix), jnp.bfloat16)
    tail = lane[-128:]
    part = np.arange(cols)[:, None]
    up_at = np.where((tail >= at) & (tail < at + rest), tail - at + part * rest, -1)
    down_at = np.where(
        (tail >= at + rest) & (tail < at + 2 * rest), tail - at - rest + part * rest + 128, -1
    )
    spot = np.arange(256)
    rest_spread = (up_at[..., None] == spot) | (down_at[..., None] == spot)
    rest_spread = jnp.asarray(rest_spread, jnp.bfloat16)

    key_lane = jnp.asarray(np.arange(qkv) % 384 == 128 + HD, jnp.float32)[None]

    one_lane = jnp.asarray(np.arange(qkv) % 384 == HD, jnp.float32)[None]
    source = np.arange(2 * width)
    bias_at = source % width // HD * 384 + source // width * 256 + source % HD
    bias_spread = jnp.asarray(bias_at[:, None] == np.arange(qkv), jnp.bfloat16)
    wide = (6 * feat + 127) // 128 * 128
    narrow = (2 * width + units + 127) // 128 * 128
    vectors = [
            norm1_gain,
            norm1_shift,
            norm2_gain,
            norm2_shift,
            bias_out,
            bias_down,
            jnp.zeros((wide - 6 * feat,), jnp.bfloat16),
            core_half(bias_query, 0),
            core_half(bias_value, 0),
            core_half(bias_up, 0),
            jnp.zeros((narrow - 2 * width - units,), jnp.bfloat16),
        ]
    params = jnp.concatenate(
        [jnp.broadcast_to(v.astype(jnp.float32)[None], (8, v.shape[0])) for v in vectors], axis=1
    )
    valid_rows = jnp.pad(valid.reshape(images, SEQ), ((0, 0), (0, pad_seq - SEQ)))
    valid_rows = jnp.broadcast_to(valid_rows.astype(jnp.float32)[:, None], (images, 8, pad_seq))
    sizes = (feat, lanes, main, qkv, mix, half_seq, 4 * feat)
    (
        wpad, wff, triple, mixed, act, slope, norm1t, norm2t, rest_weight, lse, act_rest,
        slope_rest, resid1, x_rows, branch2, branch2t, result, err_rows, features, counted,
    ) = forward_call(
        (
            *pieces(layer_input), *pieces(teacher), valid_rows, params, key_lane, one_lane, bias_spread, spread, rest_spread, attn_shard, ff_shard,
        ),
        layer_input.shape[0],
        *sizes,
    )
    grad_pieces, result_pieces, sums, bias_rows, attn_sum, ff_sum = backward_call(
        (
            branch2, rest_weight, act_rest, slope_rest, lse, features, spread, rest_spread,
            err_rows, counted, result, x_rows, resid1, norm1t, norm2t, branch2t, wpad,
            wff, triple, mixed, act, slope,
        ),
        *sizes,
    )

    def rows_of(values):
        return jnp.concatenate([values[i][:, :SEQ] for i in range(images)], axis=1).T

    def both(keep, got, axis=-1):
        return jnp.concatenate(
            [jnp.where(first, keep, got), jnp.where(first, got, keep)], axis=axis
        ).astype(jnp.float32)

    def up_of(i):
        return jnp.concatenate([ff_sum[i][:, :main], attn_sum[i][:, at : at + rest]], axis=1)

    def down_of(i):
        block = [ff_sum[i][:, main:], attn_sum[i][:, at + rest : at + 2 * rest]]
        return jnp.concatenate(block, axis=1).T

    main_rows = jnp.sum(bias_rows[:, :cols, : qkv + main], axis=1)
    head_rows = main_rows[:, :qkv].reshape(2, heads, 3, 128)[..., :HD]
    tail_rows = bias_rows[:, :cols, qkv + main :]
    tail_rows = sum(tail_rows[:, s, s * rest : (s + 1) * rest] for s in range(cols))
    unit_rows = jnp.concatenate([main_rows[:, qkv:], tail_rows], axis=1)
    return (
        rows_of(result_pieces),
        sums[7, 0],
        rows_of(grad_pieces).astype(jnp.float32),
        both(attn_sum[0][:, : 3 * width], attn_sum[1][:, : 3 * width])[None],
        both(head_rows[0, :, 0].reshape(width), head_rows[1, :, 0].reshape(width)),
        both(head_rows[0, :, 2].reshape(width), head_rows[1, :, 2].reshape(width)),
        both(attn_sum[0][:, 3 * width : at].T, attn_sum[1][:, 3 * width : at].T, 0)[:, None],
        sums[4],
        sums[0],
        sums[1],
        sums[2],
        sums[3],
        both(up_of(0), up_of(1))[None],
        both(unit_rows[0], unit_rows[1]),
        both(down_of(0), down_of(1), 0)[:, None],
        sums[5],
    )


def one_image_a_chip(mesh, tokens):
    sizes = mesh.shape
    pairs = sizes["dp"] == 2 and sizes["row"] == 4 and sizes["col"] == 4
    return pairs and tokens == SEQ * sizes["row"] * sizes["col"]


def solution(mesh):
    placed = (
        P(("dp", "col"), "row"),
        P(("dp", "col"), "row"),
        P(("dp", "col")),
        P("row", "col"),
        P("col"),
        P("col"),
        P("col", "row"),
        P("row"),
        P("row"),
        P("row"),
        P("row"),
        P("row"),
        P("row", "col"),
        P("col"),
        P("col", "row"),
        P("row"),
    )
    returned = (
            P(("dp", "col"), "row"),
            P(),
            P(("dp", "col"), "row"),
            P("row", "dp", "col"),
            P("col"),
            P("col"),
            P("col", "row", "dp"),
            P("row"),
            P("row"),
            P("row"),
            P("row"),
            P("row"),
            P("row", "dp", "col"),
            P("col"),
            P("col", "row", "dp"),
            P("row"),
        )

    def whole(layer_input, *others):
        body = on_chip if one_image_a_chip(mesh, layer_input.shape[0]) else on_device
        return jax.shard_map(
            body, mesh=mesh, in_specs=placed, out_specs=returned, check_vma=False
        )(layer_input, *others)

    return whole
```

```python
import functools

import jax
import jax.numpy as jnp
import numpy as np
from jax import lax
from jax.experimental import pallas as pl
from jax.experimental.pallas import tpu as pltpu
from jax.sharding import PartitionSpec as P

D = 1152
H = 16
HD = 72
FF = 4304
SEQ = 729


EPS = 1e-06


def feature_totals(left, right):
    return lax.psum(
        (jnp.sum(left, axis=-1, keepdims=True), jnp.sum(right, axis=-1, keepdims=True)), "row"
    )


def norm_forward(values, gain, shift):
    first_sum, second_sum = feature_totals(values, values * values)
    mean_rows = first_sum / D
    var_rows = second_sum / D - mean_rows * mean_rows
    inv_scale = lax.rsqrt(var_rows + EPS)
    normed = (values - mean_rows) * inv_scale
    return (normed, inv_scale, normed * gain + shift)


def norm_backward(grad_out, normed, inv_scale, gain):
    grad_normed = grad_out * gain
    first_sum, second_sum = feature_totals(grad_normed, grad_normed * normed)
    return inv_scale * (grad_normed - first_sum / D - normed * second_sum / D)


def first_section(local_rows, weight):
    gathered = lax.all_gather(local_rows, "col", axis=0, tiled=True)
    share_rows = gathered.shape[0] // lax.axis_size("row")

    def partial_term(row_start, row_count):
        return jnp.dot(gathered, weight, preferred_element_type=jnp.float32)

    result = lax.psum_scatter(
        partial_term(jnp.int32(0), lax.axis_size("row") * share_rows),
        "row",
        scatter_dimension=0,
        tiled=True,
    )
    return (gathered, result)


def second_section(quarter_rows, weight):
    gathered = lax.all_gather(quarter_rows, "row", axis=0, tiled=True)
    share_rows = gathered.shape[0] // lax.axis_size("col")

    def partial_term(row_start, row_count):
        return jnp.dot(gathered, weight, preferred_element_type=jnp.float32)

    result = lax.psum_scatter(
        partial_term(jnp.int32(0), lax.axis_size("col") * share_rows),
        "col",
        scatter_dimension=0,
        tiled=True,
    )
    return (gathered, result)


def second_section_back(grad_local, gathered, weight):
    grad_all = lax.all_gather(grad_local, "col", axis=0, tiled=True)
    grad_weight = lax.dot_general(
        gathered, grad_all, (((0,), (0,)), ((), ())), preferred_element_type=jnp.float32
    )
    share_rows = grad_all.shape[0] // lax.axis_size("row")

    def partial_term(row_start, row_count):
        return lax.dot_general(
            grad_all, weight, (((1,), (1,)), ((), ())), preferred_element_type=jnp.float32
        )

    result = lax.psum_scatter(
        partial_term(jnp.int32(0), lax.axis_size("row") * share_rows),
        "row",
        scatter_dimension=0,
        tiled=True,
    )
    return (grad_weight, result)


def first_section_back(grad_quarter, gathered, weight):
    grad_all = lax.all_gather(grad_quarter, "row", axis=0, tiled=True)
    grad_weight = lax.dot_general(
        gathered, grad_all, (((0,), (0,)), ((), ())), preferred_element_type=jnp.float32
    )
    share_rows = grad_all.shape[0] // lax.axis_size("col")

    def partial_term(row_start, row_count):
        return lax.dot_general(
            grad_all, weight, (((1,), (1,)), ((), ())), preferred_element_type=jnp.float32
        )

    result = lax.psum_scatter(
        partial_term(jnp.int32(0), lax.axis_size("col") * share_rows).astype(jnp.bfloat16),
        "col",
        scatter_dimension=0,
        tiled=True,
    ).astype(jnp.float32)
    return (grad_weight, result)


def attend(triple_img):
    score_scale = HD ** (-0.5)
    query_rows = triple_img[:, :, 0]
    key_rows = triple_img[:, :, 1]
    value_rows = triple_img[:, :, 2]
    raw_scores = jnp.einsum(
        "qhd,khd->hqk", query_rows, key_rows, preferred_element_type=jnp.float32
    )
    scaled = raw_scores * score_scale
    peak_score = jnp.max(scaled, axis=-1, keepdims=True)
    exp_scores = jnp.exp(scaled - peak_score)
    exp_total = jnp.sum(exp_scores, axis=-1, keepdims=True)
    soft_weights = (exp_scores / exp_total).astype(jnp.bfloat16)
    mixed_rows = jnp.einsum(
        "hqk,khd->qhd", soft_weights, value_rows, preferred_element_type=jnp.float32
    )
    return (mixed_rows.astype(jnp.bfloat16), peak_score + jnp.log(exp_total))


def attend_back(packed):
    triple_img, log_total, grad_mixed = packed
    score_scale = HD ** (-0.5)
    query_rows = triple_img[:, :, 0]
    key_rows = triple_img[:, :, 1]
    value_rows = triple_img[:, :, 2]
    raw_scores = jnp.einsum(
        "qhd,khd->hqk", query_rows, key_rows, preferred_element_type=jnp.float32
    )
    soft_weights = jnp.exp(raw_scores * score_scale - log_total)
    weights_low = soft_weights.astype(jnp.bfloat16)
    grad_values = jnp.einsum(
        "hqk,qhd->khd", weights_low, grad_mixed, preferred_element_type=jnp.float32
    )
    grad_soft = jnp.einsum(
        "qhd,khd->hqk", grad_mixed, value_rows, preferred_element_type=jnp.float32
    )
    inner_prod = jnp.sum(grad_soft * soft_weights, axis=-1, keepdims=True)
    grad_raw = (score_scale * soft_weights * (grad_soft - inner_prod)).astype(jnp.bfloat16)
    grad_query = jnp.einsum("hqk,khd->qhd", grad_raw, key_rows, preferred_element_type=jnp.float32)
    grad_keys = jnp.einsum("hqk,qhd->khd", grad_raw, query_rows, preferred_element_type=jnp.float32)
    return jnp.stack([grad_query, grad_keys, grad_values], axis=2).astype(jnp.bfloat16)


def on_device(
    layer_input,
    teacher,
    valid,
    proj_in,
    bias_query,
    bias_value,
    proj_out,
    bias_out,
    norm1_gain,
    norm1_shift,
    norm2_gain,
    norm2_shift,
    w_up,
    bias_up,
    w_down,
    bias_down,
):
    heads_here = H // lax.axis_size("col")
    head_width = heads_here * HD
    feat_here = layer_input.shape[1]
    units_here = w_up.shape[1]
    gain_one = norm1_gain.astype(jnp.float32)
    gain_two = norm2_gain.astype(jnp.float32)
    residual_in = layer_input.astype(jnp.float32)
    normed1, scale1, mid_one = norm_forward(residual_in, gain_one, norm1_shift.astype(jnp.float32))
    norm1_all, projected = first_section(mid_one.astype(jnp.bfloat16), proj_in)
    quarter = projected.shape[0]
    images = quarter // SEQ
    bias_shift = jnp.stack(
        [
            bias_query.astype(jnp.float32).reshape(heads_here, HD),
            jnp.zeros((heads_here, HD), jnp.float32),
            bias_value.astype(jnp.float32).reshape(heads_here, HD),
        ],
        axis=1,
    )
    triple = (projected.reshape(quarter, heads_here, 3, HD) + bias_shift).astype(jnp.bfloat16)
    triple_imgs = triple.reshape(images, SEQ, heads_here, 3, HD)
    mixed_imgs, log_totals = lax.map(attend, triple_imgs)
    mixed_all, attn_part = second_section(mixed_imgs.reshape(quarter, head_width), proj_out)
    resid1 = residual_in + attn_part + bias_out.astype(jnp.float32)
    normed2, scale2, mid_two = norm_forward(resid1, gain_two, norm2_shift.astype(jnp.float32))
    norm2_all, pre_part = first_section(mid_two.astype(jnp.bfloat16), w_up)
    pre = pre_part + bias_up.astype(jnp.float32)
    activated, gelu_pull = jax.vjp(lambda entry: jax.nn.gelu(entry, approximate=True), pre)
    act_all, down_part = second_section(activated.astype(jnp.bfloat16), w_down)
    result = resid1 + down_part + bias_down.astype(jnp.float32)
    mask_rows = valid.astype(jnp.float32)
    error_rows = result - teacher.astype(jnp.float32)
    err_part = jnp.sum(mask_rows[:, None] * error_rows * error_rows)
    count_part = jnp.sum(mask_rows) / lax.axis_size("row")
    err_total, valid_count = lax.psum((err_part, count_part), ("dp", "row", "col"))
    loss_value = err_total / (valid_count * D)
    tokens_all = layer_input.shape[0] * lax.axis_size("dp") * lax.axis_size("col")
    factor = tokens_all / (2.0 * valid_count)
    grad_result = 2.0 * error_rows * (mask_rows[:, None] * factor)
    grad_branch2 = grad_result.astype(jnp.bfloat16)
    grad_w_down, grad_act = second_section_back(grad_branch2, act_all, w_down)
    grad_pre = gelu_pull(grad_act)[0].astype(jnp.bfloat16)
    grad_w_up, grad_norm2 = first_section_back(grad_pre, norm2_all, w_up)
    grad_resid1 = grad_result + norm_backward(grad_norm2, normed2, scale2, gain_two)
    grad_branch1 = grad_resid1.astype(jnp.bfloat16)
    grad_proj_out, grad_mixed = second_section_back(grad_branch1, mixed_all, proj_out)
    grad_mixed_imgs = grad_mixed.astype(jnp.bfloat16).reshape(images, SEQ, heads_here, HD)
    grad_triple = lax.map(attend_back, (triple_imgs, log_totals, grad_mixed_imgs))
    grad_triple = grad_triple.reshape(quarter, heads_here, 3, HD)
    grad_proj_in, grad_norm1 = first_section_back(
        grad_triple.reshape(quarter, 3 * head_width), norm1_all, proj_in
    )
    grad_input = grad_resid1 + norm_backward(grad_norm1, normed1, scale1, gain_one)
    row_at = lax.axis_index("row") * feat_here
    col_at = lax.axis_index("col") * head_width
    feature_terms = jnp.stack(
        [
            jnp.sum(grad_norm1 * normed1, axis=0),
            jnp.sum(grad_norm1, axis=0),
            jnp.sum(grad_norm2 * normed2, axis=0),
            jnp.sum(grad_norm2, axis=0),
            jnp.sum(grad_branch1.astype(jnp.float32), axis=0),
            jnp.sum(grad_branch2.astype(jnp.float32), axis=0),
        ]
    )
    feature_full = lax.dynamic_update_slice_in_dim(
        jnp.zeros((6, D), jnp.float32), feature_terms, row_at, 1
    )
    grad_float = grad_triple.astype(jnp.float32)
    head_terms = jnp.stack(
        [
            jnp.sum(grad_float[:, :, 0], axis=0).reshape(head_width),
            jnp.sum(grad_float[:, :, 2], axis=0).reshape(head_width),
        ]
    )
    head_full = lax.dynamic_update_slice_in_dim(
        jnp.zeros((2, H * HD), jnp.float32), head_terms, col_at, 1
    )
    unit_terms = jnp.sum(grad_pre.astype(jnp.float32), axis=0)
    unit_full = lax.dynamic_update_slice_in_dim(
        jnp.zeros((FF,), jnp.float32), unit_terms, lax.axis_index("col") * units_here, 0
    )
    feature_full, head_full, unit_full = lax.psum(
        (feature_full, head_full, unit_full), ("dp", "row", "col")
    )
    feature_mine = lax.dynamic_slice_in_dim(feature_full, row_at, feat_here, 1)
    head_mine = lax.dynamic_slice_in_dim(head_full, col_at, head_width, 1)
    unit_mine = lax.dynamic_slice_in_dim(
        unit_full, lax.axis_index("col") * units_here, units_here, 0
    )
    grad_proj_in, grad_w_up = (
        lax.psum_scatter(
            grad_proj_in.astype(jnp.bfloat16), "dp", scatter_dimension=0, tiled=True
        ).astype(jnp.float32),
        lax.psum_scatter(
            grad_w_up.astype(jnp.bfloat16), "dp", scatter_dimension=0, tiled=True
        ).astype(jnp.float32),
    )
    grad_proj_out, grad_w_down = (
        lax.psum_scatter(
            grad_proj_out.astype(jnp.bfloat16), "dp", scatter_dimension=1, tiled=True
        ).astype(jnp.float32),
        lax.psum_scatter(
            grad_w_down.astype(jnp.bfloat16), "dp", scatter_dimension=1, tiled=True
        ).astype(jnp.float32),
    )
    grad_proj_in = grad_proj_in.reshape(1, grad_proj_in.shape[0], grad_proj_in.shape[1])
    grad_w_up = grad_w_up.reshape(1, grad_w_up.shape[0], grad_w_up.shape[1])
    grad_proj_out = grad_proj_out.reshape(grad_proj_out.shape[0], 1, grad_proj_out.shape[1])
    grad_w_down = grad_w_down.reshape(grad_w_down.shape[0], 1, grad_w_down.shape[1])
    return (
        result.astype(jnp.bfloat16),
        loss_value,
        grad_input,
        grad_proj_in,
        head_mine[0],
        head_mine[1],
        grad_proj_out,
        feature_mine[4],
        feature_mine[0],
        feature_mine[1],
        feature_mine[2],
        feature_mine[3],
        grad_w_up,
        unit_mine,
        grad_w_down,
        feature_mine[5],
    )


MESH = pl.DeviceIdType.MESH
F32 = jnp.float32
BF16 = jnp.bfloat16
LOG2E = 1.4426950408889634
GELU_ROOT = 0.7978845608028654


def place():
    return lax.axis_index("dp"), lax.axis_index("row"), lax.axis_index("col")


def flip(row, other):
    return lax.rem(row // 2 + other // 2, 2) * 2 + lax.rem(row + other, 2)


def neighbours():
    dp, row, col = place()
    return dict(
        core=(1 - dp, row, col),
        x=(dp, flip(row, 1), col),
        y=(dp, flip(row, 2), col),
        diagonal=(dp, flip(row, 3), col),
        next=(dp, row, lax.rem(2 * col + 3 * (col // 2) + 1, 4)),
        prev=(dp, row, lax.rem(2 * col + col // 2 + 2, 4)),
    )


def images_group():
    dp, row, col = place()
    steps = [(core, step) for core in (0, 1) for step in range(4)][1:]
    return [(lax.rem(dp + core, 2), row, lax.rem(col + step, 4)) for core, step in steps]


def meet():
    dp, row, col = place()
    plane = [(core, k) for core in (0, 1) for k in range(4)][1:]
    peers = [(lax.rem(dp + core, 2), flip(row, k), col) for core, k in plane]
    peers += [peer for i, peer in enumerate(images_group()) if i != 3]
    barrier = pltpu.get_barrier_semaphore()
    for peer in peers:
        pl.semaphore_signal(barrier, inc=1, device_id=peer, device_id_type=MESH)
    pl.semaphore_wait(barrier, len(peers))


class Shuffle:
    def __init__(self, send_sems, recv_sems, local_sem):
        self.sems = send_sems, recv_sems, local_sem
        self.pending = []

    def remote(self, source, target, i, slot, peer):
        return pltpu.make_async_remote_copy(
            source, target, self.sems[0].at[i], self.sems[1].at[slot],
            device_id=peer, device_id_type=MESH,
        )

    def spread(self, pieces, blocks):
        dp, row, col = place()
        feat, own = pieces[0].shape[0], blocks.shape[1]
        for image in (0, 1):
            for half in (0, 1):
                chip = 2 * dp + image
                slot = flip(chip, row)
                mine = (dp == half) & (chip == row)
                source = pieces[image].at[:, pl.ds(half * own, own)]
                target = blocks.at[pl.ds(pl.multiple_of(slot * feat, 16), feat)]
                copy = self.remote(source, target, 2 * image + half, slot, (half, chip, col))
                here = pltpu.make_async_copy(source, blocks.at[pl.ds(0, feat)], self.sems[2])
                self.start(copy, here, mine)
        mine = dp == row // 2
        self.into = [
            (blocks.at[pl.ds(k * feat, feat)], k, None if k else mine) for k in range(4)
        ]

    def collect(self, blocks, pieces):
        dp, row, col = place()
        feat, own = pieces.shape[1], blocks.shape[1]
        image = lax.rem(row, 2)
        for k in range(4):
            owner = flip(row, k)
            mine = (dp == row // 2) & (owner == row)
            source = blocks.at[pl.ds(k * feat, feat)]
            target = pieces.at[image, :, pl.ds(pl.multiple_of(dp * own, 128), own)]
            copy = self.remote(source, target, k, 2 * image + dp, (row // 2, owner, col))
            here = pltpu.make_async_copy(source, target, self.sems[2])
            self.start(copy, here, mine)
        self.into = []
        for image in (0, 1):
            for half in (0, 1):
                mine = (dp == half) & (2 * dp + image == row)
                target = pieces.at[image, :, pl.ds(half * own, own)]
                self.into.append((target, 2 * image + half, mine))

    def start(self, copy, here, mine):
        pl.when(jnp.logical_not(mine))(copy.start)
        pl.when(mine)(here.start)
        self.pending.append((copy, here, mine))

    def arrive(self):
        dp, row, col = place()
        here = self.pending[0][1]
        for target, slot, own in self.into:
            copy = self.remote(target, target, 0, slot, (1 - dp, row, col))
            if own is None:
                copy.wait_recv()
            else:
                pl.when(jnp.logical_not(own))(copy.wait_recv)
                pl.when(own)(here.wait)

    def finish(self):
        for copy, _, mine in self.pending:
            pl.when(jnp.logical_not(mine))(copy.wait_send)


def mm(left, right):
    return jnp.dot(left, right, preferred_element_type=F32)


def mm_nt(left, right):
    return lax.dot_general(left, right, (((1,), (1,)), ((), ())), preferred_element_type=F32)


def each_rows(count, size, body):
    @pl.loop(0, count // size)
    def _(step):
        body(pl.ds(pl.multiple_of(step * size, size), size))


def fold(values):
    return sum(values[i : i + 16] for i in range(0, values.shape[0], 16))


def spread_lanes(source, spread, width):
    blocks = []
    for j in range(width // 256):
        low = 2 * HD * j // 128 * 128
        blocks.append(mm(source[:, low : low + 256], spread[low : low + 256, 256 * j : 256 * j + 256]))
    return jnp.concatenate(blocks, axis=1)


def transpose_into(target, source):
    @pl.loop(0, source.shape[1] // 128)
    def _(step):
        at = pl.ds(pl.multiple_of(step * 128, 128), 128)
        target[at, :] = source[:, at].T


class Sender:
    def __init__(self, send_sems, recv_sems):
        self.sems = (send_sems, recv_sems)
        self.count = 0
        self.copies = []

    def __call__(self, source, target, peer):
        copy = pltpu.make_async_remote_copy(
            source,
            target,
            self.sems[0].at[self.count],
            self.sems[1].at[self.count],
            device_id=peer,
            device_id_type=MESH,
        )
        self.count += 1
        copy.start()
        self.copies.append(copy)
        return copy

    def finish(self):
        for copy in self.copies:
            copy.wait_send()


class Copier:
    def __init__(self, sems):
        self.sems = sems
        self.count = 0

    def __call__(self, source, target):
        copy = pltpu.make_async_copy(source, target, self.sems.at[self.count])
        self.count += 1
        copy.start()
        return copy


def norm_stats(values):
    mean_rows = jnp.mean(values, axis=-1, keepdims=True)
    centered = values - mean_rows
    inv_scale = lax.rsqrt(jnp.mean(centered * centered, axis=-1, keepdims=True) + EPS)
    return centered * inv_scale, inv_scale


def forward_kernel(
    own_tokens,
    x_first,
    x_second,
    teacher_first,
    teacher_second,
    valid_ref,
    params_ref,
    key_lane_ref,
    one_lane_ref,
    bias_spread_ref,
    spread_ref,
    rest_spread_ref,
    attn_ref,
    ff_ref,
    wpad_out,
    wff_out,
    triple_out,
    mixed_out,
    act_out,
    slope_out,
    norm1t_out,
    norm2t_out,
    rest_hbm,
    lse_hbm,
    act_rest_hbm,
    slope_rest_hbm,
    resid_hbm,
    x_hbm,
    branch_out,
    brancht_out,
    result_out,
    err_out,
    feature_ref,
    count_out,
    rest_out,
    lse_out,
    act_rest_out,
    slope_rest_out,
    resid_out,
    x_rows,
    x_blocks,
    teacher_blocks,
    valid_in,
    features_in,
    biases_in,
    counts_in,
    wattn,
    wff,
    wpad,
    triple,
    mixed,
    act,
    slope,
    norm1,
    norm2,
    turned,
    part,
    give1,
    got1,
    give2,
    got2,
    local_sems,
    send_sems,
    recv_sems,
    shuffle_sems,
):
    peers = neighbours()
    meet()
    feat = attn_ref.shape[0]
    half = feat // 2
    depth = 4 * feat
    tokens = norm1.shape[0]
    own = tokens // 2
    main = ff_ref.shape[1] // 2
    qkv = triple.shape[2]
    wide = features_in.shape[2]
    heads_wide = bias_spread_ref.shape[0]
    send = Sender(send_sems, recv_sems)
    keep = Copier(local_sems)

    def rows(block, low=0, size=None):
        return pl.ds(block * feat + low, feat if size is None else size)

    own_attn = keep(attn_ref, wattn.at[0, rows(0)])
    own_ff = keep(ff_ref, wff.at[0, rows(0)])
    az, ax, ay, a_low, a_high = ([None] * 4 for _ in range(5))

    def attn_source(s):
        return attn_ref if s == 0 else wattn.at[s, rows(0)]

    def attn_ring(s):
        az[s + 1] = send(attn_source(s), wattn.at[s + 1, rows(0)], peers["next"])

    def attn_plane(s):
        ax[s] = send(attn_source(s), wattn.at[s, rows(1)], peers["x"])
        ay[s] = send(attn_source(s), wattn.at[s, rows(2)], peers["y"])

    def attn_last(s):
        ax[s].wait_recv()
        a_low[s] = send(
            wattn.at[s, rows(1, 0, half)], wattn.at[s, rows(3, 0, half)], peers["y"]
        )
        ay[s].wait_recv()
        a_high[s] = send(
            wattn.at[s, rows(2, half, half)], wattn.at[s, rows(3, half, half)], peers["x"]
        )

    fz, fy, fx = ([None] * 4 for _ in range(3))

    def ff_first():
        return (
            send(ff_ref.at[pl.ds(0, half)], wff.at[0, rows(1, 0, half)], peers["x"]),
            send(ff_ref.at[pl.ds(half, half)], wff.at[0, rows(2, half, half)], peers["y"]),
        )

    def ff_ring(s):
        fz[s + 1] = [
            send(wff.at[s, piece], wff.at[s + 1, piece], peers["next"])
            for piece in (rows(0), rows(1, 0, half), rows(2, half, half))
        ]

    def ff_last(s):
        fy[s] = [
            send(wff.at[s, rows(k, 0, half)], wff.at[s, rows(k + 2, 0, half)], peers["y"])
            for k in (0, 1)
        ]
        fx[s] = [
            send(wff.at[s, rows(k, half, half)], wff.at[s, rows(k + 1, half, half)], peers["x"])
            for k in (0, 2)
        ]

    def arrive(copies):
        for copy in copies:
            copy.wait_recv()

    def attn_compute(s):
        arrive([a_low[s], a_high[s]])
        slot = s % 2
        if s == 0:
            own_attn.wait()
        if s >= 2:
            for copy in saved[s - 2]:
                copy.wait()

        def unpack(at):
            block = wattn[s, at, :]
            wpad[slot, at, :] = spread_lanes(block, spread_ref, wpad.shape[2]).astype(BF16)
            extra = mm(block[:, block.shape[1] - 128 :], rest_spread_ref[s]).astype(BF16)
            if s == 0:
                rest_out[at, :] = extra
            else:
                rest_out[at, :] = rest_out[at, :] + extra

        each_rows(depth, feat, unpack)

        def project(at):
            bias = mm(biases_in[s, :, :heads_wide].astype(BF16), bias_spread_ref[...])
            values = mm(norm1[at, :], wpad[slot, :, :qkv]) + (bias[0:1] + one_lane_ref[...])
            spot = lax.broadcasted_iota(jnp.int32, (tokens, 1), 0)
            shift = lax.axis_index("dp") * own
            token = jnp.where(spot < own, spot + shift, spot - shift)
            values = values + jnp.where(token < SEQ, 0.0, -1e30) * key_lane_ref[...]
            triple[slot, at, :] = values.astype(BF16)

        each_rows(tokens, tokens, project)
        scale = LOG2E * HD**-0.5
        for h in range(qkv // 384):
            query_at, key_at, value_at = (pl.ds((3 * h + j) * 128, 128) for j in range(3))
            value_turned = triple[slot, :, value_at].T

            def head(at, h=h, query_at=query_at, key_at=key_at, value_turned=value_turned):
                scores = mm_nt(triple[slot, :, key_at], triple[slot, at, query_at])
                peak = jnp.max(scores, axis=0, keepdims=True)
                weights = jnp.exp2((scores - peak) * scale)
                total = jnp.sum(weights, axis=0, keepdims=True)
                lse_out[2 * s + h, :, at] = peak * scale + jnp.log2(total)
                values = mm(value_turned, weights.astype(BF16)) / total
                mixed[s, at, pl.ds(h * 128, 128)] = values.T.astype(BF16)

            each_rows(tokens, own, head)

        def out(at):
            values = mm_nt(mixed[s, at, :], wpad[slot, :, qkv:])
            return values if s == 0 else part[at, :] + values

        swap = None
        if s < 3:
            part[...] = out(pl.ds(0, tokens))
        else:
            give1[...] = out(pl.ds(own, own)).astype(BF16)
            swap = send(give1, got1, peers["core"])
            part[pl.ds(0, own), :] = out(pl.ds(0, own))
        saved.append(
            [
                keep(wpad.at[slot], wpad_out.at[s]),
                keep(triple.at[slot], triple_out.at[s]),
                keep(mixed.at[s], mixed_out.at[s]),
            ]
        )
        return swap

    def gelu(pre):
        inner = GELU_ROOT * (pre + 0.044715 * pre * pre * pre)
        tanh = jnp.tanh(inner)
        rise = 0.5 * (1.0 + tanh)
        bend = 0.5 * pre * (1.0 - tanh * tanh) * (GELU_ROOT * (1.0 + 0.134145 * pre * pre))
        return (pre * rise).astype(BF16), (rise + bend).astype(BF16)

    def ff_compute(s):
        arrive(fy[s] + fx[s])

        def block(at):
            pre = mm(norm2[at, :], wff[s, :, :main]) + biases_in[s, 0:1, heads_wide : heads_wide + main]
            low, bent = gelu(pre)
            act[s, at, :] = low
            slope[s, at, :] = bent
            return part[at, :] + mm_nt(low, wff[s, :, main:])

        swap = None
        if s < 3:
            part[...] = block(pl.ds(0, tokens))
        else:
            give2[...] = block(pl.ds(own, own)).astype(BF16)
            swap = send(give2, got2, peers["core"])
            part[pl.ds(0, own), :] = block(pl.ds(0, own))
        ff_saved.extend(
            [
                keep(act.at[s], act_out.at[s]),
                keep(slope.at[s], slope_out.at[s]),
                keep(wff.at[s], wff_out.at[s]),
            ]
        )
        return swap

    def rest_compute():
        tail_at = heads_wide + main - (2 * heads_wide - wattn.shape[2] + 128)
        bias = mm(biases_in[0, :, tail_at : tail_at + 128].astype(BF16), rest_spread_ref[0, :, :128])
        for s in (1, 2, 3):
            values = biases_in[s, :, tail_at : tail_at + 128].astype(BF16)
            bias = bias + mm(values, rest_spread_ref[s, :, :128])

        def block(at):
            pre = mm(norm2[at, :], rest_out[:, :128]) + bias[0:1]
            low, bent = gelu(pre)
            act_rest_out[at, :] = low
            slope_rest_out[at, :] = bent
            part[at, :] = mm_nt(low, rest_out[:, 128:])

        each_rows(tokens, tokens, block)

    saved, ff_saved = [], []
    x_move = Shuffle(shuffle_sems.at[0], shuffle_sems.at[1], shuffle_sems.at[2, 0])
    x_move.spread((x_first, x_second), x_blocks)
    attn_ring(0)
    first = ff_first()
    attn_plane(0)
    valid_row = valid_ref[0, 0:1, :] + valid_ref[1, 0:1, :]
    counts_in[0] = jnp.broadcast_to(jnp.sum(valid_row, axis=1, keepdims=True), (8, 128))
    own_params = [
        keep(params_ref.at[:, pl.ds(0, wide)], features_in.at[0]),
        keep(params_ref.at[:, pl.ds(wide, biases_in.shape[2])], biases_in.at[0]),
    ]
    smalls = [
        send(params_ref.at[:, pl.ds(0, wide)], features_in.at[k], peers[name])
        for k, name in ((1, "x"), (2, "y"), (3, "diagonal"))
    ]
    dp, row, col = place()
    ring_two = (dp, row, 3 - col)
    smalls += [
        send(params_ref.at[:, pl.ds(wide, biases_in.shape[2])], biases_in.at[s], peer)
        for s, peer in ((1, peers["next"]), (2, ring_two), (3, peers["prev"]))
    ]
    counts = [
        send(counts_in.at[0], counts_in.at[1 + i], peer) for i, peer in enumerate(images_group())
    ]
    teacher_move = Shuffle(shuffle_sems.at[3], shuffle_sems.at[4], shuffle_sems.at[2, 1])

    valid_move = send(valid_ref, valid_in, peers["core"])

    az[1].wait_recv()
    attn_ring(1)
    attn_plane(1)
    attn_last(0)
    az[2].wait_recv()
    attn_ring(2)
    attn_plane(2)
    for copy in own_params:
        copy.wait()
    arrive(smalls)
    feature_ref[...] = jnp.zeros_like(feature_ref)
    for i in range(6):
        feature_ref[i : i + 1, :] = jnp.concatenate(
            [features_in[k, 0:1, feat * i : feat * (i + 1)] for k in range(4)], axis=1
        )
    x_move.arrive()
    for start in range(0, own, 128):
        x_rows[pl.ds(start, 128), :] = x_blocks[:, pl.ds(start, 128)].T
    late = [keep(x_rows, x_hbm)]

    def first_norm(at):
        normed, _ = norm_stats(x_rows[at, :].astype(F32))
        norm1[at, :] = (normed * feature_ref[0:1] + feature_ref[1:2]).astype(BF16)

    each_rows(own, 128, first_norm)
    swap1 = send(norm1.at[pl.ds(0, own)], norm1.at[pl.ds(own, own)], peers["core"])
    az[3].wait_recv()
    attn_plane(3)
    own_ff.wait()
    arrive(first)
    ff_ring(0)
    attn_last(1)
    swap1.wait_recv()
    attn_compute(0)
    attn_last(2)
    attn_compute(1)
    attn_last(3)
    ff_last(0)
    arrive(fz[1])
    ff_ring(1)
    ff_last(1)
    teacher_move.spread((teacher_first, teacher_second), teacher_blocks)
    attn_compute(2)
    swap2 = attn_compute(3)
    swap2.wait_recv()

    def second_norm(at):
        values = x_rows[at, :].astype(F32) + part[at, :] + got1[at, :].astype(F32) + feature_ref[4:5]
        resid_out[at, :] = values
        normed, _ = norm_stats(values)
        norm2[at, :] = (normed * feature_ref[2:3] + feature_ref[3:4]).astype(BF16)

    each_rows(own, 128, second_norm)
    late += [keep(resid_out, resid_hbm), keep(rest_out, rest_hbm), keep(lse_out, lse_hbm)]
    swap3 = send(norm2.at[pl.ds(0, own)], norm2.at[pl.ds(own, own)], peers["core"])
    arrive(fz[2])
    ff_ring(2)
    ff_last(2)
    transpose_into(turned, norm1)
    turn1 = keep(turned, norm1t_out)
    swap3.wait_recv()
    rest_compute()
    late += [keep(act_rest_out, act_rest_hbm), keep(slope_rest_out, slope_rest_hbm)]
    turn1.wait()
    transpose_into(turned, norm2)
    turn2 = keep(turned, norm2t_out)
    ff_compute(0)
    arrive(fz[3])
    ff_last(3)
    ff_compute(1)
    ff_compute(2)
    swap4 = ff_compute(3)
    err_out[...] = jnp.zeros_like(err_out)
    arrive(counts)
    count = counts_in[0]
    for i in range(1, 8):
        count = count + counts_in[i]
    count_out[...] = count
    factor = (own_tokens * 8.0) / count[0:1, 0:1]
    teacher_move.arrive()
    swap4.wait_recv()

    valid_move.wait_recv()
    image, from_here = lax.rem(row, 2), dp == row // 2

    def finish(start):
        at = pl.ds(start, 128)
        values = resid_out[at, :] + part[at, :] + got2[at, :].astype(F32) + feature_ref[5:6]
        result_out[:, at] = values.astype(BF16).T
        error = values - teacher_blocks[:, at].T.astype(F32)
        lanes_at = pl.ds(pl.multiple_of(dp * own + start, 128), 128)
        counts_row = jnp.where(
            from_here, valid_ref[image, :, lanes_at], valid_in[image, :, lanes_at]
        )
        masked = error * counts_row.T[:, 0:1]
        err_out[...] = err_out[...] + fold(error * masked)
        branch_out[at, :] = (masked * factor).astype(BF16)

    def turn(start):
        brancht_out[:, pl.ds(start, 128)] = branch_out[pl.ds(start, 128), :].T

    swaps = []
    for start in range(0, own, 128):
        finish(start)
        swaps.append(
            send(
                branch_out.at[pl.ds(start, 128)],
                branch_out.at[pl.ds(own + start, 128)],
                peers["core"],
            )
        )
        turn(start)
    for start, swap in zip(range(own, tokens, 128), swaps):
        swap.wait_recv()
        turn(start)
    turn2.wait()
    for copies in saved[2:]:
        for copy in copies:
            copy.wait()
    for copy in ff_saved:
        copy.wait()
    for copy in late:
        copy.wait()
    send.finish()
    x_move.finish()
    teacher_move.finish()


def forward_call(arrays, own_tokens, feat, lanes, main, qkv, mix, own, depth):
    tokens = 2 * own
    wide = (6 * feat + 127) // 128 * 128
    narrow = arrays[5].shape[1] - wide
    anywhere = pl.BlockSpec(memory_space=pl.ANY)
    local = pl.BlockSpec(memory_space=pltpu.VMEM)
    shapes = [
        ((4, depth, qkv + mix), BF16, anywhere),
        ((4, depth, 2 * main), BF16, anywhere),
        ((4, tokens, qkv), BF16, anywhere),
        ((4, tokens, mix), BF16, anywhere),
        ((4, tokens, main), BF16, anywhere),
        ((4, tokens, main), BF16, anywhere),
        ((depth, tokens), BF16, anywhere),
        ((depth, tokens), BF16, anywhere),
        ((depth, 256), BF16, anywhere),
        ((8, 1, tokens), F32, anywhere),
        ((tokens, 128), BF16, anywhere),
        ((tokens, 128), BF16, anywhere),
        ((own, depth), F32, anywhere),
        ((own, depth), BF16, anywhere),
        ((tokens, depth), BF16, local),
        ((depth, tokens), BF16, local),
        ((depth, own), BF16, local),
        ((16, depth), F32, local),
        ((8, depth), F32, local),
        ((8, 128), F32, local),
    ]
    return pl.pallas_call(
        functools.partial(forward_kernel, own_tokens),
        out_shape=[jax.ShapeDtypeStruct(shape, dtype) for shape, dtype, _ in shapes],
        in_specs=[anywhere] * 4 + [local] * 7 + [anywhere] * 2,
        out_specs=[spec for _, _, spec in shapes],
        scratch_shapes=[
            pltpu.VMEM((depth, 256), BF16),
            pltpu.VMEM((8, 1, tokens), F32),
            pltpu.VMEM((tokens, 128), BF16),
            pltpu.VMEM((tokens, 128), BF16),
            pltpu.VMEM((own, depth), F32),
            pltpu.VMEM((own, depth), BF16),
            pltpu.VMEM((depth, own), BF16),
            pltpu.VMEM((depth, own), BF16),
            pltpu.VMEM((2, 8, tokens), F32),
            pltpu.VMEM((4, 8, wide), F32),
            pltpu.VMEM((4, 8, narrow), F32),
            pltpu.VMEM((8, 8, 128), F32),
            pltpu.VMEM((4, depth, lanes), BF16),
            pltpu.VMEM((4, depth, 2 * main), BF16),
            pltpu.VMEM((2, depth, qkv + mix), BF16),
            pltpu.VMEM((2, tokens, qkv), BF16),
            pltpu.VMEM((4, tokens, mix), BF16),
            pltpu.VMEM((4, tokens, main), BF16),
            pltpu.VMEM((4, tokens, main), BF16),
            pltpu.VMEM((tokens, depth), BF16),
            pltpu.VMEM((tokens, depth), BF16),
            pltpu.VMEM((depth, tokens), BF16),
            pltpu.VMEM((tokens, depth), F32),
            pltpu.VMEM((own, depth), BF16),
            pltpu.VMEM((own, depth), BF16),
            pltpu.VMEM((own, depth), BF16),
            pltpu.VMEM((own, depth), BF16),
            pltpu.SemaphoreType.DMA((40,)),
            pltpu.SemaphoreType.DMA((72,)),
            pltpu.SemaphoreType.DMA((72,)),
            pltpu.SemaphoreType.DMA((5, 4)),
        ],
        compiler_params=pltpu.CompilerParams(
            collective_id=1, has_side_effects=True, vmem_limit_bytes=62 << 20
        ),
    )(*arrays)


def backward_kernel(
    branch2_ref,
    rest_ref,
    act_rest_ref,
    slope_rest_ref,
    lse_ref,
    feature_ref,
    spread_ref,
    rest_spread_ref,
    err_ref,
    count_ref,
    result_blocks,
    x_hbm,
    resid_hbm,
    norm1t_hbm,
    norm2t_hbm,
    branch2t_hbm,
    wpad_hbm,
    wff_hbm,
    triple_hbm,
    mixed_hbm,
    act_hbm,
    slope_hbm,
    grad_pieces,
    result_pieces,
    sums_out,
    bias_out,
    attn_out,
    ff_out,
    x_rows,
    grad_blocks,
    terms,
    terms_mine,
    terms_in,
    sums_in,
    bias_mine,
    bias_turn,
    bias_in,
    bias_plane,
    units_out,
    units_rest_out,
    heads_out,
    gattn,
    gff,
    wslot,
    kept,
    grad_pre,
    grad_rest,
    normt,
    brancht,
    branch1,
    part,
    give,
    got,
    grad_mid,
    dtriple,
    grad_mixed,
    grad_key,
    grad_value,
    inner_row,
    ra,
    rb,
    r1,
    r2,
    rz,
    ry,
    rx,
    rzl,
    rzh,
    rfx,
    rfy,
    local_sems,
    send_sems,
    recv_sems,
    shuffle_sems,
):
    peers = neighbours()
    feat = 2 * attn_out.shape[1]
    half = feat // 2
    depth = 4 * feat
    tokens = branch2_ref.shape[0]
    own = tokens // 2
    main = gff.shape[2] // 2
    qkv = triple_hbm.shape[2]
    send = Sender(send_sems, recv_sems)
    keep = Copier(local_sems)

    def rows(block, low=0, size=None):
        return pl.ds(block * feat + low, feat if size is None else size)

    def load_ff(s):
        slot = s % 2
        return [
            keep(wff_hbm.at[s], wslot.at[slot]),
            keep(act_hbm.at[s], kept.at[slot, :, pl.ds(0, main)]),
            keep(slope_hbm.at[s], kept.at[slot, :, pl.ds(main, main)]),
        ]

    def load_attn(s):
        slot = s % 2
        return [
            keep(wpad_hbm.at[s], wslot.at[slot]),
            keep(triple_hbm.at[s], kept.at[slot, :, pl.ds(0, qkv)]),
            keep(mixed_hbm.at[s], kept.at[slot, :, pl.ds(qkv, grad_mixed.shape[1])]),
        ]

    loads = {3: load_ff(3)}
    turns = [keep(norm2t_hbm, normt), keep(branch2t_hbm, brancht)]
    loads[2] = load_ff(2)
    load_late = [keep(resid_hbm, grad_mid), keep(x_hbm, x_rows)]
    meet()
    result_move = Shuffle(shuffle_sems.at[0], shuffle_sems.at[1], shuffle_sems.at[2, 0])
    grad_move = Shuffle(shuffle_sems.at[3], shuffle_sems.at[4], shuffle_sems.at[2, 1])
    cy, cx, zl, zh = ([None] * 4 for _ in range(4))
    ca, cb, c1, c2, cz = ([None] * 4 for _ in range(5))

    def add_into(target, at, *sources):
        size = at.size

        @pl.loop(0, size // 16)
        def _(step):
            here = pl.ds(pl.multiple_of(at.start + step * 16, 16), 16)
            there = pl.ds(pl.multiple_of(step * 16, 16), 16)
            total = target[here, :].astype(F32)
            for source in sources:
                total = total + source[there, :].astype(F32)
            target[here, :] = total.astype(BF16)

    def column_sum(values):
        return jnp.sum(values.astype(F32), axis=0, keepdims=True)

    def ff_compute(s):
        slot = s % 2
        for copy in loads[s]:
            copy.wait()
        units_out[s] = jnp.zeros((1, main), F32)

        def block(at):
            grad = mm(branch2_ref[at, :], wslot[slot, :, main : 2 * main])
            low = (grad * kept[slot, at, main:].astype(F32)).astype(BF16)
            grad_pre[at, :] = low
            units_out[s] = units_out[s] + column_sum(low)
            values = mm_nt(low, wslot[slot, :, :main])
            part[at, :] = values if s == 3 else part[at, :] + values

        each_rows(tokens, own, block)
        if s == 3:
            for copy in turns:
                copy.wait()

        def grads(at):
            gff[s, at, :main] = mm(normt[at, :], grad_pre[...]).astype(BF16)
            gff[s, at, main:] = mm(brancht[at, :], kept[slot, :, :main]).astype(BF16)

        each_rows(depth, 2 * feat, grads)
        cy[s] = [
            send(gff.at[s, rows(k, 0, half)], ry.at[s, k - 2], peers["y"]) for k in (2, 3)
        ]
        cx[s] = [
            send(gff.at[s, rows(k, half, half)], rx.at[s, k // 2], peers["x"]) for k in (1, 3)
        ]
        if s >= 2:
            loads[s - 2] = load_ff(s - 2)

    def rest_compute():
        units_rest_out[...] = jnp.zeros_like(units_rest_out)

        def block(at):
            grad = mm(branch2_ref[at, :], rest_ref[:, 128:])
            low = (grad * slope_rest_ref[at, :].astype(F32)).astype(BF16)
            grad_pre[at, :128] = low
            units_rest_out[...] = units_rest_out[...] + column_sum(low)
            return part[at, :] + mm_nt(low, rest_ref[:, :128])

        give[...] = block(pl.ds(own, own)).astype(BF16)
        swap = send(give, got, peers["core"])
        part[pl.ds(0, own), :] = block(pl.ds(0, own))

        def grads(at):
            grad_rest[at, :128] = mm(normt[at, :], grad_pre[:, :128]).astype(BF16)
            grad_rest[at, 128:] = mm(brancht[at, :], act_rest_ref[...]).astype(BF16)

        each_rows(depth, 2 * feat, grads)
        return swap

    def ff_add(s):
        for copy in cy[s] + cx[s]:
            copy.wait_recv()
        last = s == 3
        if not last:
            for copy in zl[s] + zh[s]:
                copy.wait_recv()
        lows, highs = [], []
        for i, k in enumerate((0, 1)):
            piece = rows(k, 0, half)
            add_into(gff.at[s], piece, ry.at[s, i], *([] if last else [rzl.at[s, i]]))
            lows.append((piece, i))
        for i, k in enumerate((0, 2)):
            piece = rows(k, half, half)
            add_into(gff.at[s], piece, rx.at[s, i], *([] if last else [rzh.at[s, i]]))
            highs.append((piece, i))
        if s:
            zl[s - 1] = [
                send(gff.at[s, piece], rzl.at[s - 1, i], peers["prev"]) for piece, i in lows
            ]
            zh[s - 1] = [
                send(gff.at[s, piece], rzh.at[s - 1, i], peers["prev"]) for piece, i in highs
            ]

    def attn_compute(s):
        slot = s % 2
        for copy in attn_loads[s]:
            copy.wait()

        def back_out(at):
            grad_mixed[at, :] = mm(branch1[at, :], wslot[slot, :, qkv:]).astype(BF16)

        each_rows(tokens, tokens, back_out)
        scale = HD**-0.5
        for h in range(qkv // 384):
            query_at, key_at, value_at = (pl.ds((3 * h + j) * 128, 128) for j in range(3))
            mix_at = pl.ds(h * 128, 128)
            value_of_mix = pl.ds(qkv + h * 128, 128)
            key_turned = kept[slot, :, key_at].T
            product = grad_mixed[:, mix_at].astype(F32) * kept[slot, :, value_of_mix].astype(F32)
            inner_row[...] = jnp.sum(product.T, axis=0, keepdims=True)
            grad_key[...] = jnp.zeros_like(grad_key)
            grad_value[...] = jnp.zeros_like(grad_value)

            def head(at, h=h, query_at=query_at, key_at=key_at, value_at=value_at,
                     mix_at=mix_at, key_turned=key_turned):
                query = kept[slot, at, query_at]
                grad = grad_mixed[at, mix_at]
                scores = mm_nt(kept[slot, :, key_at], query)
                weights = jnp.exp2(scores * (scale * LOG2E) - lse_ref[2 * s + h, :, at])
                grad_soft = mm_nt(kept[slot, :, value_at], grad)
                grad_raw = (weights * (grad_soft - inner_row[:, at]) * scale).astype(BF16)
                grad_value[...] += mm(weights.astype(BF16), grad)
                grad_key[...] += mm(grad_raw, query)
                dtriple[at, query_at] = mm(key_turned, grad_raw).T.astype(BF16)

            each_rows(tokens, own, head)
            dtriple[:, key_at] = grad_key[...].astype(BF16)
            dtriple[:, value_at] = grad_value[...].astype(BF16)
        heads_out[s] = jnp.zeros((1, qkv), F32)

        def back_in(at):
            values = mm_nt(dtriple[at, :], wslot[slot, :, :qkv])
            heads_out[s] = heads_out[s] + column_sum(dtriple[at, :])
            return values if s == 3 else part[at, :] + values

        swap = None
        if s:
            for at in (pl.ds(0, own), pl.ds(own, own)):
                part[at, :] = back_in(at)
        else:
            give[...] = back_in(pl.ds(own, own)).astype(BF16)
            swap = send(give, got, peers["core"])
            part[pl.ds(0, own), :] = back_in(pl.ds(0, own))

        def grads(at):
            first = mm(normt[at, :], dtriple[...]).astype(BF16)
            second = mm(brancht[at, :], kept[slot, :, qkv:]).astype(BF16)
            tiles = [0.0] * (gattn.shape[2] // 128)
            for j in range((qkv + second.shape[1]) // 256):
                low, to = 2 * HD * j // 128 * 128, 256 * j
                block = first[:, to : to + 256] if to < qkv else second[:, to - qkv : to - qkv + 256]
                moved = mm_nt(block, spread_ref[low : low + 256, to : to + 256])
                for i in (0, 1):
                    tiles[low // 128 + i] += moved[:, 128 * i : 128 * i + 128]
            tiles[-1] += mm_nt(grad_rest[at, :], rest_spread_ref[s])
            gattn[s, at, :] = jnp.concatenate(tiles, axis=1).astype(BF16)

        each_rows(depth, 2 * feat, grads)
        ca[s] = send(gattn.at[s, rows(3, 0, half)], ra.at[s], peers["y"])
        cb[s] = send(gattn.at[s, rows(3, half, half)], rb.at[s], peers["x"])
        if s >= 2:
            attn_loads[s - 2] = load_attn(s - 2)
        return swap

    def attn_plane(s):
        ca[s].wait_recv()
        add_into(gattn.at[s], rows(1, 0, half), ra.at[s])
        c1[s] = send(gattn.at[s, rows(1)], r1.at[s], peers["x"])
        cb[s].wait_recv()
        add_into(gattn.at[s], rows(2, half, half), rb.at[s])
        c2[s] = send(gattn.at[s, rows(2)], r2.at[s], peers["y"])

    def attn_ring(s):
        c1[s].wait_recv()
        c2[s].wait_recv()
        if s < 3:
            cz[s].wait_recv()
        add_into(gattn.at[s], rows(0), r1.at[s], r2.at[s], *([rz.at[s]] if s < 3 else []))
        if s:
            cz[s - 1] = send(gattn.at[s, rows(0)], rz.at[s - 1], peers["prev"])

    terms[...] = jnp.zeros_like(terms)

    def add_term(index, values):
        terms[index] = terms[index] + fold(values)

    result_move.collect(result_blocks, result_pieces)
    ff_compute(3)
    ff_compute(2)
    ff_compute(1)
    ff_add(3)
    ff_compute(0)
    attn_loads = {3: load_attn(3), 2: load_attn(2)}
    swap1 = rest_compute()
    load_norm = keep(norm1t_hbm, normt)
    swap1.wait_recv()
    for copy in load_late:
        copy.wait()

    def mid(at):
        normed, inv_scale = norm_stats(grad_mid[at, :])
        grad_norm = part[at, :] + got[at, :].astype(F32)
        add_term(2, grad_norm * normed)
        add_term(3, grad_norm)
        scaled = grad_norm * feature_ref[2:3]
        first = jnp.mean(scaled, axis=-1, keepdims=True)
        second = jnp.mean(scaled * normed, axis=-1, keepdims=True)
        grad = branch2_ref[at, :].astype(F32)
        grad = grad + inv_scale * (scaled - first - normed * second)
        grad_mid[at, :] = grad
        low = grad.astype(BF16)
        branch1[at, :] = low
        add_term(4, low.astype(F32))
        add_term(5, branch2_ref[at, :].astype(F32))

    each_rows(own, 64, mid)
    swap2 = send(branch1.at[pl.ds(0, own)], branch1.at[pl.ds(own, own)], peers["core"])
    swap2.wait_recv()
    load_norm.wait()
    transpose_into(brancht, branch1)
    attn_compute(3)
    ff_add(2)
    attn_compute(2)
    attn_plane(3)
    attn_compute(1)
    attn_plane(2)
    attn_ring(3)
    ff_add(1)
    swap1.wait_send()
    swap3 = attn_compute(0)
    attn_plane(1)
    attn_ring(2)
    attn_plane(0)
    swap3.wait_recv()

    def last(at):
        normed, inv_scale = norm_stats(x_rows[at, :].astype(F32))
        grad_norm = part[at, :] + got[at, :].astype(F32)
        add_term(0, grad_norm * normed)
        add_term(1, grad_norm)
        scaled = grad_norm * feature_ref[0:1]
        first = jnp.mean(scaled, axis=-1, keepdims=True)
        second = jnp.mean(scaled * normed, axis=-1, keepdims=True)
        grad = grad_mid[at, :] + inv_scale * (scaled - first - normed * second)
        grad_blocks[:, at] = grad.astype(BF16).T

    each_rows(own, 128, last)
    grad_move.collect(grad_blocks, grad_pieces)
    terms_mine[...] = jnp.zeros_like(terms_mine)
    bias_mine[...] = jnp.zeros_like(bias_mine)
    for i in range(7):
        if i < 6:
            row_sum = jnp.sum(terms[i], axis=0, keepdims=True)
        else:
            err = jnp.sum(jnp.sum(err_ref[...], axis=0, keepdims=True), axis=1, keepdims=True)
            row_sum = jnp.broadcast_to(err, (1, depth))
        for k in range(4):
            terms_mine[k, i : i + 1, :] = row_sum[:, k * feat : (k + 1) * feat]
    wide = bias_mine.shape[2]
    for s in range(4):
        bias_mine[s, 0:1, :qkv] = heads_out[s]
        bias_mine[s, 0:1, qkv : qkv + main] = units_out[s]
        bias_mine[s, 0:1, qkv + main :] = units_rest_out[...]
    dp, row, col = place()
    ring_two = (dp, row, 3 - col)
    sides = ((1, "x"), (2, "y"), (3, "diagonal"))
    term_sends = [send(terms_mine.at[k], terms_in.at[k - 1], peers[name]) for k, name in sides]
    bias_sends = [
        send(bias_mine.at[s], bias_turn.at[s - 1], peer)
        for s, peer in ((1, peers["prev"]), (2, ring_two), (3, peers["next"]))
    ]
    ff_add(0)
    end_low = send(gff.at[0, rows(1, 0, half)], rfx, peers["x"])
    end_high = send(gff.at[0, rows(2, half, half)], rfy, peers["y"])
    attn_ring(1)
    for copy in term_sends + bias_sends:
        copy.wait_recv()
    terms_mine[0] = terms_mine[0] + terms_in[0] + terms_in[1] + terms_in[2]
    sum_sends = [
        send(terms_mine.at[0], sums_in.at[i], peer) for i, peer in enumerate(images_group())
    ]
    bias_plane[...] = bias_mine[0]
    for s in (1, 2, 3):
        bias_plane[s : s + 1, :] = bias_turn[s - 1, 0:1, :]
    plane_sends = [send(bias_plane, bias_in.at[k - 1], peers[name]) for k, name in sides]
    end_low.wait_recv()
    end_high.wait_recv()
    add_into(gff.at[0], rows(0, 0, half), rfx)
    add_into(gff.at[0], rows(0, half, half), rfy)
    quarter = feat // 2
    keep_at = pl.ds(pl.multiple_of(dp * quarter, 16), quarter)
    give_at = pl.ds(pl.multiple_of((1 - dp) * quarter, 16), quarter)
    done = [keep(gff.at[0, keep_at], ff_out.at[0])]
    pair_sends = [send(gff.at[0, give_at], ff_out.at[1], peers["core"])]
    for copy in plane_sends + sum_sends:
        copy.wait_recv()
    bias_out[0] = bias_plane[...] + bias_in[0] + bias_in[1] + bias_in[2]
    pair_sends.append(send(bias_out.at[0], bias_out.at[1], peers["core"]))
    total = terms_mine[0]
    for i in range(7):
        total = total + sums_in[i]
    sums_out[...] = total
    sums_out[7:8, :] = total[6:7] / (count_ref[0:1, 0:1] * depth)
    attn_ring(0)
    done.append(keep(gattn.at[0, keep_at], attn_out.at[0]))
    pair_sends.append(send(gattn.at[0, give_at], attn_out.at[1], peers["core"]))
    for copy in pair_sends:
        copy.wait_recv()
    for copy in done:
        copy.wait()
    result_move.arrive()
    grad_move.arrive()
    for copy in send.copies:
        if copy is not swap1:
            copy.wait_send()
    result_move.finish()
    grad_move.finish()


def backward_call(arrays, feat, lanes, main, qkv, mix, own, depth):
    tokens = 2 * own
    half = feat // 2
    narrow = qkv + main + 128
    anywhere = pl.BlockSpec(memory_space=pl.ANY)
    local = pl.BlockSpec(memory_space=pltpu.VMEM)
    shapes = [
        ((2, feat, tokens), BF16, anywhere),
        ((2, feat, tokens), BF16, anywhere),
        ((8, feat), F32, local),
        ((2, 8, narrow), F32, local),
        ((2, half, lanes), BF16, anywhere),
        ((2, half, 2 * main), BF16, anywhere),
    ]
    return pl.pallas_call(
        backward_kernel,
        out_shape=[jax.ShapeDtypeStruct(shape, dtype) for shape, dtype, _ in shapes],
        in_specs=[local] * 10 + [anywhere] * 12,
        out_specs=[spec for _, _, spec in shapes],
        scratch_shapes=[
            pltpu.VMEM((own, depth), BF16),
            pltpu.VMEM((depth, own), BF16),
            pltpu.VMEM((6, 16, depth), F32),
            pltpu.VMEM((4, 8, feat), F32),
            pltpu.VMEM((3, 8, feat), F32),
            pltpu.VMEM((7, 8, feat), F32),
            pltpu.VMEM((4, 8, narrow), F32),
            pltpu.VMEM((3, 8, narrow), F32),
            pltpu.VMEM((3, 8, narrow), F32),
            pltpu.VMEM((8, narrow), F32),
            pltpu.VMEM((4, 1, main), F32),
            pltpu.VMEM((1, 128), F32),
            pltpu.VMEM((4, 1, qkv), F32),
            pltpu.VMEM((4, depth, lanes), BF16),
            pltpu.VMEM((4, depth, 2 * main), BF16),
            pltpu.VMEM((2, depth, 2 * main), BF16),
            pltpu.VMEM((2, tokens, qkv + mix), BF16),
            pltpu.VMEM((tokens, main), BF16),
            pltpu.VMEM((depth, 256), BF16),
            pltpu.VMEM((depth, tokens), BF16),
            pltpu.VMEM((depth, tokens), BF16),
            pltpu.VMEM((tokens, depth), BF16),
            pltpu.VMEM((tokens, depth), F32),
            pltpu.VMEM((own, depth), BF16),
            pltpu.VMEM((own, depth), BF16),
            pltpu.VMEM((own, depth), F32),
            pltpu.VMEM((tokens, qkv), BF16),
            pltpu.VMEM((tokens, mix), BF16),
            pltpu.VMEM((tokens, 128), F32),
            pltpu.VMEM((tokens, 128), F32),
            pltpu.VMEM((1, tokens), F32),
            pltpu.VMEM((4, half, lanes), BF16),
            pltpu.VMEM((4, half, lanes), BF16),
            pltpu.VMEM((4, feat, lanes), BF16),
            pltpu.VMEM((4, feat, lanes), BF16),
            pltpu.VMEM((3, feat, lanes), BF16),
            pltpu.VMEM((4, 2, half, 2 * main), BF16),
            pltpu.VMEM((4, 2, half, 2 * main), BF16),
            pltpu.VMEM((3, 2, half, 2 * main), BF16),
            pltpu.VMEM((3, 2, half, 2 * main), BF16),
            pltpu.VMEM((half, 2 * main), BF16),
            pltpu.VMEM((half, 2 * main), BF16),
            pltpu.SemaphoreType.DMA((32,)),
            pltpu.SemaphoreType.DMA((104,)),
            pltpu.SemaphoreType.DMA((104,)),
            pltpu.SemaphoreType.DMA((5, 4)),
        ],
        compiler_params=pltpu.CompilerParams(
            collective_id=2, has_side_effects=True, vmem_limit_bytes=63 << 20
        ),
    )(*arrays)
def on_chip(
    layer_input,
    teacher,
    valid,
    proj_in,
    bias_query,
    bias_value,
    proj_out,
    bias_out,
    norm1_gain,
    norm1_shift,
    norm2_gain,
    norm2_shift,
    w_up,
    bias_up,
    w_down,
    bias_down,
):
    core = lax.axis_index("dp")
    first = core == 0
    cols = lax.axis_size("col")
    feat = layer_input.shape[1]
    images = layer_input.shape[0] // SEQ
    half_seq = (SEQ + 255) // 256 * 128
    pad_seq = 2 * half_seq
    units = w_up.shape[1] // 2
    width = proj_out.shape[0] // 2
    heads = width // HD
    main = units // 128 * 128
    rest = units - main
    at = 4 * width
    lanes = (at + 2 * rest + 127) // 128 * 128
    qkv, mix = 3 * heads * 128, heads * 128

    def core_half(values, axis):
        low, high = jnp.split(values, 2, axis=axis)
        return jnp.where(first, low, high)

    def pieces(values):
        turned = values.T
        second = turned[:, SEQ:]
        return turned, jnp.pad(second, ((0, 0), (0, pad_seq - SEQ)))

    up_half, down_half = core_half(w_up, 1), core_half(w_down, 0).T
    attn_shard = jnp.concatenate(
        [
            core_half(proj_in, 1),
            core_half(proj_out, 0).T,
            up_half[:, main:],
            down_half[:, main:],
            jnp.zeros((feat, lanes - at - 2 * rest), jnp.bfloat16),
        ],
        axis=1,
    )
    ff_shard = jnp.concatenate([up_half[:, :main], down_half[:, :main]], axis=1)
    lane = np.arange(lanes)
    spread_at = np.where(lane < at, lane // HD * 128 + lane % HD, -1)
    spread = jnp.asarray(spread_at[:, None] == np.arange(qkv + mix), jnp.bfloat16)
    tail = lane[-128:]
    part = np.arange(cols)[:, None]
    up_at = np.where((tail >= at) & (tail < at + rest), tail - at + part * rest, -1)
    down_at = np.where(
        (tail >= at + rest) & (tail < at + 2 * rest), tail - at - rest + part * rest + 128, -1
    )
    spot = np.arange(256)
    rest_spread = (up_at[..., None] == spot) | (down_at[..., None] == spot)
    rest_spread = jnp.asarray(rest_spread, jnp.bfloat16)

    key_lane = jnp.asarray(np.arange(qkv) % 384 == 128 + HD, jnp.float32)[None]

    one_lane = jnp.asarray(np.arange(qkv) % 384 == HD, jnp.float32)[None]
    source = np.arange(2 * width)
    bias_at = source % width // HD * 384 + source // width * 256 + source % HD
    bias_spread = jnp.asarray(bias_at[:, None] == np.arange(qkv), jnp.bfloat16)
    wide = (6 * feat + 127) // 128 * 128
    narrow = (2 * width + units + 127) // 128 * 128
    vectors = [
        (0, norm1_gain),
        (feat, norm1_shift),
        (2 * feat, norm2_gain),
        (3 * feat, norm2_shift),
        (4 * feat, bias_out),
        (5 * feat, bias_down),
        (wide, core_half(bias_query, 0)),
        (wide + width, core_half(bias_value, 0)),
        (wide + 2 * width, core_half(bias_up, 0)),
    ]
    params = jnp.zeros((8, wide + narrow), jnp.float32)
    for start, vector in vectors:
        size = vector.shape[0]
        row_of = jnp.broadcast_to(vector.astype(jnp.float32)[None], (8, size))
        params = params + jnp.pad(row_of, ((0, 0), (start, wide + narrow - start - size)))
    valid_rows = jnp.pad(valid.reshape(images, SEQ), ((0, 0), (0, pad_seq - SEQ)))
    valid_rows = jnp.broadcast_to(valid_rows.astype(jnp.float32)[:, None], (images, 8, pad_seq))
    sizes = (feat, lanes, main, qkv, mix, half_seq, 4 * feat)
    (
        wpad, wff, triple, mixed, act, slope, norm1t, norm2t, rest_weight, lse, act_rest,
        slope_rest, resid1, x_rows, branch2, branch2t, result, err_rows, features, counted,
    ) = forward_call(
        (
            *pieces(layer_input), *pieces(teacher), valid_rows, params, key_lane, one_lane, bias_spread, spread, rest_spread, attn_shard, ff_shard,
        ),
        layer_input.shape[0],
        *sizes,
    )
    grad_pieces, result_pieces, sums, bias_rows, attn_sum, ff_sum = backward_call(
        (
            branch2, rest_weight, act_rest, slope_rest, lse, features, spread, rest_spread,
            err_rows, counted, result, x_rows, resid1, norm1t, norm2t, branch2t, wpad,
            wff, triple, mixed, act, slope,
        ),
        *sizes,
    )

    def rows_of(values):
        return jnp.concatenate([values[i][:, :SEQ] for i in range(images)], axis=1).T

    def both(keep, got, axis=-1):
        return jnp.concatenate(
            [jnp.where(first, keep, got), jnp.where(first, got, keep)], axis=axis
        ).astype(jnp.float32)

    def up_of(i):
        return jnp.concatenate([ff_sum[i][:, :main], attn_sum[i][:, at : at + rest]], axis=1)

    def down_of(i):
        block = [ff_sum[i][:, main:], attn_sum[i][:, at + rest : at + 2 * rest]]
        return jnp.concatenate(block, axis=1).T

    main_rows = jnp.sum(bias_rows[:, :cols, : qkv + main], axis=1)
    head_rows = main_rows[:, :qkv].reshape(2, heads, 3, 128)[..., :HD]
    tail_rows = bias_rows[:, :cols, qkv + main :]
    tail_rows = sum(tail_rows[:, s, s * rest : (s + 1) * rest] for s in range(cols))
    unit_rows = jnp.concatenate([main_rows[:, qkv:], tail_rows], axis=1)
    return (
        rows_of(result_pieces),
        sums[7, 0],
        rows_of(grad_pieces).astype(jnp.float32),
        both(attn_sum[0][:, : 3 * width], attn_sum[1][:, : 3 * width])[None],
        both(head_rows[0, :, 0].reshape(width), head_rows[1, :, 0].reshape(width)),
        both(head_rows[0, :, 2].reshape(width), head_rows[1, :, 2].reshape(width)),
        both(attn_sum[0][:, 3 * width : at].T, attn_sum[1][:, 3 * width : at].T, 0)[:, None],
        sums[4],
        sums[0],
        sums[1],
        sums[2],
        sums[3],
        both(up_of(0), up_of(1))[None],
        both(unit_rows[0], unit_rows[1]),
        both(down_of(0), down_of(1), 0)[:, None],
        sums[5],
    )


def one_image_a_chip(mesh, tokens):
    sizes = mesh.shape
    pairs = sizes["dp"] == 2 and sizes["row"] == 4 and sizes["col"] == 4
    return pairs and tokens == SEQ * sizes["row"] * sizes["col"]


def solution(mesh):
    placed = (
        P(("dp", "col"), "row"),
        P(("dp", "col"), "row"),
        P(("dp", "col")),
        P("row", "col"),
        P("col"),
        P("col"),
        P("col", "row"),
        P("row"),
        P("row"),
        P("row"),
        P("row"),
        P("row"),
        P("row", "col"),
        P("col"),
        P("col", "row"),
        P("row"),
    )
    returned = (
            P(("dp", "col"), "row"),
            P(),
            P(("dp", "col"), "row"),
            P("row", "dp", "col"),
            P("col"),
            P("col"),
            P("col", "row", "dp"),
            P("row"),
            P("row"),
            P("row"),
            P("row"),
            P("row"),
            P("row", "dp", "col"),
            P("col"),
            P("col", "row", "dp"),
            P("row"),
        )

    def whole(layer_input, *others):
        body = on_chip if one_image_a_chip(mesh, layer_input.shape[0]) else on_device
        return jax.shard_map(
            body, mesh=mesh, in_specs=placed, out_specs=returned, check_vma=False
        )(layer_input, *others)

    return whole
```

```python
import functools

import jax
import jax.numpy as jnp
import numpy as np
from jax import lax
from jax.experimental import pallas as pl
from jax.experimental.pallas import tpu as pltpu
from jax.sharding import PartitionSpec as P

D = 1152
H = 16
HD = 72
FF = 4304
SEQ = 729


EPS = 1e-06


def feature_totals(left, right):
    return lax.psum(
        (jnp.sum(left, axis=-1, keepdims=True), jnp.sum(right, axis=-1, keepdims=True)), "row"
    )


def norm_forward(values, gain, shift):
    first_sum, second_sum = feature_totals(values, values * values)
    mean_rows = first_sum / D
    var_rows = second_sum / D - mean_rows * mean_rows
    inv_scale = lax.rsqrt(var_rows + EPS)
    normed = (values - mean_rows) * inv_scale
    return (normed, inv_scale, normed * gain + shift)


def norm_backward(grad_out, normed, inv_scale, gain):
    grad_normed = grad_out * gain
    first_sum, second_sum = feature_totals(grad_normed, grad_normed * normed)
    return inv_scale * (grad_normed - first_sum / D - normed * second_sum / D)


def first_section(local_rows, weight):
    gathered = lax.all_gather(local_rows, "col", axis=0, tiled=True)
    share_rows = gathered.shape[0] // lax.axis_size("row")

    def partial_term(row_start, row_count):
        return jnp.dot(gathered, weight, preferred_element_type=jnp.float32)

    result = lax.psum_scatter(
        partial_term(jnp.int32(0), lax.axis_size("row") * share_rows),
        "row",
        scatter_dimension=0,
        tiled=True,
    )
    return (gathered, result)


def second_section(quarter_rows, weight):
    gathered = lax.all_gather(quarter_rows, "row", axis=0, tiled=True)
    share_rows = gathered.shape[0] // lax.axis_size("col")

    def partial_term(row_start, row_count):
        return jnp.dot(gathered, weight, preferred_element_type=jnp.float32)

    result = lax.psum_scatter(
        partial_term(jnp.int32(0), lax.axis_size("col") * share_rows),
        "col",
        scatter_dimension=0,
        tiled=True,
    )
    return (gathered, result)


def second_section_back(grad_local, gathered, weight):
    grad_all = lax.all_gather(grad_local, "col", axis=0, tiled=True)
    grad_weight = lax.dot_general(
        gathered, grad_all, (((0,), (0,)), ((), ())), preferred_element_type=jnp.float32
    )
    share_rows = grad_all.shape[0] // lax.axis_size("row")

    def partial_term(row_start, row_count):
        return lax.dot_general(
            grad_all, weight, (((1,), (1,)), ((), ())), preferred_element_type=jnp.float32
        )

    result = lax.psum_scatter(
        partial_term(jnp.int32(0), lax.axis_size("row") * share_rows),
        "row",
        scatter_dimension=0,
        tiled=True,
    )
    return (grad_weight, result)


def first_section_back(grad_quarter, gathered, weight):
    grad_all = lax.all_gather(grad_quarter, "row", axis=0, tiled=True)
    grad_weight = lax.dot_general(
        gathered, grad_all, (((0,), (0,)), ((), ())), preferred_element_type=jnp.float32
    )
    share_rows = grad_all.shape[0] // lax.axis_size("col")

    def partial_term(row_start, row_count):
        return lax.dot_general(
            grad_all, weight, (((1,), (1,)), ((), ())), preferred_element_type=jnp.float32
        )

    result = lax.psum_scatter(
        partial_term(jnp.int32(0), lax.axis_size("col") * share_rows).astype(jnp.bfloat16),
        "col",
        scatter_dimension=0,
        tiled=True,
    ).astype(jnp.float32)
    return (grad_weight, result)


def attend(triple_img):
    score_scale = HD ** (-0.5)
    query_rows = triple_img[:, :, 0]
    key_rows = triple_img[:, :, 1]
    value_rows = triple_img[:, :, 2]
    raw_scores = jnp.einsum(
        "qhd,khd->hqk", query_rows, key_rows, preferred_element_type=jnp.float32
    )
    scaled = raw_scores * score_scale
    peak_score = jnp.max(scaled, axis=-1, keepdims=True)
    exp_scores = jnp.exp(scaled - peak_score)
    exp_total = jnp.sum(exp_scores, axis=-1, keepdims=True)
    soft_weights = (exp_scores / exp_total).astype(jnp.bfloat16)
    mixed_rows = jnp.einsum(
        "hqk,khd->qhd", soft_weights, value_rows, preferred_element_type=jnp.float32
    )
    return (mixed_rows.astype(jnp.bfloat16), peak_score + jnp.log(exp_total))


def attend_back(packed):
    triple_img, log_total, grad_mixed = packed
    score_scale = HD ** (-0.5)
    query_rows = triple_img[:, :, 0]
    key_rows = triple_img[:, :, 1]
    value_rows = triple_img[:, :, 2]
    raw_scores = jnp.einsum(
        "qhd,khd->hqk", query_rows, key_rows, preferred_element_type=jnp.float32
    )
    soft_weights = jnp.exp(raw_scores * score_scale - log_total)
    weights_low = soft_weights.astype(jnp.bfloat16)
    grad_values = jnp.einsum(
        "hqk,qhd->khd", weights_low, grad_mixed, preferred_element_type=jnp.float32
    )
    grad_soft = jnp.einsum(
        "qhd,khd->hqk", grad_mixed, value_rows, preferred_element_type=jnp.float32
    )
    inner_prod = jnp.sum(grad_soft * soft_weights, axis=-1, keepdims=True)
    grad_raw = (score_scale * soft_weights * (grad_soft - inner_prod)).astype(jnp.bfloat16)
    grad_query = jnp.einsum("hqk,khd->qhd", grad_raw, key_rows, preferred_element_type=jnp.float32)
    grad_keys = jnp.einsum("hqk,qhd->khd", grad_raw, query_rows, preferred_element_type=jnp.float32)
    return jnp.stack([grad_query, grad_keys, grad_values], axis=2).astype(jnp.bfloat16)


def on_device(
    layer_input,
    teacher,
    valid,
    proj_in,
    bias_query,
    bias_value,
    proj_out,
    bias_out,
    norm1_gain,
    norm1_shift,
    norm2_gain,
    norm2_shift,
    w_up,
    bias_up,
    w_down,
    bias_down,
):
    heads_here = H // lax.axis_size("col")
    head_width = heads_here * HD
    feat_here = layer_input.shape[1]
    units_here = w_up.shape[1]
    gain_one = norm1_gain.astype(jnp.float32)
    gain_two = norm2_gain.astype(jnp.float32)
    residual_in = layer_input.astype(jnp.float32)
    normed1, scale1, mid_one = norm_forward(residual_in, gain_one, norm1_shift.astype(jnp.float32))
    norm1_all, projected = first_section(mid_one.astype(jnp.bfloat16), proj_in)
    quarter = projected.shape[0]
    images = quarter // SEQ
    bias_shift = jnp.stack(
        [
            bias_query.astype(jnp.float32).reshape(heads_here, HD),
            jnp.zeros((heads_here, HD), jnp.float32),
            bias_value.astype(jnp.float32).reshape(heads_here, HD),
        ],
        axis=1,
    )
    triple = (projected.reshape(quarter, heads_here, 3, HD) + bias_shift).astype(jnp.bfloat16)
    triple_imgs = triple.reshape(images, SEQ, heads_here, 3, HD)
    mixed_imgs, log_totals = lax.map(attend, triple_imgs)
    mixed_all, attn_part = second_section(mixed_imgs.reshape(quarter, head_width), proj_out)
    resid1 = residual_in + attn_part + bias_out.astype(jnp.float32)
    normed2, scale2, mid_two = norm_forward(resid1, gain_two, norm2_shift.astype(jnp.float32))
    norm2_all, pre_part = first_section(mid_two.astype(jnp.bfloat16), w_up)
    pre = pre_part + bias_up.astype(jnp.float32)
    activated, gelu_pull = jax.vjp(lambda entry: jax.nn.gelu(entry, approximate=True), pre)
    act_all, down_part = second_section(activated.astype(jnp.bfloat16), w_down)
    result = resid1 + down_part + bias_down.astype(jnp.float32)
    mask_rows = valid.astype(jnp.float32)
    error_rows = result - teacher.astype(jnp.float32)
    err_part = jnp.sum(mask_rows[:, None] * error_rows * error_rows)
    count_part = jnp.sum(mask_rows) / lax.axis_size("row")
    err_total, valid_count = lax.psum((err_part, count_part), ("dp", "row", "col"))
    loss_value = err_total / (valid_count * D)
    tokens_all = layer_input.shape[0] * lax.axis_size("dp") * lax.axis_size("col")
    factor = tokens_all / (2.0 * valid_count)
    grad_result = 2.0 * error_rows * (mask_rows[:, None] * factor)
    grad_branch2 = grad_result.astype(jnp.bfloat16)
    grad_w_down, grad_act = second_section_back(grad_branch2, act_all, w_down)
    grad_pre = gelu_pull(grad_act)[0].astype(jnp.bfloat16)
    grad_w_up, grad_norm2 = first_section_back(grad_pre, norm2_all, w_up)
    grad_resid1 = grad_result + norm_backward(grad_norm2, normed2, scale2, gain_two)
    grad_branch1 = grad_resid1.astype(jnp.bfloat16)
    grad_proj_out, grad_mixed = second_section_back(grad_branch1, mixed_all, proj_out)
    grad_mixed_imgs = grad_mixed.astype(jnp.bfloat16).reshape(images, SEQ, heads_here, HD)
    grad_triple = lax.map(attend_back, (triple_imgs, log_totals, grad_mixed_imgs))
    grad_triple = grad_triple.reshape(quarter, heads_here, 3, HD)
    grad_proj_in, grad_norm1 = first_section_back(
        grad_triple.reshape(quarter, 3 * head_width), norm1_all, proj_in
    )
    grad_input = grad_resid1 + norm_backward(grad_norm1, normed1, scale1, gain_one)
    row_at = lax.axis_index("row") * feat_here
    col_at = lax.axis_index("col") * head_width
    feature_terms = jnp.stack(
        [
            jnp.sum(grad_norm1 * normed1, axis=0),
            jnp.sum(grad_norm1, axis=0),
            jnp.sum(grad_norm2 * normed2, axis=0),
            jnp.sum(grad_norm2, axis=0),
            jnp.sum(grad_branch1.astype(jnp.float32), axis=0),
            jnp.sum(grad_branch2.astype(jnp.float32), axis=0),
        ]
    )
    feature_full = lax.dynamic_update_slice_in_dim(
        jnp.zeros((6, D), jnp.float32), feature_terms, row_at, 1
    )
    grad_float = grad_triple.astype(jnp.float32)
    head_terms = jnp.stack(
        [
            jnp.sum(grad_float[:, :, 0], axis=0).reshape(head_width),
            jnp.sum(grad_float[:, :, 2], axis=0).reshape(head_width),
        ]
    )
    head_full = lax.dynamic_update_slice_in_dim(
        jnp.zeros((2, H * HD), jnp.float32), head_terms, col_at, 1
    )
    unit_terms = jnp.sum(grad_pre.astype(jnp.float32), axis=0)
    unit_full = lax.dynamic_update_slice_in_dim(
        jnp.zeros((FF,), jnp.float32), unit_terms, lax.axis_index("col") * units_here, 0
    )
    feature_full, head_full, unit_full = lax.psum(
        (feature_full, head_full, unit_full), ("dp", "row", "col")
    )
    feature_mine = lax.dynamic_slice_in_dim(feature_full, row_at, feat_here, 1)
    head_mine = lax.dynamic_slice_in_dim(head_full, col_at, head_width, 1)
    unit_mine = lax.dynamic_slice_in_dim(
        unit_full, lax.axis_index("col") * units_here, units_here, 0
    )
    grad_proj_in, grad_w_up = (
        lax.psum_scatter(
            grad_proj_in.astype(jnp.bfloat16), "dp", scatter_dimension=0, tiled=True
        ).astype(jnp.float32),
        lax.psum_scatter(
            grad_w_up.astype(jnp.bfloat16), "dp", scatter_dimension=0, tiled=True
        ).astype(jnp.float32),
    )
    grad_proj_out, grad_w_down = (
        lax.psum_scatter(
            grad_proj_out.astype(jnp.bfloat16), "dp", scatter_dimension=1, tiled=True
        ).astype(jnp.float32),
        lax.psum_scatter(
            grad_w_down.astype(jnp.bfloat16), "dp", scatter_dimension=1, tiled=True
        ).astype(jnp.float32),
    )
    grad_proj_in = grad_proj_in.reshape(1, grad_proj_in.shape[0], grad_proj_in.shape[1])
    grad_w_up = grad_w_up.reshape(1, grad_w_up.shape[0], grad_w_up.shape[1])
    grad_proj_out = grad_proj_out.reshape(grad_proj_out.shape[0], 1, grad_proj_out.shape[1])
    grad_w_down = grad_w_down.reshape(grad_w_down.shape[0], 1, grad_w_down.shape[1])
    return (
        result.astype(jnp.bfloat16),
        loss_value,
        grad_input,
        grad_proj_in,
        head_mine[0],
        head_mine[1],
        grad_proj_out,
        feature_mine[4],
        feature_mine[0],
        feature_mine[1],
        feature_mine[2],
        feature_mine[3],
        grad_w_up,
        unit_mine,
        grad_w_down,
        feature_mine[5],
    )


MESH = pl.DeviceIdType.MESH
F32 = jnp.float32
BF16 = jnp.bfloat16
LOG2E = 1.4426950408889634
GELU_ROOT = 0.7978845608028654


def place():
    return lax.axis_index("dp"), lax.axis_index("row"), lax.axis_index("col")


def flip(row, other):
    return lax.rem(row // 2 + other // 2, 2) * 2 + lax.rem(row + other, 2)


def neighbours():
    dp, row, col = place()
    return dict(
        core=(1 - dp, row, col),
        x=(dp, flip(row, 1), col),
        y=(dp, flip(row, 2), col),
        diagonal=(dp, flip(row, 3), col),
        next=(dp, row, lax.rem(2 * col + 3 * (col // 2) + 1, 4)),
        prev=(dp, row, lax.rem(2 * col + col // 2 + 2, 4)),
    )


def images_group():
    dp, row, col = place()
    steps = [(core, step) for core in (0, 1) for step in range(4)][1:]
    return [(lax.rem(dp + core, 2), row, lax.rem(col + step, 4)) for core, step in steps]


def meet():
    dp, row, col = place()
    plane = [(core, k) for core in (0, 1) for k in range(4)][1:]
    peers = [(lax.rem(dp + core, 2), flip(row, k), col) for core, k in plane]
    peers += [peer for i, peer in enumerate(images_group()) if i != 3]
    barrier = pltpu.get_barrier_semaphore()
    for peer in peers:
        pl.semaphore_signal(barrier, inc=1, device_id=peer, device_id_type=MESH)
    pl.semaphore_wait(barrier, len(peers))


class Shuffle:
    def __init__(self, send_sems, recv_sems, local_sem):
        self.sems = send_sems, recv_sems, local_sem
        self.pending = []

    def remote(self, source, target, i, slot, peer):
        return pltpu.make_async_remote_copy(
            source, target, self.sems[0].at[i], self.sems[1].at[slot],
            device_id=peer, device_id_type=MESH,
        )

    def spread(self, pieces, blocks):
        dp, row, col = place()
        feat, own = pieces[0].shape[0], blocks.shape[1]
        for image in (0, 1):
            for half in (0, 1):
                chip = 2 * dp + image
                slot = flip(chip, row)
                mine = (dp == half) & (chip == row)
                source = pieces[image].at[:, pl.ds(half * own, own)]
                target = blocks.at[pl.ds(pl.multiple_of(slot * feat, 16), feat)]
                copy = self.remote(source, target, 2 * image + half, slot, (half, chip, col))
                here = pltpu.make_async_copy(source, blocks.at[pl.ds(0, feat)], self.sems[2])
                self.start(copy, here, mine)
        mine = dp == row // 2
        self.into = [
            (blocks.at[pl.ds(k * feat, feat)], k, None if k else mine) for k in range(4)
        ]

    def collect(self, blocks, pieces):
        dp, row, col = place()
        feat, own = pieces.shape[1], blocks.shape[1]
        image = lax.rem(row, 2)
        for k in range(4):
            owner = flip(row, k)
            mine = (dp == row // 2) & (owner == row)
            source = blocks.at[pl.ds(k * feat, feat)]
            target = pieces.at[image, :, pl.ds(pl.multiple_of(dp * own, 128), own)]
            copy = self.remote(source, target, k, 2 * image + dp, (row // 2, owner, col))
            here = pltpu.make_async_copy(source, target, self.sems[2])
            self.start(copy, here, mine)
        self.into = []
        for image in (0, 1):
            for half in (0, 1):
                mine = (dp == half) & (2 * dp + image == row)
                target = pieces.at[image, :, pl.ds(half * own, own)]
                self.into.append((target, 2 * image + half, mine))

    def start(self, copy, here, mine):
        pl.when(jnp.logical_not(mine))(copy.start)
        pl.when(mine)(here.start)
        self.pending.append((copy, here, mine))

    def arrive(self):
        dp, row, col = place()
        here = self.pending[0][1]
        for target, slot, own in self.into:
            copy = self.remote(target, target, 0, slot, (1 - dp, row, col))
            if own is None:
                copy.wait_recv()
            else:
                pl.when(jnp.logical_not(own))(copy.wait_recv)
                pl.when(own)(here.wait)

    def finish(self):
        for copy, _, mine in self.pending:
            pl.when(jnp.logical_not(mine))(copy.wait_send)


def mm(left, right):
    return jnp.dot(left, right, preferred_element_type=F32)


def mm_nt(left, right):
    return lax.dot_general(left, right, (((1,), (1,)), ((), ())), preferred_element_type=F32)


def each_rows(count, size, body):
    @pl.loop(0, count // size)
    def _(step):
        body(pl.ds(pl.multiple_of(step * size, size), size))


def fold(values):
    return sum(values[i : i + 16] for i in range(0, values.shape[0], 16))


def spread_lanes(source, spread, width):
    blocks = []
    for j in range(width // 256):
        low = 2 * HD * j // 128 * 128
        blocks.append(mm(source[:, low : low + 256], spread[low : low + 256, 256 * j : 256 * j + 256]))
    return jnp.concatenate(blocks, axis=1)


def transpose_into(target, source):
    @pl.loop(0, source.shape[1] // 128)
    def _(step):
        at = pl.ds(pl.multiple_of(step * 128, 128), 128)
        target[at, :] = source[:, at].T


class Sender:
    def __init__(self, send_sems, recv_sems):
        self.sems = (send_sems, recv_sems)
        self.count = 0
        self.copies = []

    def __call__(self, source, target, peer):
        copy = pltpu.make_async_remote_copy(
            source,
            target,
            self.sems[0].at[self.count],
            self.sems[1].at[self.count],
            device_id=peer,
            device_id_type=MESH,
        )
        self.count += 1
        copy.start()
        self.copies.append(copy)
        return copy

    def finish(self):
        for copy in self.copies:
            copy.wait_send()


class Copier:
    def __init__(self, sems):
        self.sems = sems
        self.count = 0

    def __call__(self, source, target):
        copy = pltpu.make_async_copy(source, target, self.sems.at[self.count])
        self.count += 1
        copy.start()
        return copy


def norm_stats(values):
    mean_rows = jnp.mean(values, axis=-1, keepdims=True)
    centered = values - mean_rows
    inv_scale = lax.rsqrt(jnp.mean(centered * centered, axis=-1, keepdims=True) + EPS)
    return centered * inv_scale, inv_scale


def forward_kernel(
    own_tokens,
    x_first,
    x_second,
    teacher_first,
    teacher_second,
    valid_ref,
    params_ref,
    key_lane_ref,
    one_lane_ref,
    bias_spread_ref,
    spread_ref,
    rest_spread_ref,
    attn_ref,
    ff_ref,
    wpad_out,
    wff_out,
    triple_out,
    mixed_out,
    act_out,
    slope_out,
    norm1t_out,
    norm2t_out,
    rest_hbm,
    lse_hbm,
    act_rest_hbm,
    slope_rest_hbm,
    resid_hbm,
    x_hbm,
    branch_out,
    brancht_out,
    result_out,
    err_out,
    feature_ref,
    count_out,
    rest_out,
    lse_out,
    act_rest_out,
    slope_rest_out,
    resid_out,
    x_rows,
    x_blocks,
    teacher_blocks,
    valid_in,
    features_in,
    biases_in,
    counts_in,
    wattn,
    wff,
    wpad,
    triple,
    mixed,
    act,
    slope,
    norm1,
    norm2,
    turned,
    part,
    give1,
    got1,
    give2,
    got2,
    local_sems,
    send_sems,
    recv_sems,
    shuffle_sems,
):
    peers = neighbours()
    meet()
    feat = attn_ref.shape[0]
    half = feat // 2
    depth = 4 * feat
    tokens = norm1.shape[0]
    own = tokens // 2
    main = ff_ref.shape[1] // 2
    qkv = triple.shape[2]
    wide = features_in.shape[2]
    heads_wide = bias_spread_ref.shape[0]
    send = Sender(send_sems, recv_sems)
    keep = Copier(local_sems)

    def rows(block, low=0, size=None):
        return pl.ds(block * feat + low, feat if size is None else size)

    own_attn = keep(attn_ref, wattn.at[0, rows(0)])
    own_ff = keep(ff_ref, wff.at[0, rows(0)])
    az, ax, ay, a_low, a_high = ([None] * 4 for _ in range(5))

    def attn_source(s):
        return attn_ref if s == 0 else wattn.at[s, rows(0)]

    def attn_ring(s):
        az[s + 1] = send(attn_source(s), wattn.at[s + 1, rows(0)], peers["next"])

    def attn_plane(s):
        ax[s] = send(attn_source(s), wattn.at[s, rows(1)], peers["x"])
        ay[s] = send(attn_source(s), wattn.at[s, rows(2)], peers["y"])

    def attn_last(s):
        ax[s].wait_recv()
        a_low[s] = send(
            wattn.at[s, rows(1, 0, half)], wattn.at[s, rows(3, 0, half)], peers["y"]
        )
        ay[s].wait_recv()
        a_high[s] = send(
            wattn.at[s, rows(2, half, half)], wattn.at[s, rows(3, half, half)], peers["x"]
        )

    fz, fy, fx = ([None] * 4 for _ in range(3))

    def ff_first():
        return (
            send(ff_ref.at[pl.ds(0, half)], wff.at[0, rows(1, 0, half)], peers["x"]),
            send(ff_ref.at[pl.ds(half, half)], wff.at[0, rows(2, half, half)], peers["y"]),
        )

    def ff_ring(s):
        fz[s + 1] = [
            send(wff.at[s, piece], wff.at[s + 1, piece], peers["next"])
            for piece in (rows(0), rows(1, 0, half), rows(2, half, half))
        ]

    def ff_last(s):
        fy[s] = [
            send(wff.at[s, rows(k, 0, half)], wff.at[s, rows(k + 2, 0, half)], peers["y"])
            for k in (0, 1)
        ]
        fx[s] = [
            send(wff.at[s, rows(k, half, half)], wff.at[s, rows(k + 1, half, half)], peers["x"])
            for k in (0, 2)
        ]

    def arrive(copies):
        for copy in copies:
            copy.wait_recv()

    def attn_compute(s):
        arrive([a_low[s], a_high[s]])
        slot = s % 2
        if s == 0:
            own_attn.wait()
        if s >= 2:
            for copy in saved[s - 2]:
                copy.wait()

        def unpack(at):
            block = wattn[s, at, :]
            wpad[slot, at, :] = spread_lanes(block, spread_ref, wpad.shape[2]).astype(BF16)
            extra = mm(block[:, block.shape[1] - 128 :], rest_spread_ref[s]).astype(BF16)
            if s == 0:
                rest_out[at, :] = extra
            else:
                rest_out[at, :] = rest_out[at, :] + extra

        each_rows(depth, feat, unpack)

        def project(at):
            bias = mm(biases_in[s, :, :heads_wide].astype(BF16), bias_spread_ref[...])
            values = mm(norm1[at, :], wpad[slot, :, :qkv]) + (bias[0:1] + one_lane_ref[...])
            spot = lax.broadcasted_iota(jnp.int32, (tokens, 1), 0)
            shift = lax.axis_index("dp") * own
            token = jnp.where(spot < own, spot + shift, spot - shift)
            values = values + jnp.where(token < SEQ, 0.0, -1e30) * key_lane_ref[...]
            triple[slot, at, :] = values.astype(BF16)

        each_rows(tokens, tokens, project)
        scale = LOG2E * HD**-0.5
        for h in range(qkv // 384):
            query_at, key_at, value_at = (pl.ds((3 * h + j) * 128, 128) for j in range(3))
            value_turned = triple[slot, :, value_at].T

            def head(at, h=h, query_at=query_at, key_at=key_at, value_turned=value_turned):
                scores = mm_nt(triple[slot, :, key_at], triple[slot, at, query_at])
                peak = jnp.max(scores, axis=0, keepdims=True)
                weights = jnp.exp2((scores - peak) * scale)
                total = jnp.sum(weights, axis=0, keepdims=True)
                lse_out[2 * s + h, :, at] = peak * scale + jnp.log2(total)
                values = mm(value_turned, weights.astype(BF16)) / total
                mixed[s, at, pl.ds(h * 128, 128)] = values.T.astype(BF16)

            each_rows(tokens, own, head)

        def out(at):
            values = mm_nt(mixed[s, at, :], wpad[slot, :, qkv:])
            return values if s == 0 else part[at, :] + values

        swap = None
        if s < 3:
            part[...] = out(pl.ds(0, tokens))
        else:
            give1[...] = out(pl.ds(own, own)).astype(BF16)
            swap = send(give1, got1, peers["core"])
            part[pl.ds(0, own), :] = out(pl.ds(0, own))
        saved.append(
            [
                keep(wpad.at[slot], wpad_out.at[s]),
                keep(triple.at[slot], triple_out.at[s]),
                keep(mixed.at[s], mixed_out.at[s]),
            ]
        )
        return swap

    def gelu(pre):
        inner = GELU_ROOT * (pre + 0.044715 * pre * pre * pre)
        tanh = jnp.tanh(inner)
        rise = 0.5 * (1.0 + tanh)
        bend = 0.5 * pre * (1.0 - tanh * tanh) * (GELU_ROOT * (1.0 + 0.134145 * pre * pre))
        return (pre * rise).astype(BF16), (rise + bend).astype(BF16)

    def ff_compute(s):
        arrive(fy[s] + fx[s])

        def block(at):
            pre = mm(norm2[at, :], wff[s, :, :main]) + biases_in[s, 0:1, heads_wide : heads_wide + main]
            low, bent = gelu(pre)
            act[s, at, :] = low
            slope[s, at, :] = bent
            return part[at, :] + mm_nt(low, wff[s, :, main:])

        swap = None
        if s < 3:
            part[...] = block(pl.ds(0, tokens))
        else:
            give2[...] = block(pl.ds(own, own)).astype(BF16)
            swap = send(give2, got2, peers["core"])
            part[pl.ds(0, own), :] = block(pl.ds(0, own))
        ff_saved.extend(
            [
                keep(act.at[s], act_out.at[s]),
                keep(slope.at[s], slope_out.at[s]),
                keep(wff.at[s], wff_out.at[s]),
            ]
        )
        return swap

    def rest_compute():
        tail_at = heads_wide + main - (2 * heads_wide - wattn.shape[2] + 128)
        bias = mm(biases_in[0, :, tail_at : tail_at + 128].astype(BF16), rest_spread_ref[0, :, :128])
        for s in (1, 2, 3):
            values = biases_in[s, :, tail_at : tail_at + 128].astype(BF16)
            bias = bias + mm(values, rest_spread_ref[s, :, :128])

        def block(at):
            pre = mm(norm2[at, :], rest_out[:, :128]) + bias[0:1]
            low, bent = gelu(pre)
            act_rest_out[at, :] = low
            slope_rest_out[at, :] = bent
            part[at, :] = mm_nt(low, rest_out[:, 128:])

        each_rows(tokens, tokens, block)

    saved, ff_saved = [], []
    x_move = Shuffle(shuffle_sems.at[0], shuffle_sems.at[1], shuffle_sems.at[2, 0])
    x_move.spread((x_first, x_second), x_blocks)
    attn_ring(0)
    first = ff_first()
    attn_plane(0)
    valid_row = valid_ref[0, 0:1, :] + valid_ref[1, 0:1, :]
    counts_in[0] = jnp.broadcast_to(jnp.sum(valid_row, axis=1, keepdims=True), (8, 128))
    own_params = [
        keep(params_ref.at[:, pl.ds(0, wide)], features_in.at[0]),
        keep(params_ref.at[:, pl.ds(wide, biases_in.shape[2])], biases_in.at[0]),
    ]
    smalls = [
        send(params_ref.at[:, pl.ds(0, wide)], features_in.at[k], peers[name])
        for k, name in ((1, "x"), (2, "y"), (3, "diagonal"))
    ]
    dp, row, col = place()
    ring_two = (dp, row, 3 - col)
    smalls += [
        send(params_ref.at[:, pl.ds(wide, biases_in.shape[2])], biases_in.at[s], peer)
        for s, peer in ((1, peers["next"]), (2, ring_two), (3, peers["prev"]))
    ]
    counts = [
        send(counts_in.at[0], counts_in.at[1 + i], peer) for i, peer in enumerate(images_group())
    ]
    teacher_move = Shuffle(shuffle_sems.at[3], shuffle_sems.at[4], shuffle_sems.at[2, 1])

    valid_move = send(valid_ref, valid_in, peers["core"])

    az[1].wait_recv()
    attn_ring(1)
    attn_plane(1)
    attn_last(0)
    az[2].wait_recv()
    attn_ring(2)
    attn_plane(2)
    for copy in own_params:
        copy.wait()
    arrive(smalls)
    feature_ref[...] = jnp.zeros_like(feature_ref)
    for i in range(6):
        feature_ref[i : i + 1, :] = jnp.concatenate(
            [features_in[k, 0:1, feat * i : feat * (i + 1)] for k in range(4)], axis=1
        )
    x_move.arrive()
    for start in range(0, own, 128):
        x_rows[pl.ds(start, 128), :] = x_blocks[:, pl.ds(start, 128)].T
    late = [keep(x_rows, x_hbm)]

    def first_norm(at):
        normed, _ = norm_stats(x_rows[at, :].astype(F32))
        norm1[at, :] = (normed * feature_ref[0:1] + feature_ref[1:2]).astype(BF16)

    each_rows(own, 128, first_norm)
    swap1 = send(norm1.at[pl.ds(0, own)], norm1.at[pl.ds(own, own)], peers["core"])
    az[3].wait_recv()
    attn_plane(3)
    own_ff.wait()
    arrive(first)
    ff_ring(0)
    attn_last(1)
    swap1.wait_recv()
    attn_compute(0)
    attn_last(2)
    attn_compute(1)
    attn_last(3)
    ff_last(0)
    arrive(fz[1])
    ff_ring(1)
    ff_last(1)
    teacher_move.spread((teacher_first, teacher_second), teacher_blocks)
    attn_compute(2)
    swap2 = attn_compute(3)
    swap2.wait_recv()

    def second_norm(at):
        values = x_rows[at, :].astype(F32) + part[at, :] + got1[at, :].astype(F32) + feature_ref[4:5]
        resid_out[at, :] = values
        normed, _ = norm_stats(values)
        norm2[at, :] = (normed * feature_ref[2:3] + feature_ref[3:4]).astype(BF16)

    each_rows(own, 128, second_norm)
    late += [keep(resid_out, resid_hbm), keep(rest_out, rest_hbm), keep(lse_out, lse_hbm)]
    swap3 = send(norm2.at[pl.ds(0, own)], norm2.at[pl.ds(own, own)], peers["core"])
    arrive(fz[2])
    ff_ring(2)
    ff_last(2)
    transpose_into(turned, norm1)
    turn1 = keep(turned, norm1t_out)
    swap3.wait_recv()
    rest_compute()
    late += [keep(act_rest_out, act_rest_hbm), keep(slope_rest_out, slope_rest_hbm)]
    turn1.wait()
    transpose_into(turned, norm2)
    turn2 = keep(turned, norm2t_out)
    ff_compute(0)
    arrive(fz[3])
    ff_last(3)
    ff_compute(1)
    ff_compute(2)
    swap4 = ff_compute(3)
    err_out[...] = jnp.zeros_like(err_out)
    arrive(counts)
    count = counts_in[0]
    for i in range(1, 8):
        count = count + counts_in[i]
    count_out[...] = count
    factor = (own_tokens * 8.0) / count[0:1, 0:1]
    teacher_move.arrive()
    swap4.wait_recv()

    valid_move.wait_recv()
    image, from_here = lax.rem(row, 2), dp == row // 2

    def finish(start):
        at = pl.ds(start, 128)
        values = resid_out[at, :] + part[at, :] + got2[at, :].astype(F32) + feature_ref[5:6]
        result_out[:, at] = values.astype(BF16).T
        error = values - teacher_blocks[:, at].T.astype(F32)
        lanes_at = pl.ds(pl.multiple_of(dp * own + start, 128), 128)
        counts_row = jnp.where(
            from_here, valid_ref[image, :, lanes_at], valid_in[image, :, lanes_at]
        )
        masked = error * counts_row.T[:, 0:1]
        err_out[...] = err_out[...] + fold(error * masked)
        branch_out[at, :] = (masked * factor).astype(BF16)

    def turn(start):
        brancht_out[:, pl.ds(start, 128)] = branch_out[pl.ds(start, 128), :].T

    swaps = []
    for start in range(0, own, 128):
        finish(start)
        swaps.append(
            send(
                branch_out.at[pl.ds(start, 128)],
                branch_out.at[pl.ds(own + start, 128)],
                peers["core"],
            )
        )
        turn(start)
    for start, swap in zip(range(own, tokens, 128), swaps):
        swap.wait_recv()
        turn(start)
    turn2.wait()
    for copies in saved[2:]:
        for copy in copies:
            copy.wait()
    for copy in ff_saved:
        copy.wait()
    for copy in late:
        copy.wait()
    send.finish()
    x_move.finish()
    teacher_move.finish()


def forward_call(arrays, own_tokens, feat, lanes, main, qkv, mix, own, depth):
    tokens = 2 * own
    wide = (6 * feat + 127) // 128 * 128
    narrow = arrays[5].shape[1] - wide
    anywhere = pl.BlockSpec(memory_space=pl.ANY)
    local = pl.BlockSpec(memory_space=pltpu.VMEM)
    shapes = [
        ((4, depth, qkv + mix), BF16, anywhere),
        ((4, depth, 2 * main), BF16, anywhere),
        ((4, tokens, qkv), BF16, anywhere),
        ((4, tokens, mix), BF16, anywhere),
        ((4, tokens, main), BF16, anywhere),
        ((4, tokens, main), BF16, anywhere),
        ((depth, tokens), BF16, anywhere),
        ((depth, tokens), BF16, anywhere),
        ((depth, 256), BF16, anywhere),
        ((8, 1, tokens), F32, anywhere),
        ((tokens, 128), BF16, anywhere),
        ((tokens, 128), BF16, anywhere),
        ((own, depth), F32, anywhere),
        ((own, depth), BF16, anywhere),
        ((tokens, depth), BF16, local),
        ((depth, tokens), BF16, local),
        ((depth, own), BF16, local),
        ((16, depth), F32, local),
        ((8, depth), F32, local),
        ((8, 128), F32, local),
    ]
    return pl.pallas_call(
        functools.partial(forward_kernel, own_tokens),
        out_shape=[jax.ShapeDtypeStruct(shape, dtype) for shape, dtype, _ in shapes],
        in_specs=[anywhere] * 4 + [local] * 7 + [anywhere] * 2,
        out_specs=[spec for _, _, spec in shapes],
        scratch_shapes=[
            pltpu.VMEM((depth, 256), BF16),
            pltpu.VMEM((8, 1, tokens), F32),
            pltpu.VMEM((tokens, 128), BF16),
            pltpu.VMEM((tokens, 128), BF16),
            pltpu.VMEM((own, depth), F32),
            pltpu.VMEM((own, depth), BF16),
            pltpu.VMEM((depth, own), BF16),
            pltpu.VMEM((depth, own), BF16),
            pltpu.VMEM((2, 8, tokens), F32),
            pltpu.VMEM((4, 8, wide), F32),
            pltpu.VMEM((4, 8, narrow), F32),
            pltpu.VMEM((8, 8, 128), F32),
            pltpu.VMEM((4, depth, lanes), BF16),
            pltpu.VMEM((4, depth, 2 * main), BF16),
            pltpu.VMEM((2, depth, qkv + mix), BF16),
            pltpu.VMEM((2, tokens, qkv), BF16),
            pltpu.VMEM((4, tokens, mix), BF16),
            pltpu.VMEM((4, tokens, main), BF16),
            pltpu.VMEM((4, tokens, main), BF16),
            pltpu.VMEM((tokens, depth), BF16),
            pltpu.VMEM((tokens, depth), BF16),
            pltpu.VMEM((depth, tokens), BF16),
            pltpu.VMEM((tokens, depth), F32),
            pltpu.VMEM((own, depth), BF16),
            pltpu.VMEM((own, depth), BF16),
            pltpu.VMEM((own, depth), BF16),
            pltpu.VMEM((own, depth), BF16),
            pltpu.SemaphoreType.DMA((40,)),
            pltpu.SemaphoreType.DMA((72,)),
            pltpu.SemaphoreType.DMA((72,)),
            pltpu.SemaphoreType.DMA((5, 4)),
        ],
        compiler_params=pltpu.CompilerParams(
            collective_id=1, has_side_effects=True, vmem_limit_bytes=62 << 20
        ),
    )(*arrays)


def backward_kernel(
    branch2_ref,
    rest_hbm,
    act_rest_hbm,
    slope_rest_hbm,
    lse_hbm,
    feature_ref,
    spread_hbm,
    rest_spread_hbm,
    err_ref,
    count_ref,
    result_blocks,
    x_hbm,
    resid_hbm,
    norm1t_hbm,
    norm2t_hbm,
    branch2t_hbm,
    wpad_hbm,
    wff_hbm,
    triple_hbm,
    mixed_hbm,
    act_hbm,
    slope_hbm,
    grad_pieces,
    result_pieces,
    sums_out,
    bias_out,
    attn_out,
    ff_out,
    rest_ref,
    act_rest_ref,
    slope_rest_ref,
    lse_ref,
    spread_ref,
    rest_spread_ref,
    x_rows,
    grad_blocks,
    terms,
    terms_mine,
    terms_in,
    sums_in,
    bias_mine,
    bias_turn,
    bias_in,
    bias_plane,
    units_out,
    units_rest_out,
    heads_out,
    gattn,
    gff,
    wslot,
    kept,
    grad_pre,
    grad_rest,
    normt,
    brancht,
    branch1,
    part,
    give,
    got,
    grad_mid,
    dtriple,
    grad_mixed,
    grad_key,
    grad_value,
    inner_row,
    ra,
    rb,
    r1,
    r2,
    rz,
    ry,
    rx,
    rzl,
    rzh,
    rfx,
    rfy,
    local_sems,
    send_sems,
    recv_sems,
    shuffle_sems,
):
    peers = neighbours()
    feat = 2 * attn_out.shape[1]
    half = feat // 2
    depth = 4 * feat
    tokens = branch2_ref.shape[0]
    own = tokens // 2
    main = gff.shape[2] // 2
    qkv = triple_hbm.shape[2]
    send = Sender(send_sems, recv_sems)
    keep = Copier(local_sems)

    def rows(block, low=0, size=None):
        return pl.ds(block * feat + low, feat if size is None else size)

    def load_ff(s):
        slot = s % 2
        return [
            keep(wff_hbm.at[s], wslot.at[slot]),
            keep(act_hbm.at[s], kept.at[slot, :, pl.ds(0, main)]),
            keep(slope_hbm.at[s], kept.at[slot, :, pl.ds(main, main)]),
        ]

    def load_attn(s):
        slot = s % 2
        return [
            keep(wpad_hbm.at[s], wslot.at[slot]),
            keep(triple_hbm.at[s], kept.at[slot, :, pl.ds(0, qkv)]),
            keep(mixed_hbm.at[s], kept.at[slot, :, pl.ds(qkv, grad_mixed.shape[1])]),
        ]

    loads = {3: load_ff(3)}
    turns = [keep(norm2t_hbm, normt), keep(branch2t_hbm, brancht)]
    loads[2] = load_ff(2)
    load_late = [
        keep(rest_hbm, rest_ref),
        keep(act_rest_hbm, act_rest_ref),
        keep(slope_rest_hbm, slope_rest_ref),
        keep(resid_hbm, grad_mid),
        keep(x_hbm, x_rows),
        keep(lse_hbm, lse_ref),
        keep(spread_hbm, spread_ref),
        keep(rest_spread_hbm, rest_spread_ref),
    ]
    meet()
    result_move = Shuffle(shuffle_sems.at[0], shuffle_sems.at[1], shuffle_sems.at[2, 0])
    grad_move = Shuffle(shuffle_sems.at[3], shuffle_sems.at[4], shuffle_sems.at[2, 1])
    cy, cx, zl, zh = ([None] * 4 for _ in range(4))
    ca, cb, c1, c2, cz = ([None] * 4 for _ in range(5))

    def add_into(target, at, *sources):
        size = at.size

        @pl.loop(0, size // 16)
        def _(step):
            here = pl.ds(pl.multiple_of(at.start + step * 16, 16), 16)
            there = pl.ds(pl.multiple_of(step * 16, 16), 16)
            total = target[here, :].astype(F32)
            for source in sources:
                total = total + source[there, :].astype(F32)
            target[here, :] = total.astype(BF16)

    def column_sum(values):
        return jnp.sum(values.astype(F32), axis=0, keepdims=True)

    def ff_compute(s):
        slot = s % 2
        for copy in loads[s]:
            copy.wait()
        units_out[s] = jnp.zeros((1, main), F32)

        def block(at):
            grad = mm(branch2_ref[at, :], wslot[slot, :, main : 2 * main])
            low = (grad * kept[slot, at, main:].astype(F32)).astype(BF16)
            grad_pre[at, :] = low
            units_out[s] = units_out[s] + column_sum(low)
            values = mm_nt(low, wslot[slot, :, :main])
            part[at, :] = values if s == 3 else part[at, :] + values

        each_rows(tokens, own, block)
        if s == 3:
            for copy in turns:
                copy.wait()

        def grads(at):
            gff[s, at, :main] = mm(normt[at, :], grad_pre[...]).astype(BF16)
            gff[s, at, main:] = mm(brancht[at, :], kept[slot, :, :main]).astype(BF16)

        each_rows(depth, 2 * feat, grads)
        cy[s] = [
            send(gff.at[s, rows(k, 0, half)], ry.at[s, k - 2], peers["y"]) for k in (2, 3)
        ]
        cx[s] = [
            send(gff.at[s, rows(k, half, half)], rx.at[s, k // 2], peers["x"]) for k in (1, 3)
        ]
        if s >= 2:
            loads[s - 2] = load_ff(s - 2)

    def rest_compute():
        units_rest_out[...] = jnp.zeros_like(units_rest_out)

        def block(at):
            grad = mm(branch2_ref[at, :], rest_ref[:, 128:])
            low = (grad * slope_rest_ref[at, :].astype(F32)).astype(BF16)
            grad_pre[at, :128] = low
            units_rest_out[...] = units_rest_out[...] + column_sum(low)
            return part[at, :] + mm_nt(low, rest_ref[:, :128])

        give[...] = block(pl.ds(own, own)).astype(BF16)
        swap = send(give, got, peers["core"])
        part[pl.ds(0, own), :] = block(pl.ds(0, own))

        def grads(at):
            grad_rest[at, :128] = mm(normt[at, :], grad_pre[:, :128]).astype(BF16)
            grad_rest[at, 128:] = mm(brancht[at, :], act_rest_ref[...]).astype(BF16)

        each_rows(depth, 2 * feat, grads)
        return swap

    def ff_add(s):
        for copy in cy[s] + cx[s]:
            copy.wait_recv()
        last = s == 3
        if not last:
            for copy in zl[s] + zh[s]:
                copy.wait_recv()
        lows, highs = [], []
        for i, k in enumerate((0, 1)):
            piece = rows(k, 0, half)
            add_into(gff.at[s], piece, ry.at[s, i], *([] if last else [rzl.at[s, i]]))
            lows.append((piece, i))
        for i, k in enumerate((0, 2)):
            piece = rows(k, half, half)
            add_into(gff.at[s], piece, rx.at[s, i], *([] if last else [rzh.at[s, i]]))
            highs.append((piece, i))
        if s:
            zl[s - 1] = [
                send(gff.at[s, piece], rzl.at[s - 1, i], peers["prev"]) for piece, i in lows
            ]
            zh[s - 1] = [
                send(gff.at[s, piece], rzh.at[s - 1, i], peers["prev"]) for piece, i in highs
            ]

    def attn_compute(s):
        slot = s % 2
        for copy in attn_loads[s]:
            copy.wait()

        def back_out(at):
            grad_mixed[at, :] = mm(branch1[at, :], wslot[slot, :, qkv:]).astype(BF16)

        each_rows(tokens, tokens, back_out)
        scale = HD**-0.5
        for h in range(qkv // 384):
            query_at, key_at, value_at = (pl.ds((3 * h + j) * 128, 128) for j in range(3))
            mix_at = pl.ds(h * 128, 128)
            value_of_mix = pl.ds(qkv + h * 128, 128)
            key_turned = kept[slot, :, key_at].T
            product = grad_mixed[:, mix_at].astype(F32) * kept[slot, :, value_of_mix].astype(F32)
            inner_row[...] = jnp.sum(product.T, axis=0, keepdims=True)
            grad_key[...] = jnp.zeros_like(grad_key)
            grad_value[...] = jnp.zeros_like(grad_value)

            def head(at, h=h, query_at=query_at, key_at=key_at, value_at=value_at,
                     mix_at=mix_at, key_turned=key_turned):
                query = kept[slot, at, query_at]
                grad = grad_mixed[at, mix_at]
                scores = mm_nt(kept[slot, :, key_at], query)
                weights = jnp.exp2(scores * (scale * LOG2E) - lse_ref[2 * s + h, :, at])
                grad_soft = mm_nt(kept[slot, :, value_at], grad)
                grad_raw = (weights * (grad_soft - inner_row[:, at]) * scale).astype(BF16)
                grad_value[...] += mm(weights.astype(BF16), grad)
                grad_key[...] += mm(grad_raw, query)
                dtriple[at, query_at] = mm(key_turned, grad_raw).T.astype(BF16)

            each_rows(tokens, own, head)
            dtriple[:, key_at] = grad_key[...].astype(BF16)
            dtriple[:, value_at] = grad_value[...].astype(BF16)
        heads_out[s] = jnp.zeros((1, qkv), F32)

        def back_in(at):
            values = mm_nt(dtriple[at, :], wslot[slot, :, :qkv])
            heads_out[s] = heads_out[s] + column_sum(dtriple[at, :])
            return values if s == 3 else part[at, :] + values

        swap = None
        if s:
            for at in (pl.ds(0, own), pl.ds(own, own)):
                part[at, :] = back_in(at)
        else:
            give[...] = back_in(pl.ds(own, own)).astype(BF16)
            swap = send(give, got, peers["core"])
            part[pl.ds(0, own), :] = back_in(pl.ds(0, own))

        def grads(at):
            first = mm(normt[at, :], dtriple[...]).astype(BF16)
            second = mm(brancht[at, :], kept[slot, :, qkv:]).astype(BF16)
            tiles = [0.0] * (gattn.shape[2] // 128)
            for j in range((qkv + second.shape[1]) // 256):
                low, to = 2 * HD * j // 128 * 128, 256 * j
                block = first[:, to : to + 256] if to < qkv else second[:, to - qkv : to - qkv + 256]
                moved = mm_nt(block, spread_ref[low : low + 256, to : to + 256])
                for i in (0, 1):
                    tiles[low // 128 + i] += moved[:, 128 * i : 128 * i + 128]
            tiles[-1] += mm_nt(grad_rest[at, :], rest_spread_ref[s])
            gattn[s, at, :] = jnp.concatenate(tiles, axis=1).astype(BF16)

        each_rows(depth, 2 * feat, grads)
        ca[s] = send(gattn.at[s, rows(3, 0, half)], ra.at[s], peers["y"])
        cb[s] = send(gattn.at[s, rows(3, half, half)], rb.at[s], peers["x"])
        if s >= 2:
            attn_loads[s - 2] = load_attn(s - 2)
        return swap

    def attn_plane(s):
        ca[s].wait_recv()
        add_into(gattn.at[s], rows(1, 0, half), ra.at[s])
        c1[s] = send(gattn.at[s, rows(1)], r1.at[s], peers["x"])
        cb[s].wait_recv()
        add_into(gattn.at[s], rows(2, half, half), rb.at[s])
        c2[s] = send(gattn.at[s, rows(2)], r2.at[s], peers["y"])

    def attn_ring(s):
        c1[s].wait_recv()
        c2[s].wait_recv()
        if s < 3:
            cz[s].wait_recv()
        add_into(gattn.at[s], rows(0), r1.at[s], r2.at[s], *([rz.at[s]] if s < 3 else []))
        if s:
            cz[s - 1] = send(gattn.at[s, rows(0)], rz.at[s - 1], peers["prev"])

    terms[...] = jnp.zeros_like(terms)

    def add_term(index, values):
        terms[index] = terms[index] + fold(values)

    result_move.collect(result_blocks, result_pieces)
    ff_compute(3)
    ff_compute(2)
    ff_compute(1)
    ff_add(3)
    ff_compute(0)
    attn_loads = {3: load_attn(3), 2: load_attn(2)}
    for copy in load_late:
        copy.wait()
    swap1 = rest_compute()
    load_norm = keep(norm1t_hbm, normt)
    swap1.wait_recv()

    def mid(at):
        normed, inv_scale = norm_stats(grad_mid[at, :])
        grad_norm = part[at, :] + got[at, :].astype(F32)
        add_term(2, grad_norm * normed)
        add_term(3, grad_norm)
        scaled = grad_norm * feature_ref[2:3]
        first = jnp.mean(scaled, axis=-1, keepdims=True)
        second = jnp.mean(scaled * normed, axis=-1, keepdims=True)
        grad = branch2_ref[at, :].astype(F32)
        grad = grad + inv_scale * (scaled - first - normed * second)
        grad_mid[at, :] = grad
        low = grad.astype(BF16)
        branch1[at, :] = low
        add_term(4, low.astype(F32))
        add_term(5, branch2_ref[at, :].astype(F32))

    each_rows(own, 64, mid)
    swap2 = send(branch1.at[pl.ds(0, own)], branch1.at[pl.ds(own, own)], peers["core"])
    swap2.wait_recv()
    load_norm.wait()
    transpose_into(brancht, branch1)
    attn_compute(3)
    ff_add(2)
    attn_compute(2)
    attn_plane(3)
    attn_compute(1)
    attn_plane(2)
    attn_ring(3)
    ff_add(1)
    swap1.wait_send()
    swap3 = attn_compute(0)
    attn_plane(1)
    attn_ring(2)
    attn_plane(0)
    swap3.wait_recv()

    def last(at):
        normed, inv_scale = norm_stats(x_rows[at, :].astype(F32))
        grad_norm = part[at, :] + got[at, :].astype(F32)
        add_term(0, grad_norm * normed)
        add_term(1, grad_norm)
        scaled = grad_norm * feature_ref[0:1]
        first = jnp.mean(scaled, axis=-1, keepdims=True)
        second = jnp.mean(scaled * normed, axis=-1, keepdims=True)
        grad = grad_mid[at, :] + inv_scale * (scaled - first - normed * second)
        grad_blocks[:, at] = grad.astype(BF16).T

    each_rows(own, 128, last)
    grad_move.collect(grad_blocks, grad_pieces)
    terms_mine[...] = jnp.zeros_like(terms_mine)
    bias_mine[...] = jnp.zeros_like(bias_mine)
    for i in range(7):
        if i < 6:
            row_sum = jnp.sum(terms[i], axis=0, keepdims=True)
        else:
            err = jnp.sum(jnp.sum(err_ref[...], axis=0, keepdims=True), axis=1, keepdims=True)
            row_sum = jnp.broadcast_to(err, (1, depth))
        for k in range(4):
            terms_mine[k, i : i + 1, :] = row_sum[:, k * feat : (k + 1) * feat]
    wide = bias_mine.shape[2]
    for s in range(4):
        bias_mine[s, 0:1, :qkv] = heads_out[s]
        bias_mine[s, 0:1, qkv : qkv + main] = units_out[s]
        bias_mine[s, 0:1, qkv + main :] = units_rest_out[...]
    dp, row, col = place()
    ring_two = (dp, row, 3 - col)
    sides = ((1, "x"), (2, "y"), (3, "diagonal"))
    term_sends = [send(terms_mine.at[k], terms_in.at[k - 1], peers[name]) for k, name in sides]
    bias_sends = [
        send(bias_mine.at[s], bias_turn.at[s - 1], peer)
        for s, peer in ((1, peers["prev"]), (2, ring_two), (3, peers["next"]))
    ]
    ff_add(0)
    end_low = send(gff.at[0, rows(1, 0, half)], rfx, peers["x"])
    end_high = send(gff.at[0, rows(2, half, half)], rfy, peers["y"])
    attn_ring(1)
    for copy in term_sends + bias_sends:
        copy.wait_recv()
    terms_mine[0] = terms_mine[0] + terms_in[0] + terms_in[1] + terms_in[2]
    sum_sends = [
        send(terms_mine.at[0], sums_in.at[i], peer) for i, peer in enumerate(images_group())
    ]
    bias_plane[...] = bias_mine[0]
    for s in (1, 2, 3):
        bias_plane[s : s + 1, :] = bias_turn[s - 1, 0:1, :]
    plane_sends = [send(bias_plane, bias_in.at[k - 1], peers[name]) for k, name in sides]
    end_low.wait_recv()
    end_high.wait_recv()
    add_into(gff.at[0], rows(0, 0, half), rfx)
    add_into(gff.at[0], rows(0, half, half), rfy)
    quarter = feat // 2
    keep_at = pl.ds(pl.multiple_of(dp * quarter, 16), quarter)
    give_at = pl.ds(pl.multiple_of((1 - dp) * quarter, 16), quarter)
    done = [keep(gff.at[0, keep_at], ff_out.at[0])]
    pair_sends = [send(gff.at[0, give_at], ff_out.at[1], peers["core"])]
    for copy in plane_sends + sum_sends:
        copy.wait_recv()
    bias_out[0] = bias_plane[...] + bias_in[0] + bias_in[1] + bias_in[2]
    pair_sends.append(send(bias_out.at[0], bias_out.at[1], peers["core"]))
    total = terms_mine[0]
    for i in range(7):
        total = total + sums_in[i]
    sums_out[...] = total
    sums_out[7:8, :] = total[6:7] / (count_ref[0:1, 0:1] * depth)
    attn_ring(0)
    done.append(keep(gattn.at[0, keep_at], attn_out.at[0]))
    pair_sends.append(send(gattn.at[0, give_at], attn_out.at[1], peers["core"]))
    for copy in pair_sends:
        copy.wait_recv()
    for copy in done:
        copy.wait()
    result_move.arrive()
    grad_move.arrive()
    for copy in send.copies:
        if copy is not swap1:
            copy.wait_send()
    result_move.finish()
    grad_move.finish()


def backward_call(arrays, feat, lanes, main, qkv, mix, own, depth):
    tokens = 2 * own
    half = feat // 2
    narrow = qkv + main + 128
    anywhere = pl.BlockSpec(memory_space=pl.ANY)
    local = pl.BlockSpec(memory_space=pltpu.VMEM)
    shapes = [
        ((2, feat, tokens), BF16, anywhere),
        ((2, feat, tokens), BF16, anywhere),
        ((8, feat), F32, local),
        ((2, 8, narrow), F32, local),
        ((2, half, lanes), BF16, anywhere),
        ((2, half, 2 * main), BF16, anywhere),
    ]
    return pl.pallas_call(
        backward_kernel,
        out_shape=[jax.ShapeDtypeStruct(shape, dtype) for shape, dtype, _ in shapes],
        in_specs=[local] + [anywhere] * 4 + [local] + [anywhere] * 2 + [local] * 2 + [anywhere] * 12,
        out_specs=[spec for _, _, spec in shapes],
        scratch_shapes=[
            pltpu.VMEM((depth, 256), BF16),
            pltpu.VMEM((tokens, 128), BF16),
            pltpu.VMEM((tokens, 128), BF16),
            pltpu.VMEM((8, 1, tokens), F32),
            pltpu.VMEM((lanes, qkv + mix), BF16),
            pltpu.VMEM((4, 128, 256), BF16),
            pltpu.VMEM((own, depth), BF16),
            pltpu.VMEM((depth, own), BF16),
            pltpu.VMEM((6, 16, depth), F32),
            pltpu.VMEM((4, 8, feat), F32),
            pltpu.VMEM((3, 8, feat), F32),
            pltpu.VMEM((7, 8, feat), F32),
            pltpu.VMEM((4, 8, narrow), F32),
            pltpu.VMEM((3, 8, narrow), F32),
            pltpu.VMEM((3, 8, narrow), F32),
            pltpu.VMEM((8, narrow), F32),
            pltpu.VMEM((4, 1, main), F32),
            pltpu.VMEM((1, 128), F32),
            pltpu.VMEM((4, 1, qkv), F32),
            pltpu.VMEM((4, depth, lanes), BF16),
            pltpu.VMEM((4, depth, 2 * main), BF16),
            pltpu.VMEM((2, depth, 2 * main), BF16),
            pltpu.VMEM((2, tokens, qkv + mix), BF16),
            pltpu.VMEM((tokens, main), BF16),
            pltpu.VMEM((depth, 256), BF16),
            pltpu.VMEM((depth, tokens), BF16),
            pltpu.VMEM((depth, tokens), BF16),
            pltpu.VMEM((tokens, depth), BF16),
            pltpu.VMEM((tokens, depth), F32),
            pltpu.VMEM((own, depth), BF16),
            pltpu.VMEM((own, depth), BF16),
            pltpu.VMEM((own, depth), F32),
            pltpu.VMEM((tokens, qkv), BF16),
            pltpu.VMEM((tokens, mix), BF16),
            pltpu.VMEM((tokens, 128), F32),
            pltpu.VMEM((tokens, 128), F32),
            pltpu.VMEM((1, tokens), F32),
            pltpu.VMEM((4, half, lanes), BF16),
            pltpu.VMEM((4, half, lanes), BF16),
            pltpu.VMEM((4, feat, lanes), BF16),
            pltpu.VMEM((4, feat, lanes), BF16),
            pltpu.VMEM((3, feat, lanes), BF16),
            pltpu.VMEM((4, 2, half, 2 * main), BF16),
            pltpu.VMEM((4, 2, half, 2 * main), BF16),
            pltpu.VMEM((3, 2, half, 2 * main), BF16),
            pltpu.VMEM((3, 2, half, 2 * main), BF16),
            pltpu.VMEM((half, 2 * main), BF16),
            pltpu.VMEM((half, 2 * main), BF16),
            pltpu.SemaphoreType.DMA((48,)),
            pltpu.SemaphoreType.DMA((104,)),
            pltpu.SemaphoreType.DMA((104,)),
            pltpu.SemaphoreType.DMA((5, 4)),
        ],
        compiler_params=pltpu.CompilerParams(
            collective_id=2, has_side_effects=True, vmem_limit_bytes=63 << 20
        ),
    )(*arrays)
def on_chip(
    layer_input,
    teacher,
    valid,
    proj_in,
    bias_query,
    bias_value,
    proj_out,
    bias_out,
    norm1_gain,
    norm1_shift,
    norm2_gain,
    norm2_shift,
    w_up,
    bias_up,
    w_down,
    bias_down,
):
    core = lax.axis_index("dp")
    first = core == 0
    cols = lax.axis_size("col")
    feat = layer_input.shape[1]
    images = layer_input.shape[0] // SEQ
    half_seq = (SEQ + 255) // 256 * 128
    pad_seq = 2 * half_seq
    units = w_up.shape[1] // 2
    width = proj_out.shape[0] // 2
    heads = width // HD
    main = units // 128 * 128
    rest = units - main
    at = 4 * width
    lanes = (at + 2 * rest + 127) // 128 * 128
    qkv, mix = 3 * heads * 128, heads * 128

    def core_half(values, axis):
        low, high = jnp.split(values, 2, axis=axis)
        return jnp.where(first, low, high)

    def pieces(values):
        turned = values.T
        second = turned[:, SEQ:]
        return turned, jnp.pad(second, ((0, 0), (0, pad_seq - SEQ)))

    up_half, down_half = core_half(w_up, 1), core_half(w_down, 0).T
    attn_shard = jnp.concatenate(
        [
            core_half(proj_in, 1),
            core_half(proj_out, 0).T,
            up_half[:, main:],
            down_half[:, main:],
            jnp.zeros((feat, lanes - at - 2 * rest), jnp.bfloat16),
        ],
        axis=1,
    )
    ff_shard = jnp.concatenate([up_half[:, :main], down_half[:, :main]], axis=1)
    lane = np.arange(lanes)
    spread_at = np.where(lane < at, lane // HD * 128 + lane % HD, -1)
    spread = jnp.asarray(spread_at[:, None] == np.arange(qkv + mix), jnp.bfloat16)
    tail = lane[-128:]
    part = np.arange(cols)[:, None]
    up_at = np.where((tail >= at) & (tail < at + rest), tail - at + part * rest, -1)
    down_at = np.where(
        (tail >= at + rest) & (tail < at + 2 * rest), tail - at - rest + part * rest + 128, -1
    )
    spot = np.arange(256)
    rest_spread = (up_at[..., None] == spot) | (down_at[..., None] == spot)
    rest_spread = jnp.asarray(rest_spread, jnp.bfloat16)

    key_lane = jnp.asarray(np.arange(qkv) % 384 == 128 + HD, jnp.float32)[None]

    one_lane = jnp.asarray(np.arange(qkv) % 384 == HD, jnp.float32)[None]
    source = np.arange(2 * width)
    bias_at = source % width // HD * 384 + source // width * 256 + source % HD
    bias_spread = jnp.asarray(bias_at[:, None] == np.arange(qkv), jnp.bfloat16)
    wide = (6 * feat + 127) // 128 * 128
    narrow = (2 * width + units + 127) // 128 * 128
    vectors = [
        (0, norm1_gain),
        (feat, norm1_shift),
        (2 * feat, norm2_gain),
        (3 * feat, norm2_shift),
        (4 * feat, bias_out),
        (5 * feat, bias_down),
        (wide, core_half(bias_query, 0)),
        (wide + width, core_half(bias_value, 0)),
        (wide + 2 * width, core_half(bias_up, 0)),
    ]
    params = jnp.zeros((8, wide + narrow), jnp.float32)
    for start, vector in vectors:
        size = vector.shape[0]
        row_of = jnp.broadcast_to(vector.astype(jnp.float32)[None], (8, size))
        params = params + jnp.pad(row_of, ((0, 0), (start, wide + narrow - start - size)))
    valid_rows = jnp.pad(valid.reshape(images, SEQ), ((0, 0), (0, pad_seq - SEQ)))
    valid_rows = jnp.broadcast_to(valid_rows.astype(jnp.float32)[:, None], (images, 8, pad_seq))
    sizes = (feat, lanes, main, qkv, mix, half_seq, 4 * feat)
    (
        wpad, wff, triple, mixed, act, slope, norm1t, norm2t, rest_weight, lse, act_rest,
        slope_rest, resid1, x_rows, branch2, branch2t, result, err_rows, features, counted,
    ) = forward_call(
        (
            *pieces(layer_input), *pieces(teacher), valid_rows, params, key_lane, one_lane, bias_spread, spread, rest_spread, attn_shard, ff_shard,
        ),
        layer_input.shape[0],
        *sizes,
    )
    grad_pieces, result_pieces, sums, bias_rows, attn_sum, ff_sum = backward_call(
        (
            branch2, rest_weight, act_rest, slope_rest, lse, features, spread, rest_spread,
            err_rows, counted, result, x_rows, resid1, norm1t, norm2t, branch2t, wpad,
            wff, triple, mixed, act, slope,
        ),
        *sizes,
    )

    def rows_of(values):
        return jnp.concatenate([values[i][:, :SEQ] for i in range(images)], axis=1).T

    def both(keep, got, axis=-1):
        return jnp.concatenate(
            [jnp.where(first, keep, got), jnp.where(first, got, keep)], axis=axis
        ).astype(jnp.float32)

    def up_of(i):
        return jnp.concatenate([ff_sum[i][:, :main], attn_sum[i][:, at : at + rest]], axis=1)

    def down_of(i):
        block = [ff_sum[i][:, main:], attn_sum[i][:, at + rest : at + 2 * rest]]
        return jnp.concatenate(block, axis=1).T

    main_rows = jnp.sum(bias_rows[:, :cols, : qkv + main], axis=1)
    head_rows = main_rows[:, :qkv].reshape(2, heads, 3, 128)[..., :HD]
    tail_rows = bias_rows[:, :cols, qkv + main :]
    tail_rows = sum(tail_rows[:, s, s * rest : (s + 1) * rest] for s in range(cols))
    unit_rows = jnp.concatenate([main_rows[:, qkv:], tail_rows], axis=1)
    return (
        rows_of(result_pieces),
        sums[7, 0],
        rows_of(grad_pieces).astype(jnp.float32),
        both(attn_sum[0][:, : 3 * width], attn_sum[1][:, : 3 * width])[None],
        both(head_rows[0, :, 0].reshape(width), head_rows[1, :, 0].reshape(width)),
        both(head_rows[0, :, 2].reshape(width), head_rows[1, :, 2].reshape(width)),
        both(attn_sum[0][:, 3 * width : at].T, attn_sum[1][:, 3 * width : at].T, 0)[:, None],
        sums[4],
        sums[0],
        sums[1],
        sums[2],
        sums[3],
        both(up_of(0), up_of(1))[None],
        both(unit_rows[0], unit_rows[1]),
        both(down_of(0), down_of(1), 0)[:, None],
        sums[5],
    )


def one_image_a_chip(mesh, tokens):
    sizes = mesh.shape
    pairs = sizes["dp"] == 2 and sizes["row"] == 4 and sizes["col"] == 4
    return pairs and tokens == SEQ * sizes["row"] * sizes["col"]


def solution(mesh):
    placed = (
        P(("dp", "col"), "row"),
        P(("dp", "col"), "row"),
        P(("dp", "col")),
        P("row", "col"),
        P("col"),
        P("col"),
        P("col", "row"),
        P("row"),
        P("row"),
        P("row"),
        P("row"),
        P("row"),
        P("row", "col"),
        P("col"),
        P("col", "row"),
        P("row"),
    )
    returned = (
            P(("dp", "col"), "row"),
            P(),
            P(("dp", "col"), "row"),
            P("row", "dp", "col"),
            P("col"),
            P("col"),
            P("col", "row", "dp"),
            P("row"),
            P("row"),
            P("row"),
            P("row"),
            P("row"),
            P("row", "dp", "col"),
            P("col"),
            P("col", "row", "dp"),
            P("row"),
        )

    def whole(layer_input, *others):
        body = on_chip if one_image_a_chip(mesh, layer_input.shape[0]) else on_device
        return jax.shard_map(
            body, mesh=mesh, in_specs=placed, out_specs=returned, check_vma=False
        )(layer_input, *others)

    return whole
```
